32 devices in a mesh: ctx: 8 (over y, x, core), fsdp: 4 (over z).
Axes of the slice: x: 2, y: 2, z: 4, core: 2. Of those that a mesh axis runs over, the one named last changes fastest.
Arguments:
- hidden: bfloat16 [4, 2, 2048, 768], P('fsdp', None, 'ctx'), may hold values from -6 to 6
- noise_mask: int32 [4, 2048], P('fsdp', 'ctx'), may hold values 0 or 1
- doc_lengths: int32 [4, 16], P('fsdp'), may hold values from 1 to 1024, 2048 in all within a row
- w_qkv: bfloat16 [768, 2304], P('fsdp'), may hold values from -0.21875 to 0.21875
- w_out: bfloat16 [768, 768], P('fsdp'), may hold values from -1.25 to 1.25
- w_up: bfloat16 [768, 3072], P('fsdp'), may hold values from -0.21875 to 0.21875
- b_up: bfloat16 [3072], P('fsdp'), may hold values from -3 to 3
- w_down: bfloat16 [3072, 768], P('fsdp'), may hold values from -0.109375 to 0.109375
- b_down: bfloat16 [768], P('fsdp'), may hold values from -2 to 2
- gain_one: bfloat16 [768], P('fsdp'), may hold values from 0.25 to 1.75
- gain_two: bfloat16 [768], P('fsdp'), may hold values from 0.25 to 1.75
- mask_embed: bfloat16 [768], P('fsdp'), may hold values from -5 to 5
- out_grad: bfloat16 [4, 2, 2048, 768], P('fsdp', None, 'ctx'), may hold values from -6 to 6
Outputs:
- layer_out: bfloat16 [4, 2, 2048, 768], P('fsdp', None, 'ctx')
- input_grad: bfloat16 [4, 2, 2048, 768], P('fsdp', None, 'ctx')
- grad_qkv: float32 [768, 2304], P(('ctx', 'fsdp'))
- grad_out: float32 [768, 768], P(('ctx', 'fsdp'))
- grad_up: float32 [768, 3072], P(('ctx', 'fsdp'))
- grad_up_bias: float32 [3072], P(('ctx', 'fsdp'))
- grad_down: float32 [3072, 768], P(('ctx', 'fsdp'))
- grad_down_bias: float32 [768], P(('ctx', 'fsdp'))
- grad_gain_one: float32 [768], P(('ctx', 'fsdp'))
- grad_gain_two: float32 [768], P(('ctx', 'fsdp'))
- grad_mask_embed: float32 [768], P(('ctx', 'fsdp'))
The draws below stay inside these ranges and needn't reach their ends.
Inputs may be any that keep to these rules, and one draw needn't show every extreme that they name: Each row of doc_lengths sums to 2048, and its longest document has exactly 1024 positions.
All inputs are finite; a program needn't handle non-finite values. No bound on the sum of `noise_mask` on one device may be relied on, other than what follows from the above.
Results may differ from the reference program's by a relative error of at most 0.015.
Values may be sent and summed in bfloat16 or wider, within the bound.
No kernel may reach another device: no remote copies, remote signals or barrier semaphores. Data moves between devices by JAX's collectives and lax.ppermute only.
A program may use at most 256 MiB of HBM per device.

```python
import math
import jax
import jax.numpy as jnp
import numpy as np
from jax import lax

D = 768
HEADS = 12
HEAD_DIM = 64
FF = 3072
BLOCK = 16
DOCS = 16
SEQS = 4
POSITIONS = 2048


def plant(drawn, rng, smallest, top_value):
    longest = drawn.shape.index(max(drawn.shape))
    spots = []
    for shift in (0, 1):
        where = [jax.random.randint(jax.random.fold_in(rng, axis), (), 0, length) for axis, length in enumerate(drawn.shape)]
        where[longest] = (where[longest] + shift) % drawn.shape[longest]
        spots.append(tuple(where))
    return drawn.at[spots[0]].set(smallest).at[spots[1]].set(top_value)


def spiked(drawn, rng, source, target, parts, factor):
    owner, partner = [(jnp.arange(drawn.shape[dim]) // (drawn.shape[dim] // parts)).reshape([-1 if axis == dim else 1 for axis in range(drawn.ndim)]) for dim in (source, target)]
    chosen = jax.random.permutation(rng, parts)[partner]
    strong = (owner == chosen) | (owner == (partner + parts // 2) % parts)
    return jnp.where(strong, factor * drawn, drawn)


def levels(stream_key, extent, shards, least, high):
    def one(dim, blocks):
        steps = jax.random.uniform(jax.random.fold_in(jax.random.fold_in(stream_key, 6), dim), (blocks,), jnp.float32, least / len(shards), high / len(shards))
        return jnp.repeat(jnp.exp(steps), extent[dim] // blocks).reshape((-1,) + (1,) * (len(extent) - dim - 1))

    factor_of = one(*shards[0])
    for cut in shards[1:]:
        factor_of = factor_of * one(*cut)
    return factor_of


def length_profile(count, total, most, slope):
    portions = [(1 << 20) // math.isqrt(grade ** slope) + 1 for grade in range(2, count + 1)]
    spare, given = total - most - (count - 1), [1] * (count - 1)
    while spare > 0:
        candidates = [i for i in range(count - 1) if given[i] < most]
        mass, budget = sum([portions[i] for i in candidates]), spare
        for i in candidates:
            addition = min(most - given[i], max(1, budget * portions[i] // mass), spare)
            given[i] = given[i] + addition
            spare = spare - addition
    return np.array([most] + given)


def uneven(stream_key, amount, total, limit, slope):
    if amount == 2:
        one = jax.random.randint(stream_key, (), max(1, total - limit), min(limit, total - 1) + 1)
        return jnp.stack([one, total - one])
    lengths = jnp.asarray(length_profile(amount, total, limit, slope), jnp.int32)
    twos = (amount - 1) // 2
    donor, receiver = lengths[1:1 + 2 * twos:2], lengths[2:2 + 2 * twos:2]
    room = jnp.minimum(donor - 1, limit - receiver)
    shifted = jax.random.randint(jax.random.fold_in(stream_key, 1), (twos,), 0, 1 << 20) % (room + 1)
    lengths = lengths.at[1:1 + 2 * twos:2].set(donor - shifted).at[2:2 + 2 * twos:2].set(receiver + shifted)
    return lengths[jax.random.permutation(jax.random.fold_in(stream_key, 2), amount)]


def normal_values(own_key, extent, scale, reach, shards=(), kind=jnp.bfloat16):
    entries = scale * jax.random.normal(own_key, extent, jnp.float32)
    if shards:
        entries = entries * levels(own_key, extent, shards, -0.22, 0.18)
    return jnp.clip(entries, -reach, reach).astype(kind)


def noise_with(key, shape, deviation, limit, split, heavy, dtype=jnp.bfloat16):
    array = deviation * jax.random.normal(key, shape, jnp.float32)
    if split:
        array = array * levels(key, shape, split, -0.22, 0.18)
    return jnp.clip(spiked(array, jax.random.fold_in(key, 3), *heavy), -limit, limit).astype(dtype)


def setup_inputs(seed: int = 0) -> dict:
    key_of = jax.random.split(jax.random.key(seed), 14)
    hidden = normal_values(key_of[0], (SEQS, 2, POSITIONS, D), 1.0, 6.0, ((0, 4), (2, 8)))
    noise_mask = plant((jax.random.randint(key_of[1], (SEQS, POSITIONS), 0, 2) < 1).astype(jnp.int32), jax.random.fold_in(key_of[1], 1), 0, 1)
    doc_lengths = jax.vmap(lambda own: uneven(own, DOCS, POSITIONS, POSITIONS // 2, 2))(jax.random.split(key_of[2], SEQS)).reshape((SEQS, DOCS)).astype(jnp.int32)
    w_qkv = normal_values(key_of[3], (D, 3 * D), D ** -0.5, 0.21875, ((0, 4),))
    w_out = normal_values(key_of[4], (D, D), (D // 32) ** -0.5, 1.25, ((0, 4),))
    w_up = normal_values(key_of[5], (D, FF), D ** -0.5, 0.21875, ((0, 4),))
    b_up = normal_values(key_of[6], (FF,), 0.5, 3.0, ((0, 4),))
    w_down = normal_values(key_of[7], (FF, D), FF ** -0.5, 0.109375, ((0, 4),))
    b_down = normal_values(key_of[8], (D,), 0.3, 2.0, ((0, 4),))
    gain_one = jnp.clip(1.0 + 0.15 * jax.random.normal(key_of[9], (D,), jnp.float32), 0.25, 1.75).astype(jnp.bfloat16)
    gain_two = jnp.clip(1.0 + 0.15 * jax.random.normal(key_of[10], (D,), jnp.float32), 0.25, 1.75).astype(jnp.bfloat16)
    mask_embed = normal_values(key_of[11], (D,), 1.0, 5.0, ((0, 4),))
    out_grad = noise_with(key_of[12], (SEQS, 2, POSITIONS, D), 1.0, 6.0, ((0, 4), (2, 8)), (2, 3, 8, 2.0))
    return dict(hidden=hidden, noise_mask=noise_mask, doc_lengths=doc_lengths, w_qkv=w_qkv, w_out=w_out, w_up=w_up, b_up=b_up, w_down=w_down, b_down=b_down, gain_one=gain_one, gain_two=gain_two, mask_embed=mask_embed, out_grad=out_grad)


@jax.custom_vjp
def low(v):
    return lax.optimization_barrier(v.astype(jnp.bfloat16)).astype(jnp.float32)

@jax.custom_vjp
def low_back(v):
    return v

def low_keep(v):
    return (low(v), None)

def low_pass(kept, grad):
    return (grad,)

def back_keep(v):
    return (v, None)

def back_low(kept, grad):
    return (low(grad),)
low.defvjp(low_keep, low_pass)
low_back.defvjp(back_keep, back_low)
LOWEST = -1e+30
EPSILON = 1e-05
PRECISE = lax.Precision.HIGHEST

def layer_norm(inputs, gain):
    average = lax.optimization_barrier(jnp.mean(inputs, axis=-1, keepdims=True))
    centered = inputs - average
    variance = lax.optimization_barrier(jnp.mean(centered * centered, axis=-1, keepdims=True))
    return centered * lax.rsqrt(variance + EPSILON) * gain

def rotary_angles(positions):
    half_dim = HEAD_DIM // 2
    frequency = jnp.exp(jnp.arange(half_dim).astype(jnp.float32) * (-2.0 * math.log(10000.0) / HEAD_DIM))
    return positions.astype(jnp.float32)[:, None] * frequency[None, :]

def rotate(heads_in, angles):
    half_dim = heads_in.shape[-1] // 2
    cosine = jnp.cos(angles)[:, None, :]
    sine_part = jnp.sin(angles)[:, None, :]
    first_half = heads_in[..., :half_dim]
    second_half = heads_in[..., half_dim:]
    return jnp.concatenate([first_half * cosine - second_half * sine_part, second_half * cosine + first_half * sine_part], axis=-1)

def segment_of(positions, doc_ends):
    return lax.optimization_barrier(jnp.sum((positions[:, None] >= doc_ends[None, :]).astype(jnp.int32), axis=1))

def visible(query_stream, query_position, query_segment, key_stream, key_position, key_segment):
    query_block = query_position // BLOCK
    key_block = key_position // BLOCK
    same_doc = query_segment[:, None] == key_segment[None, :]
    clean_key = key_stream[None, :] == 0
    noisy_query = query_stream[:, None] == 1
    before = key_block[None, :] < query_block[:, None]
    same_block = key_block[None, :] == query_block[:, None]
    from_clean = clean_key & (before | same_block & jnp.logical_not(noisy_query))
    from_noisy = jnp.logical_not(clean_key) & noisy_query & same_block
    return same_doc & (from_clean | from_noisy)

def attend(query_rows, key_rows, value_rows, stream, positions, segments):
    row_count = query_rows.shape[0]
    tile_size = math.gcd(row_count, 512)
    tile_count = row_count // tile_size

    def one_tile(tile_items):
        tile_query, tile_stream, tile_position, tile_segment = tile_items
        scores = low_back(jnp.einsum('qhd,khd->hqk', tile_query, key_rows, precision=PRECISE) * 0.125)
        allowed = visible(tile_stream, tile_position, tile_segment, stream, positions, segments)[None]
        masked = jnp.where(allowed, scores, LOWEST)
        row_max = lax.optimization_barrier(jnp.max(masked, axis=-1, keepdims=True))
        exp_terms = jnp.where(allowed, jnp.exp(masked - row_max), 0.0)
        row_sum = lax.optimization_barrier(jnp.sum(exp_terms, axis=-1, keepdims=True))
        unscaled = low_back(jnp.einsum('hqk,khd->hqd', low(exp_terms), value_rows, precision=PRECISE))
        attended = unscaled / row_sum
        return jnp.transpose(attended, (1, 0, 2)).reshape(tile_size, HEADS * HEAD_DIM)
    blocks = lax.map(jax.checkpoint(one_tile), (query_rows.reshape(tile_count, tile_size, HEADS, HEAD_DIM), stream.reshape(tile_count, tile_size), positions.reshape(tile_count, tile_size), segments.reshape(tile_count, tile_size)))
    return blocks.reshape(row_count, HEADS * HEAD_DIM)

def forward(weights_in, hidden_in, noise_row, stream, positions, segments):
    w_qkv, w_out, w_up, b_up, w_down, b_down, gain_one, gain_two, mask_embed = weights_in
    clean_rows = hidden_in[0]
    noisy_rows = jnp.where(noise_row[:, None] == 1, mask_embed[None, :], hidden_in[1])
    inputs = jnp.concatenate([clean_rows, noisy_rows], axis=0)
    row_count = inputs.shape[0]
    normed = low(layer_norm(inputs, gain_one))
    projected = low_back(jnp.dot(normed, w_qkv, precision=PRECISE))
    angles = rotary_angles(positions)
    query_rows = low(rotate(projected[:, :D].reshape(row_count, HEADS, HEAD_DIM), angles))
    key_rows = low(rotate(projected[:, D:2 * D].reshape(row_count, HEADS, HEAD_DIM), angles))
    value_rows = low(projected[:, 2 * D:].reshape(row_count, HEADS, HEAD_DIM))
    attended = attend(query_rows, key_rows, value_rows, stream, positions, segments)
    middle = low_back(inputs + jnp.dot(low(attended), w_out, precision=PRECISE))
    upper = low_back(jnp.dot(low(layer_norm(middle, gain_two)), w_up, precision=PRECISE) + b_up)
    activated = low(jax.nn.gelu(upper, approximate=True))
    return middle + jnp.dot(activated, w_down, precision=PRECISE) + b_down

def reference(hidden, noise_mask, doc_lengths, w_qkv, w_out, w_up, b_up, w_down, b_down, gain_one, gain_two, mask_embed, out_grad):
    weights_in = tuple((weight.astype(jnp.float32) for weight in (w_qkv, w_out, w_up, b_up, w_down, b_down, gain_one, gain_two, mask_embed)))
    place = jnp.arange(POSITIONS).astype(jnp.int32)
    positions = jnp.concatenate([place, place])
    stream = jnp.concatenate([jnp.zeros((POSITIONS,), jnp.int32), jnp.ones((POSITIONS,), jnp.int32)])

    def one_sequence(totals, seq_items):
        hidden_seq, noise_row, length_row, grad_seq = seq_items
        doc_ends = jnp.cumsum(length_row).astype(jnp.int32)
        segments = segment_of(positions, doc_ends)
        outputs, pullback = jax.vjp(lambda weights_arg, hidden_arg: forward(weights_arg, hidden_arg, noise_row, stream, positions, segments), weights_in, hidden_seq.astype(jnp.float32))
        weight_grads, hidden_grad = pullback(grad_seq.astype(jnp.float32).reshape(2 * POSITIONS, D))
        totals = tuple((earlier + later for earlier, later in zip(totals, weight_grads)))
        return (totals, (outputs.reshape(2, POSITIONS, D).astype(jnp.bfloat16), hidden_grad.astype(jnp.bfloat16)))
    zero_grads = tuple((jnp.zeros_like(weight) for weight in weights_in))
    totals, (layer_out, input_grad) = lax.scan(one_sequence, zero_grads, (hidden, noise_mask, doc_lengths, out_grad))
    return (layer_out, input_grad, totals[0], totals[1], totals[2], totals[3], totals[4], totals[5], totals[6], totals[7], totals[8])
```

```python
import functools
import math

import jax
import jax.numpy as jnp
from jax import lax
from jax.experimental import pallas as pl
from jax.experimental.pallas import tpu as pltpu
from jax.sharding import PartitionSpec as P

HEADS = 12
HEAD_DIM = 64
BLOCK = 16


LOWEST = -1e30
EPSILON = 1e-05


def layer_norm(inputs, gain):
    average = jnp.mean(inputs, axis=-1, keepdims=True)
    centered = inputs - average
    variance = jnp.mean(centered * centered, axis=-1, keepdims=True)
    return centered * lax.rsqrt(variance + EPSILON) * gain


def rotary_angles(positions):
    half_dim = HEAD_DIM // 2
    frequency = jnp.exp(
        jnp.arange(half_dim).astype(jnp.float32) * (-2.0 * math.log(10000.0) / HEAD_DIM)
    )
    return positions.astype(jnp.float32)[:, None] * frequency[None, :]


def rotate(heads_in, angles):
    half_dim = heads_in.shape[-1] // 2
    cosine = jnp.cos(angles)[:, None, :]
    sine_part = jnp.sin(angles)[:, None, :]
    first_half = heads_in[..., :half_dim]
    second_half = heads_in[..., half_dim:]
    return jnp.concatenate(
        [
            first_half * cosine - second_half * sine_part,
            second_half * cosine + first_half * sine_part,
        ],
        axis=-1,
    )


def segment_of(positions, doc_ends):
    return jnp.sum((positions[:, None] >= doc_ends[None, :]).astype(jnp.int32), axis=1)


def visible(query_stream, query_position, query_segment, key_stream, key_position, key_segment):
    query_block = query_position // BLOCK
    key_block = key_position // BLOCK
    same_doc = query_segment[:, None] == key_segment[None, :]
    clean_key = key_stream[None, :] == 0
    noisy_query = query_stream[:, None] == 1
    before = key_block[None, :] < query_block[:, None]
    same_block = key_block[None, :] == query_block[:, None]
    from_clean = clean_key & (before | same_block & jnp.logical_not(noisy_query))
    from_noisy = jnp.logical_not(clean_key) & noisy_query & same_block
    return same_doc & (from_clean | from_noisy)


def mix_tile(running, query_rows, key_tile, value_tile, allowed):
    run_max, run_sum, accum = running
    scores = (
        jnp.einsum("qhd,khd->hqk", query_rows, key_tile, preferred_element_type=jnp.float32) * 0.125
    )
    masked = jnp.where(allowed[None], scores, LOWEST)
    new_max = jnp.maximum(run_max, jnp.max(masked, axis=-1))
    exp_terms = jnp.where(allowed[None], jnp.exp(masked - new_max[..., None]), 0.0)
    factor = jnp.exp(run_max - new_max)
    new_sum = run_sum * factor + jnp.sum(exp_terms, axis=-1)
    accum = accum * factor[..., None] + jnp.einsum(
        "hqk,khd->hqd",
        exp_terms.astype(jnp.bfloat16),
        value_tile,
        preferred_element_type=jnp.float32,
    )
    return (new_max, new_sum, accum)


def tile_grads(query_rows, key_tile, value_tile, allowed, row_max, scaled_grad, correction):
    scores = (
        jnp.einsum("qhd,khd->hqk", query_rows, key_tile, preferred_element_type=jnp.float32) * 0.125
    )
    masked = jnp.where(allowed[None], scores, LOWEST)
    exp_terms = jnp.where(allowed[None], jnp.exp(masked - row_max[..., None]), 0.0)
    prob_grad = jnp.einsum(
        "hqd,khd->hqk", scaled_grad, value_tile, preferred_element_type=jnp.float32
    )
    score_grad = (exp_terms * (prob_grad - correction[..., None])).astype(jnp.bfloat16)
    query_part = jnp.einsum(
        "hqk,khd->qhd", score_grad, key_tile, preferred_element_type=jnp.float32
    )
    key_part = jnp.einsum(
        "hqk,qhd->khd", score_grad, query_rows, preferred_element_type=jnp.float32
    )
    value_part = jnp.einsum(
        "hqk,hqd->khd",
        exp_terms.astype(jnp.bfloat16),
        scaled_grad,
        preferred_element_type=jnp.float32,
    )
    return (query_part, key_part, value_part)


def build_inputs(hidden, noise_row, mask_row):
    clean_rows = hidden[0, 0].astype(jnp.float32)
    noisy_rows = jnp.where(
        noise_row[:, None] == 1,
        mask_row.astype(jnp.float32)[None, :],
        hidden[0, 1].astype(jnp.float32),
    )
    return jnp.concatenate([clean_rows, noisy_rows], axis=0)


def project(inputs, gathered, angles):
    row_count = inputs.shape[0]
    model_dim = inputs.shape[1]
    normed = layer_norm(inputs, gathered[6].astype(jnp.float32)).astype(jnp.bfloat16)
    projected = jnp.dot(normed, gathered[0], preferred_element_type=jnp.float32)
    query_rows = rotate(
        projected[:, :model_dim].reshape(row_count, HEADS, HEAD_DIM), angles
    ).astype(jnp.bfloat16)
    key_rows = rotate(
        projected[:, model_dim : 2 * model_dim].reshape(row_count, HEADS, HEAD_DIM), angles
    ).astype(jnp.bfloat16)
    value_rows = (
        projected[:, 2 * model_dim :].reshape(row_count, HEADS, HEAD_DIM).astype(jnp.bfloat16)
    )
    return (normed, query_rows, key_rows, value_rows)


def upper_half(inputs, attended_low, gathered):
    middle = inputs + jnp.dot(attended_low, gathered[1], preferred_element_type=jnp.float32)
    normed_two = layer_norm(middle, gathered[7].astype(jnp.float32)).astype(jnp.bfloat16)
    upper = jnp.dot(normed_two, gathered[2], preferred_element_type=jnp.float32) + gathered[
        3
    ].astype(jnp.float32)
    activated = jax.nn.gelu(upper, approximate=True).astype(jnp.bfloat16)
    return (middle, normed_two, upper, activated)


def shards(
    hidden,
    noise_mask,
    doc_lengths,
    w_qkv,
    w_out,
    w_up,
    b_up,
    w_down,
    b_down,
    gain_one,
    gain_two,
    mask_embed,
    out_grad,
):
    own_params = (w_qkv, w_out, w_up, b_up, w_down, b_down, gain_one, gain_two, mask_embed)
    local_count = hidden.shape[2]
    model_dim = hidden.shape[3]
    row_count = 2 * local_count
    ctx_index = lax.axis_index("ctx")
    offset = ctx_index * local_count
    local_place = offset + jnp.arange(local_count, dtype=jnp.int32)
    positions = jnp.concatenate([local_place, local_place])
    stream = jnp.concatenate(
        [jnp.zeros((local_count,), jnp.int32), jnp.ones((local_count,), jnp.int32)]
    )
    doc_ends = jnp.cumsum(doc_lengths[0])
    segments = segment_of(positions, doc_ends)
    angles = rotary_angles(positions)
    noise_row = noise_mask[0]
    noisy_stream = stream[local_count:]
    noisy_allowed = visible(
        stream, positions, segments, noisy_stream, positions[local_count:], segments[local_count:]
    )
    gathered = (
        lax.all_gather(own_params[0], "fsdp", axis=0, tiled=True),
        lax.all_gather(own_params[1], "fsdp", axis=0, tiled=True),
        lax.all_gather(own_params[2], "fsdp", axis=0, tiled=True),
        lax.all_gather(own_params[3], "fsdp", axis=0, tiled=True),
        lax.all_gather(own_params[4], "fsdp", axis=0, tiled=True),
        lax.all_gather(own_params[5], "fsdp", axis=0, tiled=True),
        lax.all_gather(own_params[6], "fsdp", axis=0, tiled=True),
        lax.all_gather(own_params[7], "fsdp", axis=0, tiled=True),
        lax.all_gather(own_params[8], "fsdp", axis=0, tiled=True),
    )
    inputs = build_inputs(hidden, noise_row, gathered[8])
    normed, query_rows, key_rows, value_rows = project(inputs, gathered, angles)
    clean_keys = key_rows[:local_count].reshape(local_count, model_dim)
    clean_values = value_rows[:local_count].reshape(local_count, model_dim)
    start_state = (
        jnp.full((HEADS, row_count), LOWEST, jnp.float32),
        jnp.zeros((HEADS, row_count), jnp.float32),
        jnp.zeros((HEADS, row_count, HEAD_DIM), jnp.float32),
    )
    running = start_state
    piece_keys = lax.all_gather(clean_keys, "ctx", axis=0, tiled=True)
    piece_values = lax.all_gather(clean_values, "ctx", axis=0, tiled=True)
    piece_rows = piece_keys.shape[0]
    fold_tile_size = math.gcd(piece_rows, 512)

    def step(carried, tile_index):
        tile_start = tile_index * fold_tile_size
        key_tile = lax.dynamic_slice_in_dim(piece_keys, tile_start, fold_tile_size, 0).reshape(
            fold_tile_size, HEADS, HEAD_DIM
        )
        value_tile = lax.dynamic_slice_in_dim(piece_values, tile_start, fold_tile_size, 0).reshape(
            fold_tile_size, HEADS, HEAD_DIM
        )
        key_position = tile_start + jnp.arange(fold_tile_size, dtype=jnp.int32)
        allowed = visible(
            stream,
            positions,
            segments,
            jnp.zeros((fold_tile_size,), jnp.int32),
            key_position,
            segment_of(key_position, doc_ends),
        )
        carried = lax.cond(
            jnp.any(allowed),
            lambda held: mix_tile(held, query_rows, key_tile, value_tile, allowed),
            lambda held: held,
            carried,
        )
        return (carried, None)

    running, _ = lax.scan(step, running, jnp.arange(piece_rows // fold_tile_size))
    run_max, run_sum, accum = mix_tile(
        running, query_rows, key_rows[local_count:], value_rows[local_count:], noisy_allowed
    )
    attended = accum / run_sum[..., None]
    attended_low = (
        jnp.transpose(attended, (1, 0, 2)).reshape(row_count, model_dim).astype(jnp.bfloat16)
    )
    middle, normed_two, upper, activated = upper_half(inputs, attended_low, gathered)
    result = (
        middle
        + jnp.dot(activated, gathered[4], preferred_element_type=jnp.float32)
        + gathered[5].astype(jnp.float32)
    )
    layer_out = result.astype(jnp.bfloat16).reshape(1, 2, local_count, model_dim)
    again = (
        lax.all_gather(own_params[0], "fsdp", axis=0, tiled=True),
        lax.all_gather(own_params[1], "fsdp", axis=0, tiled=True),
        lax.all_gather(own_params[2], "fsdp", axis=0, tiled=True),
        lax.all_gather(own_params[3], "fsdp", axis=0, tiled=True),
        lax.all_gather(own_params[4], "fsdp", axis=0, tiled=True),
        lax.all_gather(own_params[5], "fsdp", axis=0, tiled=True),
        lax.all_gather(own_params[6], "fsdp", axis=0, tiled=True),
        lax.all_gather(own_params[7], "fsdp", axis=0, tiled=True),
        lax.all_gather(own_params[8], "fsdp", axis=0, tiled=True),
    )
    normed, query_rows, key_rows, value_rows = project(inputs, again, angles)
    noisy_keys = key_rows[local_count:]
    noisy_values = value_rows[local_count:]
    middle, normed_two, upper, activated = upper_half(inputs, attended_low, again)
    grad_rows = out_grad[0].reshape(row_count, model_dim)
    grad_float = grad_rows.astype(jnp.float32)
    grad_down = jnp.einsum("qi,qj->ij", activated, grad_rows, preferred_element_type=jnp.float32)
    grad_down_bias = jnp.sum(grad_float, axis=0)
    activated_grad = jnp.einsum(
        "qj,ij->qi", grad_rows, again[4], preferred_element_type=jnp.float32
    )
    _, gelu_pull = jax.vjp(lambda upper_in: jax.nn.gelu(upper_in, approximate=True), upper)
    upper_grad = gelu_pull(activated_grad)[0].astype(jnp.bfloat16)
    grad_up = jnp.einsum("qi,qj->ij", normed_two, upper_grad, preferred_element_type=jnp.float32)
    grad_up_bias = jnp.sum(upper_grad.astype(jnp.float32), axis=0)
    normed_two_grad = jnp.einsum(
        "qj,ij->qi", upper_grad, again[2], preferred_element_type=jnp.float32
    )
    _, second_pull = jax.vjp(layer_norm, middle, again[7].astype(jnp.float32))
    middle_norm_grad, grad_gain_two = second_pull(normed_two_grad)
    middle_grad = (grad_float + middle_norm_grad).astype(jnp.bfloat16)
    grad_out_proj = jnp.einsum(
        "qi,qj->ij", attended_low, middle_grad, preferred_element_type=jnp.float32
    )
    attended_grad = jnp.einsum(
        "qj,ij->qi", middle_grad, again[1], preferred_element_type=jnp.float32
    )
    attended_grad = jnp.transpose(attended_grad.reshape(row_count, HEADS, HEAD_DIM), (1, 0, 2))
    scaled_grad = (attended_grad / run_sum[..., None]).astype(jnp.bfloat16)
    correction = jnp.sum(attended_grad * attended, axis=-1) / run_sum
    pair_rows = (
        lax.all_gather(
            key_rows[:local_count].reshape(local_count, model_dim), "ctx", axis=0, tiled=True
        ),
        lax.all_gather(
            value_rows[:local_count].reshape(local_count, model_dim), "ctx", axis=0, tiled=True
        ),
    )
    pair_keys, pair_values = pair_rows
    total_rows = pair_keys.shape[0]
    tile_size = math.gcd(total_rows, 512)
    zero_tile = jnp.zeros((tile_size, HEADS, HEAD_DIM), jnp.float32)

    def back_step(query_acc, tile_index):
        tile_start = tile_index * tile_size
        key_tile = lax.dynamic_slice_in_dim(pair_keys, tile_start, tile_size, 0).reshape(
            tile_size, HEADS, HEAD_DIM
        )
        value_tile = lax.dynamic_slice_in_dim(pair_values, tile_start, tile_size, 0).reshape(
            tile_size, HEADS, HEAD_DIM
        )
        key_position = tile_start + jnp.arange(tile_size, dtype=jnp.int32)
        allowed = visible(
            stream,
            positions,
            segments,
            jnp.zeros((tile_size,), jnp.int32),
            key_position,
            segment_of(key_position, doc_ends),
        )

        def live_tile(held):
            query_part, key_part, value_part = tile_grads(
                query_rows, key_tile, value_tile, allowed, run_max, scaled_grad, correction
            )
            return (held + query_part, key_part, value_part)

        query_acc, key_part, value_part = lax.cond(
            jnp.any(allowed), live_tile, lambda held: (held, zero_tile, zero_tile), query_acc
        )
        return (
            query_acc,
            (key_part.reshape(tile_size, model_dim), value_part.reshape(tile_size, model_dim)),
        )

    query_acc, (key_terms, value_terms) = lax.scan(
        back_step,
        jnp.zeros((row_count, HEADS, HEAD_DIM), jnp.float32),
        jnp.arange(total_rows // tile_size),
    )
    key_terms = key_terms.reshape(total_rows, model_dim)
    value_terms = value_terms.reshape(total_rows, model_dim)
    clean_key_grad, clean_value_grad = (
        lax.psum_scatter(
            key_terms.astype(jnp.bfloat16), "ctx", scatter_dimension=0, tiled=True
        ).astype(jnp.float32),
        lax.psum_scatter(
            value_terms.astype(jnp.bfloat16), "ctx", scatter_dimension=0, tiled=True
        ).astype(jnp.float32),
    )
    query_part, noisy_key_part, noisy_value_part = tile_grads(
        query_rows, noisy_keys, noisy_values, noisy_allowed, run_max, scaled_grad, correction
    )
    query_grad = (query_acc + query_part) * 0.125
    key_grad = (
        jnp.concatenate(
            [clean_key_grad.reshape(local_count, HEADS, HEAD_DIM), noisy_key_part], axis=0
        )
        * 0.125
    )
    value_grad = jnp.concatenate(
        [clean_value_grad.reshape(local_count, HEADS, HEAD_DIM), noisy_value_part], axis=0
    )
    _, rotate_pull = jax.vjp(lambda heads_in: rotate(heads_in, angles), query_grad)
    query_raw_grad = rotate_pull(query_grad)[0]
    key_raw_grad = rotate_pull(key_grad)[0]
    projected_grad = jnp.concatenate(
        [
            query_raw_grad.reshape(row_count, model_dim),
            key_raw_grad.reshape(row_count, model_dim),
            value_grad.reshape(row_count, model_dim),
        ],
        axis=1,
    ).astype(jnp.bfloat16)
    grad_qkv = jnp.einsum("qi,qj->ij", normed, projected_grad, preferred_element_type=jnp.float32)
    normed_grad = jnp.einsum(
        "qj,ij->qi", projected_grad, again[0], preferred_element_type=jnp.float32
    )
    _, first_pull = jax.vjp(layer_norm, inputs, again[6].astype(jnp.float32))
    inputs_norm_grad, grad_gain_one = first_pull(normed_grad)
    inputs_grad = middle_grad.astype(jnp.float32) + inputs_norm_grad
    noisy_flag = (noise_row == 1)[:, None]
    noisy_grad = inputs_grad[local_count:]
    grad_mask = jnp.sum(jnp.where(noisy_flag, noisy_grad, 0.0), axis=0)
    input_grad = jnp.concatenate(
        [inputs_grad[:local_count], jnp.where(noisy_flag, 0.0, noisy_grad)], axis=0
    )
    input_grad = input_grad.astype(jnp.bfloat16).reshape(1, 2, local_count, model_dim)
    shares = (
        lax.psum_scatter(grad_qkv, ("ctx", "fsdp"), scatter_dimension=0, tiled=True),
        lax.psum_scatter(grad_out_proj, ("ctx", "fsdp"), scatter_dimension=0, tiled=True),
        lax.psum_scatter(grad_up, ("ctx", "fsdp"), scatter_dimension=0, tiled=True),
        lax.psum_scatter(grad_up_bias, ("ctx", "fsdp"), scatter_dimension=0, tiled=True),
        lax.psum_scatter(grad_down, ("ctx", "fsdp"), scatter_dimension=0, tiled=True),
        lax.psum_scatter(grad_down_bias, ("ctx", "fsdp"), scatter_dimension=0, tiled=True),
        lax.psum_scatter(grad_gain_one, ("ctx", "fsdp"), scatter_dimension=0, tiled=True),
        lax.psum_scatter(grad_gain_two, ("ctx", "fsdp"), scatter_dimension=0, tiled=True),
        lax.psum_scatter(grad_mask, ("ctx", "fsdp"), scatter_dimension=0, tiled=True),
    )
    (
        qkv_share,
        out_share,
        up_share,
        up_bias_share,
        down_share,
        down_bias_share,
        gain_one_share,
        gain_two_share,
        mask_share,
    ) = shares
    return (
        layer_out,
        input_grad,
        qkv_share,
        out_share,
        up_share,
        up_bias_share,
        down_share,
        down_bias_share,
        gain_one_share,
        gain_two_share,
        mask_share,
    )


CHUNK = 256
GROUP = 3
WIDE = GROUP * HEAD_DIM
HALF = HEAD_DIM // 2
LANES = GROUP * CHUNK
BF = jnp.bfloat16
F32 = jnp.float32
ANY = pl.BlockSpec(memory_space=pl.ANY)
VM = pl.BlockSpec(memory_space=pltpu.VMEM)
SM = pl.BlockSpec(memory_space=pltpu.SMEM)
GELU_SCALE = math.sqrt(2.0 / math.pi)


def swap(v, bit):
    return lax.ppermute(v, "ctx", [(i, i ^ bit) for i in range(8)])


def turn(v, step):
    return lax.ppermute(v, "fsdp", [(i, (i + step) % 4) for i in range(4)])


def mm(a, b, ca=1, cb=0):
    return lax.dot_general(a, b, (((ca,), (cb,)), ((), ())), preferred_element_type=F32)


def flip(v):
    return jnp.transpose(v.astype(F32)).astype(v.dtype)


def call(body, outs, ins, args, scratch=(), limit=40, flops=0, moved=0, grid=None, out_specs=None):
    shapes = tuple(jax.ShapeDtypeStruct(s, d) for s, d in outs)
    kwargs = {} if grid is None else {"grid": grid}
    return pl.pallas_call(
        body,
        out_shape=shapes,
        in_specs=list(ins),
        out_specs=tuple(out_specs) if out_specs is not None else tuple(VM for _ in outs),
        scratch_shapes=list(scratch),
        compiler_params=pltpu.CompilerParams(vmem_limit_bytes=limit * 2**20),
        cost_estimate=pl.CostEstimate(flops=flops, bytes_accessed=moved, transcendentals=0),
        **kwargs,
    )(*args)


def run_copies(pairs, sems):
    copies = [pltpu.make_async_copy(a, b, sems.at[i]) for i, (a, b) in enumerate(pairs)]
    for copy in copies:
        copy.start()
    for copy in copies:
        copy.wait()


def at16(v):
    return pl.multiple_of(v, 16)


def split_rows(meta, own, near, far, dst, unit):
    c, z = meta[1], meta[3]
    half = unit // 2
    pairs = [(own, dst.at[pl.ds(at16(z * unit), unit)])]
    for t in range(1, 4):
        zz = lax.rem(z + 4 - t, 4)
        pairs.append((near[t - 1], dst.at[pl.ds(at16(zz * unit + c * half), half)]))
        pairs.append((far[t - 1], dst.at[pl.ds(at16(zz * unit + (1 - c) * half), half)]))
    return pairs


def norm_parts(x):
    mean = jnp.mean(x, axis=-1, keepdims=True)
    centered = x - mean
    var = jnp.mean(centered * centered, axis=-1, keepdims=True)
    scale = lax.rsqrt(var + EPSILON)
    return centered * scale, scale


def unmark(x, embed):
    x = x.astype(F32)
    flag = x[:, :1] > 1e38
    return jnp.where(flag, embed, x), flag


def turn_heads(v, cos, sin):
    parts = []
    for g in range(GROUP):
        a = v[g * HEAD_DIM : g * HEAD_DIM + HALF]
        b = v[g * HEAD_DIM + HALF : (g + 1) * HEAD_DIM]
        parts += [a * cos - b * sin, b * cos + a * sin]
    return jnp.concatenate(parts, axis=0)


def project_body(count, first, whole, meta, gain, embed, cos, sin, *refs):
    rows = refs[:count]
    refs = refs[count:]
    if whole:
        (w_ref,) = refs[:1]
        refs = refs[1:]
        q_ref, kv_ref, n_ref, mk_ref, xs, w, wp, sems = refs
        pairs = [(w_ref, w)]
    else:
        own, near, far = refs[0], refs[1:4], refs[4:7]
        q_ref, kv_ref, n_ref, mk_ref, w_out_ref, xs, w, wp, sems = refs[7:]
        pairs = split_rows(meta, own, near, far, w, 192)
    pairs += [(rows[i], xs.at[i]) for i in range(count)]
    run_copies(pairs, sems)
    for part in range(3):
        wp[part] = w[:, part * WIDE : (part + 1) * WIDE]
    if not whole:
        w_out_ref[...] = w[...]

    @pl.loop(0, count)
    def _(i):
        x, flag = unmark(xs[i], embed[...])
        hat, _ = norm_parts(x)
        n = (hat * gain[...]).astype(BF)
        n_ref[i] = n
        mk_ref[i] = jnp.broadcast_to(jnp.where(flag, 1.0, 0.0), (CHUNK, 128)).astype(BF)
        co, si = cos[first + i], sin[first + i]
        q_ref[i] = turn_heads(jnp.transpose(mm(n, wp[0])), co, si).astype(BF)
        kv_ref[i, :WIDE] = turn_heads(jnp.transpose(mm(n, wp[1])), co, si).astype(BF)
        kv_ref[i, WIDE:] = jnp.transpose(mm(n, wp[2])).astype(BF)


def project_rows(meta, gain, embed, cos, sin, rows, first, weights):
    count = len(rows)
    whole = len(weights) == 1
    dim = rows[0].shape[1]
    outs = [
        ((count, WIDE, CHUNK), BF),
        ((count, 2 * WIDE, CHUNK), BF),
        ((count, CHUNK, dim), BF),
        ((count, CHUNK, 128), BF),
    ]
    if not whole:
        outs.append(((dim, 3 * WIDE), BF))
    return call(
        functools.partial(project_body, count, first, whole),
        outs,
        [SM, VM, VM, VM, VM] + [ANY] * (count + len(weights)),
        (meta, gain, embed, cos, sin, *rows, *weights),
        scratch=[
            pltpu.VMEM((count, CHUNK, dim), BF),
            pltpu.VMEM((dim, 3 * WIDE), BF),
            pltpu.VMEM((3, dim, WIDE), BF),
            pltpu.SemaphoreType.DMA((count + len(weights),)),
        ],
        flops=2 * count * CHUNK * dim * 3 * WIDE,
        moved=count * CHUNK * dim * 6,
    )


def load_heads(meta, na, refs, qs, okv, ckv, sems):
    q_a, q_b, kv_a, kv_b, r_a, r_b = refs
    run_copies(
        [
            (q_a, qs.at[pl.ds(0, na)]),
            (q_b, qs.at[pl.ds(na, 8 - na)]),
            (kv_a, okv.at[pl.ds(0, na)]),
            (kv_b, okv.at[pl.ds(na, 8 - na)]),
        ],
        sems,
    )

    @pl.when(meta[1] == 0)
    def _():
        run_copies([(kv_a, ckv.at[pl.ds(0, na)]), (kv_b, ckv.at[pl.ds(na, 8 - na)])], sems)

    @pl.when(meta[1] != 0)
    def _():
        run_copies([(r_a, ckv.at[pl.ds(0, na)]), (r_b, ckv.at[pl.ds(na, 8 - na)])], sems)


def thrice(v):
    return jnp.concatenate([v, v, v], axis=1)


def scores_of(keys, stacked, base, low, high):
    s = mm(keys, stacked) * 0.125
    place = base + lax.broadcasted_iota(jnp.int32, (CHUNK, LANES), 0)
    return jnp.where((place >= low) & (place < high), s, LOWEST)


def stack_heads(q, stacked):
    for g in range(GROUP):
        stacked[g * HEAD_DIM : (g + 1) * HEAD_DIM, g * CHUNK : (g + 1) * CHUNK] = q[
            g * HEAD_DIM : (g + 1) * HEAD_DIM
        ]


def attend_body(na, meta, bounds, *refs):
    heads = refs[:6]
    sends = refs[6:14]
    o_ref, ml_ref, qs, okv, ckv, okr, ckr, stacked, m_s, l_s, acc, sems = refs[14:]
    load_heads(meta, na, heads, qs, okv, ckv, sems)
    stacked[...] = jnp.zeros_like(stacked)

    @pl.loop(0, 8)
    def _(s):
        okr[s] = flip(okv[s, :WIDE])
        ckr[s] = flip(ckv[s, :WIDE])

    r, c = meta[0], meta[1]

    @pl.loop(0, 8)
    def _(p):
        s = p ^ r
        stack_heads(qs[s], stacked)
        lim = bounds[p]
        low, high, nlow, nhigh = [thrice(lim[i : i + 1]) for i in range(4)]

        def tile(keys, values, base, lo, hi):
            masked = scores_of(keys, stacked[...], base, lo, hi)
            m_old = m_s[...]
            m_new = jnp.maximum(m_old, jnp.max(masked, axis=0, keepdims=True))
            e = jnp.exp(masked - m_new)
            f = jnp.exp(m_old - m_new)
            m_s[...] = m_new
            l_s[...] = l_s[...] * f + jnp.sum(e, axis=0, keepdims=True)
            e = e.astype(BF)
            for g in range(GROUP):
                cut = slice(g * CHUNK, (g + 1) * CHUNK)
                acc[g] = acc[g] * f[:, cut] + mm(
                    values[g * HEAD_DIM : (g + 1) * HEAD_DIM], e[:, cut]
                )

        m_s[...] = jnp.full_like(m_s, LOWEST)
        l_s[...] = jnp.zeros_like(l_s)
        acc[...] = jnp.zeros_like(acc)
        tile(okr[s], okv[s, WIDE:], p * CHUNK, nlow, nhigh)

        @pl.loop(meta[4 + p], p + c)
        def _(k):
            t = k ^ r ^ c
            tile(ckr[t], ckv[t, WIDE:], k * CHUNK, low, high)

        total = l_s[...]
        inv = 1.0 / total
        out = jnp.concatenate(
            [acc[g] * inv[:, g * CHUNK : (g + 1) * CHUNK] for g in range(GROUP)], axis=0
        )
        o_ref[s] = out
        ml_ref[s, 0:1] = m_s[...]
        ml_ref[s, 1:2] = total
        low_out = out.astype(BF)
        for i in range(8):

            @pl.when(s == i)
            def _():
                sends[i][...] = low_out


HEAD_SCRATCH = [
    pltpu.VMEM((8, WIDE, CHUNK), BF),
    pltpu.VMEM((8, 2 * WIDE, CHUNK), BF),
    pltpu.VMEM((8, 2 * WIDE, CHUNK), BF),
]


def attend_rows(meta, bounds, heads):
    na = heads[0].shape[0]
    outs = [((WIDE, CHUNK), BF)] * 8 + [((8, WIDE, CHUNK), F32), ((8, 8, LANES), F32)]
    return call(
        functools.partial(attend_body, na),
        outs,
        [SM, VM] + [ANY] * 6,
        (meta, bounds, *heads),
        scratch=HEAD_SCRATCH
        + [
            pltpu.VMEM((8, CHUNK, WIDE), BF),
            pltpu.VMEM((8, CHUNK, WIDE), BF),
            pltpu.VMEM((WIDE, LANES), BF),
            pltpu.VMEM((1, LANES), F32),
            pltpu.VMEM((1, LANES), F32),
            pltpu.VMEM((GROUP, HEAD_DIM, CHUNK), F32),
            pltpu.SemaphoreType.DMA((4,)),
        ],
        flops=20 * 2 * 2 * CHUNK * LANES * 256,
        moved=8 * CHUNK * WIDE * 16,
    )


def attend_back_body(na, meta, bounds, cos, sin, o_ref, ml_ref, *refs):
    heads = refs[:6]
    grads = refs[6:14]
    (
        pq_ref, own_ref, far_ref,
        qs, okv, ckv, okr, ckr, ovr, cvr, gs,
        st_q, st_g, row_q, row_g, dk_o, dv_o, dk_c, dv_c, dq, sems,
    ) = refs[14:]
    load_heads(meta, na, heads, qs, okv, ckv, sems)
    run_copies([(grads[i], gs.at[i]) for i in range(8)], sems)
    for ref in (st_q, st_g, dk_o, dv_o, dk_c, dv_c):
        ref[...] = jnp.zeros_like(ref)

    @pl.loop(0, 8)
    def _(s):
        okr[s] = flip(okv[s, :WIDE])
        ckr[s] = flip(ckv[s, :WIDE])
        ovr[s] = flip(okv[s, WIDE:])
        cvr[s] = flip(ckv[s, WIDE:])

    r, c = meta[0], meta[1]
    lane = lax.broadcasted_iota(jnp.int32, (CHUNK, WIDE), 1) // HEAD_DIM

    @pl.loop(0, 8)
    def _(p):
        s = p ^ r
        q = qs[s]
        stack_heads(q, st_q)
        total = ml_ref[s, 1:2]
        top = ml_ref[s, 0:1]
        g_in = gs[s].astype(F32)
        attended = o_ref[s]
        scaled, fix = [], []
        for g in range(GROUP):
            part = slice(g * HEAD_DIM, (g + 1) * HEAD_DIM)
            inv = 1.0 / total[:, g * CHUNK : (g + 1) * CHUNK]
            scaled.append(g_in[part] * inv)
            fix.append(jnp.sum(g_in[part] * attended[part], axis=0, keepdims=True) * inv)
        scaled = jnp.concatenate(scaled, axis=0)
        fix = jnp.concatenate(fix, axis=1)
        stack_heads(scaled.astype(BF), st_g)
        q_rows = jnp.transpose(q.astype(F32))
        g_rows = jnp.transpose(scaled)
        for g in range(GROUP):
            row_q[g * CHUNK : (g + 1) * CHUNK] = jnp.where(lane == g, q_rows, 0.0).astype(BF)
            row_g[g * CHUNK : (g + 1) * CHUNK] = jnp.where(lane == g, g_rows, 0.0).astype(BF)
        lim = bounds[p]
        low, high, nlow, nhigh = [thrice(lim[i : i + 1]) for i in range(4)]
        dq[...] = jnp.zeros_like(dq)

        def tile(k_rows, v_rows, k_cols, base, lo, hi, dk, dv):
            e = jnp.exp(scores_of(k_rows, st_q[...], base, lo, hi) - top)
            d = (e * (mm(v_rows, st_g[...]) - fix)).astype(BF)
            e = e.astype(BF)
            dv[...] += mm(e, row_g[...])
            dk[...] += mm(d, row_q[...])
            for g in range(GROUP):
                dq[g * HEAD_DIM : (g + 1) * HEAD_DIM] += mm(
                    k_cols[g * HEAD_DIM : (g + 1) * HEAD_DIM], d[:, g * CHUNK : (g + 1) * CHUNK]
                )

        tile(okr[s], ovr[s], okv[s, :WIDE], p * CHUNK, nlow, nhigh, dk_o.at[s], dv_o.at[s])

        @pl.loop(meta[4 + p], p + c)
        def _(k):
            t = k ^ r ^ c
            tile(ckr[t], cvr[t], ckv[t, :WIDE], k * CHUNK, low, high, dk_c.at[t], dv_c.at[t])

        pq_ref[s] = turn_heads(dq[...] * 0.125, cos[s], -sin[s]).astype(BF)

    both = 1.0 - c.astype(F32)

    @pl.loop(0, 8)
    def _(s):
        dk = jnp.transpose(dk_c[s])
        dv = jnp.transpose(dv_c[s])
        far_ref[s, :WIDE] = dk.astype(BF)
        far_ref[s, WIDE:] = dv.astype(BF)
        own_ref[s, :WIDE] = jnp.transpose(dk_o[s]) + both * dk
        own_ref[s, WIDE:] = jnp.transpose(dv_o[s]) + both * dv


def attend_back(meta, bounds, cos, sin, attended, stats, heads, grads):
    na = heads[0].shape[0]
    rows = pltpu.VMEM((8, CHUNK, WIDE), BF)
    sums = pltpu.VMEM((8, CHUNK, WIDE), F32)
    return call(
        functools.partial(attend_back_body, na),
        [((8, WIDE, CHUNK), BF), ((8, 2 * WIDE, CHUNK), F32), ((8, 2 * WIDE, CHUNK), BF)],
        [SM, VM, VM, VM, VM, VM] + [ANY] * 14,
        (meta, bounds, cos, sin, attended, stats, *heads, *grads),
        scratch=HEAD_SCRATCH
        + [rows] * 4
        + [
            pltpu.VMEM((8, WIDE, CHUNK), BF),
            pltpu.VMEM((WIDE, LANES), BF),
            pltpu.VMEM((WIDE, LANES), BF),
            pltpu.VMEM((LANES, WIDE), BF),
            pltpu.VMEM((LANES, WIDE), BF),
        ]
        + [sums] * 4
        + [pltpu.VMEM((WIDE, CHUNK), F32), pltpu.SemaphoreType.DMA((8,))],
        limit=48,
        flops=20 * 2 * 5 * CHUNK * LANES * 256,
        moved=8 * CHUNK * WIDE * 30,
    )


def middle_body(meta, gain, embed, x_ref, *refs):
    heads = refs[:8]
    own, near, far = refs[8], refs[9:12], refs[12:15]
    mid_ref, n_ref, att_ref, w_ref, sems = refs[15:]
    r = meta[0]
    pairs = split_rows(meta, own, near, far, w_ref, 192)
    for s in range(8):
        d = r ^ s
        pairs.append((heads[s], att_ref.at[d & 1, pl.ds(at16((d >> 1) * WIDE), WIDE)]))
    run_copies(pairs, sems)
    for stream in range(2):
        x, _ = unmark(x_ref[stream], embed[...])
        mid = x + mm(att_ref[stream], w_ref[...], 0, 0)
        hat, _ = norm_parts(mid)
        mid_ref[stream] = mid
        n_ref[stream * CHUNK : (stream + 1) * CHUNK] = (hat * gain[...]).astype(BF)


def middle_rows(meta, gain, embed, marked, heads, weights):
    dim = marked.shape[2]
    return call(
        middle_body,
        [((2, CHUNK, dim), F32), ((2 * CHUNK, dim), BF), ((2, dim, CHUNK), BF), ((dim, dim), BF)],
        [SM, VM, VM, VM] + [ANY] * 15,
        (meta, gain, embed, marked, *heads, *weights),
        scratch=[pltpu.SemaphoreType.DMA((15,))],
        flops=2 * 2 * CHUNK * dim * dim,
        moved=8 * CHUNK * dim * 2,
    )


def feed_body(meta, bias, *refs):
    n_own, n_far, g_own, g_far, up_own, down_own, ff_r, ff_x, ff_y, ff_dd, ff_du = refs[:11]
    downs, ups = (ff_r, ff_x, ff_y, ff_dd), (ff_r, ff_x, ff_y, ff_du)
    (
        out_ref, outf_ref, ng_ref, ngf_ref, gu_ref, gd_ref, gb_ref,
        ns, gs, wu, wd, acts, slopes, acc_o, acc_n, sems,
    ) = refs[11:]
    c, h, z = meta[1], meta[2], meta[3]
    rows = 2 * CHUNK
    part = bias.shape[1] // 4
    pairs = [
        (n_own, ns.at[pl.ds(0, rows)]),
        (n_far, ns.at[pl.ds(rows, rows)]),
        (g_own, gs.at[pl.ds(0, rows)]),
        (g_far, gs.at[pl.ds(rows, rows)]),
        (down_own.at[pl.ds(at16(c * part), part)], wd.at[pl.ds(at16(z * part), part)]),
    ]
    for k in range(4):
        cols = pl.ds(pl.multiple_of(k * 2 * part + c * part, 128), part)
        pairs.append((up_own.at[:, cols], wu.at[pl.ds(at16(z * 192), 192), pl.ds(k * part, part)]))
    for t in range(1, 4):
        zz = lax.rem(z + 4 - t, 4)
        for k in range(4):
            hh = h ^ k
            pairs.append((downs[k].at[t - 1, pl.ds(0, 96)], wd.at[pl.ds(at16(zz * part + hh * 96), 96)]))
            dst = pl.ds(at16(zz * 192 + hh * 48), 48)
            for b in range(2):
                pairs.append(
                    (
                        ups[k].at[t - 1, pl.ds(48 * b + (96 if k < 3 else 0), 48)],
                        wu.at[dst, pl.ds(2 * part * b, 2 * part)],
                    )
                )
    run_copies(pairs, sems)
    acc_o[...] = jnp.zeros_like(acc_o)
    acc_n[...] = jnp.zeros_like(acc_n)

    @pl.loop(0, 4)
    def _(j):
        cols = pl.ds(pl.multiple_of(j * part, 128), part)
        w_up = wu[:, cols]
        w_down = wd[pl.ds(at16(j * part), part)]
        b_up = bias[:, cols]

        def rows_of(i, total):
            span = pl.ds(pl.multiple_of(i * CHUNK, CHUNK), CHUNK)
            v = mm(ns[span], w_up) + b_up
            square = v * v
            th = jnp.tanh(GELU_SCALE * (v + 0.044715 * (v * square)))
            half = 0.5 * (1.0 + th)
            act = (v * half).astype(BF)
            slope = half + (0.5 * v) * (1.0 - th * th) * (
                GELU_SCALE * (1.0 + (3.0 * 0.044715) * square)
            )
            ug = (slope * mm(gs[span], w_down, 1, 1)).astype(BF)
            acts[span] = act
            slopes[span] = ug
            acc_o[span] += mm(act, w_down)
            acc_n[span] += mm(ug, w_up, 1, 1)
            return total + jnp.sum(ug.astype(F32), axis=0, keepdims=True)

        gb_ref[:, cols] = lax.fori_loop(0, 4, rows_of, jnp.zeros((1, part), F32))
        gd_ref[j ^ h] = mm(acts[...], gs[...], 0, 0).astype(BF)
        gu = mm(ns[...], slopes[...], 0, 0).astype(BF)
        for k in range(4):
            gu_ref[h ^ k, :, cols] = gu[192 * k : 192 * (k + 1)]

    out_ref[...] = acc_o[:rows]
    outf_ref[...] = acc_o[rows:].astype(BF)
    ng_ref[...] = acc_n[:rows]
    ngf_ref[...] = acc_n[rows:].astype(BF)


def feed_rows(meta, bias, args):
    rows = 2 * CHUNK
    dim = args[0].shape[1]
    hid = bias.shape[1]
    return call(
        feed_body,
        [
            ((rows, dim), F32),
            ((rows, dim), BF),
            ((rows, dim), F32),
            ((rows, dim), BF),
            ((4, dim // 4, hid), BF),
            ((4, hid // 4, dim), BF),
            ((1, hid), F32),
        ],
        [SM, VM] + [ANY] * 11,
        (meta, bias, *args),
        scratch=[
            pltpu.VMEM((2 * rows, dim), BF),
            pltpu.VMEM((2 * rows, dim), BF),
            pltpu.VMEM((dim, hid), BF),
            pltpu.VMEM((hid, dim), BF),
            pltpu.VMEM((2 * rows, hid // 4), BF),
            pltpu.VMEM((2 * rows, hid // 4), BF),
            pltpu.VMEM((2 * rows, dim), F32),
            pltpu.VMEM((2 * rows, dim), F32),
            pltpu.SemaphoreType.DMA((45,)),
        ],
        limit=48,
        flops=6 * 2 * 2 * rows * dim * hid,
        moved=12 * dim * hid,
    )


def middle_back_body(
    meta, gain, b_down, mid_ref, ng_ref, ngf_ref, out_ref, outf_ref, g_ref, x_ref, w_ref, *refs
):
    lay_ref, mg_ref, sum_ref = refs[:3]
    sends = refs[3:11]
    gain_sum = jnp.zeros((1, gain.shape[1]), F32)
    g_sum = gain_sum
    for stream in range(2):
        span = slice(stream * CHUNK, (stream + 1) * CHUNK)
        mid = mid_ref[stream]
        lay = mid + out_ref[span] + outf_ref[span].astype(F32) + b_down[...]
        lay_ref[stream] = lay.astype(BF)
        hat, scale = norm_parts(mid)
        ng = ng_ref[span] + ngf_ref[span].astype(F32)
        gain_sum += jnp.sum(ng * hat, axis=0, keepdims=True)
        t = ng * gain[...]
        g = g_ref[stream].astype(F32)
        g_sum += jnp.sum(g, axis=0, keepdims=True)
        t_mean = jnp.mean(t, axis=-1, keepdims=True)
        t_hat = jnp.mean(t * hat, axis=-1, keepdims=True)
        mg = (g + scale * (t - t_mean - hat * t_hat)).astype(BF)
        mg_ref[stream] = mg
        if stream == 1:
            flag = x_ref[1][:, :1].astype(F32) > 1e38
            sum_ref[2:3] = jnp.sum(jnp.where(flag, mg.astype(F32), 0.0), axis=0, keepdims=True)
    sum_ref[0:1] = gain_sum
    sum_ref[1:2] = g_sum
    for s in range(8):
        d = meta[0] ^ s
        rows = w_ref[pl.ds(at16((d >> 1) * WIDE), WIDE)]
        sends[s][...] = mm(rows, mg_ref[d & 1], 1, 1).astype(BF)


def middle_back(meta, gain, b_down, args):
    dim = gain.shape[1]
    return call(
        middle_back_body,
        [((2, CHUNK, dim), BF), ((2, CHUNK, dim), BF), ((8, dim), F32)]
        + [((WIDE, CHUNK), BF)] * 8,
        [SM] + [VM] * 10,
        (meta, gain, b_down, *args),
        flops=4 * CHUNK * dim * dim,
        moved=20 * CHUNK * dim,
    )


def out_grad_body(att_ref, mg_ref, o_ref):
    o_ref[...] = (mm(att_ref[0], mg_ref[0]) + mm(att_ref[1], mg_ref[1])).astype(BF)


def project_back_body(steps, last, meta_free, *refs):
    own, far, pq, n_ref, mk_ref, cos, sin, w_ref = (meta_free, *refs[:7])
    refs = refs[7:]
    if last:
        carry, vec = refs[:2]
        refs = refs[2:]
    ng_ref, gq_ref, gs_ref, wp, acc = refs
    i = pl.program_id(0)

    @pl.when(i == 0)
    def _():
        for part in range(3):
            wp[part] = w_ref[:, part * WIDE : (part + 1) * WIDE]
        if last:
            acc[...] = carry[...]
            gs_ref[...] = vec[...]
        else:
            acc[...] = jnp.zeros_like(acc)
            gs_ref[...] = jnp.zeros_like(gs_ref)

    kv = own[0] + far[0].astype(F32)
    parts = [
        pq[0],
        turn_heads(kv[:WIDE] * 0.125, cos[0], -sin[0]).astype(BF),
        kv[WIDE:].astype(BF),
    ]
    n = n_ref[0]
    ng = jnp.zeros((CHUNK, n.shape[1]), F32)
    for k in range(3):
        ng += mm(flip(parts[k]), wp[k], 1, 1)
        acc[k * WIDE : (k + 1) * WIDE] += mm(parts[k], n)
    ng_ref[0] = ng.astype(BF)
    gs_ref[0:1] += jnp.sum(ng * n.astype(F32), axis=0, keepdims=True)
    gs_ref[1:2] += jnp.sum(ng * mk_ref[0][:, :1].astype(F32), axis=0, keepdims=True)

    @pl.when(i == steps - 1)
    def _():
        gq_ref[...] = jnp.transpose(acc[...]).astype(BF) if last else acc[...]


def pick(order):
    def at(i):
        slot = jnp.int32(order[-1])
        for k in range(len(order) - 2, -1, -1):
            slot = jnp.where(i == k, order[k], slot)
        return slot

    return at


def project_back(order, own, far, pq, n, mk, cos, sin, w, carry=None):
    last = carry is not None
    steps = len(order)
    dim = n.shape[2]
    slot = pick(order)

    def chunk(rows, cols):
        return pl.BlockSpec((1, rows, cols), lambda i: (slot(i), 0, 0))

    def whole(*shape):
        return pl.BlockSpec(shape, lambda i: tuple(0 for _ in shape))

    wide = 3 * WIDE + HEAD_DIM
    args = [own, far, pq, n, mk, cos, sin, w]
    specs = [
        chunk(2 * WIDE, CHUNK), chunk(2 * WIDE, CHUNK), chunk(WIDE, CHUNK), chunk(CHUNK, dim),
        chunk(CHUNK, 128), chunk(HALF, CHUNK), chunk(HALF, CHUNK), whole(dim, 3 * WIDE),
    ]
    if last:
        args += list(carry)
        specs += [whole(wide, dim), whole(8, dim)]
    gq_shape = (dim, wide) if last else (wide, dim)
    return call(
        functools.partial(project_back_body, steps, last),
        [((steps, CHUNK, dim), BF), (gq_shape, BF if last else F32), ((8, dim), F32)],
        specs,
        args,
        scratch=[pltpu.VMEM((3, dim, WIDE), BF), pltpu.VMEM((wide, dim), F32)],
        grid=(steps,),
        out_specs=[
            pl.BlockSpec((1, CHUNK, dim), lambda i: (i, 0, 0)), whole(*gq_shape), whole(8, dim)
        ],
        flops=2 * 2 * steps * CHUNK * dim * 3 * WIDE,
        moved=steps * CHUNK * dim * 8,
    )


def last_body(meta, gain, embed, x_ref, mg_ref, keep_ref, far_ref, o_ref):
    c = meta[1]
    for stream, ng in ((c, keep_ref[...]), (1 - c, far_ref[...].astype(F32))):
        x, flag = unmark(x_ref[stream], embed[...])
        hat, scale = norm_parts(x)
        t = ng * gain[...]
        t_mean = jnp.mean(t, axis=-1, keepdims=True)
        t_hat = jnp.mean(t * hat, axis=-1, keepdims=True)
        grad = mg_ref[stream].astype(F32) + scale * (t - t_mean - hat * t_hat)
        o_ref[stream] = jnp.where(flag, 0.0, grad).astype(BF)


def cut(v, index, size, axis=0):
    return lax.dynamic_slice_in_dim(v, index * size, size, axis)


def at(v, index, axis=0):
    return lax.dynamic_index_in_dim(v, index, axis, keepdims=False)


def shards_by_heads(
    hidden,
    noise_mask,
    doc_lengths,
    w_qkv,
    w_out,
    w_up,
    b_up,
    w_down,
    b_down,
    gain_one,
    gain_two,
    mask_embed,
    out_grad,
):
    r = lax.axis_index("ctx")
    z = lax.axis_index("fsdp")
    c, h = r & 1, r >> 1
    dim = hidden.shape[3]
    hid = w_up.shape[1]
    part = hid // 8
    total = CHUNK * 8

    noisy = jnp.where(noise_mask[0][:, None] == 1, jnp.asarray(jnp.inf, BF), hidden[0, 1])
    marked = jnp.stack([hidden[0, 0], noisy])
    mine = at(marked, c)
    other = swap(at(marked, 1 - c), 1)
    mine_x, mine_y = swap(mine, 2), swap(mine, 4)
    other_x, other_y = swap(other, 2), swap(other, 4)
    mine_d, other_d = swap(mine_x, 4), swap(other_y, 2)

    small = jnp.concatenate([b_up, b_down, gain_one, gain_two, mask_embed])
    size = small.shape[0]
    small = jnp.pad(small, (0, 2048 - size)).reshape(16, 128)
    small = jnp.stack([small] + [turn(small, t) for t in range(1, 4)])
    small = jnp.take(small, (z - jnp.arange(4)) % 4, axis=0).reshape(4, 2048).astype(F32)
    quarter = dim // 4
    bias = at(small[:, : hid // 4].reshape(4, 2, part), c, 1).reshape(1, 4 * part)
    b_down_all, gain_a, gain_b, embed = [
        small[:, hid // 4 + k * quarter : hid // 4 + (k + 1) * quarter].reshape(1, dim)
        for k in range(4)
    ]

    own_qkv = jnp.concatenate([cut(w_qkv[:, k * dim : (k + 1) * dim], h, WIDE, 1) for k in range(3)], 1)
    half = cut(own_qkv, c, quarter // 2)
    near_qkv = [turn(half, t) for t in range(1, 4)]
    far_qkv = [swap(v, 1) for v in near_qkv]
    up_rows = cut(w_up, h, quarter // 4).reshape(quarter // 4, 4, 2, part)
    up_rows = at(up_rows, c, 2)
    share = jnp.concatenate(
        [
            cut(w_down, 4 * c + h, part // 4),
            up_rows[:, :2].reshape(quarter // 4, 2 * part),
            up_rows[:, 2:].reshape(quarter // 4, 2 * part),
        ]
    )
    ff_r = jnp.stack([turn(share, t) for t in range(1, 4)])
    ff_x, ff_y = swap(ff_r, 2), swap(ff_r, 4)
    ff_dd = swap(ff_x[:, : part // 4], 4)
    ff_du = swap(ff_y[:, part // 4 :], 2)
    half = cut(w_out, c, quarter // 2)
    near_out = [turn(half, t) for t in range(1, 4)]
    far_out = [swap(v, 1) for v in near_out]

    lengths = doc_lengths[0]
    index = jnp.arange(lengths.shape[0])
    ends = jnp.sum(jnp.where(index[None, :] <= index[:, None], lengths[None, :], 0), axis=1)
    place = jnp.arange(total, dtype=jnp.int32)
    after = ends[None, :] > place[:, None]
    start = jnp.max(jnp.where(after, 0, ends[None, :]), axis=1)
    stop = jnp.min(jnp.where(after, ends[None, :], total), axis=1)
    block = place // BLOCK * BLOCK
    limit = jnp.minimum(block + BLOCK, stop)
    clean = c == 0
    bounds = jnp.stack(
        [start, jnp.where(clean, limit, block), jnp.where(clean, start, jnp.maximum(start, block)), limit]
    )
    bounds = jnp.pad(bounds.reshape(4, 8, CHUNK).transpose(1, 0, 2), ((0, 0), (0, 4), (0, 0)))
    meta = jnp.concatenate(
        [jnp.stack([r, c, h, z]), start[::CHUNK] // CHUNK, jnp.zeros((4,), jnp.int32)]
    ).astype(jnp.int32)
    slots = (jnp.arange(8) ^ r)[:, None] * CHUNK + jnp.arange(CHUNK)[None, :]
    frequency = jnp.exp(jnp.arange(HALF).astype(F32) * (-2.0 * math.log(10000.0) / HEAD_DIM))
    angles = slots.astype(F32)[:, None, :] * frequency[None, :, None]
    cos, sin = jnp.cos(angles), jnp.sin(angles)

    rows_a = (mine, other, mine_x, other_x, mine_y, other_y)
    q_a, kv_a, n_a, mk_a, w_all = project_rows(
        meta, gain_a, embed, cos, sin, rows_a, 0, (own_qkv, *near_qkv, *far_qkv)
    )
    q_b, kv_b, n_b, mk_b = project_rows(meta, gain_a, embed, cos, sin, (mine_d, other_d), 6, (w_all,))
    give = [(i, i + 1) for i in range(0, 8, 2)]
    r_a, r_b = lax.ppermute(kv_a, "ctx", give), lax.ppermute(kv_b, "ctx", give)
    heads = (q_a, q_b, kv_a, kv_b, r_a, r_b)
    *sends, attended, stats = attend_rows(meta, bounds, heads)
    got = [sends[0]] + [swap(sends[s], s) for s in range(1, 8)]
    middle, normed, att, w_out_all = middle_rows(
        meta, gain_b, embed, marked, got, (w_out, *near_out, *far_out)
    )
    grads = out_grad[0]
    grad_rows = grads.reshape(2 * CHUNK, dim)
    out_own, out_far, ng_own, ng_far, gu, gd, gbu = feed_rows(
        meta,
        bias,
        (normed, swap(normed, 1), grad_rows, swap(grad_rows, 1), w_up, w_down, ff_r, ff_x, ff_y, ff_dd, ff_du),
    )
    ng_far, out_far = swap(ng_far, 1), swap(out_far, 1)

    layer, mid_grad, sums, *sends = middle_back(
        meta,
        gain_b,
        b_down_all,
        (middle, ng_own, ng_far, out_own, out_far, grads, marked, w_out_all),
    )
    got = [sends[0]] + [swap(sends[s], s) for s in range(1, 8)]
    (go,) = call(
        out_grad_body, [((dim, dim), BF)], [VM, VM], (att, mid_grad), flops=4 * CHUNK * dim * dim
    )
    pq, own_kv, far_kv = attend_back(meta, bounds, cos, sin, attended, stats, heads, got)
    far_kv = lax.ppermute(far_kv, "ctx", [(b, a) for a, b in give])
    n_all = jnp.concatenate([n_a, n_b])
    mk_all = jnp.concatenate([mk_a, mk_b])
    back = (own_kv, far_kv, pq, n_all, mk_all, cos, sin, w_all)
    away, *carry = project_back((2, 6, 5, 7), *back)
    in_x, in_y = swap(away[:2], 2), swap(away[2:], 4)
    stay, gq, vec = project_back((0, 4, 1, 3), *back, carry=carry)
    stay = stay.astype(F32)
    keep = stay[0] + in_x[0].astype(F32)
    keep += swap((stay[1] + in_x[1].astype(F32)).astype(BF), 4).astype(F32)
    pair = stay[2] + in_y[0].astype(F32)
    pair += swap((stay[3] + in_y[1].astype(F32)).astype(BF), 2).astype(F32)
    pair = swap(pair.astype(BF), 1)
    (input_grad,) = call(
        last_body,
        [((2, CHUNK, dim), BF)],
        [SM] + [VM] * 6,
        (meta, gain_a, embed, marked, mid_grad, keep, pair),
        moved=10 * CHUNK * dim,
    )

    def line(v):
        out = at(v, z).astype(F32)
        for t in range(1, 4):
            out += turn(at(v, (z + t) % 4).astype(BF), t).astype(F32)
        return out

    def plane_chip(v, first):
        one, two = (1, 2) if first == 0 else (2, 1)
        got = swap(jnp.stack([v[one], v[3]]), 2 * one)
        low = v[0].astype(F32) + got[0].astype(F32)
        high = (v[two].astype(F32) + got[1].astype(F32)).astype(BF)
        return low + swap(high, 2 * two).astype(F32)

    gd = line(plane_chip(gd, 0).reshape(4, part // 4, dim))
    gu = plane_chip(gu, 1).reshape(2, 4, dim // 32, 4 * part)
    gu = line(jnp.swapaxes(gu, 0, 1))
    gu_far = swap(at(gu, 1 - c).astype(BF), 1).astype(F32)
    gu = at(gu, c)
    gu = jnp.where(clean, jnp.stack([gu, gu_far]), jnp.stack([gu_far, gu]))
    gu = gu.reshape(2, dim // 32, 4, part).transpose(1, 2, 0, 3).reshape(dim // 32, hid)

    def over_core(v):
        v = v.reshape(4, 2, dim // 8, v.shape[-1])
        return at(v, c, 1).astype(F32) + swap(at(v, 1 - c, 1), 1).astype(F32)

    go = over_core(go).astype(BF)
    go_sum = at(go, h).astype(F32)
    for k in range(1, 4):
        go_sum += swap(at(go, h ^ k), 2 * k).astype(F32)
    go = line(go_sum.reshape(4, dim // 32, dim))

    gq = over_core(gq)
    gq = line(jnp.swapaxes(gq.reshape(4, 4, dim // 32, gq.shape[-1]), 0, 1))
    gq_low = gq.astype(BF)
    pieces = [at(gq, h)] + [swap(at(gq_low, h ^ k), 2 * k).astype(F32) for k in range(1, 4)]
    gq = jnp.take(jnp.stack(pieces), jnp.arange(4) ^ h, axis=0)[..., : 3 * WIDE]
    gq = gq.reshape(4, dim // 32, 3, WIDE).transpose(1, 2, 0, 3).reshape(dim // 32, 3 * dim)

    gbu = gbu.reshape(4, 1, part)
    gbu = jnp.where(clean, jnp.concatenate([gbu, 0 * gbu], 1), jnp.concatenate([0 * gbu, gbu], 1))
    flat = jnp.concatenate([gbu.reshape(-1), sums[:3].reshape(-1), vec[:2].reshape(-1)])
    flat = flat.reshape(-1, 128)
    for bit in (1, 2, 4):
        flat = flat + swap(flat, bit)
    flat = flat + turn(flat, 1) + turn(flat, 2) + turn(flat, 3)
    flat = flat.reshape(-1)
    gbu = flat[:hid]
    g_gain_b, g_b_down, m_direct, g_gain_a, m_norm = [
        flat[hid + k * dim : hid + (k + 1) * dim] for k in range(5)
    ]
    g_gain_a = g_gain_a / gain_a[0]
    hat, scale = norm_parts(embed)
    t = m_norm[None] * gain_a
    t_mean = jnp.mean(t, axis=-1, keepdims=True)
    t_hat = jnp.mean(t * hat, axis=-1, keepdims=True)
    g_embed = m_direct + (scale * (t - t_mean - hat * t_hat))[0]
    own = 4 * r + z
    return (
        layer[None],
        input_grad[None],
        gq,
        go,
        gu,
        cut(gbu, own, hid // 32),
        gd,
        cut(g_b_down, own, dim // 32),
        cut(g_gain_a, own, dim // 32),
        cut(g_gain_b, own, dim // 32),
        cut(g_embed, own, dim // 32),
    )


def solution(mesh):
    plain = (mesh.shape["ctx"], mesh.shape["fsdp"]) != (8, 4)
    placed = (
        P("fsdp", None, "ctx", None),
        P("fsdp", "ctx"),
        P("fsdp", None),
        P("fsdp", None),
        P("fsdp", None),
        P("fsdp", None),
        P("fsdp"),
        P("fsdp", None),
        P("fsdp"),
        P("fsdp"),
        P("fsdp"),
        P("fsdp"),
        P("fsdp", None, "ctx", None),
    )
    return jax.shard_map(
        shards if plain else shards_by_heads,
        mesh=mesh,
        in_specs=placed,
        out_specs=(
            P("fsdp", None, "ctx", None),
            P("fsdp", None, "ctx", None),
            P(("ctx", "fsdp"), None),
            P(("ctx", "fsdp"), None),
            P(("ctx", "fsdp"), None),
            P(("ctx", "fsdp")),
            P(("ctx", "fsdp"), None),
            P(("ctx", "fsdp")),
            P(("ctx", "fsdp")),
            P(("ctx", "fsdp")),
            P(("ctx", "fsdp")),
        ),
        check_vma=False,
    )
```

```python
import functools
import math

import jax
import jax.numpy as jnp
from jax import lax
from jax.experimental import pallas as pl
from jax.experimental.pallas import tpu as pltpu
from jax.sharding import PartitionSpec as P

HEADS = 12
HEAD_DIM = 64
BLOCK = 16


LOWEST = -1e30
EPSILON = 1e-05


def layer_norm(inputs, gain):
    average = jnp.mean(inputs, axis=-1, keepdims=True)
    centered = inputs - average
    variance = jnp.mean(centered * centered, axis=-1, keepdims=True)
    return centered * lax.rsqrt(variance + EPSILON) * gain


def rotary_angles(positions):
    half_dim = HEAD_DIM // 2
    frequency = jnp.exp(
        jnp.arange(half_dim).astype(jnp.float32) * (-2.0 * math.log(10000.0) / HEAD_DIM)
    )
    return positions.astype(jnp.float32)[:, None] * frequency[None, :]


def rotate(heads_in, angles):
    half_dim = heads_in.shape[-1] // 2
    cosine = jnp.cos(angles)[:, None, :]
    sine_part = jnp.sin(angles)[:, None, :]
    first_half = heads_in[..., :half_dim]
    second_half = heads_in[..., half_dim:]
    return jnp.concatenate(
        [
            first_half * cosine - second_half * sine_part,
            second_half * cosine + first_half * sine_part,
        ],
        axis=-1,
    )


def segment_of(positions, doc_ends):
    return jnp.sum((positions[:, None] >= doc_ends[None, :]).astype(jnp.int32), axis=1)


def visible(query_stream, query_position, query_segment, key_stream, key_position, key_segment):
    query_block = query_position // BLOCK
    key_block = key_position // BLOCK
    same_doc = query_segment[:, None] == key_segment[None, :]
    clean_key = key_stream[None, :] == 0
    noisy_query = query_stream[:, None] == 1
    before = key_block[None, :] < query_block[:, None]
    same_block = key_block[None, :] == query_block[:, None]
    from_clean = clean_key & (before | same_block & jnp.logical_not(noisy_query))
    from_noisy = jnp.logical_not(clean_key) & noisy_query & same_block
    return same_doc & (from_clean | from_noisy)


def mix_tile(running, query_rows, key_tile, value_tile, allowed):
    run_max, run_sum, accum = running
    scores = (
        jnp.einsum("qhd,khd->hqk", query_rows, key_tile, preferred_element_type=jnp.float32) * 0.125
    )
    masked = jnp.where(allowed[None], scores, LOWEST)
    new_max = jnp.maximum(run_max, jnp.max(masked, axis=-1))
    exp_terms = jnp.where(allowed[None], jnp.exp(masked - new_max[..., None]), 0.0)
    factor = jnp.exp(run_max - new_max)
    new_sum = run_sum * factor + jnp.sum(exp_terms, axis=-1)
    accum = accum * factor[..., None] + jnp.einsum(
        "hqk,khd->hqd",
        exp_terms.astype(jnp.bfloat16),
        value_tile,
        preferred_element_type=jnp.float32,
    )
    return (new_max, new_sum, accum)


def tile_grads(query_rows, key_tile, value_tile, allowed, row_max, scaled_grad, correction):
    scores = (
        jnp.einsum("qhd,khd->hqk", query_rows, key_tile, preferred_element_type=jnp.float32) * 0.125
    )
    masked = jnp.where(allowed[None], scores, LOWEST)
    exp_terms = jnp.where(allowed[None], jnp.exp(masked - row_max[..., None]), 0.0)
    prob_grad = jnp.einsum(
        "hqd,khd->hqk", scaled_grad, value_tile, preferred_element_type=jnp.float32
    )
    score_grad = (exp_terms * (prob_grad - correction[..., None])).astype(jnp.bfloat16)
    query_part = jnp.einsum(
        "hqk,khd->qhd", score_grad, key_tile, preferred_element_type=jnp.float32
    )
    key_part = jnp.einsum(
        "hqk,qhd->khd", score_grad, query_rows, preferred_element_type=jnp.float32
    )
    value_part = jnp.einsum(
        "hqk,hqd->khd",
        exp_terms.astype(jnp.bfloat16),
        scaled_grad,
        preferred_element_type=jnp.float32,
    )
    return (query_part, key_part, value_part)


def build_inputs(hidden, noise_row, mask_row):
    clean_rows = hidden[0, 0].astype(jnp.float32)
    noisy_rows = jnp.where(
        noise_row[:, None] == 1,
        mask_row.astype(jnp.float32)[None, :],
        hidden[0, 1].astype(jnp.float32),
    )
    return jnp.concatenate([clean_rows, noisy_rows], axis=0)


def project(inputs, gathered, angles):
    row_count = inputs.shape[0]
    model_dim = inputs.shape[1]
    normed = layer_norm(inputs, gathered[6].astype(jnp.float32)).astype(jnp.bfloat16)
    projected = jnp.dot(normed, gathered[0], preferred_element_type=jnp.float32)
    query_rows = rotate(
        projected[:, :model_dim].reshape(row_count, HEADS, HEAD_DIM), angles
    ).astype(jnp.bfloat16)
    key_rows = rotate(
        projected[:, model_dim : 2 * model_dim].reshape(row_count, HEADS, HEAD_DIM), angles
    ).astype(jnp.bfloat16)
    value_rows = (
        projected[:, 2 * model_dim :].reshape(row_count, HEADS, HEAD_DIM).astype(jnp.bfloat16)
    )
    return (normed, query_rows, key_rows, value_rows)


def upper_half(inputs, attended_low, gathered):
    middle = inputs + jnp.dot(attended_low, gathered[1], preferred_element_type=jnp.float32)
    normed_two = layer_norm(middle, gathered[7].astype(jnp.float32)).astype(jnp.bfloat16)
    upper = jnp.dot(normed_two, gathered[2], preferred_element_type=jnp.float32) + gathered[
        3
    ].astype(jnp.float32)
    activated = jax.nn.gelu(upper, approximate=True).astype(jnp.bfloat16)
    return (middle, normed_two, upper, activated)


def shards(
    hidden,
    noise_mask,
    doc_lengths,
    w_qkv,
    w_out,
    w_up,
    b_up,
    w_down,
    b_down,
    gain_one,
    gain_two,
    mask_embed,
    out_grad,
):
    own_params = (w_qkv, w_out, w_up, b_up, w_down, b_down, gain_one, gain_two, mask_embed)
    local_count = hidden.shape[2]
    model_dim = hidden.shape[3]
    row_count = 2 * local_count
    ctx_index = lax.axis_index("ctx")
    offset = ctx_index * local_count
    local_place = offset + jnp.arange(local_count, dtype=jnp.int32)
    positions = jnp.concatenate([local_place, local_place])
    stream = jnp.concatenate(
        [jnp.zeros((local_count,), jnp.int32), jnp.ones((local_count,), jnp.int32)]
    )
    doc_ends = jnp.cumsum(doc_lengths[0])
    segments = segment_of(positions, doc_ends)
    angles = rotary_angles(positions)
    noise_row = noise_mask[0]
    noisy_stream = stream[local_count:]
    noisy_allowed = visible(
        stream, positions, segments, noisy_stream, positions[local_count:], segments[local_count:]
    )
    gathered = (
        lax.all_gather(own_params[0], "fsdp", axis=0, tiled=True),
        lax.all_gather(own_params[1], "fsdp", axis=0, tiled=True),
        lax.all_gather(own_params[2], "fsdp", axis=0, tiled=True),
        lax.all_gather(own_params[3], "fsdp", axis=0, tiled=True),
        lax.all_gather(own_params[4], "fsdp", axis=0, tiled=True),
        lax.all_gather(own_params[5], "fsdp", axis=0, tiled=True),
        lax.all_gather(own_params[6], "fsdp", axis=0, tiled=True),
        lax.all_gather(own_params[7], "fsdp", axis=0, tiled=True),
        lax.all_gather(own_params[8], "fsdp", axis=0, tiled=True),
    )
    inputs = build_inputs(hidden, noise_row, gathered[8])
    normed, query_rows, key_rows, value_rows = project(inputs, gathered, angles)
    clean_keys = key_rows[:local_count].reshape(local_count, model_dim)
    clean_values = value_rows[:local_count].reshape(local_count, model_dim)
    start_state = (
        jnp.full((HEADS, row_count), LOWEST, jnp.float32),
        jnp.zeros((HEADS, row_count), jnp.float32),
        jnp.zeros((HEADS, row_count, HEAD_DIM), jnp.float32),
    )
    running = start_state
    piece_keys = lax.all_gather(clean_keys, "ctx", axis=0, tiled=True)
    piece_values = lax.all_gather(clean_values, "ctx", axis=0, tiled=True)
    piece_rows = piece_keys.shape[0]
    fold_tile_size = math.gcd(piece_rows, 512)

    def step(carried, tile_index):
        tile_start = tile_index * fold_tile_size
        key_tile = lax.dynamic_slice_in_dim(piece_keys, tile_start, fold_tile_size, 0).reshape(
            fold_tile_size, HEADS, HEAD_DIM
        )
        value_tile = lax.dynamic_slice_in_dim(piece_values, tile_start, fold_tile_size, 0).reshape(
            fold_tile_size, HEADS, HEAD_DIM
        )
        key_position = tile_start + jnp.arange(fold_tile_size, dtype=jnp.int32)
        allowed = visible(
            stream,
            positions,
            segments,
            jnp.zeros((fold_tile_size,), jnp.int32),
            key_position,
            segment_of(key_position, doc_ends),
        )
        carried = lax.cond(
            jnp.any(allowed),
            lambda held: mix_tile(held, query_rows, key_tile, value_tile, allowed),
            lambda held: held,
            carried,
        )
        return (carried, None)

    running, _ = lax.scan(step, running, jnp.arange(piece_rows // fold_tile_size))
    run_max, run_sum, accum = mix_tile(
        running, query_rows, key_rows[local_count:], value_rows[local_count:], noisy_allowed
    )
    attended = accum / run_sum[..., None]
    attended_low = (
        jnp.transpose(attended, (1, 0, 2)).reshape(row_count, model_dim).astype(jnp.bfloat16)
    )
    middle, normed_two, upper, activated = upper_half(inputs, attended_low, gathered)
    result = (
        middle
        + jnp.dot(activated, gathered[4], preferred_element_type=jnp.float32)
        + gathered[5].astype(jnp.float32)
    )
    layer_out = result.astype(jnp.bfloat16).reshape(1, 2, local_count, model_dim)
    again = (
        lax.all_gather(own_params[0], "fsdp", axis=0, tiled=True),
        lax.all_gather(own_params[1], "fsdp", axis=0, tiled=True),
        lax.all_gather(own_params[2], "fsdp", axis=0, tiled=True),
        lax.all_gather(own_params[3], "fsdp", axis=0, tiled=True),
        lax.all_gather(own_params[4], "fsdp", axis=0, tiled=True),
        lax.all_gather(own_params[5], "fsdp", axis=0, tiled=True),
        lax.all_gather(own_params[6], "fsdp", axis=0, tiled=True),
        lax.all_gather(own_params[7], "fsdp", axis=0, tiled=True),
        lax.all_gather(own_params[8], "fsdp", axis=0, tiled=True),
    )
    normed, query_rows, key_rows, value_rows = project(inputs, again, angles)
    noisy_keys = key_rows[local_count:]
    noisy_values = value_rows[local_count:]
    middle, normed_two, upper, activated = upper_half(inputs, attended_low, again)
    grad_rows = out_grad[0].reshape(row_count, model_dim)
    grad_float = grad_rows.astype(jnp.float32)
    grad_down = jnp.einsum("qi,qj->ij", activated, grad_rows, preferred_element_type=jnp.float32)
    grad_down_bias = jnp.sum(grad_float, axis=0)
    activated_grad = jnp.einsum(
        "qj,ij->qi", grad_rows, again[4], preferred_element_type=jnp.float32
    )
    _, gelu_pull = jax.vjp(lambda upper_in: jax.nn.gelu(upper_in, approximate=True), upper)
    upper_grad = gelu_pull(activated_grad)[0].astype(jnp.bfloat16)
    grad_up = jnp.einsum("qi,qj->ij", normed_two, upper_grad, preferred_element_type=jnp.float32)
    grad_up_bias = jnp.sum(upper_grad.astype(jnp.float32), axis=0)
    normed_two_grad = jnp.einsum(
        "qj,ij->qi", upper_grad, again[2], preferred_element_type=jnp.float32
    )
    _, second_pull = jax.vjp(layer_norm, middle, again[7].astype(jnp.float32))
    middle_norm_grad, grad_gain_two = second_pull(normed_two_grad)
    middle_grad = (grad_float + middle_norm_grad).astype(jnp.bfloat16)
    grad_out_proj = jnp.einsum(
        "qi,qj->ij", attended_low, middle_grad, preferred_element_type=jnp.float32
    )
    attended_grad = jnp.einsum(
        "qj,ij->qi", middle_grad, again[1], preferred_element_type=jnp.float32
    )
    attended_grad = jnp.transpose(attended_grad.reshape(row_count, HEADS, HEAD_DIM), (1, 0, 2))
    scaled_grad = (attended_grad / run_sum[..., None]).astype(jnp.bfloat16)
    correction = jnp.sum(attended_grad * attended, axis=-1) / run_sum
    pair_rows = (
        lax.all_gather(
            key_rows[:local_count].reshape(local_count, model_dim), "ctx", axis=0, tiled=True
        ),
        lax.all_gather(
            value_rows[:local_count].reshape(local_count, model_dim), "ctx", axis=0, tiled=True
        ),
    )
    pair_keys, pair_values = pair_rows
    total_rows = pair_keys.shape[0]
    tile_size = math.gcd(total_rows, 512)
    zero_tile = jnp.zeros((tile_size, HEADS, HEAD_DIM), jnp.float32)

    def back_step(query_acc, tile_index):
        tile_start = tile_index * tile_size
        key_tile = lax.dynamic_slice_in_dim(pair_keys, tile_start, tile_size, 0).reshape(
            tile_size, HEADS, HEAD_DIM
        )
        value_tile = lax.dynamic_slice_in_dim(pair_values, tile_start, tile_size, 0).reshape(
            tile_size, HEADS, HEAD_DIM
        )
        key_position = tile_start + jnp.arange(tile_size, dtype=jnp.int32)
        allowed = visible(
            stream,
            positions,
            segments,
            jnp.zeros((tile_size,), jnp.int32),
            key_position,
            segment_of(key_position, doc_ends),
        )

        def live_tile(held):
            query_part, key_part, value_part = tile_grads(
                query_rows, key_tile, value_tile, allowed, run_max, scaled_grad, correction
            )
            return (held + query_part, key_part, value_part)

        query_acc, key_part, value_part = lax.cond(
            jnp.any(allowed), live_tile, lambda held: (held, zero_tile, zero_tile), query_acc
        )
        return (
            query_acc,
            (key_part.reshape(tile_size, model_dim), value_part.reshape(tile_size, model_dim)),
        )

    query_acc, (key_terms, value_terms) = lax.scan(
        back_step,
        jnp.zeros((row_count, HEADS, HEAD_DIM), jnp.float32),
        jnp.arange(total_rows // tile_size),
    )
    key_terms = key_terms.reshape(total_rows, model_dim)
    value_terms = value_terms.reshape(total_rows, model_dim)
    clean_key_grad, clean_value_grad = (
        lax.psum_scatter(
            key_terms.astype(jnp.bfloat16), "ctx", scatter_dimension=0, tiled=True
        ).astype(jnp.float32),
        lax.psum_scatter(
            value_terms.astype(jnp.bfloat16), "ctx", scatter_dimension=0, tiled=True
        ).astype(jnp.float32),
    )
    query_part, noisy_key_part, noisy_value_part = tile_grads(
        query_rows, noisy_keys, noisy_values, noisy_allowed, run_max, scaled_grad, correction
    )
    query_grad = (query_acc + query_part) * 0.125
    key_grad = (
        jnp.concatenate(
            [clean_key_grad.reshape(local_count, HEADS, HEAD_DIM), noisy_key_part], axis=0
        )
        * 0.125
    )
    value_grad = jnp.concatenate(
        [clean_value_grad.reshape(local_count, HEADS, HEAD_DIM), noisy_value_part], axis=0
    )
    _, rotate_pull = jax.vjp(lambda heads_in: rotate(heads_in, angles), query_grad)
    query_raw_grad = rotate_pull(query_grad)[0]
    key_raw_grad = rotate_pull(key_grad)[0]
    projected_grad = jnp.concatenate(
        [
            query_raw_grad.reshape(row_count, model_dim),
            key_raw_grad.reshape(row_count, model_dim),
            value_grad.reshape(row_count, model_dim),
        ],
        axis=1,
    ).astype(jnp.bfloat16)
    grad_qkv = jnp.einsum("qi,qj->ij", normed, projected_grad, preferred_element_type=jnp.float32)
    normed_grad = jnp.einsum(
        "qj,ij->qi", projected_grad, again[0], preferred_element_type=jnp.float32
    )
    _, first_pull = jax.vjp(layer_norm, inputs, again[6].astype(jnp.float32))
    inputs_norm_grad, grad_gain_one = first_pull(normed_grad)
    inputs_grad = middle_grad.astype(jnp.float32) + inputs_norm_grad
    noisy_flag = (noise_row == 1)[:, None]
    noisy_grad = inputs_grad[local_count:]
    grad_mask = jnp.sum(jnp.where(noisy_flag, noisy_grad, 0.0), axis=0)
    input_grad = jnp.concatenate(
        [inputs_grad[:local_count], jnp.where(noisy_flag, 0.0, noisy_grad)], axis=0
    )
    input_grad = input_grad.astype(jnp.bfloat16).reshape(1, 2, local_count, model_dim)
    shares = (
        lax.psum_scatter(grad_qkv, ("ctx", "fsdp"), scatter_dimension=0, tiled=True),
        lax.psum_scatter(grad_out_proj, ("ctx", "fsdp"), scatter_dimension=0, tiled=True),
        lax.psum_scatter(grad_up, ("ctx", "fsdp"), scatter_dimension=0, tiled=True),
        lax.psum_scatter(grad_up_bias, ("ctx", "fsdp"), scatter_dimension=0, tiled=True),
        lax.psum_scatter(grad_down, ("ctx", "fsdp"), scatter_dimension=0, tiled=True),
        lax.psum_scatter(grad_down_bias, ("ctx", "fsdp"), scatter_dimension=0, tiled=True),
        lax.psum_scatter(grad_gain_one, ("ctx", "fsdp"), scatter_dimension=0, tiled=True),
        lax.psum_scatter(grad_gain_two, ("ctx", "fsdp"), scatter_dimension=0, tiled=True),
        lax.psum_scatter(grad_mask, ("ctx", "fsdp"), scatter_dimension=0, tiled=True),
    )
    (
        qkv_share,
        out_share,
        up_share,
        up_bias_share,
        down_share,
        down_bias_share,
        gain_one_share,
        gain_two_share,
        mask_share,
    ) = shares
    return (
        layer_out,
        input_grad,
        qkv_share,
        out_share,
        up_share,
        up_bias_share,
        down_share,
        down_bias_share,
        gain_one_share,
        gain_two_share,
        mask_share,
    )


CHUNK = 256
COST = 10**9
GROUP = 3
WIDE = GROUP * HEAD_DIM
HALF = HEAD_DIM // 2
LANES = GROUP * CHUNK
BF = jnp.bfloat16
F32 = jnp.float32
HB = pl.BlockSpec(memory_space=pltpu.HBM)
SM = pl.BlockSpec(memory_space=pltpu.SMEM)
GELU_SCALE = math.sqrt(2.0 / math.pi)


def swap(v, bit):
    return lax.ppermute(v, "ctx", [(i, i ^ bit) for i in range(8)])


def turn(v, step):
    return lax.ppermute(v, "fsdp", [(i, (i + step) % 4) for i in range(4)])


def mm(a, b, ca=1, cb=0):
    return lax.dot_general(a, b, (((ca,), (cb,)), ((), ())), preferred_element_type=F32)


def flip(v):
    return jnp.transpose(v.astype(F32)).astype(v.dtype)


def call(body, outs, kinds, args, scratch=(), flops=0, moved=0):
    staged = [i for i, kind in enumerate(kinds) if kind == "V"]
    space = {"S": SM, "V": HB, "A": HB}
    count, made = len(args), len(outs)

    def run(*refs):
        ins, sinks, rest = list(refs[:count]), refs[count : count + made], refs[count + made :]
        held, results = rest[: len(staged)], rest[len(staged) : len(staged) + made]
        sem_in, sem_out, sems = rest[len(staged) + made : len(staged) + made + 3]
        rest = rest[len(staged) + made + 3 :]
        first = [
            pltpu.make_async_copy(ins[i], held[k], sem_in.at[k]) for k, i in enumerate(staged)
        ]
        for copy in first:
            copy.start()
        for k, i in enumerate(staged):
            ins[i] = held[k]

        def load(pairs):
            more = [pltpu.make_async_copy(a, b, sems.at[i]) for i, (a, b) in enumerate(pairs)]
            for copy in more:
                copy.start()
            for copy in more + first:
                copy.wait()

        body(load, *ins, *results, *rest)
        last = [pltpu.make_async_copy(results[k], sinks[k], sem_out.at[k]) for k in range(made)]
        for copy in last:
            copy.start()
        for copy in last:
            copy.wait()

    return pl.pallas_call(
        run,
        out_shape=tuple(jax.ShapeDtypeStruct(s, d) for s, d in outs),
        in_specs=[space[kind] for kind in kinds],
        out_specs=tuple(HB for _ in outs),
        scratch_shapes=[pltpu.VMEM(args[i].shape, args[i].dtype) for i in staged]
        + [pltpu.VMEM(s, d) for s, d in outs]
        + [
            pltpu.SemaphoreType.DMA((max(1, len(staged)),)),
            pltpu.SemaphoreType.DMA((made,)),
            pltpu.SemaphoreType.DMA((48,)),
        ]
        + list(scratch),
        compiler_params=pltpu.CompilerParams(vmem_limit_bytes=56 * 2**20),
        cost_estimate=pl.CostEstimate(flops=1 + flops // COST, bytes_accessed=1 + moved // COST, transcendentals=0),
    )(*args)


def at16(v):
    return pl.multiple_of(v, 16)


def shard_rows(meta, near, far, dst, unit):
    half = unit // 2
    pairs = []
    for zz in range(4):
        for core, part in ((meta[1], near), (1 - meta[1], far)):
            to = at16(zz * unit + core * half)
            pairs.append((part.at[zz, pl.ds(0, half)], dst.at[pl.ds(to, half)]))
    return pairs


def norm_parts(x):
    mean = jnp.mean(x, axis=-1, keepdims=True)
    centered = x - mean
    var = jnp.mean(centered * centered, axis=-1, keepdims=True)
    scale = lax.rsqrt(var + EPSILON)
    return centered * scale, scale


def unmark(x, embed):
    x = x.astype(F32)
    flag = x[:, :1] > 1e38
    return jnp.where(flag, embed, x), flag


def turn_heads(v, cos, sin):
    parts = []
    for g in range(GROUP):
        a = v[g * HEAD_DIM : g * HEAD_DIM + HALF]
        b = v[g * HEAD_DIM + HALF : (g + 1) * HEAD_DIM]
        parts += [a * cos - b * sin, b * cos + a * sin]
    return jnp.concatenate(parts, axis=0)


def project_body(load, meta, gain, embed, cos, sin, *refs):
    rows, refs = refs[:8], refs[8:]
    near, far, q_ref, kv_a, kv_b, n_ref, mk_ref, w, xs, wp = refs
    load(shard_rows(meta, near, far, w, 192) + [(rows[i], xs.at[i]) for i in range(8)])
    for part in range(3):
        wp[part] = w[:, part * WIDE : (part + 1) * WIDE]

    @pl.loop(0, 8)
    def _(i):
        x, flag = unmark(xs[i], embed[...])
        hat, _ = norm_parts(x)
        n = (hat * gain[...]).astype(BF)
        n_ref[i] = n
        mk_ref[i] = jnp.broadcast_to(jnp.where(flag, 1.0, 0.0), (CHUNK, 128)).astype(BF)
        q_ref[i] = turn_heads(jnp.transpose(mm(n, wp[0])), cos[i], sin[i]).astype(BF)
        keys = turn_heads(jnp.transpose(mm(n, wp[1])), cos[i], sin[i]).astype(BF)
        values = jnp.transpose(mm(n, wp[2])).astype(BF)
        for half, ref in enumerate((kv_a, kv_b)):

            @pl.when(i // 4 == half)
            def _():
                ref[i % 4, :WIDE] = keys
                ref[i % 4, WIDE:] = values


def project_rows(meta, gain, embed, cos, sin, rows, weights):
    dim = rows[0].shape[1]
    wide = weights[0].shape[-1]
    return call(
        project_body,
        [
            ((8, WIDE, CHUNK), BF),
            ((4, 2 * WIDE, CHUNK), BF),
            ((4, 2 * WIDE, CHUNK), BF),
            ((8, CHUNK, dim), BF),
            ((8, CHUNK, 128), BF),
            ((dim, wide), BF),
        ],
        "SVVVV" + "A" * 10,
        (meta, gain, embed, cos, sin, *rows, *weights),
        scratch=[pltpu.VMEM((8, CHUNK, dim), BF), pltpu.VMEM((3, dim, WIDE), BF)],
        flops=2 * 8 * CHUNK * dim * 3 * WIDE,
        moved=8 * CHUNK * dim * 6,
    )


def head_pairs(refs, qs, kv):
    pairs = [(refs[0], qs)]
    for i, ref in enumerate(refs[1:]):
        pairs.append((ref, kv.at[i // 2, pl.ds(i % 2 * 4, 4)]))
    return pairs


def thrice(v):
    return jnp.concatenate([v, v, v], axis=1)


def scores_of(keys, stacked, base, low, high):
    s = mm(keys, stacked) * 0.125
    place = base + lax.broadcasted_iota(jnp.int32, (CHUNK, LANES), 0)
    return jnp.where((place >= low) & (place < high), s, LOWEST)


def stack_heads(q, stacked):
    for g in range(GROUP):
        stacked[g * HEAD_DIM : (g + 1) * HEAD_DIM, g * CHUNK : (g + 1) * CHUNK] = q[
            g * HEAD_DIM : (g + 1) * HEAD_DIM
        ]


def attend_body(load, meta, bounds, *refs):
    heads = refs[:5]
    send, o_ref, ml_ref, qs, kv, kr, stacked, m_s, l_s, acc = refs[5:]
    load(head_pairs(heads, qs, kv))
    stacked[...] = jnp.zeros_like(stacked)

    @pl.loop(0, 8)
    def _(s):
        for own in range(2):
            kr[own, s] = flip(kv[own, s, :WIDE])

    r, c = meta[0], meta[1]

    @pl.loop(0, 8)
    def _(p):
        s = p ^ r
        stack_heads(qs[s], stacked)
        lim = bounds[p]
        low, high, nlow, nhigh = [thrice(lim[i : i + 1]) for i in range(4)]

        def tile(keys, values, base, lo, hi):
            masked = scores_of(keys, stacked[...], base, lo, hi)
            m_old = m_s[...]
            m_new = jnp.maximum(m_old, jnp.max(masked, axis=0, keepdims=True))
            e = jnp.exp(masked - m_new)
            f = jnp.exp(m_old - m_new)
            m_s[...] = m_new
            l_s[...] = l_s[...] * f + jnp.sum(e, axis=0, keepdims=True)
            e = e.astype(BF)
            for g in range(GROUP):
                cut = slice(g * CHUNK, (g + 1) * CHUNK)
                acc[g] = acc[g] * f[:, cut] + mm(
                    values[g * HEAD_DIM : (g + 1) * HEAD_DIM], e[:, cut]
                )

        m_s[...] = jnp.full_like(m_s, LOWEST)
        l_s[...] = jnp.zeros_like(l_s)
        acc[...] = jnp.zeros_like(acc)
        tile(kr[0, s], kv[0, s, WIDE:], p * CHUNK, nlow, nhigh)

        @pl.loop(meta[4 + p], p + c)
        def _(k):
            t = k ^ r ^ c
            tile(kr[c, t], kv[c, t, WIDE:], k * CHUNK, low, high)

        total = l_s[...]
        inv = 1.0 / total
        out = jnp.concatenate(
            [acc[g] * inv[:, g * CHUNK : (g + 1) * CHUNK] for g in range(GROUP)], axis=0
        )
        o_ref[s] = out
        ml_ref[s, 0:1] = m_s[...]
        ml_ref[s, 1:2] = total
        send[p] = out.astype(BF)


HEAD_SCRATCH = [pltpu.VMEM((8, WIDE, CHUNK), BF), pltpu.VMEM((2, 8, 2 * WIDE, CHUNK), BF)]


def attend_rows(meta, bounds, heads):
    return call(
        attend_body,
        [((8, WIDE, CHUNK), BF), ((8, WIDE, CHUNK), F32), ((8, 8, LANES), F32)],
        "SV" + "A" * 5,
        (meta, bounds, *heads),
        scratch=HEAD_SCRATCH
        + [
            pltpu.VMEM((2, 8, CHUNK, WIDE), BF),
            pltpu.VMEM((WIDE, LANES), BF),
            pltpu.VMEM((1, LANES), F32),
            pltpu.VMEM((1, LANES), F32),
            pltpu.VMEM((GROUP, HEAD_DIM, CHUNK), F32),
        ],
        flops=20 * 2 * 2 * CHUNK * LANES * 256,
        moved=8 * CHUNK * WIDE * 16,
    )


def attend_back_body(load, meta, bounds, cos, sin, o_ref, ml_ref, *refs):
    heads, gs = refs[:5], refs[5]
    (
        pq_ref, own_ref, far_a, far_b, far_c, far_d,
        qs, kv, kr, vr, st_q, st_g, row_q, row_g, dk_o, dv_o, dk_c, dv_c, dq,
    ) = refs[6:]
    for ref in (st_q, st_g, dk_o, dv_o, dk_c, dv_c):
        ref[...] = jnp.zeros_like(ref)
    load(head_pairs(heads, qs, kv))

    @pl.loop(0, 8)
    def _(s):
        for own in range(2):
            kr[own, s] = flip(kv[own, s, :WIDE])
            vr[own, s] = flip(kv[own, s, WIDE:])

    r, c = meta[0], meta[1]
    lane = lax.broadcasted_iota(jnp.int32, (CHUNK, WIDE), 1) // HEAD_DIM

    @pl.loop(0, 8)
    def _(p):
        s = p ^ r
        q = qs[s]
        stack_heads(q, st_q)
        total = ml_ref[s, 1:2]
        top = ml_ref[s, 0:1]
        g_in = gs[p].astype(F32)
        attended = o_ref[s]
        scaled, fix = [], []
        for g in range(GROUP):
            part = slice(g * HEAD_DIM, (g + 1) * HEAD_DIM)
            inv = 1.0 / total[:, g * CHUNK : (g + 1) * CHUNK]
            scaled.append(g_in[part] * inv)
            fix.append(jnp.sum(g_in[part] * attended[part], axis=0, keepdims=True) * inv)
        scaled = jnp.concatenate(scaled, axis=0)
        fix = jnp.concatenate(fix, axis=1)
        stack_heads(scaled.astype(BF), st_g)
        q_rows = jnp.transpose(q.astype(F32))
        g_rows = jnp.transpose(scaled)
        for g in range(GROUP):
            row_q[g * CHUNK : (g + 1) * CHUNK] = jnp.where(lane == g, q_rows, 0.0).astype(BF)
            row_g[g * CHUNK : (g + 1) * CHUNK] = jnp.where(lane == g, g_rows, 0.0).astype(BF)
        lim = bounds[p]
        low, high, nlow, nhigh = [thrice(lim[i : i + 1]) for i in range(4)]
        dq[...] = jnp.zeros_like(dq)

        def tile(k_rows, v_rows, k_cols, base, lo, hi, dk, dv):
            e = jnp.exp(scores_of(k_rows, st_q[...], base, lo, hi) - top)
            d = (e * (mm(v_rows, st_g[...]) - fix)).astype(BF)
            e = e.astype(BF)
            dv[...] += mm(e, row_g[...])
            dk[...] += mm(d, row_q[...])
            for g in range(GROUP):
                dq[g * HEAD_DIM : (g + 1) * HEAD_DIM] += mm(
                    k_cols[g * HEAD_DIM : (g + 1) * HEAD_DIM], d[:, g * CHUNK : (g + 1) * CHUNK]
                )

        tile(kr[0, s], vr[0, s], kv[0, s, :WIDE], p * CHUNK, nlow, nhigh, dk_o.at[s], dv_o.at[s])

        @pl.loop(meta[4 + p], p + c)
        def _(k):
            t = k ^ r ^ c
            tile(kr[c, t], vr[c, t], kv[c, t, :WIDE], k * CHUNK, low, high, dk_c.at[t], dv_c.at[t])

        pq_ref[s] = turn_heads(dq[...] * 0.125, cos[s], -sin[s]).astype(BF)

    both = 1.0 - c.astype(F32)

    for s in range(8):
        dk = jnp.transpose(dk_c[s])
        dv = jnp.transpose(dv_c[s])
        far_ref = (far_a, far_b, far_c, far_d)[s // 2]
        far_ref[s % 2, :WIDE] = dk.astype(BF)
        far_ref[s % 2, WIDE:] = dv.astype(BF)
        own_ref[s, :WIDE] = jnp.transpose(dk_o[s]) + both * dk
        own_ref[s, WIDE:] = jnp.transpose(dv_o[s]) + both * dv


def attend_back(meta, bounds, cos, sin, attended, stats, heads, grads):
    rows = pltpu.VMEM((2, 8, CHUNK, WIDE), BF)
    sums = pltpu.VMEM((8, CHUNK, WIDE), F32)
    return call(
        attend_back_body,
        [((8, WIDE, CHUNK), BF), ((8, 2 * WIDE, CHUNK), F32)] + [((2, 2 * WIDE, CHUNK), BF)] * 4,
        "SVVVVV" + "A" * 5 + "V",
        (meta, bounds, cos, sin, attended, stats, *heads, grads),
        scratch=HEAD_SCRATCH
        + [
            rows,
            rows,
            pltpu.VMEM((WIDE, LANES), BF),
            pltpu.VMEM((WIDE, LANES), BF),
            pltpu.VMEM((LANES, WIDE), BF),
            pltpu.VMEM((LANES, WIDE), BF),
        ]
        + [sums] * 4
        + [pltpu.VMEM((WIDE, CHUNK), F32)],
        flops=20 * 2 * 5 * CHUNK * LANES * 256,
        moved=8 * CHUNK * WIDE * 30,
    )


def share_pairs(meta, own, parts, dst, unit, skip):
    h, z = meta[2], meta[3]
    part = unit // 4
    pairs = [(own, dst.at[pl.ds(at16(z * unit), unit)])]
    for t in range(1, 4):
        zz = (z + 4 - t) & 3
        for k in range(4):
            to = at16(zz * unit + (h ^ k) * part)
            pairs.append((parts[k].at[t - 1, pl.ds(skip, part)], dst.at[pl.ds(to, part)]))
    return pairs


def middle_body(load, meta, gain, embed, x_ref, heads, own, *refs):
    parts = refs[:4]
    mid_ref, n_ref, att_ref, w_ref = refs[4:]
    pairs = share_pairs(meta, own, parts, w_ref, 192, 0)
    for d in range(8):
        pairs.append((heads.at[d], att_ref.at[d % 2, pl.ds(d // 2 * WIDE, WIDE)]))
    load(pairs)
    for stream in range(2):
        x, _ = unmark(x_ref[stream], embed[...])
        mid = x + mm(att_ref[stream], w_ref[...], 0, 0)
        hat, _ = norm_parts(mid)
        mid_ref[stream] = mid
        n_ref[stream * CHUNK : (stream + 1) * CHUNK] = (hat * gain[...]).astype(BF)


def middle_rows(meta, gain, embed, marked, heads, own, parts):
    dim = marked.shape[2]
    return call(
        middle_body,
        [((2, CHUNK, dim), F32), ((2 * CHUNK, dim), BF), ((2, dim, CHUNK), BF), ((dim, dim), BF)],
        "SVVV" + "A" * 6,
        (meta, gain, embed, marked, heads, own, *parts),
        flops=2 * 2 * CHUNK * dim * dim,
        moved=8 * CHUNK * dim * 2,
    )


def feed_body(load, meta, bias, n_own, n_far, g_own, g_far, up_own, down_own, *refs):
    shares = refs[:4]
    (
        out_ref, outf_ref, ngf_ref, ng_ref, gb_ref, d_ref, u_ref,
        ns, gs, wu, wd, acts, slopes,
    ) = refs[4:]
    c, h, z = meta[1], meta[2], meta[3]
    rows = 2 * CHUNK
    part = bias.shape[1] // 4
    pairs = [
        (n_own, ns.at[pl.ds(0, rows)]),
        (n_far, ns.at[pl.ds(rows, rows)]),
        (g_own, gs.at[pl.ds(0, rows)]),
        (g_far, gs.at[pl.ds(rows, rows)]),
    ]
    pairs += share_pairs(meta, down_own.at[pl.ds(at16(c * part), part)], shares, wd, part, 48)
    for k in range(4):
        cols = pl.ds(pl.multiple_of(k * 2 * part + c * part, 128), part)
        pairs.append((up_own.at[:, cols], wu.at[pl.ds(at16(z * 192), 192), pl.ds(k * part, part)]))
    for t in range(1, 4):
        zz = (z + 4 - t) & 3
        for k in range(4):
            dst = pl.ds(at16(zz * 192 + (h ^ k) * 48), 48)
            for b in range(2):
                pairs.append(
                    (
                        shares[k].at[t - 1, pl.ds(144 + 48 * b, 48)],
                        wu.at[dst, pl.ds(2 * part * b, 2 * part)],
                    )
                )
    load(pairs)
    gb_ref[...] = jnp.zeros_like(gb_ref)

    def forward_and_back(span, out, ng):
        v = mm(ns[span], wu[...]) + bias[...]
        square = v * v
        th = jnp.tanh(v * (GELU_SCALE + (GELU_SCALE * 0.044715) * square))
        half = 0.5 + 0.5 * th
        act = (v * half).astype(BF)
        slope = half + (v * half) * (1.0 - th) * (GELU_SCALE + (3.0 * 0.044715 * GELU_SCALE) * square)
        acts[span] = act
        ug = (slope * mm(gs[span], wd[...], 1, 1)).astype(BF)
        slopes[span] = ug
        gb_ref[...] += jnp.sum(ug.astype(F32), axis=0, keepdims=True)
        out[...] = mm(act, wd[...]).astype(out.dtype)
        ng[...] = mm(ug, wu[...], 1, 1).astype(ng.dtype)

    @pl.loop(0, 2)
    def _(i):
        low = pl.ds(pl.multiple_of(i * CHUNK, CHUNK), CHUNK)
        forward_and_back(low, out_ref.at[low], ng_ref.at[low])
        forward_and_back(
            pl.ds(pl.multiple_of(rows + i * CHUNK, CHUNK), CHUNK), outf_ref.at[low], ngf_ref.at[low]
        )

    @pl.loop(0, 4)
    def _(j):
        cols = pl.ds(pl.multiple_of(j * part, 128), part)
        gd = mm(acts[:, cols], gs[...], 0, 0).astype(BF)
        for b in range(4):
            d_ref[b, j] = gd[96 * b : 96 * (b + 1)]
        gu = mm(ns[...], slopes[:, cols], 0, 0)
        side = pl.ds(pl.multiple_of((j & 1) * part, 128), part)
        line = pl.ds(at16((j >> 1) * 48), 48)
        for b in range(16):
            first = 192 * (b // 4) + 24 * (b % 4)
            block = jnp.concatenate([gu[first : first + 24], gu[first + 96 : first + 120]])
            u_ref[b // 4, b % 4, line, side] = block.astype(BF)


def feed_rows(meta, bias, args):
    rows = 2 * CHUNK
    dim = args[0].shape[1]
    hid = bias.shape[1]
    return call(
        feed_body,
        [((rows, dim), F32), ((rows, dim), BF), ((rows, dim), BF), ((rows, dim), F32)]
        + [((1, hid), F32)]
        + [((4, 4, hid // 16, dim), BF)] * 2,
        "SV" + "A" * 10,
        (meta, bias, *args),
        scratch=[
            pltpu.VMEM((2 * rows, dim), BF),
            pltpu.VMEM((2 * rows, dim), BF),
            pltpu.VMEM((dim, hid), BF),
            pltpu.VMEM((hid, dim), BF),
            pltpu.VMEM((2 * rows, hid), BF),
            pltpu.VMEM((2 * rows, hid), BF),
        ],
        flops=6 * 2 * 2 * rows * dim * hid,
        moved=12 * dim * hid,
    )


def pack_body(load, meta, w_out, w_down, w_up, share):
    c, h = meta[1], meta[2]
    part = w_up.shape[1] // 8
    pairs = [
        (w_out.at[pl.ds(at16(48 * h), 48)], share.at[pl.ds(0, 48)]),
        (w_down.at[pl.ds(at16(part * c + 96 * h), 96)], share.at[pl.ds(48, 96)]),
    ]
    for k in range(4):
        cols = pl.ds(pl.multiple_of((2 * k + c) * part, 128), part)
        to = share.at[pl.ds(144 + 48 * (k // 2), 48), pl.ds(part * (k % 2), part)]
        pairs.append((w_up.at[pl.ds(at16(48 * h), 48), cols], to))
    load(pairs)


def pack_share(place, w_out, w_down, w_up):
    return call(pack_body, [((240, w_out.shape[1]), BF)], "SAAA", (place, w_out, w_down, w_up))[0]


def middle_back_body(
    load, meta, gain, b_down, mid_ref, ng_ref, out_ref, outf_ref, ngf_ref, g_ref, x_ref, w_ref,
    lay_ref, mg_ref, sum_ref, send,
):
    load([])
    gain_sum = jnp.zeros((1, gain.shape[1]), F32)
    g_sum = gain_sum
    for stream in range(2):
        span = slice(stream * CHUNK, (stream + 1) * CHUNK)
        mid = mid_ref[stream]
        lay = mid + out_ref[span] + outf_ref[span].astype(F32) + b_down[...]
        lay_ref[stream] = lay.astype(BF)
        hat, scale = norm_parts(mid)
        ng = ng_ref[span] + ngf_ref[span].astype(F32)
        gain_sum += jnp.sum(ng * hat, axis=0, keepdims=True)
        t = ng * gain[...]
        g = g_ref[stream].astype(F32)
        g_sum += jnp.sum(g, axis=0, keepdims=True)
        t_mean = jnp.mean(t, axis=-1, keepdims=True)
        t_hat = jnp.mean(t * hat, axis=-1, keepdims=True)
        mg = (g + scale * (t - t_mean - hat * t_hat)).astype(BF)
        mg_ref[stream] = mg
        if stream == 1:
            flag = x_ref[1][:, :1].astype(F32) > 1e38
            sum_ref[2:3] = jnp.sum(jnp.where(flag, mg.astype(F32), 0.0), axis=0, keepdims=True)
    sum_ref[0:1] = gain_sum
    sum_ref[1:2] = g_sum
    for d in range(8):
        send[d] = mm(w_ref[d // 2 * WIDE : (d // 2 + 1) * WIDE], mg_ref[d % 2], 1, 1).astype(BF)


def middle_back(meta, gain, b_down, args):
    dim = gain.shape[1]
    return call(
        middle_back_body,
        [((2, CHUNK, dim), BF), ((2, CHUNK, dim), BF), ((8, dim), F32), ((8, WIDE, CHUNK), BF)],
        "S" + "V" * 10,
        (meta, gain, b_down, *args),
        flops=4 * CHUNK * dim * dim,
        moved=20 * CHUNK * dim,
    )


def by_z(grad, ref):
    for zz in range(4):
        for h in range(4):
            first = 192 * h + 24 * zz
            pair = jnp.concatenate([grad[first : first + 24], grad[first + 96 : first + 120]])
            ref[zz, 48 * h : 48 * (h + 1)] = pair.astype(BF)


def out_grad_body(load, att_ref, mg_ref, o_ref):
    load([])
    by_z(mm(att_ref[0], mg_ref[0]) + mm(att_ref[1], mg_ref[1]), o_ref)


def project_back_body(
    own, f0, f1, f2, f3, pq, n_ref, mk_ref, cos, sin, w_ref,
    away_x, away_y, stay, gq_ref, gs_ref, wp, acc,
):
    i = pl.program_id(0)

    @pl.when(i == 0)
    def _():
        for part in range(3):
            wp[part] = w_ref[:, part * WIDE : (part + 1) * WIDE]
        acc[...] = jnp.zeros_like(acc)
        gs_ref[...] = jnp.zeros_like(gs_ref)

    piece = jnp.where(i % 4 == 0, 1 - i // 4, jnp.where(i == 1, 3, jnp.where(i == 3, 3, jnp.where(i == 7, 1, jnp.where(i == 6, 0, 2)))))
    far = jnp.where(piece < 2, jnp.where(piece == 0, f0[0], f1[0]), jnp.where(piece == 2, f2[0], f3[0]))
    kv = own[0] + far.astype(F32)
    parts = [
        pq[0],
        turn_heads(kv[:WIDE] * 0.125, cos[0], -sin[0]).astype(BF),
        kv[WIDE:].astype(BF),
    ]
    n, mk = n_ref[0], mk_ref[0]
    ng = jnp.zeros((CHUNK, n.shape[1]), F32)
    for k in range(3):
        ng += mm(flip(parts[k]), wp[k], 1, 1)
        acc[k * WIDE : (k + 1) * WIDE] += mm(parts[k], n)
    low = ng.astype(BF)

    @pl.when(i < 2)
    def _():
        away_x[0] = low

    @pl.when((i >= 2) & (i < 4))
    def _():
        away_y[0] = low

    @pl.when(i >= 4)
    def _():
        stay[0] = ng

    gs_ref[0:1] += jnp.sum(ng * n.astype(F32), axis=0, keepdims=True)
    gs_ref[1:2] += jnp.sum(ng * mk[:, :1].astype(F32), axis=0, keepdims=True)

    @pl.when(i == 7)
    def _():
        by_z(jnp.transpose(acc[...]), gq_ref)


def pick(order):
    def slot_of(i):
        slot = jnp.int32(order[-1])
        for k in range(len(order) - 2, -1, -1):
            slot = jnp.where(i == k, order[k], slot)
        return slot

    return slot_of


def project_back(own, far, pq, n, mk, cos, sin, w):
    dim = n.shape[2]
    wide = w.shape[1] + HEAD_DIM
    slot = pick((2, 6, 5, 7, 0, 4, 1, 3))

    def block(rows, cols, index):
        return pl.BlockSpec((1, rows, cols), lambda i: (index(i), 0, 0))

    def whole(*shape):
        return pl.BlockSpec(shape, lambda i: tuple(0 for _ in shape))

    return pl.pallas_call(
        project_back_body,
        grid=(8,),
        out_shape=(
            jax.ShapeDtypeStruct((2, CHUNK, dim), BF),
            jax.ShapeDtypeStruct((2, CHUNK, dim), BF),
            jax.ShapeDtypeStruct((4, CHUNK, dim), F32),
            jax.ShapeDtypeStruct((4, dim // 4, wide), BF),
            jax.ShapeDtypeStruct((8, dim), F32),
        ),
        in_specs=[
            block(2 * WIDE, CHUNK, slot),
            *[block(2 * WIDE, CHUNK, lambda i: slot(i) % 2)] * 4,
            block(WIDE, CHUNK, slot),
            block(CHUNK, dim, slot), block(CHUNK, 128, slot),
            block(HALF, CHUNK, slot), block(HALF, CHUNK, slot), whole(*w.shape),
        ],
        out_specs=(
            block(CHUNK, dim, lambda i: jnp.minimum(i, 1)),
            block(CHUNK, dim, lambda i: jnp.clip(i - 2, 0, 1)),
            block(CHUNK, dim, lambda i: jnp.clip(i - 4, 0, 3)),
            whole(4, dim // 4, wide),
            whole(8, dim),
        ),
        scratch_shapes=[pltpu.VMEM((3, dim, WIDE), BF), pltpu.VMEM((wide, dim), F32)],
        compiler_params=pltpu.CompilerParams(vmem_limit_bytes=56 * 2**20),
        cost_estimate=pl.CostEstimate(
            flops=1 + 4 * 8 * CHUNK * dim * 3 * WIDE // COST, bytes_accessed=1, transcendentals=0
        ),
    )(own, *far, pq, n, mk, cos, sin, w)


def last_body(load, meta, gain, embed, x_ref, mg_ref, keep_ref, far_ref, o_ref):
    load([])
    c = meta[1]
    for stream, ng in ((c, keep_ref[...]), (1 - c, far_ref[...].astype(F32))):
        x, flag = unmark(x_ref[stream], embed[...])
        hat, scale = norm_parts(x)
        t = ng * gain[...]
        t_mean = jnp.mean(t, axis=-1, keepdims=True)
        t_hat = jnp.mean(t * hat, axis=-1, keepdims=True)
        grad = mg_ref[stream].astype(F32) + scale * (t - t_mean - hat * t_hat)
        o_ref[stream] = jnp.where(flag, 0.0, grad).astype(BF)


def cut(v, index, size, axis=0):
    return lax.dynamic_slice_in_dim(v, index * size, size, axis)


def at(v, index, axis=0):
    return lax.dynamic_index_in_dim(v, index, axis, keepdims=False)


def after(value, *needed):
    return lax.optimization_barrier((value, *needed))[0]


def add(a, b):
    return a.astype(F32) + b.astype(F32)


def exchange(v):
    return lax.all_to_all(v, "ctx", 0, 0, tiled=True)


def exchange_chips(v):
    groups = [[i + core for i in range(0, 8, 2)] for core in range(2)]
    return lax.all_to_all(v, "ctx", 0, 0, axis_index_groups=groups, tiled=True)


def exchange_z(v):
    return lax.all_to_all(v, "fsdp", 0, 0, tiled=True)


def shards_by_heads(
    hidden,
    noise_mask,
    doc_lengths,
    w_qkv,
    w_out,
    w_up,
    b_up,
    w_down,
    b_down,
    gain_one,
    gain_two,
    mask_embed,
    out_grad,
):
    r = lax.axis_index("ctx")
    z = lax.axis_index("fsdp")
    c, h = r & 1, r >> 1
    dim = hidden.shape[3]
    hid = w_up.shape[1]
    part = hid // 8
    total = CHUNK * 8
    clean = c == 0

    share = pack_share(jnp.stack([r, c, h, z]).astype(jnp.int32), w_out, w_down, w_up)
    ff_t = lax.all_gather(share, "fsdp")
    hidden = after(hidden, share)

    noisy = jnp.where(noise_mask[0][:, None] == 1, jnp.asarray(jnp.inf, BF), hidden[0, 1])
    mine = jnp.where(clean, hidden[0, 0], noisy)
    other = swap(jnp.where(clean, noisy, hidden[0, 0]), 1)
    mine_x, mine_y = swap(mine, 2), swap(mine, 4)
    other_x, other_y = swap(other, 2), swap(other, 4)
    marked = jnp.stack([hidden[0, 0], noisy])

    size = hid // 4 + dim
    w_qkv = after(w_qkv, other)
    small = jnp.concatenate([b_up, b_down, gain_one, gain_two, mask_embed])
    small = jnp.pad(small, (0, 16 * 3 * WIDE - size)).reshape(16, 3 * WIDE)
    own_qkv = jnp.concatenate([cut(w_qkv[:, k * dim : (k + 1) * dim], h, WIDE, 1) for k in range(3)], 1)
    quarter = dim // 4
    half = jnp.concatenate([cut(own_qkv, c, quarter // 2), small])
    half = jnp.broadcast_to(half, (4, *half.shape))
    near = exchange_z(half)
    far = swap(near, 1)
    small = near[:, quarter // 2 :].reshape(4, -1)[:, :size].astype(F32)
    bias = at(small[:, : hid // 4].reshape(4, 2, part), c, 1).reshape(1, 4 * part)
    b_down_all, gain_a, gain_b, embed = [
        small[:, hid // 4 + k * quarter : hid // 4 + (k + 1) * quarter].reshape(1, dim)
        for k in range(4)
    ]
    mine_d, other_d = swap(mine_x, 4), swap(other_y, 2)

    lengths = doc_lengths[0]
    index = jnp.arange(lengths.shape[0])
    ends = jnp.sum(jnp.where(index[None, :] <= index[:, None], lengths[None, :], 0), axis=1)
    place = jnp.arange(total, dtype=jnp.int32)
    later = ends[None, :] > place[:, None]
    start = jnp.max(jnp.where(later, 0, ends[None, :]), axis=1)
    stop = jnp.min(jnp.where(later, ends[None, :], total), axis=1)
    block = place // BLOCK * BLOCK
    limit = jnp.minimum(block + BLOCK, stop)
    bounds = jnp.stack(
        [start, jnp.where(clean, limit, block), jnp.where(clean, start, jnp.maximum(start, block)), limit]
    )
    bounds = jnp.pad(bounds.reshape(4, 8, CHUNK).transpose(1, 0, 2), ((0, 0), (0, 4), (0, 0)))
    meta = jnp.concatenate(
        [jnp.stack([r, c, h, z]), start[::CHUNK] // CHUNK, jnp.zeros((4,), jnp.int32)]
    ).astype(jnp.int32)
    slots = (jnp.arange(8) ^ r)[:, None] * CHUNK + jnp.arange(CHUNK)[None, :]
    frequency = jnp.exp(jnp.arange(HALF).astype(F32) * (-2.0 * math.log(10000.0) / HEAD_DIM))
    angles = slots.astype(F32)[:, None, :] * frequency[None, :, None]
    cos, sin = jnp.cos(angles), jnp.sin(angles)
    grads = out_grad[0]
    grad_rows = grads.reshape(2 * CHUNK, dim)

    ff_r = jnp.take(ff_t, (z - jnp.arange(1, 4)) % 4, axis=0)
    near, ff_r = lax.optimization_barrier((near, ff_r))
    shares = (ff_r, swap(ff_r, 2), swap(ff_r, 4), swap(ff_r, 6))
    rows = (mine, other, mine_x, other_x, mine_y, other_y, mine_d, other_d)
    q, *kv, normed_one, marks, w_all = project_rows(meta, gain_a, embed, cos, sin, rows, (near, far))
    give = [(i, i + 1) for i in range(0, 8, 2)]
    heads = (q, *kv, *[lax.ppermute(v, "ctx", give) for v in kv])
    send, attended, stats = attend_rows(meta, bounds, heads)
    grad_far = swap(after(grad_rows, kv[0]), 1)
    middle, normed, att, w_out_all = middle_rows(
        meta, gain_b, embed, marked, exchange(send), w_out, shares
    )
    out_own, out_far, ng_far, ng_own, gbu, gd, gu = feed_rows(
        meta, bias, (normed, swap(normed, 1), grad_rows, grad_far, w_up, w_down, *shares)
    )
    ng_far, out_far = swap(ng_far, 1), swap(out_far, 1)
    gd = lax.psum_scatter(gd.reshape(-1, dim), "fsdp", scatter_dimension=0, tiled=True)

    layer, mid_grad, sums, send = middle_back(
        meta, gain_b, b_down_all, (middle, ng_own, out_own, out_far, ng_far, grads, marked, w_out_all)
    )
    got = exchange(send)
    (go,) = call(
        out_grad_body, [((4, dim // 4, dim), BF)], "VV", (att, mid_grad), flops=4 * CHUNK * dim * dim
    )
    got, gu, go = lax.optimization_barrier((got, gu, go))
    go = lax.psum_scatter(go.reshape(-1, dim), "fsdp", scatter_dimension=0, tiled=True)
    gu = exchange_chips(gu)
    pq, own_kv, *far_kv = attend_back(meta, bounds, cos, sin, attended, stats, heads, got)
    far_kv = [lax.ppermute(v, "ctx", [(b, a) for a, b in give]) for v in far_kv]

    gu = jnp.sum(after(gu, pq).astype(F32), axis=0).astype(BF).reshape(-1, dim)
    gd = after(gd, pq).reshape(4, part // 4, dim)
    *far_kv, gu, gd = lax.optimization_barrier((*far_kv, gu, gd))
    gu = lax.psum_scatter(gu, "fsdp", scatter_dimension=0, tiled=True)

    away_x, away_y, stay, gq, vec = project_back(
        own_kv, far_kv, pq, normed_one, marks, cos, sin, w_all
    )
    in_x, in_y = swap(away_x, 2), swap(away_y, 4)
    gd = exchange_chips(gd)
    gbu = gbu.reshape(4, 1, part)
    gbu = jnp.where(clean, jnp.concatenate([gbu, 0 * gbu], 1), jnp.concatenate([0 * gbu, gbu], 1))
    flat = jnp.concatenate([gbu.reshape(-1), sums[:3].reshape(-1), vec[:2].reshape(-1)])
    wide = gq.shape[2]
    length = flat.shape[0]

    def parts_of(v):
        return jnp.pad(v, (0, 16 * wide - length)).reshape(16, wide).astype(BF)

    rows = dim // 4
    flat = jnp.broadcast_to(parts_of(flat), (4, 16, wide))
    gq = after(jnp.concatenate([gq, flat], 1).reshape(-1, wide), go)
    gq = lax.psum_scatter(gq, "fsdp", scatter_dimension=0, tiled=True)
    over_y, over_x = add(stay[1], in_x[1]).astype(BF), add(stay[3], in_y[1]).astype(BF)
    near_one, near_two = swap(over_y, 4), swap(over_x, 2)
    gq = after(gq, over_y, over_x, gd)
    flat = jnp.broadcast_to(gq[rows:], (8, 16, wide))
    gq = jnp.concatenate([gq[:rows].reshape(8, dim // 32, wide), flat], 1)
    go = jnp.pad(go.reshape(8, dim // 32, dim), ((0, 0), (0, 16), (0, 0)))
    gq = exchange(jnp.concatenate([gq, go], 2))
    keep = add(stay[0], in_x[0]) + near_one.astype(F32)
    pair = (add(stay[2], in_y[0]) + near_two.astype(F32)).astype(BF)
    pair = swap(pair, 1)
    gu = after(gu, over_y, over_x)
    gq = after(gq, keep, pair)
    (input_grad,) = call(
        last_body,
        [((2, CHUNK, dim), BF)],
        "S" + "V" * 6,
        (meta, gain_a, embed, marked, mid_grad, keep, pair),
        moved=10 * CHUNK * dim,
    )

    gd = jnp.sum(gd.astype(F32), axis=0).reshape(part // 4, dim)
    gu = gu.astype(F32).reshape(2, 2, dim // 32, 2 * part).transpose(1, 2, 0, 3)
    gu = gu.reshape(2, dim // 32, 4 * part)
    gu_far = swap(at(gu, 1 - c).astype(BF), 1).astype(F32)
    gu = at(gu, c)
    gu = jnp.where(clean, jnp.stack([gu, gu_far]), jnp.stack([gu_far, gu]))
    gu = gu.reshape(2, dim // 32, 4, part).transpose(1, 2, 0, 3).reshape(dim // 32, hid)
    go = jnp.sum(gq[:, : dim // 32, wide:].astype(F32), axis=0)
    flat = jnp.sum(gq[:, dim // 32 :, :wide].astype(F32), axis=0).reshape(-1)[:length]
    gq = gq[:, : dim // 32, :wide].reshape(4, 2, dim // 32, wide)
    gq = add(gq[:, 0], gq[:, 1])[..., : 3 * WIDE]
    gq = gq.reshape(4, dim // 32, 3, WIDE).transpose(1, 2, 0, 3).reshape(dim // 32, 3 * dim)

    gbu = flat[:hid]
    g_gain_b, g_b_down, m_direct, g_gain_a, m_norm = [
        flat[hid + k * dim : hid + (k + 1) * dim] for k in range(5)
    ]
    g_gain_a = g_gain_a / gain_a[0]
    hat, scale = norm_parts(embed)
    t = m_norm[None] * gain_a
    t_mean = jnp.mean(t, axis=-1, keepdims=True)
    t_hat = jnp.mean(t * hat, axis=-1, keepdims=True)
    g_embed = m_direct + (scale * (t - t_mean - hat * t_hat))[0]
    own = 4 * r + z
    return (
        layer[None],
        input_grad[None],
        gq,
        go,
        gu,
        cut(gbu, own, hid // 32),
        gd,
        cut(g_b_down, own, dim // 32),
        cut(g_gain_a, own, dim // 32),
        cut(g_gain_b, own, dim // 32),
        cut(g_embed, own, dim // 32),
    )


def solution(mesh):
    plain = (mesh.shape["ctx"], mesh.shape["fsdp"]) != (8, 4)
    placed = (
        P("fsdp", None, "ctx", None),
        P("fsdp", "ctx"),
        P("fsdp", None),
        P("fsdp", None),
        P("fsdp", None),
        P("fsdp", None),
        P("fsdp"),
        P("fsdp", None),
        P("fsdp"),
        P("fsdp"),
        P("fsdp"),
        P("fsdp"),
        P("fsdp", None, "ctx", None),
    )
    return jax.shard_map(
        shards if plain else shards_by_heads,
        mesh=mesh,
        in_specs=placed,
        out_specs=(
            P("fsdp", None, "ctx", None),
            P("fsdp", None, "ctx", None),
            P(("ctx", "fsdp"), None),
            P(("ctx", "fsdp"), None),
            P(("ctx", "fsdp"), None),
            P(("ctx", "fsdp")),
            P(("ctx", "fsdp"), None),
            P(("ctx", "fsdp")),
            P(("ctx", "fsdp")),
            P(("ctx", "fsdp")),
            P(("ctx", "fsdp")),
        ),
        check_vma=False,
    )
```

```python
import functools
import math

import jax
import jax.numpy as jnp
from jax import lax
from jax.experimental import pallas as pl
from jax.experimental.pallas import tpu as pltpu
from jax.sharding import PartitionSpec as P

HEADS = 12
HEAD_DIM = 64
BLOCK = 16


LOWEST = -1e30
EPSILON = 1e-05


def layer_norm(inputs, gain):
    average = jnp.mean(inputs, axis=-1, keepdims=True)
    centered = inputs - average
    variance = jnp.mean(centered * centered, axis=-1, keepdims=True)
    return centered * lax.rsqrt(variance + EPSILON) * gain


def rotary_angles(positions):
    half_dim = HEAD_DIM // 2
    frequency = jnp.exp(
        jnp.arange(half_dim).astype(jnp.float32) * (-2.0 * math.log(10000.0) / HEAD_DIM)
    )
    return positions.astype(jnp.float32)[:, None] * frequency[None, :]


def rotate(heads_in, angles):
    half_dim = heads_in.shape[-1] // 2
    cosine = jnp.cos(angles)[:, None, :]
    sine_part = jnp.sin(angles)[:, None, :]
    first_half = heads_in[..., :half_dim]
    second_half = heads_in[..., half_dim:]
    return jnp.concatenate(
        [
            first_half * cosine - second_half * sine_part,
            second_half * cosine + first_half * sine_part,
        ],
        axis=-1,
    )


def segment_of(positions, doc_ends):
    return jnp.sum((positions[:, None] >= doc_ends[None, :]).astype(jnp.int32), axis=1)


def visible(query_stream, query_position, query_segment, key_stream, key_position, key_segment):
    query_block = query_position // BLOCK
    key_block = key_position // BLOCK
    same_doc = query_segment[:, None] == key_segment[None, :]
    clean_key = key_stream[None, :] == 0
    noisy_query = query_stream[:, None] == 1
    before = key_block[None, :] < query_block[:, None]
    same_block = key_block[None, :] == query_block[:, None]
    from_clean = clean_key & (before | same_block & jnp.logical_not(noisy_query))
    from_noisy = jnp.logical_not(clean_key) & noisy_query & same_block
    return same_doc & (from_clean | from_noisy)


def mix_tile(running, query_rows, key_tile, value_tile, allowed):
    run_max, run_sum, accum = running
    scores = (
        jnp.einsum("qhd,khd->hqk", query_rows, key_tile, preferred_element_type=jnp.float32) * 0.125
    )
    masked = jnp.where(allowed[None], scores, LOWEST)
    new_max = jnp.maximum(run_max, jnp.max(masked, axis=-1))
    exp_terms = jnp.where(allowed[None], jnp.exp(masked - new_max[..., None]), 0.0)
    factor = jnp.exp(run_max - new_max)
    new_sum = run_sum * factor + jnp.sum(exp_terms, axis=-1)
    accum = accum * factor[..., None] + jnp.einsum(
        "hqk,khd->hqd",
        exp_terms.astype(jnp.bfloat16),
        value_tile,
        preferred_element_type=jnp.float32,
    )
    return (new_max, new_sum, accum)


def tile_grads(query_rows, key_tile, value_tile, allowed, row_max, scaled_grad, correction):
    scores = (
        jnp.einsum("qhd,khd->hqk", query_rows, key_tile, preferred_element_type=jnp.float32) * 0.125
    )
    masked = jnp.where(allowed[None], scores, LOWEST)
    exp_terms = jnp.where(allowed[None], jnp.exp(masked - row_max[..., None]), 0.0)
    prob_grad = jnp.einsum(
        "hqd,khd->hqk", scaled_grad, value_tile, preferred_element_type=jnp.float32
    )
    score_grad = (exp_terms * (prob_grad - correction[..., None])).astype(jnp.bfloat16)
    query_part = jnp.einsum(
        "hqk,khd->qhd", score_grad, key_tile, preferred_element_type=jnp.float32
    )
    key_part = jnp.einsum(
        "hqk,qhd->khd", score_grad, query_rows, preferred_element_type=jnp.float32
    )
    value_part = jnp.einsum(
        "hqk,hqd->khd",
        exp_terms.astype(jnp.bfloat16),
        scaled_grad,
        preferred_element_type=jnp.float32,
    )
    return (query_part, key_part, value_part)


def build_inputs(hidden, noise_row, mask_row):
    clean_rows = hidden[0, 0].astype(jnp.float32)
    noisy_rows = jnp.where(
        noise_row[:, None] == 1,
        mask_row.astype(jnp.float32)[None, :],
        hidden[0, 1].astype(jnp.float32),
    )
    return jnp.concatenate([clean_rows, noisy_rows], axis=0)


def project(inputs, gathered, angles):
    row_count = inputs.shape[0]
    model_dim = inputs.shape[1]
    normed = layer_norm(inputs, gathered[6].astype(jnp.float32)).astype(jnp.bfloat16)
    projected = jnp.dot(normed, gathered[0], preferred_element_type=jnp.float32)
    query_rows = rotate(
        projected[:, :model_dim].reshape(row_count, HEADS, HEAD_DIM), angles
    ).astype(jnp.bfloat16)
    key_rows = rotate(
        projected[:, model_dim : 2 * model_dim].reshape(row_count, HEADS, HEAD_DIM), angles
    ).astype(jnp.bfloat16)
    value_rows = (
        projected[:, 2 * model_dim :].reshape(row_count, HEADS, HEAD_DIM).astype(jnp.bfloat16)
    )
    return (normed, query_rows, key_rows, value_rows)


def upper_half(inputs, attended_low, gathered):
    middle = inputs + jnp.dot(attended_low, gathered[1], preferred_element_type=jnp.float32)
    normed_two = layer_norm(middle, gathered[7].astype(jnp.float32)).astype(jnp.bfloat16)
    upper = jnp.dot(normed_two, gathered[2], preferred_element_type=jnp.float32) + gathered[
        3
    ].astype(jnp.float32)
    activated = jax.nn.gelu(upper, approximate=True).astype(jnp.bfloat16)
    return (middle, normed_two, upper, activated)


def shards(
    hidden,
    noise_mask,
    doc_lengths,
    w_qkv,
    w_out,
    w_up,
    b_up,
    w_down,
    b_down,
    gain_one,
    gain_two,
    mask_embed,
    out_grad,
):
    own_params = (w_qkv, w_out, w_up, b_up, w_down, b_down, gain_one, gain_two, mask_embed)
    local_count = hidden.shape[2]
    model_dim = hidden.shape[3]
    row_count = 2 * local_count
    ctx_index = lax.axis_index("ctx")
    offset = ctx_index * local_count
    local_place = offset + jnp.arange(local_count, dtype=jnp.int32)
    positions = jnp.concatenate([local_place, local_place])
    stream = jnp.concatenate(
        [jnp.zeros((local_count,), jnp.int32), jnp.ones((local_count,), jnp.int32)]
    )
    doc_ends = jnp.cumsum(doc_lengths[0])
    segments = segment_of(positions, doc_ends)
    angles = rotary_angles(positions)
    noise_row = noise_mask[0]
    noisy_stream = stream[local_count:]
    noisy_allowed = visible(
        stream, positions, segments, noisy_stream, positions[local_count:], segments[local_count:]
    )
    gathered = (
        lax.all_gather(own_params[0], "fsdp", axis=0, tiled=True),
        lax.all_gather(own_params[1], "fsdp", axis=0, tiled=True),
        lax.all_gather(own_params[2], "fsdp", axis=0, tiled=True),
        lax.all_gather(own_params[3], "fsdp", axis=0, tiled=True),
        lax.all_gather(own_params[4], "fsdp", axis=0, tiled=True),
        lax.all_gather(own_params[5], "fsdp", axis=0, tiled=True),
        lax.all_gather(own_params[6], "fsdp", axis=0, tiled=True),
        lax.all_gather(own_params[7], "fsdp", axis=0, tiled=True),
        lax.all_gather(own_params[8], "fsdp", axis=0, tiled=True),
    )
    inputs = build_inputs(hidden, noise_row, gathered[8])
    normed, query_rows, key_rows, value_rows = project(inputs, gathered, angles)
    clean_keys = key_rows[:local_count].reshape(local_count, model_dim)
    clean_values = value_rows[:local_count].reshape(local_count, model_dim)
    start_state = (
        jnp.full((HEADS, row_count), LOWEST, jnp.float32),
        jnp.zeros((HEADS, row_count), jnp.float32),
        jnp.zeros((HEADS, row_count, HEAD_DIM), jnp.float32),
    )
    running = start_state
    piece_keys = lax.all_gather(clean_keys, "ctx", axis=0, tiled=True)
    piece_values = lax.all_gather(clean_values, "ctx", axis=0, tiled=True)
    piece_rows = piece_keys.shape[0]
    fold_tile_size = math.gcd(piece_rows, 512)

    def step(carried, tile_index):
        tile_start = tile_index * fold_tile_size
        key_tile = lax.dynamic_slice_in_dim(piece_keys, tile_start, fold_tile_size, 0).reshape(
            fold_tile_size, HEADS, HEAD_DIM
        )
        value_tile = lax.dynamic_slice_in_dim(piece_values, tile_start, fold_tile_size, 0).reshape(
            fold_tile_size, HEADS, HEAD_DIM
        )
        key_position = tile_start + jnp.arange(fold_tile_size, dtype=jnp.int32)
        allowed = visible(
            stream,
            positions,
            segments,
            jnp.zeros((fold_tile_size,), jnp.int32),
            key_position,
            segment_of(key_position, doc_ends),
        )
        carried = lax.cond(
            jnp.any(allowed),
            lambda held: mix_tile(held, query_rows, key_tile, value_tile, allowed),
            lambda held: held,
            carried,
        )
        return (carried, None)

    running, _ = lax.scan(step, running, jnp.arange(piece_rows // fold_tile_size))
    run_max, run_sum, accum = mix_tile(
        running, query_rows, key_rows[local_count:], value_rows[local_count:], noisy_allowed
    )
    attended = accum / run_sum[..., None]
    attended_low = (
        jnp.transpose(attended, (1, 0, 2)).reshape(row_count, model_dim).astype(jnp.bfloat16)
    )
    middle, normed_two, upper, activated = upper_half(inputs, attended_low, gathered)
    result = (
        middle
        + jnp.dot(activated, gathered[4], preferred_element_type=jnp.float32)
        + gathered[5].astype(jnp.float32)
    )
    layer_out = result.astype(jnp.bfloat16).reshape(1, 2, local_count, model_dim)
    again = (
        lax.all_gather(own_params[0], "fsdp", axis=0, tiled=True),
        lax.all_gather(own_params[1], "fsdp", axis=0, tiled=True),
        lax.all_gather(own_params[2], "fsdp", axis=0, tiled=True),
        lax.all_gather(own_params[3], "fsdp", axis=0, tiled=True),
        lax.all_gather(own_params[4], "fsdp", axis=0, tiled=True),
        lax.all_gather(own_params[5], "fsdp", axis=0, tiled=True),
        lax.all_gather(own_params[6], "fsdp", axis=0, tiled=True),
        lax.all_gather(own_params[7], "fsdp", axis=0, tiled=True),
        lax.all_gather(own_params[8], "fsdp", axis=0, tiled=True),
    )
    normed, query_rows, key_rows, value_rows = project(inputs, again, angles)
    noisy_keys = key_rows[local_count:]
    noisy_values = value_rows[local_count:]
    middle, normed_two, upper, activated = upper_half(inputs, attended_low, again)
    grad_rows = out_grad[0].reshape(row_count, model_dim)
    grad_float = grad_rows.astype(jnp.float32)
    grad_down = jnp.einsum("qi,qj->ij", activated, grad_rows, preferred_element_type=jnp.float32)
    grad_down_bias = jnp.sum(grad_float, axis=0)
    activated_grad = jnp.einsum(
        "qj,ij->qi", grad_rows, again[4], preferred_element_type=jnp.float32
    )
    _, gelu_pull = jax.vjp(lambda upper_in: jax.nn.gelu(upper_in, approximate=True), upper)
    upper_grad = gelu_pull(activated_grad)[0].astype(jnp.bfloat16)
    grad_up = jnp.einsum("qi,qj->ij", normed_two, upper_grad, preferred_element_type=jnp.float32)
    grad_up_bias = jnp.sum(upper_grad.astype(jnp.float32), axis=0)
    normed_two_grad = jnp.einsum(
        "qj,ij->qi", upper_grad, again[2], preferred_element_type=jnp.float32
    )
    _, second_pull = jax.vjp(layer_norm, middle, again[7].astype(jnp.float32))
    middle_norm_grad, grad_gain_two = second_pull(normed_two_grad)
    middle_grad = (grad_float + middle_norm_grad).astype(jnp.bfloat16)
    grad_out_proj = jnp.einsum(
        "qi,qj->ij", attended_low, middle_grad, preferred_element_type=jnp.float32
    )
    attended_grad = jnp.einsum(
        "qj,ij->qi", middle_grad, again[1], preferred_element_type=jnp.float32
    )
    attended_grad = jnp.transpose(attended_grad.reshape(row_count, HEADS, HEAD_DIM), (1, 0, 2))
    scaled_grad = (attended_grad / run_sum[..., None]).astype(jnp.bfloat16)
    correction = jnp.sum(attended_grad * attended, axis=-1) / run_sum
    pair_rows = (
        lax.all_gather(
            key_rows[:local_count].reshape(local_count, model_dim), "ctx", axis=0, tiled=True
        ),
        lax.all_gather(
            value_rows[:local_count].reshape(local_count, model_dim), "ctx", axis=0, tiled=True
        ),
    )
    pair_keys, pair_values = pair_rows
    total_rows = pair_keys.shape[0]
    tile_size = math.gcd(total_rows, 512)
    zero_tile = jnp.zeros((tile_size, HEADS, HEAD_DIM), jnp.float32)

    def back_step(query_acc, tile_index):
        tile_start = tile_index * tile_size
        key_tile = lax.dynamic_slice_in_dim(pair_keys, tile_start, tile_size, 0).reshape(
            tile_size, HEADS, HEAD_DIM
        )
        value_tile = lax.dynamic_slice_in_dim(pair_values, tile_start, tile_size, 0).reshape(
            tile_size, HEADS, HEAD_DIM
        )
        key_position = tile_start + jnp.arange(tile_size, dtype=jnp.int32)
        allowed = visible(
            stream,
            positions,
            segments,
            jnp.zeros((tile_size,), jnp.int32),
            key_position,
            segment_of(key_position, doc_ends),
        )

        def live_tile(held):
            query_part, key_part, value_part = tile_grads(
                query_rows, key_tile, value_tile, allowed, run_max, scaled_grad, correction
            )
            return (held + query_part, key_part, value_part)

        query_acc, key_part, value_part = lax.cond(
            jnp.any(allowed), live_tile, lambda held: (held, zero_tile, zero_tile), query_acc
        )
        return (
            query_acc,
            (key_part.reshape(tile_size, model_dim), value_part.reshape(tile_size, model_dim)),
        )

    query_acc, (key_terms, value_terms) = lax.scan(
        back_step,
        jnp.zeros((row_count, HEADS, HEAD_DIM), jnp.float32),
        jnp.arange(total_rows // tile_size),
    )
    key_terms = key_terms.reshape(total_rows, model_dim)
    value_terms = value_terms.reshape(total_rows, model_dim)
    clean_key_grad, clean_value_grad = (
        lax.psum_scatter(
            key_terms.astype(jnp.bfloat16), "ctx", scatter_dimension=0, tiled=True
        ).astype(jnp.float32),
        lax.psum_scatter(
            value_terms.astype(jnp.bfloat16), "ctx", scatter_dimension=0, tiled=True
        ).astype(jnp.float32),
    )
    query_part, noisy_key_part, noisy_value_part = tile_grads(
        query_rows, noisy_keys, noisy_values, noisy_allowed, run_max, scaled_grad, correction
    )
    query_grad = (query_acc + query_part) * 0.125
    key_grad = (
        jnp.concatenate(
            [clean_key_grad.reshape(local_count, HEADS, HEAD_DIM), noisy_key_part], axis=0
        )
        * 0.125
    )
    value_grad = jnp.concatenate(
        [clean_value_grad.reshape(local_count, HEADS, HEAD_DIM), noisy_value_part], axis=0
    )
    _, rotate_pull = jax.vjp(lambda heads_in: rotate(heads_in, angles), query_grad)
    query_raw_grad = rotate_pull(query_grad)[0]
    key_raw_grad = rotate_pull(key_grad)[0]
    projected_grad = jnp.concatenate(
        [
            query_raw_grad.reshape(row_count, model_dim),
            key_raw_grad.reshape(row_count, model_dim),
            value_grad.reshape(row_count, model_dim),
        ],
        axis=1,
    ).astype(jnp.bfloat16)
    grad_qkv = jnp.einsum("qi,qj->ij", normed, projected_grad, preferred_element_type=jnp.float32)
    normed_grad = jnp.einsum(
        "qj,ij->qi", projected_grad, again[0], preferred_element_type=jnp.float32
    )
    _, first_pull = jax.vjp(layer_norm, inputs, again[6].astype(jnp.float32))
    inputs_norm_grad, grad_gain_one = first_pull(normed_grad)
    inputs_grad = middle_grad.astype(jnp.float32) + inputs_norm_grad
    noisy_flag = (noise_row == 1)[:, None]
    noisy_grad = inputs_grad[local_count:]
    grad_mask = jnp.sum(jnp.where(noisy_flag, noisy_grad, 0.0), axis=0)
    input_grad = jnp.concatenate(
        [inputs_grad[:local_count], jnp.where(noisy_flag, 0.0, noisy_grad)], axis=0
    )
    input_grad = input_grad.astype(jnp.bfloat16).reshape(1, 2, local_count, model_dim)
    shares = (
        lax.psum_scatter(grad_qkv, ("ctx", "fsdp"), scatter_dimension=0, tiled=True),
        lax.psum_scatter(grad_out_proj, ("ctx", "fsdp"), scatter_dimension=0, tiled=True),
        lax.psum_scatter(grad_up, ("ctx", "fsdp"), scatter_dimension=0, tiled=True),
        lax.psum_scatter(grad_up_bias, ("ctx", "fsdp"), scatter_dimension=0, tiled=True),
        lax.psum_scatter(grad_down, ("ctx", "fsdp"), scatter_dimension=0, tiled=True),
        lax.psum_scatter(grad_down_bias, ("ctx", "fsdp"), scatter_dimension=0, tiled=True),
        lax.psum_scatter(grad_gain_one, ("ctx", "fsdp"), scatter_dimension=0, tiled=True),
        lax.psum_scatter(grad_gain_two, ("ctx", "fsdp"), scatter_dimension=0, tiled=True),
        lax.psum_scatter(grad_mask, ("ctx", "fsdp"), scatter_dimension=0, tiled=True),
    )
    (
        qkv_share,
        out_share,
        up_share,
        up_bias_share,
        down_share,
        down_bias_share,
        gain_one_share,
        gain_two_share,
        mask_share,
    ) = shares
    return (
        layer_out,
        input_grad,
        qkv_share,
        out_share,
        up_share,
        up_bias_share,
        down_share,
        down_bias_share,
        gain_one_share,
        gain_two_share,
        mask_share,
    )


CHUNK = 256
COST = 10**9
GROUP = 3
WIDE = GROUP * HEAD_DIM
HALF = HEAD_DIM // 2
LANES = GROUP * CHUNK
BF = jnp.bfloat16
F32 = jnp.float32
HB = pl.BlockSpec(memory_space=pltpu.HBM)
SM = pl.BlockSpec(memory_space=pltpu.SMEM)
GELU_SCALE = math.sqrt(2.0 / math.pi)


def swap(v, bit):
    return lax.ppermute(v, "ctx", [(i, i ^ bit) for i in range(8)])


def turn(v, step):
    return lax.ppermute(v, "fsdp", [(i, (i + step) % 4) for i in range(4)])


def mm(a, b, ca=1, cb=0):
    return lax.dot_general(a, b, (((ca,), (cb,)), ((), ())), preferred_element_type=F32)


def flip(v):
    return jnp.transpose(v.astype(F32)).astype(v.dtype)


def call(body, outs, kinds, args, scratch=(), flops=0, moved=0):
    staged = [i for i, kind in enumerate(kinds) if kind == "V"]
    space = {"S": SM, "V": HB, "A": HB}
    count, made = len(args), len(outs)

    def run(*refs):
        ins, sinks, rest = list(refs[:count]), refs[count : count + made], refs[count + made :]
        held, results = rest[: len(staged)], rest[len(staged) : len(staged) + made]
        sem_in, sem_out, sems = rest[len(staged) + made : len(staged) + made + 3]
        rest = rest[len(staged) + made + 3 :]
        first = [
            pltpu.make_async_copy(ins[i], held[k], sem_in.at[k]) for k, i in enumerate(staged)
        ]
        for copy in first:
            copy.start()
        for k, i in enumerate(staged):
            ins[i] = held[k]

        def load(pairs):
            more = [pltpu.make_async_copy(a, b, sems.at[i]) for i, (a, b) in enumerate(pairs)]
            for copy in more:
                copy.start()
            for copy in more + first:
                copy.wait()

        body(load, *ins, *results, *rest)
        last = [pltpu.make_async_copy(results[k], sinks[k], sem_out.at[k]) for k in range(made)]
        for copy in last:
            copy.start()
        for copy in last:
            copy.wait()

    return pl.pallas_call(
        run,
        out_shape=tuple(jax.ShapeDtypeStruct(s, d) for s, d in outs),
        in_specs=[space[kind] for kind in kinds],
        out_specs=tuple(HB for _ in outs),
        scratch_shapes=[pltpu.VMEM(args[i].shape, args[i].dtype) for i in staged]
        + [pltpu.VMEM(s, d) for s, d in outs]
        + [
            pltpu.SemaphoreType.DMA((max(1, len(staged)),)),
            pltpu.SemaphoreType.DMA((made,)),
            pltpu.SemaphoreType.DMA((48,)),
        ]
        + list(scratch),
        compiler_params=pltpu.CompilerParams(vmem_limit_bytes=56 * 2**20),
        cost_estimate=pl.CostEstimate(flops=1 + flops // COST, bytes_accessed=1 + moved // COST, transcendentals=0),
    )(*args)


def at16(v):
    return pl.multiple_of(v, 16)


def shard_rows(meta, near, far, dst, unit):
    half = unit // 2
    pairs = []
    for zz in range(4):
        for core, part in ((meta[1], near), (1 - meta[1], far)):
            to = at16(zz * unit + core * half)
            pairs.append((part.at[zz, pl.ds(0, half)], dst.at[pl.ds(to, half)]))
    return pairs


def norm_parts(x):
    mean = jnp.mean(x, axis=-1, keepdims=True)
    centered = x - mean
    var = jnp.mean(centered * centered, axis=-1, keepdims=True)
    scale = lax.rsqrt(var + EPSILON)
    return centered * scale, scale


def unmark(x, embed):
    x = x.astype(F32)
    flag = x[:, :1] > 1e38
    return jnp.where(flag, embed, x), flag


def turn_heads(v, cos, sin):
    parts = []
    for g in range(GROUP):
        a = v[g * HEAD_DIM : g * HEAD_DIM + HALF]
        b = v[g * HEAD_DIM + HALF : (g + 1) * HEAD_DIM]
        parts += [a * cos - b * sin, b * cos + a * sin]
    return jnp.concatenate(parts, axis=0)


def project_body(load, meta, gain, embed, cos, sin, *refs):
    rows, refs = refs[:8], refs[8:]
    near, far, q_ref, kv_a, kv_b, n_ref, mk_ref, w, xs, wp = refs
    load(shard_rows(meta, near, far, w, 192) + [(rows[i], xs.at[i]) for i in range(8)])
    for part in range(3):
        wp[part] = w[:, part * WIDE : (part + 1) * WIDE]

    @pl.loop(0, 8)
    def _(i):
        x, flag = unmark(xs[i], embed[...])
        hat, _ = norm_parts(x)
        n = (hat * gain[...]).astype(BF)
        n_ref[i] = n
        mk_ref[i] = jnp.broadcast_to(jnp.where(flag, 1.0, 0.0), (CHUNK, 128)).astype(BF)
        q_ref[i] = turn_heads(jnp.transpose(mm(n, wp[0])), cos[i], sin[i]).astype(BF)
        keys = turn_heads(jnp.transpose(mm(n, wp[1])), cos[i], sin[i]).astype(BF)
        values = jnp.transpose(mm(n, wp[2])).astype(BF)
        for half, ref in enumerate((kv_a, kv_b)):

            @pl.when(i // 4 == half)
            def _():
                ref[i % 4, :WIDE] = keys
                ref[i % 4, WIDE:] = values


def project_rows(meta, gain, embed, cos, sin, rows, weights):
    dim = rows[0].shape[1]
    wide = weights[0].shape[-1]
    return call(
        project_body,
        [
            ((8, WIDE, CHUNK), BF),
            ((4, 2 * WIDE, CHUNK), BF),
            ((4, 2 * WIDE, CHUNK), BF),
            ((8, CHUNK, dim), BF),
            ((8, CHUNK, 128), BF),
            ((dim, wide), BF),
        ],
        "SVVVV" + "A" * 10,
        (meta, gain, embed, cos, sin, *rows, *weights),
        scratch=[pltpu.VMEM((8, CHUNK, dim), BF), pltpu.VMEM((3, dim, WIDE), BF)],
        flops=2 * 8 * CHUNK * dim * 3 * WIDE,
        moved=8 * CHUNK * dim * 6,
    )


def head_pairs(refs, qs, kv):
    pairs = [(refs[0], qs)]
    for i, ref in enumerate(refs[1:]):
        pairs.append((ref, kv.at[i // 2, pl.ds(i % 2 * 4, 4)]))
    return pairs


def thrice(v):
    return jnp.concatenate([v, v, v], axis=1)


def scores_of(keys, stacked, base, low, high, plain):
    s = mm(keys, stacked)
    if plain:
        return s
    place = base + lax.broadcasted_iota(jnp.int32, (CHUNK, LANES), 0)
    return jnp.where((place >= low) & (place < high), s, LOWEST)


def each_tile(meta, p, lims, tile):
    r, c = meta[0], meta[1]

    @pl.loop(meta[4 + p], p + c + 1)
    def _(k):
        own = k == p + c
        source = jnp.where(own, 0, c)
        slot = jnp.where(own, p ^ r, k ^ r ^ c)
        base = jnp.where(own, p, k) * CHUNK
        whole = (k < p) & (meta[12 + p] <= base)

        @pl.when(whole)
        def _():
            tile(source, slot, own, base, None, None, True)

        @pl.when(jnp.logical_not(whole))
        def _():
            low, high, nlow, nhigh = lims
            tile(source, slot, own, base, jnp.where(own, nlow, low), jnp.where(own, nhigh, high), False)


def stack_heads(q, stacked):
    for g in range(GROUP):
        stacked[g * HEAD_DIM : (g + 1) * HEAD_DIM, g * CHUNK : (g + 1) * CHUNK] = q[
            g * HEAD_DIM : (g + 1) * HEAD_DIM
        ]


def attend_body(load, meta, bounds, *refs):
    heads = refs[:5]
    send, o_ref, ml_ref, qs, kv, kr, stacked, m_s, l_s, acc = refs[5:]
    load(head_pairs(heads, qs, kv))
    stacked[...] = jnp.zeros_like(stacked)

    @pl.loop(0, 8)
    def _(s):
        for own in range(2):
            kr[own, s] = flip(kv[own, s, :WIDE])

    r = meta[0]

    @pl.loop(0, 8)
    def _(p):
        s = p ^ r
        stack_heads(qs[s] * 0.125, stacked)
        lims = [thrice(bounds[p, i : i + 1]) for i in range(4)]

        def tile(source, slot, own, base, lo, hi, plain):
            masked = scores_of(kr[source, slot], stacked[...], base, lo, hi, plain)
            m_old = m_s[...]
            m_new = jnp.maximum(m_old, jnp.max(masked, axis=0, keepdims=True))
            e = jnp.exp(masked - m_new)
            f = jnp.exp(m_old - m_new)
            m_s[...] = m_new
            l_s[...] = l_s[...] * f + jnp.sum(e, axis=0, keepdims=True)
            e = e.astype(BF)
            for g in range(GROUP):
                cut = slice(g * CHUNK, (g + 1) * CHUNK)
                first = WIDE + g * HEAD_DIM
                acc[g] = acc[g] * f[:, cut] + mm(kv[source, slot, first : first + HEAD_DIM], e[:, cut])

        m_s[...] = jnp.full_like(m_s, LOWEST)
        l_s[...] = jnp.zeros_like(l_s)
        acc[...] = jnp.zeros_like(acc)
        each_tile(meta, p, lims, tile)
        total = l_s[...]
        inv = 1.0 / total
        out = jnp.concatenate(
            [acc[g] * inv[:, g * CHUNK : (g + 1) * CHUNK] for g in range(GROUP)], axis=0
        )
        o_ref[s] = out
        ml_ref[s, 0:1] = m_s[...]
        ml_ref[s, 1:2] = total
        send[p] = out.astype(BF)


HEAD_SCRATCH = [pltpu.VMEM((8, WIDE, CHUNK), BF), pltpu.VMEM((2, 8, 2 * WIDE, CHUNK), BF)]


def attend_rows(meta, bounds, heads):
    return call(
        attend_body,
        [((8, WIDE, CHUNK), BF), ((8, WIDE, CHUNK), F32), ((8, 8, LANES), F32)],
        "SV" + "A" * 5,
        (meta, bounds, *heads),
        scratch=HEAD_SCRATCH
        + [
            pltpu.VMEM((2, 8, CHUNK, WIDE), BF),
            pltpu.VMEM((WIDE, LANES), BF),
            pltpu.VMEM((1, LANES), F32),
            pltpu.VMEM((1, LANES), F32),
            pltpu.VMEM((GROUP, HEAD_DIM, CHUNK), F32),
        ],
        flops=20 * 2 * 2 * CHUNK * LANES * 256,
        moved=8 * CHUNK * WIDE * 16,
    )


def attend_back_body(load, meta, bounds, cos, sin, o_ref, ml_ref, *refs):
    heads, gs = refs[:5], refs[5]
    (
        pq_ref, own_ref, far_a, far_b,
        qs, kv, kr, vr, st_q, st_g, row_q, row_g, dk, dv, dq,
    ) = refs[6:]
    for ref in (st_q, st_g, dk, dv):
        ref[...] = jnp.zeros_like(ref)
    load(head_pairs(heads, qs, kv))

    @pl.loop(0, 8)
    def _(s):
        for own in range(2):
            kr[own, s] = flip(kv[own, s, :WIDE])
            vr[own, s] = flip(kv[own, s, WIDE:])

    r, c = meta[0], meta[1]
    lane = lax.broadcasted_iota(jnp.int32, (CHUNK, WIDE), 1) // HEAD_DIM

    @pl.loop(0, 8)
    def _(p):
        s = p ^ r
        q = qs[s] * 0.125
        stack_heads(q, st_q)
        total = ml_ref[s, 1:2]
        top = ml_ref[s, 0:1]
        g_in = gs[p].astype(F32)
        attended = o_ref[s]
        scaled, fix = [], []
        for g in range(GROUP):
            part = slice(g * HEAD_DIM, (g + 1) * HEAD_DIM)
            inv = 1.0 / total[:, g * CHUNK : (g + 1) * CHUNK]
            scaled.append(g_in[part] * inv)
            fix.append(jnp.sum(g_in[part] * attended[part], axis=0, keepdims=True) * inv)
        scaled = jnp.concatenate(scaled, axis=0)
        fix = jnp.concatenate(fix, axis=1)
        stack_heads(scaled.astype(BF), st_g)
        q_rows = jnp.transpose(q.astype(F32))
        g_rows = jnp.transpose(scaled)
        for g in range(GROUP):
            row_q[g * CHUNK : (g + 1) * CHUNK] = jnp.where(lane == g, q_rows, 0.0).astype(BF)
            row_g[g * CHUNK : (g + 1) * CHUNK] = jnp.where(lane == g, g_rows, 0.0).astype(BF)
        lims = [thrice(bounds[p, i : i + 1]) for i in range(4)]
        dq[...] = jnp.zeros_like(dq)

        def tile(source, slot, own, base, lo, hi, plain):
            e = jnp.exp(scores_of(kr[source, slot], st_q[...], base, lo, hi, plain) - top)
            d = (e * (mm(vr[source, slot], st_g[...]) - fix)).astype(BF)
            e = e.astype(BF)
            kind = jnp.where(own, 0, 1)
            dv[kind, slot] += mm(e, row_g[...])
            dk[kind, slot] += mm(d, row_q[...])
            for g in range(GROUP):
                part = slice(g * HEAD_DIM, (g + 1) * HEAD_DIM)
                dq[part] += mm(kv[source, slot, part], d[:, g * CHUNK : (g + 1) * CHUNK])

        each_tile(meta, p, lims, tile)
        pq_ref[s] = turn_heads(dq[...] * 0.125, cos[s], -sin[s]).astype(BF)

    both = 1.0 - c.astype(F32)

    @pl.loop(0, 8)
    def _(s):
        far_k, far_v = jnp.transpose(dk[1, s]), jnp.transpose(dv[1, s])
        for half, far_ref in enumerate((far_a, far_b)):

            @pl.when(s // 4 == half)
            def _():
                far_ref[s % 4, :WIDE] = far_k.astype(BF)
                far_ref[s % 4, WIDE:] = far_v.astype(BF)

        own_ref[s, :WIDE] = jnp.transpose(dk[0, s]) + both * far_k
        own_ref[s, WIDE:] = jnp.transpose(dv[0, s]) + both * far_v


def attend_back(meta, bounds, cos, sin, attended, stats, heads, grads):
    rows = pltpu.VMEM((2, 8, CHUNK, WIDE), BF)
    sums = pltpu.VMEM((2, 8, CHUNK, WIDE), F32)
    return call(
        attend_back_body,
        [((8, WIDE, CHUNK), BF), ((8, 2 * WIDE, CHUNK), F32)] + [((4, 2 * WIDE, CHUNK), BF)] * 2,
        "SVVVVV" + "A" * 5 + "V",
        (meta, bounds, cos, sin, attended, stats, *heads, grads),
        scratch=HEAD_SCRATCH
        + [
            rows,
            rows,
            pltpu.VMEM((WIDE, LANES), BF),
            pltpu.VMEM((WIDE, LANES), BF),
            pltpu.VMEM((LANES, WIDE), BF),
            pltpu.VMEM((LANES, WIDE), BF),
        ]
        + [sums] * 2
        + [pltpu.VMEM((WIDE, CHUNK), F32)],
        flops=20 * 2 * 5 * CHUNK * LANES * 256,
        moved=8 * CHUNK * WIDE * 30,
    )


def share_pairs(meta, own, parts, dst, unit, skip):
    h, z = meta[2], meta[3]
    part = unit // 4
    pairs = [(own, dst.at[pl.ds(at16(z * unit), unit)])]
    for t in range(1, 4):
        zz = (z + 4 - t) & 3
        for k in range(4):
            to = at16(zz * unit + (h ^ k) * part)
            pairs.append((parts[k].at[t - 1, pl.ds(skip, part)], dst.at[pl.ds(to, part)]))
    return pairs


def middle_body(load, meta, gain, embed, x_ref, heads, own, *refs):
    mid_ref, n_ref, att_ref, w_ref = refs[4:]
    pairs = share_pairs(meta, own, refs[:4], w_ref, 192, 0)
    for d in range(8):
        pairs.append((heads.at[d], att_ref.at[d % 2, pl.ds(d // 2 * WIDE, WIDE)]))
    load(pairs)

    @pl.loop(0, 2)
    def _(stream):
        x, _ = unmark(x_ref[stream], embed[...])
        mid = x + mm(att_ref[stream], w_ref[...], 0, 0)
        hat, _ = norm_parts(mid)
        mid_ref[stream] = mid
        n_ref[pl.ds(pl.multiple_of(stream * CHUNK, CHUNK), CHUNK)] = (hat * gain[...]).astype(BF)


def middle_rows(meta, gain, embed, marked, heads, own, parts):
    dim = marked.shape[2]
    return call(
        middle_body,
        [((2, CHUNK, dim), F32), ((2 * CHUNK, dim), BF), ((2, dim, CHUNK), BF), ((dim, dim), BF)],
        "SVVV" + "A" * 6,
        (meta, gain, embed, marked, heads, own, *parts),
        flops=2 * 2 * CHUNK * dim * dim,
        moved=8 * CHUNK * dim * 2,
    )


def feed_body(load, meta, bias, n_own, n_far, g_own, g_far, up_own, down_own, *refs):
    shares, refs = refs[:4], refs[4:]
    (
        out_ref, outf_ref, ngf_ref, ng_ref, gb_ref, d_ref, u_ref,
        ns, gs, wu, wd, acts, slopes,
    ) = refs
    c, h, z = meta[1], meta[2], meta[3]
    rows = 2 * CHUNK
    part = bias.shape[1] // 4
    pairs = [
        (n_own, ns.at[pl.ds(0, rows)]),
        (n_far, ns.at[pl.ds(rows, rows)]),
        (g_own, gs.at[pl.ds(0, rows)]),
        (g_far, gs.at[pl.ds(rows, rows)]),
    ]
    pairs += share_pairs(meta, down_own.at[pl.ds(at16(c * part), part)], shares, wd, part, 48)
    for k in range(4):
        cols = pl.ds(pl.multiple_of(k * 2 * part + c * part, 128), part)
        pairs.append((up_own.at[:, cols], wu.at[pl.ds(at16(z * 192), 192), pl.ds(k * part, part)]))
    for t in range(1, 4):
        zz = (z + 4 - t) & 3
        for k in range(4):
            dst = pl.ds(at16(zz * 192 + (h ^ k) * 48), 48)
            for b in range(2):
                pairs.append(
                    (
                        shares[k].at[t - 1, pl.ds(144 + 48 * b, 48)],
                        wu.at[dst, pl.ds(2 * part * b, 2 * part)],
                    )
                )
    load(pairs)
    gb_ref[...] = jnp.zeros_like(gb_ref)

    @pl.loop(0, 4)
    def _(i):
        span = pl.ds(pl.multiple_of(i * CHUNK, CHUNK), CHUNK)
        v = mm(ns[span], wu[...]) + bias[...]
        square = v * v
        th = jnp.tanh(v * (GELU_SCALE + (GELU_SCALE * 0.044715) * square))
        half = 0.5 + 0.5 * th
        act = (v * half).astype(BF)
        slope = half + (v * half) * (1.0 - th) * (GELU_SCALE + (3.0 * 0.044715 * GELU_SCALE) * square)
        acts[span] = act
        ug = (slope * mm(gs[span], wd[...], 1, 1)).astype(BF)
        slopes[span] = ug
        gb_ref[...] += jnp.sum(ug.astype(F32), axis=0, keepdims=True)
        out = mm(act, wd[...]).astype(BF)
        ng = mm(ug, wu[...], 1, 1).astype(BF)
        to = pl.ds(pl.multiple_of((i & 1) * CHUNK, CHUNK), CHUNK)

        @pl.when(i < 2)
        def _():
            out_ref[to] = out
            ng_ref[to] = ng

        @pl.when(i >= 2)
        def _():
            outf_ref[to] = out
            ngf_ref[to] = ng

    @pl.loop(0, 4)
    def _(j):
        cols = pl.ds(pl.multiple_of(j * part, 128), part)
        gd = mm(acts[:, cols], gs[...], 0, 0).astype(BF)
        for b in range(4):
            d_ref[b, j ^ h] = gd[96 * b : 96 * (b + 1)]
        gu = mm(ns[...], slopes[:, cols], 0, 0)
        side = pl.ds(pl.multiple_of((j & 1) * part, 128), part)
        line = pl.ds(at16((j >> 1) * 48), 48)
        for b in range(16):
            first = 192 * (b // 4) + 24 * (b % 4)
            block = jnp.concatenate([gu[first : first + 24], gu[first + 96 : first + 120]])
            u_ref[b // 4, b % 4, line, side] = block.astype(BF)


def feed_rows(meta, bias, args):
    rows = 2 * CHUNK
    dim = args[0].shape[1]
    hid = bias.shape[1]
    return call(
        feed_body,
        [((rows, dim), BF)] * 4
        + [((1, hid), F32)]
        + [((4, 4, hid // 16, dim), BF)] * 2,
        "SV" + "A" * 10,
        (meta, bias, *args),
        scratch=[
            pltpu.VMEM((2 * rows, dim), BF),
            pltpu.VMEM((2 * rows, dim), BF),
            pltpu.VMEM((dim, hid), BF),
            pltpu.VMEM((hid, dim), BF),
            pltpu.VMEM((2 * rows, hid), BF),
            pltpu.VMEM((2 * rows, hid), BF),
        ],
        flops=6 * 2 * 2 * rows * dim * hid,
        moved=12 * dim * hid,
    )


def pack_body(load, meta, w_out, w_down, w_up, share):
    c, h = meta[1], meta[2]
    part = w_up.shape[1] // 8
    pairs = [
        (w_out.at[pl.ds(at16(48 * h), 48)], share.at[pl.ds(0, 48)]),
        (w_down.at[pl.ds(at16(part * c + 96 * h), 96)], share.at[pl.ds(48, 96)]),
    ]
    for k in range(4):
        cols = pl.ds(pl.multiple_of((2 * k + c) * part, 128), part)
        to = share.at[pl.ds(144 + 48 * (k // 2), 48), pl.ds(part * (k % 2), part)]
        pairs.append((w_up.at[pl.ds(at16(48 * h), 48), cols], to))
    load(pairs)


def pack_share(place, w_out, w_down, w_up):
    return call(pack_body, [((240, w_out.shape[1]), BF)], "SAAA", (place, w_out, w_down, w_up))[0]


def middle_back_body(
    load, meta, gain, b_down, mid_ref, ng_ref, out_ref, outf_ref, ngf_ref, g_ref, x_ref, w_ref,
    lay_ref, mg_ref, sum_ref, send,
):
    load([])
    sum_ref[...] = jnp.zeros_like(sum_ref)

    @pl.loop(0, 2)
    def _(stream):
        span = pl.ds(pl.multiple_of(stream * CHUNK, CHUNK), CHUNK)
        mid = mid_ref[stream]
        lay = mid + out_ref[span].astype(F32) + outf_ref[span].astype(F32) + b_down[...]
        lay_ref[stream] = lay.astype(BF)
        hat, scale = norm_parts(mid)
        ng = ng_ref[span].astype(F32) + ngf_ref[span].astype(F32)
        sum_ref[0:1] += jnp.sum(ng * hat, axis=0, keepdims=True)
        t = ng * gain[...]
        g = g_ref[stream].astype(F32)
        sum_ref[1:2] += jnp.sum(g, axis=0, keepdims=True)
        t_mean = jnp.mean(t, axis=-1, keepdims=True)
        t_hat = jnp.mean(t * hat, axis=-1, keepdims=True)
        mg = (g + scale * (t - t_mean - hat * t_hat)).astype(BF)
        mg_ref[stream] = mg
        flag = (x_ref[stream][:, :1].astype(F32) > 1e38) & (stream == 1)
        sum_ref[2:3] += jnp.sum(jnp.where(flag, mg.astype(F32), 0.0), axis=0, keepdims=True)
        for d in range(4):
            send[2 * d + stream] = mm(w_ref[d * WIDE : (d + 1) * WIDE], mg, 1, 1).astype(BF)


def middle_back(meta, gain, b_down, args):
    dim = gain.shape[1]
    return call(
        middle_back_body,
        [((2, CHUNK, dim), BF), ((2, CHUNK, dim), BF), ((8, dim), F32), ((8, WIDE, CHUNK), BF)],
        "S" + "V" * 10,
        (meta, gain, b_down, *args),
        flops=4 * CHUNK * dim * dim,
        moved=20 * CHUNK * dim,
    )


def by_z(grad, ref):
    for zz in range(4):
        for h in range(4):
            first = 192 * h + 24 * zz
            pair = jnp.concatenate([grad[first : first + 24], grad[first + 96 : first + 120]])
            ref[zz, 48 * h : 48 * (h + 1)] = pair.astype(BF)


def out_grad_body(load, att_ref, mg_ref, up, o_ref):
    load([(up.at[h], o_ref.at[h, :, pl.ds(0, 96)]) for h in range(4)])
    grad = mm(att_ref[0], mg_ref[0]) + mm(att_ref[1], mg_ref[1])
    for b in range(16):
        first = 192 * (b // 4) + 24 * (b % 4)
        pair = jnp.concatenate([grad[first : first + 24], grad[first + 96 : first + 120]])
        o_ref[b // 4, b % 4, 96:] = pair.astype(BF)


def project_back_body(
    own, f0, f1, pq, n_ref, mk_ref, cos, sin, w_ref,
    away_x, away_y, stay, gq_ref, gs_ref, wp, acc,
):
    i = pl.program_id(0)

    @pl.when(i == 0)
    def _():
        for part in range(3):
            wp[part] = w_ref[:, part * WIDE : (part + 1) * WIDE]
        acc[...] = jnp.zeros_like(acc)
        gs_ref[...] = jnp.zeros_like(gs_ref)

    early = (i == 0) | (i == 4) | (i == 6) | (i == 7)
    far = jnp.where(early, f0[0], f1[0])
    kv = own[0] + far.astype(F32)
    parts = [
        pq[0],
        turn_heads(kv[:WIDE], cos[0], -sin[0]).astype(BF),
        kv[WIDE:].astype(BF),
    ]
    n, mk = n_ref[0], mk_ref[0]
    ng = jnp.zeros((CHUNK, n.shape[1]), F32)
    for k in range(3):
        ng += mm(flip(parts[k]), wp[k], 1, 1)
        acc[k * WIDE : (k + 1) * WIDE] += mm(parts[k], n)
    low = ng.astype(BF)

    @pl.when(i < 2)
    def _():
        away_x[0] = low

    @pl.when((i >= 2) & (i < 4))
    def _():
        away_y[0] = low

    @pl.when(i >= 4)
    def _():
        stay[0] = ng

    gs_ref[0:1] += jnp.sum(ng * n.astype(F32), axis=0, keepdims=True)
    gs_ref[1:2] += jnp.sum(ng * mk[:, :1].astype(F32), axis=0, keepdims=True)

    @pl.when(i == 7)
    def _():
        by_z(jnp.transpose(acc[...]), gq_ref)


def pick(order):
    def slot_of(i):
        slot = jnp.int32(order[-1])
        for k in range(len(order) - 2, -1, -1):
            slot = jnp.where(i == k, order[k], slot)
        return slot

    return slot_of


def project_back(own, far, pq, n, mk, cos, sin, w):
    dim = n.shape[2]
    wide = w.shape[1] + HEAD_DIM
    slot = pick((2, 6, 5, 7, 0, 4, 1, 3))

    def block(rows, cols, index):
        return pl.BlockSpec((1, rows, cols), lambda i: (index(i), 0, 0))

    def whole(*shape):
        return pl.BlockSpec(shape, lambda i: tuple(0 for _ in shape))

    return pl.pallas_call(
        project_back_body,
        grid=(8,),
        out_shape=(
            jax.ShapeDtypeStruct((2, CHUNK, dim), BF),
            jax.ShapeDtypeStruct((2, CHUNK, dim), BF),
            jax.ShapeDtypeStruct((4, CHUNK, dim), F32),
            jax.ShapeDtypeStruct((4, dim // 4, wide), BF),
            jax.ShapeDtypeStruct((8, dim), F32),
        ),
        in_specs=[
            block(2 * WIDE, CHUNK, slot),
            *[block(2 * WIDE, CHUNK, lambda i: slot(i) % 4)] * 2,
            block(WIDE, CHUNK, slot),
            block(CHUNK, dim, slot), block(CHUNK, 128, slot),
            block(HALF, CHUNK, slot), block(HALF, CHUNK, slot), whole(*w.shape),
        ],
        out_specs=(
            block(CHUNK, dim, lambda i: jnp.minimum(i, 1)),
            block(CHUNK, dim, lambda i: jnp.clip(i - 2, 0, 1)),
            block(CHUNK, dim, lambda i: jnp.clip(i - 4, 0, 3)),
            whole(4, dim // 4, wide),
            whole(8, dim),
        ),
        scratch_shapes=[pltpu.VMEM((3, dim, WIDE), BF), pltpu.VMEM((wide, dim), F32)],
        compiler_params=pltpu.CompilerParams(vmem_limit_bytes=56 * 2**20),
        cost_estimate=pl.CostEstimate(
            flops=1 + 4 * 8 * CHUNK * dim * 3 * WIDE // COST, bytes_accessed=1, transcendentals=0
        ),
    )(own, *far, pq, n, mk, cos, sin, w)


def last_body(load, meta, gain, embed, x_ref, mg_ref, keep_ref, far_ref, o_ref):
    load([])

    @pl.loop(0, 2)
    def _(stream):
        ng = jnp.where(stream == meta[1], keep_ref[...], far_ref[...].astype(F32))
        x, flag = unmark(x_ref[stream], embed[...])
        hat, scale = norm_parts(x)
        t = ng * gain[...]
        t_mean = jnp.mean(t, axis=-1, keepdims=True)
        t_hat = jnp.mean(t * hat, axis=-1, keepdims=True)
        grad = mg_ref[stream].astype(F32) + scale * (t - t_mean - hat * t_hat)
        o_ref[stream] = jnp.where(flag, 0.0, grad).astype(BF)


def finish_body(load, meta, gain, embed, x_ref, up_own, up_far, *refs):
    gd_refs, (gq_ref, go_ref, gu_ref, gd_ref, bu_ref, rows_ref, sums) = refs[:4], refs[4:]
    load([])
    r, c, z = meta[0], meta[1], meta[3]
    own = 4 * r + z
    small = gq_ref.shape[0]
    for h in range(4):
        part = x_ref[2 * h, :small].astype(F32) + x_ref[2 * h + 1, :small].astype(F32)
        for k in range(3):
            first = k * 4 * WIDE + h * WIDE
            gq_ref[:, first : first + WIDE] = part[:, k * WIDE : (k + 1) * WIDE]
    total = add(gd_refs[0][...], gd_refs[1][...])
    gd_ref[...] = total + add(gd_refs[2][...], gd_refs[3][...])

    rows = up_own[...].astype(F32)
    mine = [jnp.where(c == 0, rows[48 * q : 48 * q + 24], rows[48 * q + 24 : 48 * q + 48]) for q in range(3)]
    go_ref[...] = mine[2] + up_far[2].astype(F32)
    part = gu_ref.shape[1] // 8
    for q in range(2):
        for side in range(2):
            lanes = slice(side * part, (side + 1) * part)
            for core, block in ((c, mine[q]), (1 - c, up_far[q].astype(F32))):
                first = pl.multiple_of((2 * (2 * q + side) + core) * part, 128)
                gu_ref[:, pl.ds(first, part)] = block[:, lanes]

    total = x_ref[0, small:, :part].astype(F32)
    for d in range(1, 8):
        total += x_ref[d, small:, :part].astype(F32)
    sums[...] = total

    def pair(i):
        return total[8 + 2 * i : 10 + 2 * i]

    def over(v):
        return jnp.sum(v, keepdims=True) * (1.0 / (2 * part))

    centered = embed[...] - over(embed[...])
    scale = lax.rsqrt(over(centered * centered) + EPSILON)
    hat = centered * scale
    t = pair(4) * gain[...]
    sums[12:14] = pair(2) + scale * (t - over(t) - hat * over(t * hat))
    sums[14:16] = pair(3) / gain[...]
    row = sums[pl.ds(own // 4, 1)]
    bu_ref[...] = pltpu.roll(row, (4 * 96 - own % 4 * 96) % part, 1)[:, :96]
    shift = (16 * 24 - own % 16 * 24) % part
    for i in range(4):
        row = sums[pl.ds(8 + 2 * i + own // 16, 1)]
        rows_ref[i : i + 1] = pltpu.roll(row, shift, 1)[:, :24]


def cut(v, index, size, axis=0):
    return lax.dynamic_slice_in_dim(v, index * size, size, axis)


def at(v, index, axis=0):
    return lax.dynamic_index_in_dim(v, index, axis, keepdims=False)


def after(value, *needed):
    return lax.optimization_barrier((value, *needed))[0]


def add(a, b):
    return a.astype(F32) + b.astype(F32)


def exchange(v):
    return lax.all_to_all(v, "ctx", 0, 0, tiled=True)


def exchange_chips(v):
    groups = [[i + core for i in range(0, 8, 2)] for core in range(2)]
    return lax.all_to_all(v, "ctx", 0, 0, axis_index_groups=groups, tiled=True)


def exchange_z(v):
    return lax.all_to_all(v, "fsdp", 0, 0, tiled=True)


def shards_by_heads(
    hidden,
    noise_mask,
    doc_lengths,
    w_qkv,
    w_out,
    w_up,
    b_up,
    w_down,
    b_down,
    gain_one,
    gain_two,
    mask_embed,
    out_grad,
):
    r = lax.axis_index("ctx")
    z = lax.axis_index("fsdp")
    c, h = r & 1, r >> 1
    dim = hidden.shape[3]
    hid = w_up.shape[1]
    part = hid // 8
    total = CHUNK * 8
    clean = c == 0

    share = pack_share(jnp.stack([r, c, h, z]).astype(jnp.int32), w_out, w_down, w_up)
    ff_t = lax.all_gather(share, "fsdp")
    hidden = after(hidden, share)

    noisy = jnp.where(noise_mask[0][:, None] == 1, jnp.asarray(jnp.inf, BF), hidden[0, 1])
    mine = jnp.where(clean, hidden[0, 0], noisy)
    other = swap(jnp.where(clean, noisy, hidden[0, 0]), 1)
    mine_x, mine_y = swap(mine, 2), swap(mine, 4)
    other_x, other_y = swap(other, 2), swap(other, 4)
    marked = jnp.stack([hidden[0, 0], noisy])

    lengths = doc_lengths[0]
    index = jnp.arange(lengths.shape[0])
    ends = jnp.sum(jnp.where(index[None, :] <= index[:, None], lengths[None, :], 0), axis=1)
    place = jnp.arange(total, dtype=jnp.int32)
    later = ends[None, :] > place[:, None]
    start = jnp.max(jnp.where(later, 0, ends[None, :]), axis=1)
    stop = jnp.min(jnp.where(later, ends[None, :], total), axis=1)
    block = place // BLOCK * BLOCK
    limit = jnp.minimum(block + BLOCK, stop)
    bounds = jnp.stack(
        [start, jnp.where(clean, limit, block), jnp.where(clean, start, jnp.maximum(start, block)), limit]
    )
    bounds = jnp.pad(bounds.reshape(4, 8, CHUNK).transpose(1, 0, 2), ((0, 0), (0, 4), (0, 0)))
    meta = jnp.concatenate(
        [jnp.stack([r, c, h, z]), start[::CHUNK] // CHUNK, start[CHUNK - 1 :: CHUNK]]
    ).astype(jnp.int32)
    slots = (jnp.arange(8) ^ r)[:, None] * CHUNK + jnp.arange(CHUNK)[None, :]
    frequency = jnp.exp(jnp.arange(HALF).astype(F32) * (-2.0 * math.log(10000.0) / HEAD_DIM))
    angles = slots.astype(F32)[:, None, :] * frequency[None, :, None]
    cos, sin = jnp.cos(angles), jnp.sin(angles)
    size = hid // 4 + dim
    w_qkv = after(w_qkv, other)
    small = jnp.concatenate([b_up, b_down, gain_one, gain_two, mask_embed])
    small = jnp.pad(small, (0, 16 * 3 * WIDE - size)).reshape(16, 3 * WIDE)
    own_qkv = jnp.concatenate([cut(w_qkv[:, k * dim : (k + 1) * dim], h, WIDE, 1) for k in range(3)], 1)
    quarter = dim // 4
    half = jnp.concatenate([cut(own_qkv, c, quarter // 2), small])
    half = jnp.broadcast_to(half, (4, *half.shape))
    near = exchange_z(half)
    mine_x, mine_y, other_x, other_y, cos, sin, bounds, meta = lax.optimization_barrier(
        (mine_x, mine_y, other_x, other_y, cos, sin, bounds, meta)
    )
    mine_d, other_d = swap(mine_x, 4), swap(other_y, 2)
    mine_d, other_d, near = lax.optimization_barrier((mine_d, other_d, near))
    far = swap(near, 1)
    small = near[:, quarter // 2 :].reshape(4, -1)[:, :size].astype(F32)
    bias = at(small[:, : hid // 4].reshape(4, 2, part), c, 1).reshape(1, 4 * part)
    b_down_all, gain_a, gain_b, embed = [
        small[:, hid // 4 + k * quarter : hid // 4 + (k + 1) * quarter].reshape(1, dim)
        for k in range(4)
    ]

    grads = out_grad[0]
    grad_rows = grads.reshape(2 * CHUNK, dim)

    ff_r = jnp.take(ff_t, (z - jnp.arange(1, 4)) % 4, axis=0)
    far, ff_r = lax.optimization_barrier((far, ff_r))
    shares = (ff_r, swap(ff_r, 2), swap(ff_r, 4), swap(ff_r, 6))
    rows = (mine, other, mine_x, other_x, mine_y, other_y, mine_d, other_d)
    q, *kv, normed_one, marks, w_all = project_rows(meta, gain_a, embed, cos, sin, rows, (near, far))
    give = [(i, i + 1) for i in range(0, 8, 2)]
    heads = (q, *kv, *[lax.ppermute(v, "ctx", give) for v in kv])
    send, attended, stats = attend_rows(meta, bounds, heads)
    send, *shares = lax.optimization_barrier((send, *shares))
    grad_far = swap(after(grad_rows, kv[0]), 1)
    middle, normed, att, w_out_all = middle_rows(
        meta, gain_b, embed, marked, exchange(send), w_out, shares
    )
    out_own, out_far, ng_far, ng_own, gbu, gd, gu = feed_rows(
        meta, bias, (normed, swap(normed, 1), grad_rows, grad_far, w_up, w_down, *shares)
    )
    ng_far, out_far = swap(ng_far, 1), swap(out_far, 1)
    gd = lax.psum_scatter(gd.reshape(-1, dim), "fsdp", scatter_dimension=0, tiled=True)

    layer, mid_grad, sums, send = middle_back(
        meta, gain_b, b_down_all, (middle, ng_own, out_own, out_far, ng_far, grads, marked, w_out_all)
    )
    got = exchange(send)
    (up_out,) = call(
        out_grad_body, [((4, 4, part // 4 + dim // 16, dim), BF)], "VVA", (att, mid_grad, gu), flops=4 * CHUNK * dim * dim
    )
    got, up_out = lax.optimization_barrier((got, up_out))
    up_out = exchange_chips(up_out)
    pq, own_kv, *far_kv = attend_back(meta, bounds, cos, sin, attended, stats, heads, got)
    far_kv = [lax.ppermute(v, "ctx", [(b, a) for a, b in give]) for v in far_kv]

    up_out = jnp.sum(after(up_out, pq).astype(F32), axis=0).astype(BF).reshape(-1, dim)
    gd = after(gd, pq).reshape(4, part // 4, dim)
    *far_kv, up_out, gd = lax.optimization_barrier((*far_kv, up_out, gd))
    up_out = lax.psum_scatter(up_out, "fsdp", scatter_dimension=0, tiled=True)

    away_x, away_y, stay, gq, vec = project_back(
        own_kv, far_kv, pq, normed_one, marks, cos, sin, w_all
    )
    in_x, in_y = swap(away_x, 2), swap(away_y, 4)
    gbu = gbu.reshape(4, 1, part)
    gbu = jnp.where(clean, jnp.concatenate([gbu, 0 * gbu], 1), jnp.concatenate([0 * gbu, gbu], 1))
    flat = jnp.concatenate([gbu.reshape(-1), sums[:3].reshape(-1), vec[:2].reshape(-1)])
    wide = gq.shape[2]
    length = flat.shape[0]

    def parts_of(v):
        v = v.reshape(length // part, part)
        return jnp.pad(v, ((0, 24 - length // part), (0, wide - part))).astype(BF)

    rows = dim // 4
    flat = jnp.broadcast_to(parts_of(flat), (4, 24, wide))
    gq = jnp.concatenate([gq, flat], 1).reshape(-1, wide)
    gq = lax.psum_scatter(gq, "fsdp", scatter_dimension=0, tiled=True)
    over_y, over_x = add(stay[1], in_x[1]).astype(BF), add(stay[3], in_y[1]).astype(BF)
    near_one, near_two = swap(over_y, 4), swap(over_x, 2)
    gd = after(gd, over_y, over_x)
    gd = [gd[0]] + [swap(gd[k], 2 * k) for k in range(1, 4)]
    gq = after(gq, over_y, over_x)
    flat = jnp.broadcast_to(gq[rows:], (8, 24, wide))
    gq = jnp.concatenate([gq[:rows].reshape(8, dim // 32, wide), flat], 1)
    near_one, near_two, gq = lax.optimization_barrier((near_one, near_two, gq))
    gq = exchange(gq)
    keep = add(stay[0], in_x[0]) + near_one.astype(F32)
    pair = (add(stay[2], in_y[0]) + near_two.astype(F32)).astype(BF)
    pair = swap(pair, 1)
    *gd, gq = lax.optimization_barrier((*gd, gq, keep, pair))[:5]
    (input_grad,) = call(
        last_body,
        [((2, CHUNK, dim), BF)],
        "S" + "V" * 6,
        (meta, gain_a, embed, marked, mid_grad, keep, pair),
        moved=10 * CHUNK * dim,
    )

    up_sum = after(up_out, input_grad)
    up_out = up_sum.reshape(3, 2, dim // 32, dim)
    up_far = swap(at(up_out, 1 - c, 1), 1)
    small = dim // 32
    gq, go, gu, gd, gbu, rows = call(
        finish_body,
        [
            ((small, 3 * dim), F32),
            ((small, dim), F32),
            ((small, hid), F32),
            ((part // 4, dim), F32),
            ((1, hid // 32), F32),
            ((4, small), F32),
        ],
        "S" + "V" * 9,
        (meta, gain_a.reshape(2, part), embed.reshape(2, part), gq, up_sum, up_far, *gd),
        scratch=[pltpu.VMEM((24, part), F32)],
        moved=8 * dim * dim,
    )
    return (
        layer[None],
        input_grad[None],
        gq,
        go,
        gu,
        gbu[0],
        gd,
        rows[1],
        rows[3],
        rows[0],
        rows[2],
    )


def solution(mesh):
    plain = (mesh.shape["ctx"], mesh.shape["fsdp"]) != (8, 4)
    placed = (
        P("fsdp", None, "ctx", None),
        P("fsdp", "ctx"),
        P("fsdp", None),
        P("fsdp", None),
        P("fsdp", None),
        P("fsdp", None),
        P("fsdp"),
        P("fsdp", None),
        P("fsdp"),
        P("fsdp"),
        P("fsdp"),
        P("fsdp"),
        P("fsdp", None, "ctx", None),
    )
    return jax.shard_map(
        shards if plain else shards_by_heads,
        mesh=mesh,
        in_specs=placed,
        out_specs=(
            P("fsdp", None, "ctx", None),
            P("fsdp", None, "ctx", None),
            P(("ctx", "fsdp"), None),
            P(("ctx", "fsdp"), None),
            P(("ctx", "fsdp"), None),
            P(("ctx", "fsdp")),
            P(("ctx", "fsdp"), None),
            P(("ctx", "fsdp")),
            P(("ctx", "fsdp")),
            P(("ctx", "fsdp")),
            P(("ctx", "fsdp")),
        ),
        check_vma=False,
    )
```

```python
import functools
import math

import jax
import jax.numpy as jnp
from jax import lax
from jax.experimental import pallas as pl
from jax.experimental.pallas import tpu as pltpu
from jax.sharding import PartitionSpec as P

HEADS = 12
HEAD_DIM = 64
BLOCK = 16


LOWEST = -1e30
EPSILON = 1e-05


def layer_norm(inputs, gain):
    average = jnp.mean(inputs, axis=-1, keepdims=True)
    centered = inputs - average
    variance = jnp.mean(centered * centered, axis=-1, keepdims=True)
    return centered * lax.rsqrt(variance + EPSILON) * gain


def rotary_angles(positions):
    half_dim = HEAD_DIM // 2
    frequency = jnp.exp(
        jnp.arange(half_dim).astype(jnp.float32) * (-2.0 * math.log(10000.0) / HEAD_DIM)
    )
    return positions.astype(jnp.float32)[:, None] * frequency[None, :]


def rotate(heads_in, angles):
    half_dim = heads_in.shape[-1] // 2
    cosine = jnp.cos(angles)[:, None, :]
    sine_part = jnp.sin(angles)[:, None, :]
    first_half = heads_in[..., :half_dim]
    second_half = heads_in[..., half_dim:]
    return jnp.concatenate(
        [
            first_half * cosine - second_half * sine_part,
            second_half * cosine + first_half * sine_part,
        ],
        axis=-1,
    )


def segment_of(positions, doc_ends):
    return jnp.sum((positions[:, None] >= doc_ends[None, :]).astype(jnp.int32), axis=1)


def visible(query_stream, query_position, query_segment, key_stream, key_position, key_segment):
    query_block = query_position // BLOCK
    key_block = key_position // BLOCK
    same_doc = query_segment[:, None] == key_segment[None, :]
    clean_key = key_stream[None, :] == 0
    noisy_query = query_stream[:, None] == 1
    before = key_block[None, :] < query_block[:, None]
    same_block = key_block[None, :] == query_block[:, None]
    from_clean = clean_key & (before | same_block & jnp.logical_not(noisy_query))
    from_noisy = jnp.logical_not(clean_key) & noisy_query & same_block
    return same_doc & (from_clean | from_noisy)


def mix_tile(running, query_rows, key_tile, value_tile, allowed):
    run_max, run_sum, accum = running
    scores = (
        jnp.einsum("qhd,khd->hqk", query_rows, key_tile, preferred_element_type=jnp.float32) * 0.125
    )
    masked = jnp.where(allowed[None], scores, LOWEST)
    new_max = jnp.maximum(run_max, jnp.max(masked, axis=-1))
    exp_terms = jnp.where(allowed[None], jnp.exp(masked - new_max[..., None]), 0.0)
    factor = jnp.exp(run_max - new_max)
    new_sum = run_sum * factor + jnp.sum(exp_terms, axis=-1)
    accum = accum * factor[..., None] + jnp.einsum(
        "hqk,khd->hqd",
        exp_terms.astype(jnp.bfloat16),
        value_tile,
        preferred_element_type=jnp.float32,
    )
    return (new_max, new_sum, accum)


def tile_grads(query_rows, key_tile, value_tile, allowed, row_max, scaled_grad, correction):
    scores = (
        jnp.einsum("qhd,khd->hqk", query_rows, key_tile, preferred_element_type=jnp.float32) * 0.125
    )
    masked = jnp.where(allowed[None], scores, LOWEST)
    exp_terms = jnp.where(allowed[None], jnp.exp(masked - row_max[..., None]), 0.0)
    prob_grad = jnp.einsum(
        "hqd,khd->hqk", scaled_grad, value_tile, preferred_element_type=jnp.float32
    )
    score_grad = (exp_terms * (prob_grad - correction[..., None])).astype(jnp.bfloat16)
    query_part = jnp.einsum(
        "hqk,khd->qhd", score_grad, key_tile, preferred_element_type=jnp.float32
    )
    key_part = jnp.einsum(
        "hqk,qhd->khd", score_grad, query_rows, preferred_element_type=jnp.float32
    )
    value_part = jnp.einsum(
        "hqk,hqd->khd",
        exp_terms.astype(jnp.bfloat16),
        scaled_grad,
        preferred_element_type=jnp.float32,
    )
    return (query_part, key_part, value_part)


def build_inputs(hidden, noise_row, mask_row):
    clean_rows = hidden[0, 0].astype(jnp.float32)
    noisy_rows = jnp.where(
        noise_row[:, None] == 1,
        mask_row.astype(jnp.float32)[None, :],
        hidden[0, 1].astype(jnp.float32),
    )
    return jnp.concatenate([clean_rows, noisy_rows], axis=0)


def project(inputs, gathered, angles):
    row_count = inputs.shape[0]
    model_dim = inputs.shape[1]
    normed = layer_norm(inputs, gathered[6].astype(jnp.float32)).astype(jnp.bfloat16)
    projected = jnp.dot(normed, gathered[0], preferred_element_type=jnp.float32)
    query_rows = rotate(
        projected[:, :model_dim].reshape(row_count, HEADS, HEAD_DIM), angles
    ).astype(jnp.bfloat16)
    key_rows = rotate(
        projected[:, model_dim : 2 * model_dim].reshape(row_count, HEADS, HEAD_DIM), angles
    ).astype(jnp.bfloat16)
    value_rows = (
        projected[:, 2 * model_dim :].reshape(row_count, HEADS, HEAD_DIM).astype(jnp.bfloat16)
    )
    return (normed, query_rows, key_rows, value_rows)


def upper_half(inputs, attended_low, gathered):
    middle = inputs + jnp.dot(attended_low, gathered[1], preferred_element_type=jnp.float32)
    normed_two = layer_norm(middle, gathered[7].astype(jnp.float32)).astype(jnp.bfloat16)
    upper = jnp.dot(normed_two, gathered[2], preferred_element_type=jnp.float32) + gathered[
        3
    ].astype(jnp.float32)
    activated = jax.nn.gelu(upper, approximate=True).astype(jnp.bfloat16)
    return (middle, normed_two, upper, activated)


def shards(
    hidden,
    noise_mask,
    doc_lengths,
    w_qkv,
    w_out,
    w_up,
    b_up,
    w_down,
    b_down,
    gain_one,
    gain_two,
    mask_embed,
    out_grad,
):
    own_params = (w_qkv, w_out, w_up, b_up, w_down, b_down, gain_one, gain_two, mask_embed)
    local_count = hidden.shape[2]
    model_dim = hidden.shape[3]
    row_count = 2 * local_count
    ctx_index = lax.axis_index("ctx")
    offset = ctx_index * local_count
    local_place = offset + jnp.arange(local_count, dtype=jnp.int32)
    positions = jnp.concatenate([local_place, local_place])
    stream = jnp.concatenate(
        [jnp.zeros((local_count,), jnp.int32), jnp.ones((local_count,), jnp.int32)]
    )
    doc_ends = jnp.cumsum(doc_lengths[0])
    segments = segment_of(positions, doc_ends)
    angles = rotary_angles(positions)
    noise_row = noise_mask[0]
    noisy_stream = stream[local_count:]
    noisy_allowed = visible(
        stream, positions, segments, noisy_stream, positions[local_count:], segments[local_count:]
    )
    gathered = (
        lax.all_gather(own_params[0], "fsdp", axis=0, tiled=True),
        lax.all_gather(own_params[1], "fsdp", axis=0, tiled=True),
        lax.all_gather(own_params[2], "fsdp", axis=0, tiled=True),
        lax.all_gather(own_params[3], "fsdp", axis=0, tiled=True),
        lax.all_gather(own_params[4], "fsdp", axis=0, tiled=True),
        lax.all_gather(own_params[5], "fsdp", axis=0, tiled=True),
        lax.all_gather(own_params[6], "fsdp", axis=0, tiled=True),
        lax.all_gather(own_params[7], "fsdp", axis=0, tiled=True),
        lax.all_gather(own_params[8], "fsdp", axis=0, tiled=True),
    )
    inputs = build_inputs(hidden, noise_row, gathered[8])
    normed, query_rows, key_rows, value_rows = project(inputs, gathered, angles)
    clean_keys = key_rows[:local_count].reshape(local_count, model_dim)
    clean_values = value_rows[:local_count].reshape(local_count, model_dim)
    start_state = (
        jnp.full((HEADS, row_count), LOWEST, jnp.float32),
        jnp.zeros((HEADS, row_count), jnp.float32),
        jnp.zeros((HEADS, row_count, HEAD_DIM), jnp.float32),
    )
    running = start_state
    piece_keys = lax.all_gather(clean_keys, "ctx", axis=0, tiled=True)
    piece_values = lax.all_gather(clean_values, "ctx", axis=0, tiled=True)
    piece_rows = piece_keys.shape[0]
    fold_tile_size = math.gcd(piece_rows, 512)

    def step(carried, tile_index):
        tile_start = tile_index * fold_tile_size
        key_tile = lax.dynamic_slice_in_dim(piece_keys, tile_start, fold_tile_size, 0).reshape(
            fold_tile_size, HEADS, HEAD_DIM
        )
        value_tile = lax.dynamic_slice_in_dim(piece_values, tile_start, fold_tile_size, 0).reshape(
            fold_tile_size, HEADS, HEAD_DIM
        )
        key_position = tile_start + jnp.arange(fold_tile_size, dtype=jnp.int32)
        allowed = visible(
            stream,
            positions,
            segments,
            jnp.zeros((fold_tile_size,), jnp.int32),
            key_position,
            segment_of(key_position, doc_ends),
        )
        carried = lax.cond(
            jnp.any(allowed),
            lambda held: mix_tile(held, query_rows, key_tile, value_tile, allowed),
            lambda held: held,
            carried,
        )
        return (carried, None)

    running, _ = lax.scan(step, running, jnp.arange(piece_rows // fold_tile_size))
    run_max, run_sum, accum = mix_tile(
        running, query_rows, key_rows[local_count:], value_rows[local_count:], noisy_allowed
    )
    attended = accum / run_sum[..., None]
    attended_low = (
        jnp.transpose(attended, (1, 0, 2)).reshape(row_count, model_dim).astype(jnp.bfloat16)
    )
    middle, normed_two, upper, activated = upper_half(inputs, attended_low, gathered)
    result = (
        middle
        + jnp.dot(activated, gathered[4], preferred_element_type=jnp.float32)
        + gathered[5].astype(jnp.float32)
    )
    layer_out = result.astype(jnp.bfloat16).reshape(1, 2, local_count, model_dim)
    again = (
        lax.all_gather(own_params[0], "fsdp", axis=0, tiled=True),
        lax.all_gather(own_params[1], "fsdp", axis=0, tiled=True),
        lax.all_gather(own_params[2], "fsdp", axis=0, tiled=True),
        lax.all_gather(own_params[3], "fsdp", axis=0, tiled=True),
        lax.all_gather(own_params[4], "fsdp", axis=0, tiled=True),
        lax.all_gather(own_params[5], "fsdp", axis=0, tiled=True),
        lax.all_gather(own_params[6], "fsdp", axis=0, tiled=True),
        lax.all_gather(own_params[7], "fsdp", axis=0, tiled=True),
        lax.all_gather(own_params[8], "fsdp", axis=0, tiled=True),
    )
    normed, query_rows, key_rows, value_rows = project(inputs, again, angles)
    noisy_keys = key_rows[local_count:]
    noisy_values = value_rows[local_count:]
    middle, normed_two, upper, activated = upper_half(inputs, attended_low, again)
    grad_rows = out_grad[0].reshape(row_count, model_dim)
    grad_float = grad_rows.astype(jnp.float32)
    grad_down = jnp.einsum("qi,qj->ij", activated, grad_rows, preferred_element_type=jnp.float32)
    grad_down_bias = jnp.sum(grad_float, axis=0)
    activated_grad = jnp.einsum(
        "qj,ij->qi", grad_rows, again[4], preferred_element_type=jnp.float32
    )
    _, gelu_pull = jax.vjp(lambda upper_in: jax.nn.gelu(upper_in, approximate=True), upper)
    upper_grad = gelu_pull(activated_grad)[0].astype(jnp.bfloat16)
    grad_up = jnp.einsum("qi,qj->ij", normed_two, upper_grad, preferred_element_type=jnp.float32)
    grad_up_bias = jnp.sum(upper_grad.astype(jnp.float32), axis=0)
    normed_two_grad = jnp.einsum(
        "qj,ij->qi", upper_grad, again[2], preferred_element_type=jnp.float32
    )
    _, second_pull = jax.vjp(layer_norm, middle, again[7].astype(jnp.float32))
    middle_norm_grad, grad_gain_two = second_pull(normed_two_grad)
    middle_grad = (grad_float + middle_norm_grad).astype(jnp.bfloat16)
    grad_out_proj = jnp.einsum(
        "qi,qj->ij", attended_low, middle_grad, preferred_element_type=jnp.float32
    )
    attended_grad = jnp.einsum(
        "qj,ij->qi", middle_grad, again[1], preferred_element_type=jnp.float32
    )
    attended_grad = jnp.transpose(attended_grad.reshape(row_count, HEADS, HEAD_DIM), (1, 0, 2))
    scaled_grad = (attended_grad / run_sum[..., None]).astype(jnp.bfloat16)
    correction = jnp.sum(attended_grad * attended, axis=-1) / run_sum
    pair_rows = (
        lax.all_gather(
            key_rows[:local_count].reshape(local_count, model_dim), "ctx", axis=0, tiled=True
        ),
        lax.all_gather(
            value_rows[:local_count].reshape(local_count, model_dim), "ctx", axis=0, tiled=True
        ),
    )
    pair_keys, pair_values = pair_rows
    total_rows = pair_keys.shape[0]
    tile_size = math.gcd(total_rows, 512)
    zero_tile = jnp.zeros((tile_size, HEADS, HEAD_DIM), jnp.float32)

    def back_step(query_acc, tile_index):
        tile_start = tile_index * tile_size
        key_tile = lax.dynamic_slice_in_dim(pair_keys, tile_start, tile_size, 0).reshape(
            tile_size, HEADS, HEAD_DIM
        )
        value_tile = lax.dynamic_slice_in_dim(pair_values, tile_start, tile_size, 0).reshape(
            tile_size, HEADS, HEAD_DIM
        )
        key_position = tile_start + jnp.arange(tile_size, dtype=jnp.int32)
        allowed = visible(
            stream,
            positions,
            segments,
            jnp.zeros((tile_size,), jnp.int32),
            key_position,
            segment_of(key_position, doc_ends),
        )

        def live_tile(held):
            query_part, key_part, value_part = tile_grads(
                query_rows, key_tile, value_tile, allowed, run_max, scaled_grad, correction
            )
            return (held + query_part, key_part, value_part)

        query_acc, key_part, value_part = lax.cond(
            jnp.any(allowed), live_tile, lambda held: (held, zero_tile, zero_tile), query_acc
        )
        return (
            query_acc,
            (key_part.reshape(tile_size, model_dim), value_part.reshape(tile_size, model_dim)),
        )

    query_acc, (key_terms, value_terms) = lax.scan(
        back_step,
        jnp.zeros((row_count, HEADS, HEAD_DIM), jnp.float32),
        jnp.arange(total_rows // tile_size),
    )
    key_terms = key_terms.reshape(total_rows, model_dim)
    value_terms = value_terms.reshape(total_rows, model_dim)
    clean_key_grad, clean_value_grad = (
        lax.psum_scatter(
            key_terms.astype(jnp.bfloat16), "ctx", scatter_dimension=0, tiled=True
        ).astype(jnp.float32),
        lax.psum_scatter(
            value_terms.astype(jnp.bfloat16), "ctx", scatter_dimension=0, tiled=True
        ).astype(jnp.float32),
    )
    query_part, noisy_key_part, noisy_value_part = tile_grads(
        query_rows, noisy_keys, noisy_values, noisy_allowed, run_max, scaled_grad, correction
    )
    query_grad = (query_acc + query_part) * 0.125
    key_grad = (
        jnp.concatenate(
            [clean_key_grad.reshape(local_count, HEADS, HEAD_DIM), noisy_key_part], axis=0
        )
        * 0.125
    )
    value_grad = jnp.concatenate(
        [clean_value_grad.reshape(local_count, HEADS, HEAD_DIM), noisy_value_part], axis=0
    )
    _, rotate_pull = jax.vjp(lambda heads_in: rotate(heads_in, angles), query_grad)
    query_raw_grad = rotate_pull(query_grad)[0]
    key_raw_grad = rotate_pull(key_grad)[0]
    projected_grad = jnp.concatenate(
        [
            query_raw_grad.reshape(row_count, model_dim),
            key_raw_grad.reshape(row_count, model_dim),
            value_grad.reshape(row_count, model_dim),
        ],
        axis=1,
    ).astype(jnp.bfloat16)
    grad_qkv = jnp.einsum("qi,qj->ij", normed, projected_grad, preferred_element_type=jnp.float32)
    normed_grad = jnp.einsum(
        "qj,ij->qi", projected_grad, again[0], preferred_element_type=jnp.float32
    )
    _, first_pull = jax.vjp(layer_norm, inputs, again[6].astype(jnp.float32))
    inputs_norm_grad, grad_gain_one = first_pull(normed_grad)
    inputs_grad = middle_grad.astype(jnp.float32) + inputs_norm_grad
    noisy_flag = (noise_row == 1)[:, None]
    noisy_grad = inputs_grad[local_count:]
    grad_mask = jnp.sum(jnp.where(noisy_flag, noisy_grad, 0.0), axis=0)
    input_grad = jnp.concatenate(
        [inputs_grad[:local_count], jnp.where(noisy_flag, 0.0, noisy_grad)], axis=0
    )
    input_grad = input_grad.astype(jnp.bfloat16).reshape(1, 2, local_count, model_dim)
    shares = (
        lax.psum_scatter(grad_qkv, ("ctx", "fsdp"), scatter_dimension=0, tiled=True),
        lax.psum_scatter(grad_out_proj, ("ctx", "fsdp"), scatter_dimension=0, tiled=True),
        lax.psum_scatter(grad_up, ("ctx", "fsdp"), scatter_dimension=0, tiled=True),
        lax.psum_scatter(grad_up_bias, ("ctx", "fsdp"), scatter_dimension=0, tiled=True),
        lax.psum_scatter(grad_down, ("ctx", "fsdp"), scatter_dimension=0, tiled=True),
        lax.psum_scatter(grad_down_bias, ("ctx", "fsdp"), scatter_dimension=0, tiled=True),
        lax.psum_scatter(grad_gain_one, ("ctx", "fsdp"), scatter_dimension=0, tiled=True),
        lax.psum_scatter(grad_gain_two, ("ctx", "fsdp"), scatter_dimension=0, tiled=True),
        lax.psum_scatter(grad_mask, ("ctx", "fsdp"), scatter_dimension=0, tiled=True),
    )
    (
        qkv_share,
        out_share,
        up_share,
        up_bias_share,
        down_share,
        down_bias_share,
        gain_one_share,
        gain_two_share,
        mask_share,
    ) = shares
    return (
        layer_out,
        input_grad,
        qkv_share,
        out_share,
        up_share,
        up_bias_share,
        down_share,
        down_bias_share,
        gain_one_share,
        gain_two_share,
        mask_share,
    )


CHUNK = 256
COST = 10**9
GROUP = 3
WIDE = GROUP * HEAD_DIM
HALF = HEAD_DIM // 2
LANES = GROUP * CHUNK
BF = jnp.bfloat16
F32 = jnp.float32
HB = pl.BlockSpec(memory_space=pltpu.HBM)
SM = pl.BlockSpec(memory_space=pltpu.SMEM)
GELU_SCALE = math.sqrt(2.0 / math.pi)


def swap(v, bit):
    return lax.ppermute(v, "ctx", [(i, i ^ bit) for i in range(8)])


def turn(v, step):
    return lax.ppermute(v, "fsdp", [(i, (i + step) % 4) for i in range(4)])


def mm(a, b, ca=1, cb=0):
    return lax.dot_general(a, b, (((ca,), (cb,)), ((), ())), preferred_element_type=F32)


def flip(v):
    return jnp.transpose(v.astype(F32)).astype(v.dtype)


def call(body, outs, kinds, args, scratch=(), flops=0, moved=0):
    staged = [i for i, kind in enumerate(kinds) if kind == "V"]
    space = {"S": SM, "V": HB, "A": HB}
    count, made = len(args), len(outs)

    def run(*refs):
        ins, sinks, rest = list(refs[:count]), refs[count : count + made], refs[count + made :]
        held, results = rest[: len(staged)], rest[len(staged) : len(staged) + made]
        sem_in, sem_out, sems = rest[len(staged) + made : len(staged) + made + 3]
        rest = rest[len(staged) + made + 3 :]
        first = [
            pltpu.make_async_copy(ins[i], held[k], sem_in.at[k]) for k, i in enumerate(staged)
        ]
        for copy in first:
            copy.start()
        for k, i in enumerate(staged):
            ins[i] = held[k]

        def load(pairs):
            more = [pltpu.make_async_copy(a, b, sems.at[i]) for i, (a, b) in enumerate(pairs)]
            for copy in more:
                copy.start()
            for copy in more + first:
                copy.wait()

        body(load, *ins, *results, *rest)
        last = [pltpu.make_async_copy(results[k], sinks[k], sem_out.at[k]) for k in range(made)]
        for copy in last:
            copy.start()
        for copy in last:
            copy.wait()

    return pl.pallas_call(
        run,
        out_shape=tuple(jax.ShapeDtypeStruct(s, d) for s, d in outs),
        in_specs=[space[kind] for kind in kinds],
        out_specs=tuple(HB for _ in outs),
        scratch_shapes=[pltpu.VMEM(args[i].shape, args[i].dtype) for i in staged]
        + [pltpu.VMEM(s, d) for s, d in outs]
        + [
            pltpu.SemaphoreType.DMA((max(1, len(staged)),)),
            pltpu.SemaphoreType.DMA((made,)),
            pltpu.SemaphoreType.DMA((48,)),
        ]
        + list(scratch),
        compiler_params=pltpu.CompilerParams(vmem_limit_bytes=56 * 2**20),
        cost_estimate=pl.CostEstimate(flops=1 + flops // COST, bytes_accessed=1 + moved // COST, transcendentals=0),
    )(*args)


def at16(v):
    return pl.multiple_of(v, 16)


def shard_rows(meta, near, far, dst, unit):
    half = unit // 2
    pairs = []
    for zz in range(4):
        for core, part in ((meta[1], near), (1 - meta[1], far)):
            to = at16(zz * unit + core * half)
            pairs.append((part.at[zz, pl.ds(0, half)], dst.at[pl.ds(to, half)]))
    return pairs


def norm_parts(x):
    mean = jnp.mean(x, axis=-1, keepdims=True)
    centered = x - mean
    var = jnp.mean(centered * centered, axis=-1, keepdims=True)
    scale = lax.rsqrt(var + EPSILON)
    return centered * scale, scale


def unmark(x, embed):
    x = x.astype(F32)
    flag = x[:, :1] > 1e38
    return jnp.where(flag, embed, x), flag


def turn_heads(v, cos, sin):
    parts = []
    for g in range(GROUP):
        a = v[g * HEAD_DIM : g * HEAD_DIM + HALF]
        b = v[g * HEAD_DIM + HALF : (g + 1) * HEAD_DIM]
        parts += [a * cos - b * sin, b * cos + a * sin]
    return jnp.concatenate(parts, axis=0)


def project_body(load, meta, gain, embed, cos, sin, *refs):
    rows, refs = refs[:8], refs[8:]
    near, far, q_ref, kv_a, kv_b, n_ref, mk_ref, w, xs, wp = refs
    load(shard_rows(meta, near, far, w, 192) + [(rows[i], xs.at[i]) for i in range(8)])
    for part in range(3):
        wp[part] = w[:, part * WIDE : (part + 1) * WIDE]

    @pl.loop(0, 8)
    def _(i):
        x, flag = unmark(xs[i], embed[...])
        hat, _ = norm_parts(x)
        n = (hat * gain[...]).astype(BF)
        n_ref[i] = n
        mk_ref[i] = jnp.broadcast_to(jnp.where(flag, 1.0, 0.0), (CHUNK, 128)).astype(BF)
        q_ref[i] = turn_heads(jnp.transpose(mm(n, wp[0])), cos[i], sin[i]).astype(BF)
        keys = turn_heads(jnp.transpose(mm(n, wp[1])), cos[i], sin[i]).astype(BF)
        values = jnp.transpose(mm(n, wp[2])).astype(BF)
        for half, ref in enumerate((kv_a, kv_b)):

            @pl.when(i // 4 == half)
            def _():
                ref[i % 4, :WIDE] = keys
                ref[i % 4, WIDE:] = values


def project_rows(meta, gain, embed, cos, sin, rows, weights):
    dim = rows[0].shape[1]
    wide = weights[0].shape[-1]
    return call(
        project_body,
        [
            ((8, WIDE, CHUNK), BF),
            ((4, 2 * WIDE, CHUNK), BF),
            ((4, 2 * WIDE, CHUNK), BF),
            ((8, CHUNK, dim), BF),
            ((8, CHUNK, 128), BF),
            ((dim, wide), BF),
        ],
        "SVVVV" + "A" * 10,
        (meta, gain, embed, cos, sin, *rows, *weights),
        scratch=[pltpu.VMEM((8, CHUNK, dim), BF), pltpu.VMEM((3, dim, WIDE), BF)],
        flops=2 * 8 * CHUNK * dim * 3 * WIDE,
        moved=8 * CHUNK * dim * 6,
    )


def head_pairs(refs, qs, kv):
    pairs = [(refs[0], qs)]
    for i, ref in enumerate(refs[1:]):
        pairs.append((ref, kv.at[i // 2, pl.ds(i % 2 * 4, 4)]))
    return pairs


def thrice(v):
    return jnp.concatenate([v, v, v], axis=1)


def scores_of(keys, stacked, base, low, high, plain):
    s = mm(keys, stacked)
    if plain:
        return s
    place = base + lax.broadcasted_iota(jnp.int32, s.shape, 0)
    return jnp.where((place >= low) & (place < high), s, LOWEST)


def head_lanes(v, g):
    return None if v is None else v[:, g * CHUNK : (g + 1) * CHUNK]


def each_tile(meta, p, lims, tile, halves):
    r, c = meta[0], meta[1]

    @pl.loop(meta[4 + p], p + 1)
    def _(k):
        own = (k == p) & (c == 0)
        slot = jnp.where(own, p ^ r, k ^ r ^ c)
        whole = (k < p) & (meta[12 + p] <= k * CHUNK)

        @pl.when(whole)
        def _():
            tile(slot, own, k * CHUNK, None, None, True)

        @pl.when(jnp.logical_not(whole))
        def _():
            tile(slot, own, k * CHUNK, lims[0], lims[1], False)

    @pl.when(c != 0)
    def _():
        halves(p ^ r, p * CHUNK, lims[2], lims[3])


HALF_CHUNK = CHUNK // 2


def half_lanes(v, half):
    return jnp.concatenate([v[:, half_span(g, half)] for g in range(GROUP)], axis=1)


def half_span(g, half):
    first = g * CHUNK + half * HALF_CHUNK
    return slice(first, first + HALF_CHUNK)


def stack_heads(q, stacked):
    for g in range(GROUP):
        stacked[g * HEAD_DIM : (g + 1) * HEAD_DIM, g * CHUNK : (g + 1) * CHUNK] = q[
            g * HEAD_DIM : (g + 1) * HEAD_DIM
        ]


def attend_body(load, meta, bounds, *refs):
    heads = refs[:5]
    send, o_ref, ml_ref, qs, kv, kr, stacked, m_s, l_s, acc = refs[5:]
    load(head_pairs(heads, qs, kv))
    stacked[...] = jnp.zeros_like(stacked)

    @pl.loop(0, 8)
    def _(s):
        for own in range(2):
            kr[own, s] = flip(kv[own, s, :WIDE])

    r, c = meta[0], meta[1]

    @pl.loop(0, 8)
    def _(p):
        s = p ^ r
        stack_heads(qs[s] * 0.125, stacked)
        lims = [thrice(bounds[p, i : i + 1]) for i in range(4)]

        def tile(slot, own, base, lo, hi, plain):
            keys = kr[c, slot]
            scores = [
                scores_of(keys, head_lanes(stacked, g), base, head_lanes(lo, g), head_lanes(hi, g), plain)
                for g in range(GROUP)
            ]
            for g in range(GROUP):
                cut = slice(g * CHUNK, (g + 1) * CHUNK)
                first = WIDE + g * HEAD_DIM
                m_old = m_s[:, cut]
                m_new = jnp.maximum(m_old, jnp.max(scores[g], axis=0, keepdims=True))
                e = jnp.exp(scores[g] - m_new)
                f = jnp.exp(m_old - m_new)
                m_s[:, cut] = m_new
                l_s[:, cut] = l_s[:, cut] * f + jnp.sum(e, axis=0, keepdims=True)
                acc[g] = acc[g] * f + mm(kv[c, slot, first : first + HEAD_DIM], e.astype(BF))

        def halves(slot, base, lo, hi):
            for half in range(2):
                keys = slice(half * HALF_CHUNK, (half + 1) * HALF_CHUNK)
                masked = scores_of(
                    kr[0, slot, keys], half_lanes(stacked[...], half), base + half * HALF_CHUNK,
                    half_lanes(lo, half), half_lanes(hi, half), False,
                )
                m_old = half_lanes(m_s[...], half)
                m_new = jnp.maximum(m_old, jnp.max(masked, axis=0, keepdims=True))
                e = jnp.exp(masked - m_new)
                f = jnp.exp(m_old - m_new)
                total = half_lanes(l_s[...], half) * f + jnp.sum(e, axis=0, keepdims=True)
                e = e.astype(BF)
                for g in range(GROUP):
                    cut = slice(g * HALF_CHUNK, (g + 1) * HALF_CHUNK)
                    first = WIDE + g * HEAD_DIM
                    m_s[:, half_span(g, half)] = m_new[:, cut]
                    l_s[:, half_span(g, half)] = total[:, cut]
                    new = mm(kv[0, slot, first : first + HEAD_DIM, keys], e[:, cut])
                    acc[g, :, keys] = acc[g, :, keys] * f[:, cut] + new

        m_s[...] = jnp.full_like(m_s, LOWEST)
        l_s[...] = jnp.zeros_like(l_s)
        acc[...] = jnp.zeros_like(acc)
        each_tile(meta, p, lims, tile, halves)
        total = l_s[...]
        inv = 1.0 / total
        out = jnp.concatenate(
            [acc[g] * inv[:, g * CHUNK : (g + 1) * CHUNK] for g in range(GROUP)], axis=0
        )
        o_ref[s] = out
        ml_ref[s, 0:1] = m_s[...]
        ml_ref[s, 1:2] = total
        send[p] = out.astype(BF)


HEAD_SCRATCH = [pltpu.VMEM((8, WIDE, CHUNK), BF), pltpu.VMEM((2, 8, 2 * WIDE, CHUNK), BF)]


def attend_rows(meta, bounds, heads):
    return call(
        attend_body,
        [((8, WIDE, CHUNK), BF), ((8, WIDE, CHUNK), F32), ((8, 8, LANES), F32)],
        "SV" + "A" * 5,
        (meta, bounds, *heads),
        scratch=HEAD_SCRATCH
        + [
            pltpu.VMEM((2, 8, CHUNK, WIDE), BF),
            pltpu.VMEM((WIDE, LANES), BF),
            pltpu.VMEM((1, LANES), F32),
            pltpu.VMEM((1, LANES), F32),
            pltpu.VMEM((GROUP, HEAD_DIM, CHUNK), F32),
        ],
        flops=20 * 2 * 2 * CHUNK * LANES * 256,
        moved=8 * CHUNK * WIDE * 16,
    )


def rows_body(load, *refs):
    kv, (k_rows, v_rows) = refs[:4], refs[4:]
    load([])
    for i in range(4):

        @pl.loop(0, 4)
        def _(s):
            k_rows[i // 2, i % 2 * 4 + s] = flip(kv[i][s, :WIDE])
            v_rows[i // 2, i % 2 * 4 + s] = flip(kv[i][s, WIDE:])


def rows_of_heads(heads):
    return call(rows_body, [((2, 8, CHUNK, WIDE), BF)] * 2, "VVVV", heads[1:], flops=1)


def attend_back_body(load, meta, bounds, cos, sin, o_ref, ml_ref, *refs):
    heads, k_rows, v_rows, gs = refs[:5], refs[5], refs[6], refs[7]
    (
        pq_ref, own_ref, far_a, far_b,
        qs, kv, kr, vr, st_q, st_g, row_q, row_g, dk, dv, dq,
    ) = refs[8:]
    for ref in (st_q, st_g, dk, dv):
        ref[...] = jnp.zeros_like(ref)
    load(head_pairs(heads, qs, kv) + [(k_rows, kr), (v_rows, vr)])
    r, c = meta[0], meta[1]
    lane = lax.broadcasted_iota(jnp.int32, (CHUNK, WIDE), 1) // HEAD_DIM

    @pl.loop(0, 8)
    def _(p):
        s = p ^ r
        q = qs[s] * 0.125
        stack_heads(q, st_q)
        total = ml_ref[s, 1:2]
        top = ml_ref[s, 0:1]
        g_in = gs[p].astype(F32)
        attended = o_ref[s]
        scaled, fix = [], []
        for g in range(GROUP):
            part = slice(g * HEAD_DIM, (g + 1) * HEAD_DIM)
            inv = 1.0 / total[:, g * CHUNK : (g + 1) * CHUNK]
            scaled.append(g_in[part] * inv)
            fix.append(jnp.sum(g_in[part] * attended[part], axis=0, keepdims=True) * inv)
        scaled = jnp.concatenate(scaled, axis=0)
        fix = jnp.concatenate(fix, axis=1)
        stack_heads(scaled.astype(BF), st_g)
        q_rows = jnp.transpose(q.astype(F32))
        g_rows = jnp.transpose(scaled)
        for g in range(GROUP):
            row_q[g * CHUNK : (g + 1) * CHUNK] = jnp.where(lane == g, q_rows, 0.0).astype(BF)
            row_g[g * CHUNK : (g + 1) * CHUNK] = jnp.where(lane == g, g_rows, 0.0).astype(BF)
        lims = [thrice(bounds[p, i : i + 1]) for i in range(4)]
        dq[...] = jnp.zeros_like(dq)

        def tile(slot, own, base, lo, hi, plain):
            e = jnp.exp(scores_of(kr[c, slot], st_q[...], base, lo, hi, plain) - top)
            d = (e * (mm(vr[c, slot], st_g[...]) - fix)).astype(BF)
            e = e.astype(BF)
            kind = jnp.where(own, 0, 1)
            dv[kind, slot] += mm(e, row_g[...])
            dk[kind, slot] += mm(d, row_q[...])
            for g in range(GROUP):
                part = slice(g * HEAD_DIM, (g + 1) * HEAD_DIM)
                dq[part] += mm(kv[c, slot, part], d[:, g * CHUNK : (g + 1) * CHUNK])

        def halves(slot, base, lo, hi):
            for half in range(2):
                keys = slice(half * HALF_CHUNK, (half + 1) * HALF_CHUNK)
                s_half = scores_of(
                    kr[0, slot, keys], half_lanes(st_q[...], half), base + half * HALF_CHUNK,
                    half_lanes(lo, half), half_lanes(hi, half), False,
                )
                e = jnp.exp(s_half - half_lanes(top, half))
                d = e * (mm(vr[0, slot, keys], half_lanes(st_g[...], half)) - half_lanes(fix, half))
                e, d = e.astype(BF), d.astype(BF)
                rows_of = [jnp.concatenate([ref[half_span(g, half)] for g in range(GROUP)]) for ref in (row_g, row_q)]
                dv[0, slot, keys] += mm(e, rows_of[0])
                dk[0, slot, keys] += mm(d, rows_of[1])
                for g in range(GROUP):
                    part = slice(g * HEAD_DIM, (g + 1) * HEAD_DIM)
                    cut = slice(g * HALF_CHUNK, (g + 1) * HALF_CHUNK)
                    dq[part, keys] += mm(kv[0, slot, part, keys], d[:, cut])

        each_tile(meta, p, lims, tile, halves)
        pq_ref[s] = turn_heads(dq[...] * 0.125, cos[s], -sin[s]).astype(BF)

    both = 1.0 - c.astype(F32)

    @pl.loop(0, 8)
    def _(s):
        far_k, far_v = jnp.transpose(dk[1, s]), jnp.transpose(dv[1, s])
        for half, far_ref in enumerate((far_a, far_b)):

            @pl.when(s // 4 == half)
            def _():
                far_ref[s % 4, :WIDE] = far_k.astype(BF)
                far_ref[s % 4, WIDE:] = far_v.astype(BF)

        own_ref[s, :WIDE] = (jnp.transpose(dk[0, s]) + both * far_k).astype(BF)
        own_ref[s, WIDE:] = (jnp.transpose(dv[0, s]) + both * far_v).astype(BF)


def attend_back(meta, bounds, cos, sin, attended, stats, heads, rows_first, grads):
    rows = pltpu.VMEM((2, 8, CHUNK, WIDE), BF)
    sums = pltpu.VMEM((2, 8, CHUNK, WIDE), F32)
    return call(
        attend_back_body,
        [((8, WIDE, CHUNK), BF), ((8, 2 * WIDE, CHUNK), BF)] + [((4, 2 * WIDE, CHUNK), BF)] * 2,
        "SVVVVV" + "A" * 7 + "V",
        (meta, bounds, cos, sin, attended, stats, *heads, *rows_first, grads),
        scratch=HEAD_SCRATCH
        + [
            rows,
            rows,
            pltpu.VMEM((WIDE, LANES), BF),
            pltpu.VMEM((WIDE, LANES), BF),
            pltpu.VMEM((LANES, WIDE), BF),
            pltpu.VMEM((LANES, WIDE), BF),
        ]
        + [sums] * 2
        + [pltpu.VMEM((WIDE, CHUNK), F32)],
        flops=20 * 2 * 5 * CHUNK * LANES * 256,
        moved=8 * CHUNK * WIDE * 30,
    )


def share_pairs(meta, own, parts, dst, unit, skip):
    h, z = meta[2], meta[3]
    part = unit // 4
    pairs = [(own, dst.at[pl.ds(at16(z * unit), unit)])]
    for t in range(1, 4):
        zz = (z + 4 - t) & 3
        for k in range(4):
            to = at16(zz * unit + (h ^ k) * part)
            pairs.append((parts[k].at[t - 1, pl.ds(skip, part)], dst.at[pl.ds(to, part)]))
    return pairs


def middle_body(load, meta, gain, embed, x_ref, heads, own, *refs):
    mid_ref, n_ref, att_ref, w_ref = refs[4:]
    pairs = share_pairs(meta, own, refs[:4], w_ref, 192, 0)
    for d in range(8):
        pairs.append((heads.at[d], att_ref.at[d % 2, pl.ds(d // 2 * WIDE, WIDE)]))
    load(pairs)

    @pl.loop(0, 2)
    def _(stream):
        x, _ = unmark(x_ref[stream], embed[...])
        mid = x + mm(att_ref[stream], w_ref[...], 0, 0)
        hat, _ = norm_parts(mid)
        mid_ref[stream] = mid
        n_ref[pl.ds(pl.multiple_of(stream * CHUNK, CHUNK), CHUNK)] = (hat * gain[...]).astype(BF)


def middle_rows(meta, gain, embed, marked, heads, own, parts):
    dim = marked.shape[2]
    return call(
        middle_body,
        [((2, CHUNK, dim), F32), ((2 * CHUNK, dim), BF), ((2, dim, CHUNK), BF), ((dim, dim), BF)],
        "SVVV" + "A" * 6,
        (meta, gain, embed, marked, heads, own, *parts),
        flops=2 * 2 * CHUNK * dim * dim,
        moved=8 * CHUNK * dim * 2,
    )


def feed_body(load, meta, bias, n_own, n_far, g_own, g_far, up_own, down_own, *refs):
    shares, refs = refs[:4], refs[4:]
    (
        out_ref, outf_ref, ngf_ref, ng_ref, gb_ref, d_ref, u_ref,
        ns, gs, wu, wd, acts, slopes,
    ) = refs
    c, h, z = meta[1], meta[2], meta[3]
    rows = 2 * CHUNK
    part = bias.shape[1] // 4
    pairs = [
        (n_own, ns.at[pl.ds(0, rows)]),
        (n_far, ns.at[pl.ds(rows, rows)]),
        (g_own, gs.at[pl.ds(0, rows)]),
        (g_far, gs.at[pl.ds(rows, rows)]),
    ]
    pairs += share_pairs(meta, down_own.at[pl.ds(at16(c * part), part)], shares, wd, part, 48)
    for k in range(4):
        cols = pl.ds(pl.multiple_of(k * 2 * part + c * part, 128), part)
        pairs.append((up_own.at[:, cols], wu.at[pl.ds(at16(z * 192), 192), pl.ds(k * part, part)]))
    for t in range(1, 4):
        zz = (z + 4 - t) & 3
        for k in range(4):
            dst = pl.ds(at16(zz * 192 + (h ^ k) * 48), 48)
            for b in range(2):
                pairs.append(
                    (
                        shares[k].at[t - 1, pl.ds(144 + 48 * b, 48)],
                        wu.at[dst, pl.ds(2 * part * b, 2 * part)],
                    )
                )
    load(pairs)
    gb_ref[...] = jnp.zeros_like(gb_ref)

    @pl.loop(0, 4)
    def _(i):
        span = pl.ds(pl.multiple_of(i * CHUNK, CHUNK), CHUNK)
        v = mm(ns[span], wu[...]) + bias[...]
        square = v * v
        th = jnp.tanh(v * (GELU_SCALE + (GELU_SCALE * 0.044715) * square))
        half = 0.5 + 0.5 * th
        act = (v * half).astype(BF)
        slope = half + (v * half) * (1.0 - th) * (GELU_SCALE + (3.0 * 0.044715 * GELU_SCALE) * square)
        acts[span] = act
        ug = (slope * mm(gs[span], wd[...], 1, 1)).astype(BF)
        slopes[span] = ug
        gb_ref[...] += jnp.sum(ug.astype(F32), axis=0, keepdims=True)
        out = mm(act, wd[...]).astype(BF)
        ng = mm(ug, wu[...], 1, 1).astype(BF)
        to = pl.ds(pl.multiple_of((i & 1) * CHUNK, CHUNK), CHUNK)

        @pl.when(i < 2)
        def _():
            out_ref[to] = out
            ng_ref[to] = ng

        @pl.when(i >= 2)
        def _():
            outf_ref[to] = out
            ngf_ref[to] = ng

    @pl.loop(0, 4)
    def _(j):
        cols = pl.ds(pl.multiple_of(j * part, 128), part)
        gd = mm(acts[:, cols], gs[...], 0, 0).astype(BF)
        for b in range(4):
            d_ref[b, j ^ h] = gd[96 * b : 96 * (b + 1)]
        gu = mm(ns[...], slopes[:, cols], 0, 0)
        side = pl.ds(pl.multiple_of((j & 1) * part, 128), part)
        line = pl.ds(at16((j >> 1) * 48), 48)
        for b in range(16):
            first = 192 * (b // 4) + 24 * (b % 4)
            block = jnp.concatenate([gu[first : first + 24], gu[first + 96 : first + 120]])
            u_ref[(b // 4) ^ h, b % 4, line, side] = block.astype(BF)


def feed_rows(meta, bias, args):
    rows = 2 * CHUNK
    dim = args[0].shape[1]
    hid = bias.shape[1]
    return call(
        feed_body,
        [((rows, dim), BF)] * 4
        + [((1, hid), F32)]
        + [((4, 4, hid // 16, dim), BF)] * 2,
        "SV" + "A" * 10,
        (meta, bias, *args),
        scratch=[
            pltpu.VMEM((2 * rows, dim), BF),
            pltpu.VMEM((2 * rows, dim), BF),
            pltpu.VMEM((dim, hid), BF),
            pltpu.VMEM((hid, dim), BF),
            pltpu.VMEM((2 * rows, hid), BF),
            pltpu.VMEM((2 * rows, hid), BF),
        ],
        flops=6 * 2 * 2 * rows * dim * hid,
        moved=12 * dim * hid,
    )


def pack_body(load, meta, w_out, w_down, w_up, share):
    c, h = meta[1], meta[2]
    part = w_up.shape[1] // 8
    pairs = [
        (w_out.at[pl.ds(at16(48 * h), 48)], share.at[pl.ds(0, 48)]),
        (w_down.at[pl.ds(at16(part * c + 96 * h), 96)], share.at[pl.ds(48, 96)]),
    ]
    for k in range(4):
        cols = pl.ds(pl.multiple_of((2 * k + c) * part, 128), part)
        to = share.at[pl.ds(144 + 48 * (k // 2), 48), pl.ds(part * (k % 2), part)]
        pairs.append((w_up.at[pl.ds(at16(48 * h), 48), cols], to))
    load(pairs)


def pack_share(place, w_out, w_down, w_up):
    return call(pack_body, [((240, w_out.shape[1]), BF)], "SAAA", (place, w_out, w_down, w_up))[0]


def middle_back_body(
    load, meta, gain, b_down, mid_ref, ng_ref, out_ref, outf_ref, ngf_ref, g_ref, x_ref, w_ref,
    lay_ref, mg_ref, sum_ref, send,
):
    load([])
    sum_ref[...] = jnp.zeros_like(sum_ref)

    @pl.loop(0, 2)
    def _(stream):
        span = pl.ds(pl.multiple_of(stream * CHUNK, CHUNK), CHUNK)
        mid = mid_ref[stream]
        lay = mid + out_ref[span].astype(F32) + outf_ref[span].astype(F32) + b_down[...]
        lay_ref[stream] = lay.astype(BF)
        hat, scale = norm_parts(mid)
        ng = ng_ref[span].astype(F32) + ngf_ref[span].astype(F32)
        sum_ref[0:1] += jnp.sum(ng * hat, axis=0, keepdims=True)
        t = ng * gain[...]
        g = g_ref[stream].astype(F32)
        sum_ref[1:2] += jnp.sum(g, axis=0, keepdims=True)
        t_mean = jnp.mean(t, axis=-1, keepdims=True)
        t_hat = jnp.mean(t * hat, axis=-1, keepdims=True)
        mg = (g + scale * (t - t_mean - hat * t_hat)).astype(BF)
        mg_ref[stream] = mg
        flag = (x_ref[stream][:, :1].astype(F32) > 1e38) & (stream == 1)
        sum_ref[2:3] += jnp.sum(jnp.where(flag, mg.astype(F32), 0.0), axis=0, keepdims=True)
        for d in range(4):
            send[2 * d + stream] = mm(w_ref[d * WIDE : (d + 1) * WIDE], mg, 1, 1).astype(BF)


def middle_back(meta, gain, b_down, args):
    dim = gain.shape[1]
    return call(
        middle_back_body,
        [((2, CHUNK, dim), BF), ((2, CHUNK, dim), BF), ((8, dim), F32), ((8, WIDE, CHUNK), BF)],
        "S" + "V" * 10,
        (meta, gain, b_down, *args),
        flops=4 * CHUNK * dim * dim,
        moved=20 * CHUNK * dim,
    )


def by_z(grad, ref):
    for zz in range(4):
        for h in range(4):
            first = 192 * h + 24 * zz
            pair = jnp.concatenate([grad[first : first + 24], grad[first + 96 : first + 120]])
            ref[zz, 48 * h : 48 * (h + 1)] = pair.astype(BF)


def out_grad_body(load, meta, att_ref, mg_ref, up, *o_refs):
    load([(up.at[k], o_refs[k].at[:, pl.ds(0, 96)]) for k in range(4)])
    grad = mm(att_ref[0], mg_ref[0]) + mm(att_ref[1], mg_ref[1])
    for owner in range(4):
        blocks = []
        for b in range(4):
            first = 192 * owner + 24 * b
            blocks.append(jnp.concatenate([grad[first : first + 24], grad[first + 96 : first + 120]]).astype(BF))
        for k in range(4):

            @pl.when((owner ^ meta[2]) == k)
            def _():
                for b in range(4):
                    o_refs[k][b, 96:] = blocks[b]


def project_back_body(
    own, f0, f1, pq, n_ref, mk_ref, cos, sin, w_ref, flat,
    away_x, away_y, stay, gq_ref, wp, acc, gs_ref, sums,
):
    i = pl.program_id(0)

    @pl.when(i == 0)
    def _():
        for part in range(3):
            wp[part] = w_ref[:, part * WIDE : (part + 1) * WIDE]
        acc[...] = jnp.zeros_like(acc)
        gs_ref[...] = jnp.zeros_like(gs_ref)

    early = (i == 0) | (i == 4) | (i == 6) | (i == 7)
    far = jnp.where(early, f0[0], f1[0])
    kv = own[0].astype(F32) + far.astype(F32)
    parts = [
        pq[0],
        turn_heads(kv[:WIDE], cos[0], -sin[0]).astype(BF),
        kv[WIDE:].astype(BF),
    ]
    n, mk = n_ref[0], mk_ref[0]
    ng = jnp.zeros((CHUNK, n.shape[1]), F32)
    for k in range(3):
        ng += mm(flip(parts[k]), wp[k], 1, 1)
        acc[k * WIDE : (k + 1) * WIDE] += mm(parts[k], n)
    low = ng.astype(BF)

    @pl.when(i < 2)
    def _():
        away_x[0] = low

    @pl.when((i >= 2) & (i < 4))
    def _():
        away_y[0] = low

    @pl.when(i >= 4)
    def _():
        stay[0] = ng

    gs_ref[0:1] += jnp.sum(ng * n.astype(F32), axis=0, keepdims=True)
    gs_ref[1:2] += jnp.sum(ng * mk[:, :1].astype(F32), axis=0, keepdims=True)

    @pl.when(i == 7)
    def _():
        by_z(jnp.transpose(acc[...]), gq_ref)
        part = sums.shape[1]
        sums[...] = flat[...]
        for k in range(2):
            for side in range(2):
                to = 14 + 2 * k + side
                sums[to : to + 1] = gs_ref[k : k + 1, side * part : (side + 1) * part]
        tail = sums[...].astype(BF)
        rows = gq_ref.shape[1] - 24
        for zz in range(4):
            gq_ref[zz, rows:] = jnp.zeros((24, gq_ref.shape[2]), BF)
            gq_ref[zz, rows:, :part] = tail


def pick(order):
    def slot_of(i):
        slot = jnp.int32(order[-1])
        for k in range(len(order) - 2, -1, -1):
            slot = jnp.where(i == k, order[k], slot)
        return slot

    return slot_of


def project_back(own, far, pq, n, mk, cos, sin, w, flat):
    dim = n.shape[2]
    wide = w.shape[1] + HEAD_DIM
    slot = pick((2, 6, 5, 7, 0, 4, 1, 3))

    def block(rows, cols, index):
        return pl.BlockSpec((1, rows, cols), lambda i: (index(i), 0, 0))

    def whole(*shape):
        return pl.BlockSpec(shape, lambda i: tuple(0 for _ in shape))

    return pl.pallas_call(
        project_back_body,
        grid=(8,),
        out_shape=(
            jax.ShapeDtypeStruct((2, CHUNK, dim), BF),
            jax.ShapeDtypeStruct((2, CHUNK, dim), BF),
            jax.ShapeDtypeStruct((4, CHUNK, dim), F32),
            jax.ShapeDtypeStruct((4, dim // 4 + 24, wide), BF),
        ),
        in_specs=[
            block(2 * WIDE, CHUNK, slot),
            *[block(2 * WIDE, CHUNK, lambda i: slot(i) % 4)] * 2,
            block(WIDE, CHUNK, slot),
            block(CHUNK, dim, slot), block(CHUNK, 128, slot),
            block(HALF, CHUNK, slot), block(HALF, CHUNK, slot), whole(*w.shape), whole(*flat.shape),
        ],
        out_specs=(
            block(CHUNK, dim, lambda i: jnp.minimum(i, 1)),
            block(CHUNK, dim, lambda i: jnp.clip(i - 2, 0, 1)),
            block(CHUNK, dim, lambda i: jnp.clip(i - 4, 0, 3)),
            whole(4, dim // 4 + 24, wide),
        ),
        scratch_shapes=[
            pltpu.VMEM((3, dim, WIDE), BF),
            pltpu.VMEM((wide, dim), F32),
            pltpu.VMEM((8, dim), F32),
            pltpu.VMEM(flat.shape, F32),
        ],
        compiler_params=pltpu.CompilerParams(vmem_limit_bytes=56 * 2**20),
        cost_estimate=pl.CostEstimate(
            flops=1 + 4 * 8 * CHUNK * dim * 3 * WIDE // COST, bytes_accessed=1, transcendentals=0
        ),
    )(own, *far, pq, n, mk, cos, sin, w, flat)


def last_body(load, meta, gain, embed, x_ref, mg_ref, keep_ref, far_ref, o_ref):
    load([])

    @pl.loop(0, 2)
    def _(stream):
        ng = jnp.where(stream == meta[1], keep_ref[...], far_ref[...].astype(F32))
        x, flag = unmark(x_ref[stream], embed[...])
        hat, scale = norm_parts(x)
        t = ng * gain[...]
        t_mean = jnp.mean(t, axis=-1, keepdims=True)
        t_hat = jnp.mean(t * hat, axis=-1, keepdims=True)
        grad = mg_ref[stream].astype(F32) + scale * (t - t_mean - hat * t_hat)
        o_ref[stream] = jnp.where(flag, 0.0, grad).astype(BF)


def finish_body(load, meta, gain, embed, x_ref, up_own, up_far, *refs):
    gd_refs, (gq_ref, go_ref, gu_ref, gd_ref, bu_ref, rows_ref, sums) = refs[:4], refs[4:]
    load([])
    r, c, z = meta[0], meta[1], meta[3]
    own = 4 * r + z
    small = gq_ref.shape[0]
    for h in range(4):
        part = x_ref[2 * h, :small].astype(F32) + x_ref[2 * h + 1, :small].astype(F32)
        for k in range(3):
            first = k * 4 * WIDE + h * WIDE
            gq_ref[:, first : first + WIDE] = part[:, k * WIDE : (k + 1) * WIDE]
    total = add(gd_refs[0][...], gd_refs[1][...])
    gd_ref[...] = total + add(gd_refs[2][...], gd_refs[3][...])

    rows = up_own[...].astype(F32)
    mine = [jnp.where(c == 0, rows[48 * q : 48 * q + 24], rows[48 * q + 24 : 48 * q + 48]) for q in range(3)]
    go_ref[...] = mine[2] + up_far[2].astype(F32)
    part = gu_ref.shape[1] // 8
    for q in range(2):
        for side in range(2):
            lanes = slice(side * part, (side + 1) * part)
            for core, block in ((c, mine[q]), (1 - c, up_far[q].astype(F32))):
                first = pl.multiple_of((2 * (2 * q + side) + core) * part, 128)
                gu_ref[:, pl.ds(first, part)] = block[:, lanes]

    total = x_ref[0, small:, :part].astype(F32)
    for d in range(1, 8):
        total += x_ref[d, small:, :part].astype(F32)
    sums[...] = total

    def pair(i):
        return total[8 + 2 * i : 10 + 2 * i]

    def over(v):
        return jnp.sum(v, keepdims=True) * (1.0 / (2 * part))

    centered = embed[...] - over(embed[...])
    scale = lax.rsqrt(over(centered * centered) + EPSILON)
    hat = centered * scale
    t = pair(4) * gain[...]
    sums[12:14] = pair(2) + scale * (t - over(t) - hat * over(t * hat))
    sums[14:16] = pair(3) / gain[...]
    row = sums[pl.ds(own // 4, 1)]
    bu_ref[...] = pltpu.roll(row, (4 * 96 - own % 4 * 96) % part, 1)[:, :96]
    shift = (16 * 24 - own % 16 * 24) % part
    for i in range(4):
        row = sums[pl.ds(8 + 2 * i + own // 16, 1)]
        rows_ref[i : i + 1] = pltpu.roll(row, shift, 1)[:, :24]


def cut(v, index, size, axis=0):
    return lax.dynamic_slice_in_dim(v, index * size, size, axis)


def at(v, index, axis=0):
    return lax.dynamic_index_in_dim(v, index, axis, keepdims=False)


def after(value, *needed):
    return lax.optimization_barrier((value, *needed))[0]


def add(a, b):
    return a.astype(F32) + b.astype(F32)


def exchange(v):
    return lax.all_to_all(v, "ctx", 0, 0, tiled=True)


def exchange_chips(v):
    groups = [[i + core for i in range(0, 8, 2)] for core in range(2)]
    return lax.all_to_all(v, "ctx", 0, 0, axis_index_groups=groups, tiled=True)


def exchange_z(v):
    return lax.all_to_all(v, "fsdp", 0, 0, tiled=True)


def shards_by_heads(
    hidden,
    noise_mask,
    doc_lengths,
    w_qkv,
    w_out,
    w_up,
    b_up,
    w_down,
    b_down,
    gain_one,
    gain_two,
    mask_embed,
    out_grad,
):
    r = lax.axis_index("ctx")
    z = lax.axis_index("fsdp")
    c, h = r & 1, r >> 1
    dim = hidden.shape[3]
    hid = w_up.shape[1]
    part = hid // 8
    total = CHUNK * 8
    clean = c == 0

    share = pack_share(jnp.stack([r, c, h, z]).astype(jnp.int32), w_out, w_down, w_up)
    ff_t = lax.all_gather(share, "fsdp")
    hidden = after(hidden, share)

    noisy = jnp.where(noise_mask[0][:, None] == 1, jnp.asarray(jnp.inf, BF), hidden[0, 1])
    mine = jnp.where(clean, hidden[0, 0], noisy)
    other = swap(jnp.where(clean, noisy, hidden[0, 0]), 1)
    mine_x, mine_y = swap(mine, 2), swap(mine, 4)
    other_x, other_y = swap(other, 2), swap(other, 4)
    marked = jnp.stack([hidden[0, 0], noisy])

    lengths = doc_lengths[0]
    index = jnp.arange(lengths.shape[0])
    ends = jnp.sum(jnp.where(index[None, :] <= index[:, None], lengths[None, :], 0), axis=1)
    place = jnp.arange(total, dtype=jnp.int32)
    later = ends[None, :] > place[:, None]
    start = jnp.max(jnp.where(later, 0, ends[None, :]), axis=1)
    stop = jnp.min(jnp.where(later, ends[None, :], total), axis=1)
    block = place // BLOCK * BLOCK
    limit = jnp.minimum(block + BLOCK, stop)
    bounds = jnp.stack(
        [start, jnp.where(clean, limit, block), jnp.where(clean, start, jnp.maximum(start, block)), limit]
    )
    bounds = jnp.pad(bounds.reshape(4, 8, CHUNK).transpose(1, 0, 2), ((0, 0), (0, 4), (0, 0)))
    meta = jnp.concatenate(
        [jnp.stack([r, c, h, z]), start[::CHUNK] // CHUNK, start[CHUNK - 1 :: CHUNK]]
    ).astype(jnp.int32)
    slots = (jnp.arange(8) ^ r)[:, None] * CHUNK + jnp.arange(CHUNK)[None, :]
    frequency = jnp.exp(jnp.arange(HALF).astype(F32) * (-2.0 * math.log(10000.0) / HEAD_DIM))
    angles = slots.astype(F32)[:, None, :] * frequency[None, :, None]
    cos, sin = jnp.cos(angles), jnp.sin(angles)
    size = hid // 4 + dim
    w_qkv = after(w_qkv, other)
    small = jnp.concatenate([b_up, b_down, gain_one, gain_two, mask_embed])
    small = jnp.pad(small, (0, 16 * 3 * WIDE - size)).reshape(16, 3 * WIDE)
    own_qkv = jnp.concatenate([cut(w_qkv[:, k * dim : (k + 1) * dim], h, WIDE, 1) for k in range(3)], 1)
    quarter = dim // 4
    half = jnp.concatenate([cut(own_qkv, c, quarter // 2), small])
    half = jnp.broadcast_to(half, (4, *half.shape))
    near = exchange_z(half)
    mine_x, mine_y, other_x, other_y, cos, sin, bounds, meta = lax.optimization_barrier(
        (mine_x, mine_y, other_x, other_y, cos, sin, bounds, meta)
    )
    mine_d, other_d = swap(mine_x, 4), swap(other_y, 2)
    mine_d, other_d, near = lax.optimization_barrier((mine_d, other_d, near))
    far = swap(near, 1)
    small = near[:, quarter // 2 :].reshape(4, -1)[:, :size].astype(F32)
    bias = at(small[:, : hid // 4].reshape(4, 2, part), c, 1).reshape(1, 4 * part)
    b_down_all, gain_a, gain_b, embed = [
        small[:, hid // 4 + k * quarter : hid // 4 + (k + 1) * quarter].reshape(1, dim)
        for k in range(4)
    ]

    grads = out_grad[0]
    grad_rows = grads.reshape(2 * CHUNK, dim)

    ff_r = jnp.take(ff_t, (z - jnp.arange(1, 4)) % 4, axis=0)
    far, ff_r = lax.optimization_barrier((far, ff_r))
    shares = (ff_r, swap(ff_r, 2), swap(ff_r, 4), swap(ff_r, 6))
    rows = (mine, other, mine_x, other_x, mine_y, other_y, mine_d, other_d)
    q, *kv, normed_one, marks, w_all = project_rows(meta, gain_a, embed, cos, sin, rows, (near, far))
    give = [(i, i + 1) for i in range(0, 8, 2)]
    heads = (q, *kv, *[lax.ppermute(v, "ctx", give) for v in kv])
    send, attended, stats = attend_rows(meta, bounds, heads)
    send, *shares = lax.optimization_barrier((send, *shares))
    grad_far = swap(after(grad_rows, kv[0]), 1)
    heads_late = lax.optimization_barrier((*heads, send))[:5]
    rows_first = rows_of_heads(heads_late)
    got, *rows_first = lax.optimization_barrier((exchange(send), *rows_first))
    middle, normed, att, w_out_all = middle_rows(meta, gain_b, embed, marked, got, w_out, shares)
    out_own, out_far, ng_far, ng_own, gbu, gd, gu = feed_rows(
        meta, bias, (normed, swap(normed, 1), grad_rows, grad_far, w_up, w_down, *shares)
    )
    ng_far, out_far = swap(ng_far, 1), swap(out_far, 1)
    gd = lax.psum_scatter(gd.reshape(-1, dim), "fsdp", scatter_dimension=0, tiled=True)

    layer, mid_grad, sums, send = middle_back(
        meta, gain_b, b_down_all, (middle, ng_own, out_own, out_far, ng_far, grads, marked, w_out_all)
    )
    got = exchange(send)
    up_out = call(
        out_grad_body,
        [((4, part // 4 + dim // 16, dim), BF)] * 4,
        "SVVA",
        (meta, att, mid_grad, gu),
        flops=4 * CHUNK * dim * dim,
    )
    gbu = gbu.reshape(4, 1, part)
    gbu = jnp.where(clean, jnp.concatenate([gbu, 0 * gbu], 1), jnp.concatenate([0 * gbu, gbu], 1))
    flat = jnp.concatenate([gbu.reshape(8, part), sums[:3].reshape(6, part), jnp.zeros((10, part), F32)])
    got, flat, *up_out = lax.optimization_barrier((got, flat, *up_out))
    up_out = [up_out[0]] + [swap(up_out[k], 2 * k) for k in range(1, 4)]
    pq, own_kv, *far_kv = attend_back(meta, bounds, cos, sin, attended, stats, heads, rows_first, got)
    far_kv = [lax.ppermute(v, "ctx", [(b, a) for a, b in give]) for v in far_kv]

    *up_out, _ = lax.optimization_barrier((*up_out, pq))
    up_out = (add(up_out[0], up_out[1]) + add(up_out[2], up_out[3])).astype(BF).reshape(-1, dim)
    gd = after(gd, pq).reshape(4, part // 4, dim)
    *far_kv, up_out, gd = lax.optimization_barrier((*far_kv, up_out, gd))
    up_out = lax.psum_scatter(up_out, "fsdp", scatter_dimension=0, tiled=True)

    away_x, away_y, stay, gq = project_back(
        own_kv, far_kv, pq, normed_one, marks, cos, sin, w_all, flat
    )
    in_x, in_y = swap(away_x, 2), swap(away_y, 4)
    wide = gq.shape[2]
    rows = dim // 4
    gq = gq.reshape(-1, wide)
    gq = lax.psum_scatter(gq, "fsdp", scatter_dimension=0, tiled=True)
    over_y, over_x = add(stay[1], in_x[1]).astype(BF), add(stay[3], in_y[1]).astype(BF)
    near_one, near_two = swap(over_y, 4), swap(over_x, 2)
    gd = after(gd, over_y, over_x)
    gd = [gd[0]] + [swap(gd[k], 2 * k) for k in range(1, 4)]
    gq = after(gq, over_y, over_x)
    flat = jnp.broadcast_to(gq[rows:], (8, 24, wide))
    gq = jnp.concatenate([gq[:rows].reshape(8, dim // 32, wide), flat], 1)
    near_one, near_two, gq = lax.optimization_barrier((near_one, near_two, gq))
    gq = exchange(gq)
    keep = add(stay[0], in_x[0]) + near_one.astype(F32)
    pair = (add(stay[2], in_y[0]) + near_two.astype(F32)).astype(BF)
    pair = swap(pair, 1)
    *gd, gq = lax.optimization_barrier((*gd, gq, keep, pair))[:5]
    (input_grad,) = call(
        last_body,
        [((2, CHUNK, dim), BF)],
        "S" + "V" * 6,
        (meta, gain_a, embed, marked, mid_grad, keep, pair),
        moved=10 * CHUNK * dim,
    )

    up_sum = after(up_out, input_grad)
    up_out = up_sum.reshape(3, 2, dim // 32, dim)
    up_far = swap(at(up_out, 1 - c, 1), 1)
    small = dim // 32
    gq, go, gu, gd, gbu, rows = call(
        finish_body,
        [
            ((small, 3 * dim), F32),
            ((small, dim), F32),
            ((small, hid), F32),
            ((part // 4, dim), F32),
            ((1, hid // 32), F32),
            ((4, small), F32),
        ],
        "S" + "V" * 9,
        (meta, gain_a.reshape(2, part), embed.reshape(2, part), gq, up_sum, up_far, *gd),
        scratch=[pltpu.VMEM((24, part), F32)],
        moved=8 * dim * dim,
    )
    return (
        layer[None],
        input_grad[None],
        gq,
        go,
        gu,
        gbu[0],
        gd,
        rows[1],
        rows[3],
        rows[0],
        rows[2],
    )


def solution(mesh):
    plain = (mesh.shape["ctx"], mesh.shape["fsdp"]) != (8, 4)
    placed = (
        P("fsdp", None, "ctx", None),
        P("fsdp", "ctx"),
        P("fsdp", None),
        P("fsdp", None),
        P("fsdp", None),
        P("fsdp", None),
        P("fsdp"),
        P("fsdp", None),
        P("fsdp"),
        P("fsdp"),
        P("fsdp"),
        P("fsdp"),
        P("fsdp", None, "ctx", None),
    )
    return jax.shard_map(
        shards if plain else shards_by_heads,
        mesh=mesh,
        in_specs=placed,
        out_specs=(
            P("fsdp", None, "ctx", None),
            P("fsdp", None, "ctx", None),
            P(("ctx", "fsdp"), None),
            P(("ctx", "fsdp"), None),
            P(("ctx", "fsdp"), None),
            P(("ctx", "fsdp")),
            P(("ctx", "fsdp"), None),
            P(("ctx", "fsdp")),
            P(("ctx", "fsdp")),
            P(("ctx", "fsdp")),
            P(("ctx", "fsdp")),
        ),
        check_vma=False,
    )
```

```python
import functools
import math

import jax
import jax.numpy as jnp
from jax import lax
from jax.experimental import pallas as pl
from jax.experimental.pallas import tpu as pltpu
from jax.sharding import PartitionSpec as P

HEADS = 12
HEAD_DIM = 64
BLOCK = 16


LOWEST = -1e30
EPSILON = 1e-05


def layer_norm(inputs, gain):
    average = jnp.mean(inputs, axis=-1, keepdims=True)
    centered = inputs - average
    variance = jnp.mean(centered * centered, axis=-1, keepdims=True)
    return centered * lax.rsqrt(variance + EPSILON) * gain


def rotary_angles(positions):
    half_dim = HEAD_DIM // 2
    frequency = jnp.exp(
        jnp.arange(half_dim).astype(jnp.float32) * (-2.0 * math.log(10000.0) / HEAD_DIM)
    )
    return positions.astype(jnp.float32)[:, None] * frequency[None, :]


def rotate(heads_in, angles):
    half_dim = heads_in.shape[-1] // 2
    cosine = jnp.cos(angles)[:, None, :]
    sine_part = jnp.sin(angles)[:, None, :]
    first_half = heads_in[..., :half_dim]
    second_half = heads_in[..., half_dim:]
    return jnp.concatenate(
        [
            first_half * cosine - second_half * sine_part,
            second_half * cosine + first_half * sine_part,
        ],
        axis=-1,
    )


def segment_of(positions, doc_ends):
    return jnp.sum((positions[:, None] >= doc_ends[None, :]).astype(jnp.int32), axis=1)


def visible(query_stream, query_position, query_segment, key_stream, key_position, key_segment):
    query_block = query_position // BLOCK
    key_block = key_position // BLOCK
    same_doc = query_segment[:, None] == key_segment[None, :]
    clean_key = key_stream[None, :] == 0
    noisy_query = query_stream[:, None] == 1
    before = key_block[None, :] < query_block[:, None]
    same_block = key_block[None, :] == query_block[:, None]
    from_clean = clean_key & (before | same_block & jnp.logical_not(noisy_query))
    from_noisy = jnp.logical_not(clean_key) & noisy_query & same_block
    return same_doc & (from_clean | from_noisy)


def mix_tile(running, query_rows, key_tile, value_tile, allowed):
    run_max, run_sum, accum = running
    scores = (
        jnp.einsum("qhd,khd->hqk", query_rows, key_tile, preferred_element_type=jnp.float32) * 0.125
    )
    masked = jnp.where(allowed[None], scores, LOWEST)
    new_max = jnp.maximum(run_max, jnp.max(masked, axis=-1))
    exp_terms = jnp.where(allowed[None], jnp.exp(masked - new_max[..., None]), 0.0)
    factor = jnp.exp(run_max - new_max)
    new_sum = run_sum * factor + jnp.sum(exp_terms, axis=-1)
    accum = accum * factor[..., None] + jnp.einsum(
        "hqk,khd->hqd",
        exp_terms.astype(jnp.bfloat16),
        value_tile,
        preferred_element_type=jnp.float32,
    )
    return (new_max, new_sum, accum)


def tile_grads(query_rows, key_tile, value_tile, allowed, row_max, scaled_grad, correction):
    scores = (
        jnp.einsum("qhd,khd->hqk", query_rows, key_tile, preferred_element_type=jnp.float32) * 0.125
    )
    masked = jnp.where(allowed[None], scores, LOWEST)
    exp_terms = jnp.where(allowed[None], jnp.exp(masked - row_max[..., None]), 0.0)
    prob_grad = jnp.einsum(
        "hqd,khd->hqk", scaled_grad, value_tile, preferred_element_type=jnp.float32
    )
    score_grad = (exp_terms * (prob_grad - correction[..., None])).astype(jnp.bfloat16)
    query_part = jnp.einsum(
        "hqk,khd->qhd", score_grad, key_tile, preferred_element_type=jnp.float32
    )
    key_part = jnp.einsum(
        "hqk,qhd->khd", score_grad, query_rows, preferred_element_type=jnp.float32
    )
    value_part = jnp.einsum(
        "hqk,hqd->khd",
        exp_terms.astype(jnp.bfloat16),
        scaled_grad,
        preferred_element_type=jnp.float32,
    )
    return (query_part, key_part, value_part)


def build_inputs(hidden, noise_row, mask_row):
    clean_rows = hidden[0, 0].astype(jnp.float32)
    noisy_rows = jnp.where(
        noise_row[:, None] == 1,
        mask_row.astype(jnp.float32)[None, :],
        hidden[0, 1].astype(jnp.float32),
    )
    return jnp.concatenate([clean_rows, noisy_rows], axis=0)


def project(inputs, gathered, angles):
    row_count = inputs.shape[0]
    model_dim = inputs.shape[1]
    normed = layer_norm(inputs, gathered[6].astype(jnp.float32)).astype(jnp.bfloat16)
    projected = jnp.dot(normed, gathered[0], preferred_element_type=jnp.float32)
    query_rows = rotate(
        projected[:, :model_dim].reshape(row_count, HEADS, HEAD_DIM), angles
    ).astype(jnp.bfloat16)
    key_rows = rotate(
        projected[:, model_dim : 2 * model_dim].reshape(row_count, HEADS, HEAD_DIM), angles
    ).astype(jnp.bfloat16)
    value_rows = (
        projected[:, 2 * model_dim :].reshape(row_count, HEADS, HEAD_DIM).astype(jnp.bfloat16)
    )
    return (normed, query_rows, key_rows, value_rows)


def upper_half(inputs, attended_low, gathered):
    middle = inputs + jnp.dot(attended_low, gathered[1], preferred_element_type=jnp.float32)
    normed_two = layer_norm(middle, gathered[7].astype(jnp.float32)).astype(jnp.bfloat16)
    upper = jnp.dot(normed_two, gathered[2], preferred_element_type=jnp.float32) + gathered[
        3
    ].astype(jnp.float32)
    activated = jax.nn.gelu(upper, approximate=True).astype(jnp.bfloat16)
    return (middle, normed_two, upper, activated)


def shards(
    hidden,
    noise_mask,
    doc_lengths,
    w_qkv,
    w_out,
    w_up,
    b_up,
    w_down,
    b_down,
    gain_one,
    gain_two,
    mask_embed,
    out_grad,
):
    own_params = (w_qkv, w_out, w_up, b_up, w_down, b_down, gain_one, gain_two, mask_embed)
    local_count = hidden.shape[2]
    model_dim = hidden.shape[3]
    row_count = 2 * local_count
    ctx_index = lax.axis_index("ctx")
    offset = ctx_index * local_count
    local_place = offset + jnp.arange(local_count, dtype=jnp.int32)
    positions = jnp.concatenate([local_place, local_place])
    stream = jnp.concatenate(
        [jnp.zeros((local_count,), jnp.int32), jnp.ones((local_count,), jnp.int32)]
    )
    doc_ends = jnp.cumsum(doc_lengths[0])
    segments = segment_of(positions, doc_ends)
    angles = rotary_angles(positions)
    noise_row = noise_mask[0]
    noisy_stream = stream[local_count:]
    noisy_allowed = visible(
        stream, positions, segments, noisy_stream, positions[local_count:], segments[local_count:]
    )
    gathered = (
        lax.all_gather(own_params[0], "fsdp", axis=0, tiled=True),
        lax.all_gather(own_params[1], "fsdp", axis=0, tiled=True),
        lax.all_gather(own_params[2], "fsdp", axis=0, tiled=True),
        lax.all_gather(own_params[3], "fsdp", axis=0, tiled=True),
        lax.all_gather(own_params[4], "fsdp", axis=0, tiled=True),
        lax.all_gather(own_params[5], "fsdp", axis=0, tiled=True),
        lax.all_gather(own_params[6], "fsdp", axis=0, tiled=True),
        lax.all_gather(own_params[7], "fsdp", axis=0, tiled=True),
        lax.all_gather(own_params[8], "fsdp", axis=0, tiled=True),
    )
    inputs = build_inputs(hidden, noise_row, gathered[8])
    normed, query_rows, key_rows, value_rows = project(inputs, gathered, angles)
    clean_keys = key_rows[:local_count].reshape(local_count, model_dim)
    clean_values = value_rows[:local_count].reshape(local_count, model_dim)
    start_state = (
        jnp.full((HEADS, row_count), LOWEST, jnp.float32),
        jnp.zeros((HEADS, row_count), jnp.float32),
        jnp.zeros((HEADS, row_count, HEAD_DIM), jnp.float32),
    )
    running = start_state
    piece_keys = lax.all_gather(clean_keys, "ctx", axis=0, tiled=True)
    piece_values = lax.all_gather(clean_values, "ctx", axis=0, tiled=True)
    piece_rows = piece_keys.shape[0]
    fold_tile_size = math.gcd(piece_rows, 512)

    def step(carried, tile_index):
        tile_start = tile_index * fold_tile_size
        key_tile = lax.dynamic_slice_in_dim(piece_keys, tile_start, fold_tile_size, 0).reshape(
            fold_tile_size, HEADS, HEAD_DIM
        )
        value_tile = lax.dynamic_slice_in_dim(piece_values, tile_start, fold_tile_size, 0).reshape(
            fold_tile_size, HEADS, HEAD_DIM
        )
        key_position = tile_start + jnp.arange(fold_tile_size, dtype=jnp.int32)
        allowed = visible(
            stream,
            positions,
            segments,
            jnp.zeros((fold_tile_size,), jnp.int32),
            key_position,
            segment_of(key_position, doc_ends),
        )
        carried = lax.cond(
            jnp.any(allowed),
            lambda held: mix_tile(held, query_rows, key_tile, value_tile, allowed),
            lambda held: held,
            carried,
        )
        return (carried, None)

    running, _ = lax.scan(step, running, jnp.arange(piece_rows // fold_tile_size))
    run_max, run_sum, accum = mix_tile(
        running, query_rows, key_rows[local_count:], value_rows[local_count:], noisy_allowed
    )
    attended = accum / run_sum[..., None]
    attended_low = (
        jnp.transpose(attended, (1, 0, 2)).reshape(row_count, model_dim).astype(jnp.bfloat16)
    )
    middle, normed_two, upper, activated = upper_half(inputs, attended_low, gathered)
    result = (
        middle
        + jnp.dot(activated, gathered[4], preferred_element_type=jnp.float32)
        + gathered[5].astype(jnp.float32)
    )
    layer_out = result.astype(jnp.bfloat16).reshape(1, 2, local_count, model_dim)
    again = (
        lax.all_gather(own_params[0], "fsdp", axis=0, tiled=True),
        lax.all_gather(own_params[1], "fsdp", axis=0, tiled=True),
        lax.all_gather(own_params[2], "fsdp", axis=0, tiled=True),
        lax.all_gather(own_params[3], "fsdp", axis=0, tiled=True),
        lax.all_gather(own_params[4], "fsdp", axis=0, tiled=True),
        lax.all_gather(own_params[5], "fsdp", axis=0, tiled=True),
        lax.all_gather(own_params[6], "fsdp", axis=0, tiled=True),
        lax.all_gather(own_params[7], "fsdp", axis=0, tiled=True),
        lax.all_gather(own_params[8], "fsdp", axis=0, tiled=True),
    )
    normed, query_rows, key_rows, value_rows = project(inputs, again, angles)
    noisy_keys = key_rows[local_count:]
    noisy_values = value_rows[local_count:]
    middle, normed_two, upper, activated = upper_half(inputs, attended_low, again)
    grad_rows = out_grad[0].reshape(row_count, model_dim)
    grad_float = grad_rows.astype(jnp.float32)
    grad_down = jnp.einsum("qi,qj->ij", activated, grad_rows, preferred_element_type=jnp.float32)
    grad_down_bias = jnp.sum(grad_float, axis=0)
    activated_grad = jnp.einsum(
        "qj,ij->qi", grad_rows, again[4], preferred_element_type=jnp.float32
    )
    _, gelu_pull = jax.vjp(lambda upper_in: jax.nn.gelu(upper_in, approximate=True), upper)
    upper_grad = gelu_pull(activated_grad)[0].astype(jnp.bfloat16)
    grad_up = jnp.einsum("qi,qj->ij", normed_two, upper_grad, preferred_element_type=jnp.float32)
    grad_up_bias = jnp.sum(upper_grad.astype(jnp.float32), axis=0)
    normed_two_grad = jnp.einsum(
        "qj,ij->qi", upper_grad, again[2], preferred_element_type=jnp.float32
    )
    _, second_pull = jax.vjp(layer_norm, middle, again[7].astype(jnp.float32))
    middle_norm_grad, grad_gain_two = second_pull(normed_two_grad)
    middle_grad = (grad_float + middle_norm_grad).astype(jnp.bfloat16)
    grad_out_proj = jnp.einsum(
        "qi,qj->ij", attended_low, middle_grad, preferred_element_type=jnp.float32
    )
    attended_grad = jnp.einsum(
        "qj,ij->qi", middle_grad, again[1], preferred_element_type=jnp.float32
    )
    attended_grad = jnp.transpose(attended_grad.reshape(row_count, HEADS, HEAD_DIM), (1, 0, 2))
    scaled_grad = (attended_grad / run_sum[..., None]).astype(jnp.bfloat16)
    correction = jnp.sum(attended_grad * attended, axis=-1) / run_sum
    pair_rows = (
        lax.all_gather(
            key_rows[:local_count].reshape(local_count, model_dim), "ctx", axis=0, tiled=True
        ),
        lax.all_gather(
            value_rows[:local_count].reshape(local_count, model_dim), "ctx", axis=0, tiled=True
        ),
    )
    pair_keys, pair_values = pair_rows
    total_rows = pair_keys.shape[0]
    tile_size = math.gcd(total_rows, 512)
    zero_tile = jnp.zeros((tile_size, HEADS, HEAD_DIM), jnp.float32)

    def back_step(query_acc, tile_index):
        tile_start = tile_index * tile_size
        key_tile = lax.dynamic_slice_in_dim(pair_keys, tile_start, tile_size, 0).reshape(
            tile_size, HEADS, HEAD_DIM
        )
        value_tile = lax.dynamic_slice_in_dim(pair_values, tile_start, tile_size, 0).reshape(
            tile_size, HEADS, HEAD_DIM
        )
        key_position = tile_start + jnp.arange(tile_size, dtype=jnp.int32)
        allowed = visible(
            stream,
            positions,
            segments,
            jnp.zeros((tile_size,), jnp.int32),
            key_position,
            segment_of(key_position, doc_ends),
        )

        def live_tile(held):
            query_part, key_part, value_part = tile_grads(
                query_rows, key_tile, value_tile, allowed, run_max, scaled_grad, correction
            )
            return (held + query_part, key_part, value_part)

        query_acc, key_part, value_part = lax.cond(
            jnp.any(allowed), live_tile, lambda held: (held, zero_tile, zero_tile), query_acc
        )
        return (
            query_acc,
            (key_part.reshape(tile_size, model_dim), value_part.reshape(tile_size, model_dim)),
        )

    query_acc, (key_terms, value_terms) = lax.scan(
        back_step,
        jnp.zeros((row_count, HEADS, HEAD_DIM), jnp.float32),
        jnp.arange(total_rows // tile_size),
    )
    key_terms = key_terms.reshape(total_rows, model_dim)
    value_terms = value_terms.reshape(total_rows, model_dim)
    clean_key_grad, clean_value_grad = (
        lax.psum_scatter(
            key_terms.astype(jnp.bfloat16), "ctx", scatter_dimension=0, tiled=True
        ).astype(jnp.float32),
        lax.psum_scatter(
            value_terms.astype(jnp.bfloat16), "ctx", scatter_dimension=0, tiled=True
        ).astype(jnp.float32),
    )
    query_part, noisy_key_part, noisy_value_part = tile_grads(
        query_rows, noisy_keys, noisy_values, noisy_allowed, run_max, scaled_grad, correction
    )
    query_grad = (query_acc + query_part) * 0.125
    key_grad = (
        jnp.concatenate(
            [clean_key_grad.reshape(local_count, HEADS, HEAD_DIM), noisy_key_part], axis=0
        )
        * 0.125
    )
    value_grad = jnp.concatenate(
        [clean_value_grad.reshape(local_count, HEADS, HEAD_DIM), noisy_value_part], axis=0
    )
    _, rotate_pull = jax.vjp(lambda heads_in: rotate(heads_in, angles), query_grad)
    query_raw_grad = rotate_pull(query_grad)[0]
    key_raw_grad = rotate_pull(key_grad)[0]
    projected_grad = jnp.concatenate(
        [
            query_raw_grad.reshape(row_count, model_dim),
            key_raw_grad.reshape(row_count, model_dim),
            value_grad.reshape(row_count, model_dim),
        ],
        axis=1,
    ).astype(jnp.bfloat16)
    grad_qkv = jnp.einsum("qi,qj->ij", normed, projected_grad, preferred_element_type=jnp.float32)
    normed_grad = jnp.einsum(
        "qj,ij->qi", projected_grad, again[0], preferred_element_type=jnp.float32
    )
    _, first_pull = jax.vjp(layer_norm, inputs, again[6].astype(jnp.float32))
    inputs_norm_grad, grad_gain_one = first_pull(normed_grad)
    inputs_grad = middle_grad.astype(jnp.float32) + inputs_norm_grad
    noisy_flag = (noise_row == 1)[:, None]
    noisy_grad = inputs_grad[local_count:]
    grad_mask = jnp.sum(jnp.where(noisy_flag, noisy_grad, 0.0), axis=0)
    input_grad = jnp.concatenate(
        [inputs_grad[:local_count], jnp.where(noisy_flag, 0.0, noisy_grad)], axis=0
    )
    input_grad = input_grad.astype(jnp.bfloat16).reshape(1, 2, local_count, model_dim)
    shares = (
        lax.psum_scatter(grad_qkv, ("ctx", "fsdp"), scatter_dimension=0, tiled=True),
        lax.psum_scatter(grad_out_proj, ("ctx", "fsdp"), scatter_dimension=0, tiled=True),
        lax.psum_scatter(grad_up, ("ctx", "fsdp"), scatter_dimension=0, tiled=True),
        lax.psum_scatter(grad_up_bias, ("ctx", "fsdp"), scatter_dimension=0, tiled=True),
        lax.psum_scatter(grad_down, ("ctx", "fsdp"), scatter_dimension=0, tiled=True),
        lax.psum_scatter(grad_down_bias, ("ctx", "fsdp"), scatter_dimension=0, tiled=True),
        lax.psum_scatter(grad_gain_one, ("ctx", "fsdp"), scatter_dimension=0, tiled=True),
        lax.psum_scatter(grad_gain_two, ("ctx", "fsdp"), scatter_dimension=0, tiled=True),
        lax.psum_scatter(grad_mask, ("ctx", "fsdp"), scatter_dimension=0, tiled=True),
    )
    (
        qkv_share,
        out_share,
        up_share,
        up_bias_share,
        down_share,
        down_bias_share,
        gain_one_share,
        gain_two_share,
        mask_share,
    ) = shares
    return (
        layer_out,
        input_grad,
        qkv_share,
        out_share,
        up_share,
        up_bias_share,
        down_share,
        down_bias_share,
        gain_one_share,
        gain_two_share,
        mask_share,
    )


CHUNK = 256
COST = 10**9
GROUP = 3
WIDE = GROUP * HEAD_DIM
HALF = HEAD_DIM // 2
LANES = GROUP * CHUNK
BF = jnp.bfloat16
F32 = jnp.float32
HB = pl.BlockSpec(memory_space=pltpu.HBM)
SM = pl.BlockSpec(memory_space=pltpu.SMEM)
GELU_SCALE = math.sqrt(2.0 / math.pi)


def swap(v, bit):
    return lax.ppermute(v, "ctx", [(i, i ^ bit) for i in range(8)])


def turn(v, step):
    return lax.ppermute(v, "fsdp", [(i, (i + step) % 4) for i in range(4)])


def mm(a, b, ca=1, cb=0):
    return lax.dot_general(a, b, (((ca,), (cb,)), ((), ())), preferred_element_type=F32)


def flip(v):
    return jnp.transpose(v.astype(F32)).astype(v.dtype)


def call(body, outs, kinds, args, scratch=(), flops=0, moved=0, raw=()):
    staged = [i for i, kind in enumerate(kinds) if kind == "V"]
    space = {"S": SM, "V": HB, "A": HB}
    count = len(args)
    kept = [k for k in range(len(outs)) if k not in raw]
    made = len(kept)

    def run(*refs):
        ins, sinks, rest = list(refs[:count]), list(refs[count : count + len(outs)]), refs[count + len(outs) :]
        held, buffers = rest[: len(staged)], rest[len(staged) : len(staged) + made]
        results = list(sinks)
        for i, k in enumerate(kept):
            results[k] = buffers[i]
        sem_in, sem_out, sems = rest[len(staged) + made : len(staged) + made + 3]
        rest = rest[len(staged) + made + 3 :]
        first = [
            pltpu.make_async_copy(ins[i], held[k], sem_in.at[k]) for k, i in enumerate(staged)
        ]
        for copy in first:
            copy.start()
        for k, i in enumerate(staged):
            ins[i] = held[k]

        def load(pairs):
            more = [pltpu.make_async_copy(a, b, sems.at[i]) for i, (a, b) in enumerate(pairs)]
            for copy in more:
                copy.start()
            for copy in more + first:
                copy.wait()

        body(load, *ins, *results, *rest)
        last = [pltpu.make_async_copy(results[k], sinks[k], sem_out.at[i]) for i, k in enumerate(kept)]
        for copy in last:
            copy.start()
        for copy in last:
            copy.wait()

    return pl.pallas_call(
        run,
        out_shape=tuple(jax.ShapeDtypeStruct(s, d) for s, d in outs),
        in_specs=[space[kind] for kind in kinds],
        out_specs=tuple(HB for _ in outs),
        scratch_shapes=[pltpu.VMEM(args[i].shape, args[i].dtype) for i in staged]
        + [pltpu.VMEM(*outs[k]) for k in kept]
        + [
            pltpu.SemaphoreType.DMA((max(1, len(staged)),)),
            pltpu.SemaphoreType.DMA((made,)),
            pltpu.SemaphoreType.DMA((48,)),
        ]
        + list(scratch),
        compiler_params=pltpu.CompilerParams(vmem_limit_bytes=56 * 2**20),
        cost_estimate=pl.CostEstimate(flops=1 + flops // COST, bytes_accessed=1 + moved // COST, transcendentals=0),
    )(*args)


def at16(v):
    return pl.multiple_of(v, 16)


def shard_rows(meta, near, far, dst, unit):
    half = unit // 2
    pairs = []
    for zz in range(4):
        for core, part in ((meta[1], near), (1 - meta[1], far)):
            to = at16(zz * unit + core * half)
            pairs.append((part.at[zz, pl.ds(0, half)], dst.at[pl.ds(to, half)]))
    return pairs


def norm_parts(x):
    mean = jnp.mean(x, axis=-1, keepdims=True)
    centered = x - mean
    var = jnp.mean(centered * centered, axis=-1, keepdims=True)
    scale = lax.rsqrt(var + EPSILON)
    return centered * scale, scale


def unmark(x, embed):
    x = x.astype(F32)
    flag = x[:, :1] > 1e38
    return jnp.where(flag, embed, x), flag


def turn_heads(v, cos, sin):
    parts = []
    for g in range(GROUP):
        a = v[g * HEAD_DIM : g * HEAD_DIM + HALF]
        b = v[g * HEAD_DIM + HALF : (g + 1) * HEAD_DIM]
        parts += [a * cos - b * sin, b * cos + a * sin]
    return jnp.concatenate(parts, axis=0)


def project_body(load, meta, gain, embed, cos, sin, *refs):
    rows, refs = refs[:8], refs[8:]
    near, far, q_ref, kv_a, kv_b, n_out, mk_ref, w, xs, wp, n_ref, out_sems = refs
    load(shard_rows(meta, near, far, w, 192) + [(rows[i], xs.at[i]) for i in range(8)])
    for part in range(3):
        wp[part] = w[:, part * WIDE : (part + 1) * WIDE]

    @pl.loop(0, 8)
    def _(i):
        x, flag = unmark(xs[i], embed[...])
        hat, _ = norm_parts(x)
        n = (hat * gain[...]).astype(BF)
        n_ref[i] = n
        pltpu.make_async_copy(n_ref.at[i], n_out.at[i], out_sems.at[i]).start()
        mk_ref[i] = jnp.broadcast_to(jnp.where(flag, 1.0, 0.0), (CHUNK, 128)).astype(BF)
        q_ref[i] = turn_heads(jnp.transpose(mm(n, wp[0])), cos[i], sin[i]).astype(BF)
        keys = turn_heads(jnp.transpose(mm(n, wp[1])), cos[i], sin[i]).astype(BF)
        values = jnp.transpose(mm(n, wp[2])).astype(BF)
        for half, ref in enumerate((kv_a, kv_b)):

            @pl.when(i // 4 == half)
            def _():
                ref[i % 4, :WIDE] = keys
                ref[i % 4, WIDE:] = values

    for i in range(8):
        pltpu.make_async_copy(n_ref.at[i], n_out.at[i], out_sems.at[i]).wait()


def project_rows(meta, gain, embed, cos, sin, rows, weights):
    dim = rows[0].shape[1]
    wide = weights[0].shape[-1]
    return call(
        project_body,
        [
            ((8, WIDE, CHUNK), BF),
            ((4, 2 * WIDE, CHUNK), BF),
            ((4, 2 * WIDE, CHUNK), BF),
            ((8, CHUNK, dim), BF),
            ((8, CHUNK, 128), BF),
            ((dim, wide), BF),
        ],
        "SVVVV" + "A" * 10,
        (meta, gain, embed, cos, sin, *rows, *weights),
        scratch=[
            pltpu.VMEM((8, CHUNK, dim), BF),
            pltpu.VMEM((3, dim, WIDE), BF),
            pltpu.VMEM((8, CHUNK, dim), BF),
            pltpu.SemaphoreType.DMA((8,)),
        ],
        raw=(3,),
        flops=2 * 8 * CHUNK * dim * 3 * WIDE,
        moved=8 * CHUNK * dim * 6,
    )


def head_pairs(refs, qs, kv):
    pairs = [(refs[0], qs)]
    for i, ref in enumerate(refs[1:]):
        pairs.append((ref, kv.at[i // 2, pl.ds(i % 2 * 4, 4)]))
    return pairs


def thrice(v):
    return jnp.concatenate([v, v, v], axis=1)


def scores_of(keys, stacked, base, low, high, plain):
    s = mm(keys, stacked)
    if plain:
        return s
    place = base + lax.broadcasted_iota(jnp.int32, s.shape, 0)
    return jnp.where((place >= low) & (place < high), s, LOWEST)


def head_lanes(v, g):
    return None if v is None else v[:, g * CHUNK : (g + 1) * CHUNK]


def each_tile(meta, p, lims, tile, halves):
    r, c = meta[0], meta[1]

    @pl.loop(meta[4 + p], p + 1)
    def _(k):
        own = (k == p) & (c == 0)
        slot = jnp.where(own, p ^ r, k ^ r ^ c)
        whole = (k < p) & (meta[12 + p] <= k * CHUNK)

        @pl.when(whole)
        def _():
            tile(slot, own, k * CHUNK, None, None, True)

        @pl.when(jnp.logical_not(whole))
        def _():
            tile(slot, own, k * CHUNK, lims[0], lims[1], False)

    @pl.when(c != 0)
    def _():
        halves(p ^ r, p * CHUNK, lims[2], lims[3])


HALF_CHUNK = CHUNK // 2


def half_lanes(v, half):
    return jnp.concatenate([v[:, half_span(g, half)] for g in range(GROUP)], axis=1)


def half_span(g, half):
    first = g * CHUNK + half * HALF_CHUNK
    return slice(first, first + HALF_CHUNK)


def stack_heads(q, stacked):
    for g in range(GROUP):
        stacked[g * HEAD_DIM : (g + 1) * HEAD_DIM, g * CHUNK : (g + 1) * CHUNK] = q[
            g * HEAD_DIM : (g + 1) * HEAD_DIM
        ]


def attend_body(load, meta, bounds, *refs):
    heads = refs[:5]
    send, o_ref, ml_ref, qs, kv, kr, stacked, m_s, l_s, acc = refs[5:]
    load(head_pairs(heads, qs, kv))
    stacked[...] = jnp.zeros_like(stacked)

    @pl.loop(0, 8)
    def _(s):
        for own in range(2):
            kr[own, s] = flip(kv[own, s, :WIDE])

    r, c = meta[0], meta[1]

    @pl.loop(0, 8)
    def _(p):
        s = p ^ r
        stack_heads(qs[s] * 0.125, stacked)
        lims = [thrice(bounds[p, i : i + 1]) for i in range(4)]

        def tile(slot, own, base, lo, hi, plain):
            keys = kr[c, slot]
            scores = [
                scores_of(keys, head_lanes(stacked, g), base, head_lanes(lo, g), head_lanes(hi, g), plain)
                for g in range(GROUP)
            ]
            for g in range(GROUP):
                cut = slice(g * CHUNK, (g + 1) * CHUNK)
                first = WIDE + g * HEAD_DIM
                m_old = m_s[:, cut]
                m_new = jnp.maximum(m_old, jnp.max(scores[g], axis=0, keepdims=True))
                e = jnp.exp(scores[g] - m_new)
                f = jnp.exp(m_old - m_new)
                m_s[:, cut] = m_new
                l_s[:, cut] = l_s[:, cut] * f + jnp.sum(e, axis=0, keepdims=True)
                acc[g] = acc[g] * f + mm(kv[c, slot, first : first + HEAD_DIM], e.astype(BF))

        def halves(slot, base, lo, hi):
            for half in range(2):
                keys = slice(half * HALF_CHUNK, (half + 1) * HALF_CHUNK)
                masked = scores_of(
                    kr[0, slot, keys], half_lanes(stacked[...], half), base + half * HALF_CHUNK,
                    half_lanes(lo, half), half_lanes(hi, half), False,
                )
                m_old = half_lanes(m_s[...], half)
                m_new = jnp.maximum(m_old, jnp.max(masked, axis=0, keepdims=True))
                e = jnp.exp(masked - m_new)
                f = jnp.exp(m_old - m_new)
                total = half_lanes(l_s[...], half) * f + jnp.sum(e, axis=0, keepdims=True)
                e = e.astype(BF)
                for g in range(GROUP):
                    cut = slice(g * HALF_CHUNK, (g + 1) * HALF_CHUNK)
                    first = WIDE + g * HEAD_DIM
                    m_s[:, half_span(g, half)] = m_new[:, cut]
                    l_s[:, half_span(g, half)] = total[:, cut]
                    new = mm(kv[0, slot, first : first + HEAD_DIM, keys], e[:, cut])
                    acc[g, :, keys] = acc[g, :, keys] * f[:, cut] + new

        m_s[...] = jnp.full_like(m_s, LOWEST)
        l_s[...] = jnp.zeros_like(l_s)
        acc[...] = jnp.zeros_like(acc)
        each_tile(meta, p, lims, tile, halves)
        total = l_s[...]
        inv = 1.0 / total
        out = jnp.concatenate(
            [acc[g] * inv[:, g * CHUNK : (g + 1) * CHUNK] for g in range(GROUP)], axis=0
        )
        o_ref[s] = out
        ml_ref[s, 0:1] = m_s[...]
        ml_ref[s, 1:2] = total
        send[p] = out.astype(BF)


HEAD_SCRATCH = [pltpu.VMEM((8, WIDE, CHUNK), BF), pltpu.VMEM((2, 8, 2 * WIDE, CHUNK), BF)]


def attend_rows(meta, bounds, heads):
    return call(
        attend_body,
        [((8, WIDE, CHUNK), BF), ((8, WIDE, CHUNK), F32), ((8, 8, LANES), F32)],
        "SV" + "A" * 5,
        (meta, bounds, *heads),
        scratch=HEAD_SCRATCH
        + [
            pltpu.VMEM((2, 8, CHUNK, WIDE), BF),
            pltpu.VMEM((WIDE, LANES), BF),
            pltpu.VMEM((1, LANES), F32),
            pltpu.VMEM((1, LANES), F32),
            pltpu.VMEM((GROUP, HEAD_DIM, CHUNK), F32),
        ],
        flops=20 * 2 * 2 * CHUNK * LANES * 256,
        moved=8 * CHUNK * WIDE * 16,
    )


def rows_body(load, *refs):
    kv, (k_rows, v_rows) = refs[:4], refs[4:]
    load([])
    for i in range(4):

        @pl.loop(0, 4)
        def _(s):
            k_rows[i // 2, i % 2 * 4 + s] = flip(kv[i][s, :WIDE])
            v_rows[i // 2, i % 2 * 4 + s] = flip(kv[i][s, WIDE:])


def rows_of_heads(heads):
    return call(rows_body, [((2, 8, CHUNK, WIDE), BF)] * 2, "VVVV", heads[1:], flops=1)


def attend_back_body(load, meta, bounds, cos, sin, o_ref, ml_ref, *refs):
    heads, k_rows, v_rows, gs = refs[:5], refs[5], refs[6], refs[7]
    (
        pq_ref, own_ref, far_a, far_b,
        qs, kv, kr, vr, st_q, st_g, row_q, row_g, dk, dv, dq,
    ) = refs[8:]
    for ref in (st_q, st_g, dk, dv):
        ref[...] = jnp.zeros_like(ref)
    load(head_pairs(heads, qs, kv) + [(k_rows, kr), (v_rows, vr)])
    r, c = meta[0], meta[1]
    lane = lax.broadcasted_iota(jnp.int32, (CHUNK, WIDE), 1) // HEAD_DIM

    @pl.loop(0, 8)
    def _(p):
        s = p ^ r
        q = qs[s] * 0.125
        stack_heads(q, st_q)
        total = ml_ref[s, 1:2]
        top = ml_ref[s, 0:1]
        g_in = gs[p].astype(F32)
        attended = o_ref[s]
        scaled, fix = [], []
        for g in range(GROUP):
            part = slice(g * HEAD_DIM, (g + 1) * HEAD_DIM)
            inv = 1.0 / total[:, g * CHUNK : (g + 1) * CHUNK]
            scaled.append(g_in[part] * inv)
            fix.append(jnp.sum(g_in[part] * attended[part], axis=0, keepdims=True) * inv)
        scaled = jnp.concatenate(scaled, axis=0)
        fix = jnp.concatenate(fix, axis=1)
        stack_heads(scaled.astype(BF), st_g)
        q_rows = jnp.transpose(q.astype(F32))
        g_rows = jnp.transpose(scaled)
        for g in range(GROUP):
            row_q[g * CHUNK : (g + 1) * CHUNK] = jnp.where(lane == g, q_rows, 0.0).astype(BF)
            row_g[g * CHUNK : (g + 1) * CHUNK] = jnp.where(lane == g, g_rows, 0.0).astype(BF)
        lims = [thrice(bounds[p, i : i + 1]) for i in range(4)]
        dq[...] = jnp.zeros_like(dq)

        def tile(slot, own, base, lo, hi, plain):
            e = jnp.exp(scores_of(kr[c, slot], st_q[...], base, lo, hi, plain) - top)
            d = (e * (mm(vr[c, slot], st_g[...]) - fix)).astype(BF)
            e = e.astype(BF)
            kind = jnp.where(own, 0, 1)
            dv[kind, slot] += mm(e, row_g[...])
            dk[kind, slot] += mm(d, row_q[...])
            for g in range(GROUP):
                part = slice(g * HEAD_DIM, (g + 1) * HEAD_DIM)
                dq[part] += mm(kv[c, slot, part], d[:, g * CHUNK : (g + 1) * CHUNK])

        def halves(slot, base, lo, hi):
            for half in range(2):
                keys = slice(half * HALF_CHUNK, (half + 1) * HALF_CHUNK)
                s_half = scores_of(
                    kr[0, slot, keys], half_lanes(st_q[...], half), base + half * HALF_CHUNK,
                    half_lanes(lo, half), half_lanes(hi, half), False,
                )
                e = jnp.exp(s_half - half_lanes(top, half))
                d = e * (mm(vr[0, slot, keys], half_lanes(st_g[...], half)) - half_lanes(fix, half))
                e, d = e.astype(BF), d.astype(BF)
                rows_of = [jnp.concatenate([ref[half_span(g, half)] for g in range(GROUP)]) for ref in (row_g, row_q)]
                dv[0, slot, keys] += mm(e, rows_of[0])
                dk[0, slot, keys] += mm(d, rows_of[1])
                for g in range(GROUP):
                    part = slice(g * HEAD_DIM, (g + 1) * HEAD_DIM)
                    cut = slice(g * HALF_CHUNK, (g + 1) * HALF_CHUNK)
                    dq[part, keys] += mm(kv[0, slot, part, keys], d[:, cut])

        each_tile(meta, p, lims, tile, halves)
        pq_ref[s] = turn_heads(dq[...] * 0.125, cos[s], -sin[s]).astype(BF)

    both = 1.0 - c.astype(F32)

    @pl.loop(0, 8)
    def _(s):
        far_k, far_v = jnp.transpose(dk[1, s]), jnp.transpose(dv[1, s])
        for half, far_ref in enumerate((far_a, far_b)):

            @pl.when(s // 4 == half)
            def _():
                far_ref[s % 4, :WIDE] = far_k.astype(BF)
                far_ref[s % 4, WIDE:] = far_v.astype(BF)

        own_ref[s, :WIDE] = (jnp.transpose(dk[0, s]) + both * far_k).astype(BF)
        own_ref[s, WIDE:] = (jnp.transpose(dv[0, s]) + both * far_v).astype(BF)


def attend_back(meta, bounds, cos, sin, attended, stats, heads, rows_first, grads):
    rows = pltpu.VMEM((2, 8, CHUNK, WIDE), BF)
    sums = pltpu.VMEM((2, 8, CHUNK, WIDE), F32)
    return call(
        attend_back_body,
        [((8, WIDE, CHUNK), BF), ((8, 2 * WIDE, CHUNK), BF)] + [((4, 2 * WIDE, CHUNK), BF)] * 2,
        "SVVVVV" + "A" * 7 + "V",
        (meta, bounds, cos, sin, attended, stats, *heads, *rows_first, grads),
        scratch=HEAD_SCRATCH
        + [
            rows,
            rows,
            pltpu.VMEM((WIDE, LANES), BF),
            pltpu.VMEM((WIDE, LANES), BF),
            pltpu.VMEM((LANES, WIDE), BF),
            pltpu.VMEM((LANES, WIDE), BF),
        ]
        + [sums] * 2
        + [pltpu.VMEM((WIDE, CHUNK), F32)],
        flops=20 * 2 * 5 * CHUNK * LANES * 256,
        moved=8 * CHUNK * WIDE * 30,
    )


def share_pairs(meta, own, parts, dst, unit, skip):
    h, z = meta[2], meta[3]
    part = unit // 4
    pairs = [(own, dst.at[pl.ds(at16(z * unit), unit)])]
    for t in range(1, 4):
        zz = (z + 4 - t) & 3
        for k in range(4):
            to = at16(zz * unit + (h ^ k) * part)
            pairs.append((parts[k].at[t - 1, pl.ds(skip, part)], dst.at[pl.ds(to, part)]))
    return pairs


def middle_body(load, meta, gain, embed, x_ref, heads, own, *refs):
    mid_ref, n_ref, att_ref, w_ref = refs[4:]
    pairs = share_pairs(meta, own, refs[:4], w_ref, 192, 0)
    for d in range(8):
        pairs.append((heads.at[d], att_ref.at[d % 2, pl.ds(d // 2 * WIDE, WIDE)]))
    load(pairs)

    @pl.loop(0, 2)
    def _(stream):
        x, _ = unmark(x_ref[stream], embed[...])
        mid = x + mm(att_ref[stream], w_ref[...], 0, 0)
        hat, _ = norm_parts(mid)
        mid_ref[stream] = mid
        n_ref[pl.ds(pl.multiple_of(stream * CHUNK, CHUNK), CHUNK)] = (hat * gain[...]).astype(BF)


def middle_rows(meta, gain, embed, marked, heads, own, parts):
    dim = marked.shape[2]
    return call(
        middle_body,
        [((2, CHUNK, dim), F32), ((2 * CHUNK, dim), BF), ((2, dim, CHUNK), BF), ((dim, dim), BF)],
        "SVVV" + "A" * 6,
        (meta, gain, embed, marked, heads, own, *parts),
        flops=2 * 2 * CHUNK * dim * dim,
        moved=8 * CHUNK * dim * 2,
    )


def feed_body(load, meta, bias, n_own, n_far, g_own, g_far, up_own, down_own, *refs):
    shares, refs = refs[:4], refs[4:]
    (
        *sinks, gb_ref, d_out, u_ref,
        ns, gs, wu, wd, acts, slopes, out_ref, outf_ref, ngf_ref, ng_ref, d_ref, out_sems,
    ) = refs
    c, h, z = meta[1], meta[2], meta[3]
    rows = 2 * CHUNK
    part = bias.shape[1] // 4
    pairs = [
        (n_own, ns.at[pl.ds(0, rows)]),
        (n_far, ns.at[pl.ds(rows, rows)]),
        (g_own, gs.at[pl.ds(0, rows)]),
        (g_far, gs.at[pl.ds(rows, rows)]),
    ]
    pairs += share_pairs(meta, down_own.at[pl.ds(at16(c * part), part)], shares, wd, part, 48)
    for k in range(4):
        cols = pl.ds(pl.multiple_of(k * 2 * part + c * part, 128), part)
        pairs.append((up_own.at[:, cols], wu.at[pl.ds(at16(z * 192), 192), pl.ds(k * part, part)]))
    for t in range(1, 4):
        zz = (z + 4 - t) & 3
        for k in range(4):
            dst = pl.ds(at16(zz * 192 + (h ^ k) * 48), 48)
            for b in range(2):
                pairs.append(
                    (
                        shares[k].at[t - 1, pl.ds(144 + 48 * b, 48)],
                        wu.at[dst, pl.ds(2 * part * b, 2 * part)],
                    )
                )
    load(pairs)
    gb_ref[...] = jnp.zeros_like(gb_ref)

    @pl.loop(0, 4)
    def _(i):
        span = pl.ds(pl.multiple_of(i * CHUNK, CHUNK), CHUNK)
        v = mm(ns[span], wu[...]) + bias[...]
        square = v * v
        th = jnp.tanh(v * (GELU_SCALE + (GELU_SCALE * 0.044715) * square))
        half = 0.5 + 0.5 * th
        act = (v * half).astype(BF)
        slope = half + (v * half) * (1.0 - th) * (GELU_SCALE + (3.0 * 0.044715 * GELU_SCALE) * square)
        acts[span] = act
        ug = (slope * mm(gs[span], wd[...], 1, 1)).astype(BF)
        slopes[span] = ug
        gb_ref[...] += jnp.sum(ug.astype(F32), axis=0, keepdims=True)
        out = mm(act, wd[...]).astype(BF)
        ng = mm(ug, wu[...], 1, 1).astype(BF)
        to = pl.ds(pl.multiple_of((i & 1) * CHUNK, CHUNK), CHUNK)

        @pl.when(i < 2)
        def _():
            out_ref[to] = out
            ng_ref[to] = ng

        @pl.when(i >= 2)
        def _():
            outf_ref[to] = out
            ngf_ref[to] = ng

    early = [
        pltpu.make_async_copy(ref, sinks[k], out_sems.at[k])
        for k, ref in enumerate((out_ref, outf_ref, ngf_ref, ng_ref))
    ]
    for copy in early:
        copy.start()

    @pl.loop(0, 4)
    def _(j):
        cols = pl.ds(pl.multiple_of(j * part, 128), part)
        gd = mm(acts[:, cols], gs[...], 0, 0).astype(BF)
        for b in range(4):
            d_ref[b, j ^ h] = gd[96 * b : 96 * (b + 1)]
        pltpu.make_async_copy(d_ref.at[:, j ^ h], d_out.at[:, j ^ h], out_sems.at[4 + j]).start()
        gu = mm(ns[...], slopes[:, cols], 0, 0)
        side = pl.ds(pl.multiple_of((j & 1) * part, 128), part)
        line = pl.ds(at16((j >> 1) * 48), 48)
        for b in range(16):
            first = 192 * (b // 4) + 24 * (b % 4)
            block = jnp.concatenate([gu[first : first + 24], gu[first + 96 : first + 120]])
            u_ref[(b // 4) ^ h, b % 4, line, side] = block.astype(BF)

    for copy in early:
        copy.wait()
    for j in range(4):
        pltpu.make_async_copy(d_ref.at[:, j ^ h], d_out.at[:, j ^ h], out_sems.at[4 + j]).wait()


def feed_rows(meta, bias, args):
    rows = 2 * CHUNK
    dim = args[0].shape[1]
    hid = bias.shape[1]
    return call(
        feed_body,
        [((rows, dim), BF)] * 4
        + [((1, hid), F32)]
        + [((4, 4, hid // 16, dim), BF)] * 2,
        "SV" + "A" * 10,
        (meta, bias, *args),
        scratch=[
            pltpu.VMEM((2 * rows, dim), BF),
            pltpu.VMEM((2 * rows, dim), BF),
            pltpu.VMEM((dim, hid), BF),
            pltpu.VMEM((hid, dim), BF),
            pltpu.VMEM((2 * rows, hid), BF),
            pltpu.VMEM((2 * rows, hid), BF),
        ]
        + [pltpu.VMEM((rows, dim), BF)] * 4
        + [pltpu.VMEM((4, 4, hid // 16, dim), BF), pltpu.SemaphoreType.DMA((8,))],
        raw=(0, 1, 2, 3, 5),
        flops=6 * 2 * 2 * rows * dim * hid,
        moved=12 * dim * hid,
    )


def pack_body(load, meta, w_out, w_down, w_up, share):
    c, h = meta[1], meta[2]
    part = w_up.shape[1] // 8
    pairs = [
        (w_out.at[pl.ds(at16(48 * h), 48)], share.at[pl.ds(0, 48)]),
        (w_down.at[pl.ds(at16(part * c + 96 * h), 96)], share.at[pl.ds(48, 96)]),
    ]
    for k in range(4):
        cols = pl.ds(pl.multiple_of((2 * k + c) * part, 128), part)
        to = share.at[pl.ds(144 + 48 * (k // 2), 48), pl.ds(part * (k % 2), part)]
        pairs.append((w_up.at[pl.ds(at16(48 * h), 48), cols], to))
    load(pairs)


def pack_share(place, w_out, w_down, w_up):
    return call(pack_body, [((240, w_out.shape[1]), BF)], "SAAA", (place, w_out, w_down, w_up))[0]


def middle_back_body(
    load, meta, gain, b_down, mid_ref, ng_ref, out_ref, outf_ref, ngf_ref, g_ref, x_ref, w_ref,
    lay_ref, mg_ref, sum_ref, send,
):
    load([])
    sum_ref[...] = jnp.zeros_like(sum_ref)

    @pl.loop(0, 2)
    def _(stream):
        span = pl.ds(pl.multiple_of(stream * CHUNK, CHUNK), CHUNK)
        mid = mid_ref[stream]
        lay = mid + out_ref[span].astype(F32) + outf_ref[span].astype(F32) + b_down[...]
        lay_ref[stream] = lay.astype(BF)
        hat, scale = norm_parts(mid)
        ng = ng_ref[span].astype(F32) + ngf_ref[span].astype(F32)
        sum_ref[0:1] += jnp.sum(ng * hat, axis=0, keepdims=True)
        t = ng * gain[...]
        g = g_ref[stream].astype(F32)
        sum_ref[1:2] += jnp.sum(g, axis=0, keepdims=True)
        t_mean = jnp.mean(t, axis=-1, keepdims=True)
        t_hat = jnp.mean(t * hat, axis=-1, keepdims=True)
        mg = (g + scale * (t - t_mean - hat * t_hat)).astype(BF)
        mg_ref[stream] = mg
        flag = (x_ref[stream][:, :1].astype(F32) > 1e38) & (stream == 1)
        sum_ref[2:3] += jnp.sum(jnp.where(flag, mg.astype(F32), 0.0), axis=0, keepdims=True)
        for d in range(4):
            send[2 * d + stream] = mm(w_ref[d * WIDE : (d + 1) * WIDE], mg, 1, 1).astype(BF)


def middle_back(meta, gain, b_down, args):
    dim = gain.shape[1]
    return call(
        middle_back_body,
        [((2, CHUNK, dim), BF), ((2, CHUNK, dim), BF), ((8, dim), F32), ((8, WIDE, CHUNK), BF)],
        "S" + "V" * 10,
        (meta, gain, b_down, *args),
        flops=4 * CHUNK * dim * dim,
        moved=20 * CHUNK * dim,
    )


def by_z(grad, ref):
    for zz in range(4):
        for h in range(4):
            first = 192 * h + 24 * zz
            pair = jnp.concatenate([grad[first : first + 24], grad[first + 96 : first + 120]])
            ref[zz, 48 * h : 48 * (h + 1)] = pair.astype(BF)


def out_grad_body(load, meta, att_ref, mg_ref, up, *o_refs):
    load([(up.at[k], o_refs[k].at[:, pl.ds(0, 96)]) for k in range(4)])
    grad = mm(att_ref[0], mg_ref[0]) + mm(att_ref[1], mg_ref[1])
    for owner in range(4):
        blocks = []
        for b in range(4):
            first = 192 * owner + 24 * b
            blocks.append(jnp.concatenate([grad[first : first + 24], grad[first + 96 : first + 120]]).astype(BF))
        for k in range(4):

            @pl.when((owner ^ meta[2]) == k)
            def _():
                for b in range(4):
                    o_refs[k][b, 96:] = blocks[b]


def project_back_body(
    own, f0, f1, pq, n_ref, mk_ref, cos, sin, w_ref, flat,
    away_x, away_y, stay, gq_ref, wp, acc, gs_ref, sums,
):
    i = pl.program_id(0)

    @pl.when(i == 0)
    def _():
        for part in range(3):
            wp[part] = w_ref[:, part * WIDE : (part + 1) * WIDE]
        acc[...] = jnp.zeros_like(acc)
        gs_ref[...] = jnp.zeros_like(gs_ref)

    early = (i == 0) | (i == 4) | (i == 6) | (i == 7)
    far = jnp.where(early, f0[0], f1[0])
    kv = own[0].astype(F32) + far.astype(F32)
    parts = [
        pq[0],
        turn_heads(kv[:WIDE], cos[0], -sin[0]).astype(BF),
        kv[WIDE:].astype(BF),
    ]
    n, mk = n_ref[0], mk_ref[0]
    ng = jnp.zeros((CHUNK, n.shape[1]), F32)
    for k in range(3):
        ng += mm(flip(parts[k]), wp[k], 1, 1)
        acc[k * WIDE : (k + 1) * WIDE] += mm(parts[k], n)
    low = ng.astype(BF)

    @pl.when(i < 2)
    def _():
        away_x[0] = low

    @pl.when((i >= 2) & (i < 4))
    def _():
        away_y[0] = low

    @pl.when(i >= 4)
    def _():
        stay[0] = ng

    gs_ref[0:1] += jnp.sum(ng * n.astype(F32), axis=0, keepdims=True)
    gs_ref[1:2] += jnp.sum(ng * mk[:, :1].astype(F32), axis=0, keepdims=True)

    @pl.when(i == 7)
    def _():
        by_z(jnp.transpose(acc[...]), gq_ref)
        part = sums.shape[1]
        sums[...] = flat[...]
        for k in range(2):
            for side in range(2):
                to = 14 + 2 * k + side
                sums[to : to + 1] = gs_ref[k : k + 1, side * part : (side + 1) * part]
        tail = sums[...].astype(BF)
        rows = gq_ref.shape[1] - 24
        for zz in range(4):
            gq_ref[zz, rows:] = jnp.zeros((24, gq_ref.shape[2]), BF)
            gq_ref[zz, rows:, :part] = tail


def pick(order):
    def slot_of(i):
        slot = jnp.int32(order[-1])
        for k in range(len(order) - 2, -1, -1):
            slot = jnp.where(i == k, order[k], slot)
        return slot

    return slot_of


def project_back(own, far, pq, n, mk, cos, sin, w, flat):
    dim = n.shape[2]
    wide = w.shape[1] + HEAD_DIM
    slot = pick((2, 6, 5, 7, 0, 4, 1, 3))

    def block(rows, cols, index):
        return pl.BlockSpec((1, rows, cols), lambda i: (index(i), 0, 0))

    def whole(*shape):
        return pl.BlockSpec(shape, lambda i: tuple(0 for _ in shape))

    return pl.pallas_call(
        project_back_body,
        grid=(8,),
        out_shape=(
            jax.ShapeDtypeStruct((2, CHUNK, dim), BF),
            jax.ShapeDtypeStruct((2, CHUNK, dim), BF),
            jax.ShapeDtypeStruct((4, CHUNK, dim), F32),
            jax.ShapeDtypeStruct((4, dim // 4 + 24, wide), BF),
        ),
        in_specs=[
            block(2 * WIDE, CHUNK, slot),
            *[block(2 * WIDE, CHUNK, lambda i: slot(i) % 4)] * 2,
            block(WIDE, CHUNK, slot),
            block(CHUNK, dim, slot), block(CHUNK, 128, slot),
            block(HALF, CHUNK, slot), block(HALF, CHUNK, slot), whole(*w.shape), whole(*flat.shape),
        ],
        out_specs=(
            block(CHUNK, dim, lambda i: jnp.minimum(i, 1)),
            block(CHUNK, dim, lambda i: jnp.clip(i - 2, 0, 1)),
            block(CHUNK, dim, lambda i: jnp.clip(i - 4, 0, 3)),
            whole(4, dim // 4 + 24, wide),
        ),
        scratch_shapes=[
            pltpu.VMEM((3, dim, WIDE), BF),
            pltpu.VMEM((wide, dim), F32),
            pltpu.VMEM((8, dim), F32),
            pltpu.VMEM(flat.shape, F32),
        ],
        compiler_params=pltpu.CompilerParams(vmem_limit_bytes=56 * 2**20),
        cost_estimate=pl.CostEstimate(
            flops=1 + 4 * 8 * CHUNK * dim * 3 * WIDE // COST, bytes_accessed=1, transcendentals=0
        ),
    )(own, *far, pq, n, mk, cos, sin, w, flat)


def last_body(load, meta, gain, embed, x_ref, mg_ref, keep_ref, far_ref, o_ref):
    load([])

    @pl.loop(0, 2)
    def _(stream):
        ng = jnp.where(stream == meta[1], keep_ref[...], far_ref[...].astype(F32))
        x, flag = unmark(x_ref[stream], embed[...])
        hat, scale = norm_parts(x)
        t = ng * gain[...]
        t_mean = jnp.mean(t, axis=-1, keepdims=True)
        t_hat = jnp.mean(t * hat, axis=-1, keepdims=True)
        grad = mg_ref[stream].astype(F32) + scale * (t - t_mean - hat * t_hat)
        o_ref[stream] = jnp.where(flag, 0.0, grad).astype(BF)


def finish_body(load, meta, gain, embed, x_ref, up_own, up_far, *refs):
    gd_refs, (gq_ref, go_ref, gu_ref, gd_ref, bu_ref, rows_ref, sums) = refs[:4], refs[4:]
    load([])
    r, c, z = meta[0], meta[1], meta[3]
    own = 4 * r + z
    small = gq_ref.shape[0]
    for h in range(4):
        part = x_ref[2 * h, :small].astype(F32) + x_ref[2 * h + 1, :small].astype(F32)
        for k in range(3):
            first = k * 4 * WIDE + h * WIDE
            gq_ref[:, first : first + WIDE] = part[:, k * WIDE : (k + 1) * WIDE]
    total = add(gd_refs[0][...], gd_refs[1][...])
    gd_ref[...] = total + add(gd_refs[2][...], gd_refs[3][...])

    rows = up_own[...].astype(F32)
    mine = [jnp.where(c == 0, rows[48 * q : 48 * q + 24], rows[48 * q + 24 : 48 * q + 48]) for q in range(3)]
    go_ref[...] = mine[2] + up_far[2].astype(F32)
    part = gu_ref.shape[1] // 8
    for q in range(2):
        for side in range(2):
            lanes = slice(side * part, (side + 1) * part)
            for core, block in ((c, mine[q]), (1 - c, up_far[q].astype(F32))):
                first = pl.multiple_of((2 * (2 * q + side) + core) * part, 128)
                gu_ref[:, pl.ds(first, part)] = block[:, lanes]

    total = x_ref[0, small:, :part].astype(F32)
    for d in range(1, 8):
        total += x_ref[d, small:, :part].astype(F32)
    sums[...] = total

    def pair(i):
        return total[8 + 2 * i : 10 + 2 * i]

    def over(v):
        return jnp.sum(v, keepdims=True) * (1.0 / (2 * part))

    centered = embed[...] - over(embed[...])
    scale = lax.rsqrt(over(centered * centered) + EPSILON)
    hat = centered * scale
    t = pair(4) * gain[...]
    sums[12:14] = pair(2) + scale * (t - over(t) - hat * over(t * hat))
    sums[14:16] = pair(3) / gain[...]
    row = sums[pl.ds(own // 4, 1)]
    bu_ref[...] = pltpu.roll(row, (4 * 96 - own % 4 * 96) % part, 1)[:, :96]
    shift = (16 * 24 - own % 16 * 24) % part
    for i in range(4):
        row = sums[pl.ds(8 + 2 * i + own // 16, 1)]
        rows_ref[i : i + 1] = pltpu.roll(row, shift, 1)[:, :24]


def cut(v, index, size, axis=0):
    return lax.dynamic_slice_in_dim(v, index * size, size, axis)


def at(v, index, axis=0):
    return lax.dynamic_index_in_dim(v, index, axis, keepdims=False)


def after(value, *needed):
    return lax.optimization_barrier((value, *needed))[0]


def add(a, b):
    return a.astype(F32) + b.astype(F32)


def exchange(v):
    return lax.all_to_all(v, "ctx", 0, 0, tiled=True)


def exchange_chips(v):
    groups = [[i + core for i in range(0, 8, 2)] for core in range(2)]
    return lax.all_to_all(v, "ctx", 0, 0, axis_index_groups=groups, tiled=True)


def exchange_z(v):
    return lax.all_to_all(v, "fsdp", 0, 0, tiled=True)


def shards_by_heads(
    hidden,
    noise_mask,
    doc_lengths,
    w_qkv,
    w_out,
    w_up,
    b_up,
    w_down,
    b_down,
    gain_one,
    gain_two,
    mask_embed,
    out_grad,
):
    r = lax.axis_index("ctx")
    z = lax.axis_index("fsdp")
    c, h = r & 1, r >> 1
    dim = hidden.shape[3]
    hid = w_up.shape[1]
    part = hid // 8
    total = CHUNK * 8
    clean = c == 0

    share = pack_share(jnp.stack([r, c, h, z]).astype(jnp.int32), w_out, w_down, w_up)
    ff_t = lax.all_gather(share, "fsdp")
    hidden = after(hidden, share)

    noisy = jnp.where(noise_mask[0][:, None] == 1, jnp.asarray(jnp.inf, BF), hidden[0, 1])
    mine = jnp.where(clean, hidden[0, 0], noisy)
    other = swap(jnp.where(clean, noisy, hidden[0, 0]), 1)
    mine_x, mine_y = swap(mine, 2), swap(mine, 4)
    other_x, other_y = swap(other, 2), swap(other, 4)
    marked = jnp.stack([hidden[0, 0], noisy])

    lengths = doc_lengths[0]
    index = jnp.arange(lengths.shape[0])
    ends = jnp.sum(jnp.where(index[None, :] <= index[:, None], lengths[None, :], 0), axis=1)
    place = jnp.arange(total, dtype=jnp.int32)
    later = ends[None, :] > place[:, None]
    start = jnp.max(jnp.where(later, 0, ends[None, :]), axis=1)
    stop = jnp.min(jnp.where(later, ends[None, :], total), axis=1)
    block = place // BLOCK * BLOCK
    limit = jnp.minimum(block + BLOCK, stop)
    bounds = jnp.stack(
        [start, jnp.where(clean, limit, block), jnp.where(clean, start, jnp.maximum(start, block)), limit]
    )
    bounds = jnp.pad(bounds.reshape(4, 8, CHUNK).transpose(1, 0, 2), ((0, 0), (0, 4), (0, 0)))
    meta = jnp.concatenate(
        [jnp.stack([r, c, h, z]), start[::CHUNK] // CHUNK, start[CHUNK - 1 :: CHUNK]]
    ).astype(jnp.int32)
    slots = (jnp.arange(8) ^ r)[:, None] * CHUNK + jnp.arange(CHUNK)[None, :]
    frequency = jnp.exp(jnp.arange(HALF).astype(F32) * (-2.0 * math.log(10000.0) / HEAD_DIM))
    angles = slots.astype(F32)[:, None, :] * frequency[None, :, None]
    cos, sin = jnp.cos(angles), jnp.sin(angles)
    size = hid // 4 + dim
    w_qkv = after(w_qkv, other)
    small = jnp.concatenate([b_up, b_down, gain_one, gain_two, mask_embed])
    small = jnp.pad(small, (0, 16 * 3 * WIDE - size)).reshape(16, 3 * WIDE)
    own_qkv = jnp.concatenate([cut(w_qkv[:, k * dim : (k + 1) * dim], h, WIDE, 1) for k in range(3)], 1)
    quarter = dim // 4
    half = jnp.concatenate([cut(own_qkv, c, quarter // 2), small])
    half = jnp.broadcast_to(half, (4, *half.shape))
    near = exchange_z(half)
    mine_x, mine_y, other_x, other_y, cos, sin, bounds, meta = lax.optimization_barrier(
        (mine_x, mine_y, other_x, other_y, cos, sin, bounds, meta)
    )
    mine_d, other_d = swap(mine_x, 4), swap(other_y, 2)
    mine_d, other_d, near = lax.optimization_barrier((mine_d, other_d, near))
    far = swap(near, 1)
    small = near[:, quarter // 2 :].reshape(4, -1)[:, :size].astype(F32)
    bias = at(small[:, : hid // 4].reshape(4, 2, part), c, 1).reshape(1, 4 * part)
    b_down_all, gain_a, gain_b, embed = [
        small[:, hid // 4 + k * quarter : hid // 4 + (k + 1) * quarter].reshape(1, dim)
        for k in range(4)
    ]

    grads = out_grad[0]
    grad_rows = grads.reshape(2 * CHUNK, dim)

    ff_r = jnp.take(ff_t, (z - jnp.arange(1, 4)) % 4, axis=0)
    far, ff_r = lax.optimization_barrier((far, ff_r))
    shares = (ff_r, swap(ff_r, 2), swap(ff_r, 4), swap(ff_r, 6))
    rows = (mine, other, mine_x, other_x, mine_y, other_y, mine_d, other_d)
    q, *kv, normed_one, marks, w_all = project_rows(meta, gain_a, embed, cos, sin, rows, (near, far))
    give = [(i, i + 1) for i in range(0, 8, 2)]
    heads = (q, *kv, *[lax.ppermute(v, "ctx", give) for v in kv])
    send, attended, stats = attend_rows(meta, bounds, heads)
    send, *shares = lax.optimization_barrier((send, *shares))
    grad_far = swap(after(grad_rows, kv[0]), 1)
    heads_late = lax.optimization_barrier((*heads, send))[:5]
    rows_first = rows_of_heads(heads_late)
    got, *rows_first = lax.optimization_barrier((exchange(send), *rows_first))
    middle, normed, att, w_out_all = middle_rows(meta, gain_b, embed, marked, got, w_out, shares)
    out_own, out_far, ng_far, ng_own, gbu, gd, gu = feed_rows(
        meta, bias, (normed, swap(normed, 1), grad_rows, grad_far, w_up, w_down, *shares)
    )
    ng_far, out_far = swap(ng_far, 1), swap(out_far, 1)
    gd = lax.psum_scatter(gd.reshape(-1, dim), "fsdp", scatter_dimension=0, tiled=True)

    layer, mid_grad, sums, send = middle_back(
        meta, gain_b, b_down_all, (middle, ng_own, out_own, out_far, ng_far, grads, marked, w_out_all)
    )
    got = exchange(send)
    up_out = call(
        out_grad_body,
        [((4, part // 4 + dim // 16, dim), BF)] * 4,
        "SVVA",
        (meta, att, mid_grad, gu),
        flops=4 * CHUNK * dim * dim,
    )
    gbu = gbu.reshape(4, 1, part)
    gbu = jnp.where(clean, jnp.concatenate([gbu, 0 * gbu], 1), jnp.concatenate([0 * gbu, gbu], 1))
    flat = jnp.concatenate([gbu.reshape(8, part), sums[:3].reshape(6, part), jnp.zeros((10, part), F32)])
    got, flat, *up_out = lax.optimization_barrier((got, flat, *up_out))
    up_out = [up_out[0]] + [swap(up_out[k], 2 * k) for k in range(1, 4)]
    pq, own_kv, *far_kv = attend_back(meta, bounds, cos, sin, attended, stats, heads, rows_first, got)
    far_kv = [lax.ppermute(v, "ctx", [(b, a) for a, b in give]) for v in far_kv]

    *up_out, _ = lax.optimization_barrier((*up_out, pq))
    up_out = (add(up_out[0], up_out[1]) + add(up_out[2], up_out[3])).astype(BF).reshape(-1, dim)
    gd = after(gd, pq).reshape(4, part // 4, dim)
    *far_kv, up_out, gd = lax.optimization_barrier((*far_kv, up_out, gd))
    up_out = lax.psum_scatter(up_out, "fsdp", scatter_dimension=0, tiled=True)

    away_x, away_y, stay, gq = project_back(
        own_kv, far_kv, pq, normed_one, marks, cos, sin, w_all, flat
    )
    in_x, in_y = swap(away_x, 2), swap(away_y, 4)
    wide = gq.shape[2]
    rows = dim // 4
    gq = gq.reshape(-1, wide)
    gq = lax.psum_scatter(gq, "fsdp", scatter_dimension=0, tiled=True)
    over_y, over_x = add(stay[1], in_x[1]).astype(BF), add(stay[3], in_y[1]).astype(BF)
    near_one, near_two = swap(over_y, 4), swap(over_x, 2)
    gd = after(gd, over_y, over_x)
    gd = [gd[0]] + [swap(gd[k], 2 * k) for k in range(1, 4)]
    gq = after(gq, over_y, over_x)
    flat = jnp.broadcast_to(gq[rows:], (8, 24, wide))
    gq = jnp.concatenate([gq[:rows].reshape(8, dim // 32, wide), flat], 1)
    near_one, near_two, gq = lax.optimization_barrier((near_one, near_two, gq))
    gq = exchange(gq)
    keep = add(stay[0], in_x[0]) + near_one.astype(F32)
    pair = (add(stay[2], in_y[0]) + near_two.astype(F32)).astype(BF)
    pair = swap(pair, 1)
    *gd, gq = lax.optimization_barrier((*gd, gq, keep, pair))[:5]
    (input_grad,) = call(
        last_body,
        [((2, CHUNK, dim), BF)],
        "S" + "V" * 6,
        (meta, gain_a, embed, marked, mid_grad, keep, pair),
        moved=10 * CHUNK * dim,
    )

    up_sum = after(up_out, input_grad)
    up_out = up_sum.reshape(3, 2, dim // 32, dim)
    up_far = swap(at(up_out, 1 - c, 1), 1)
    small = dim // 32
    gq, go, gu, gd, gbu, rows = call(
        finish_body,
        [
            ((small, 3 * dim), F32),
            ((small, dim), F32),
            ((small, hid), F32),
            ((part // 4, dim), F32),
            ((1, hid // 32), F32),
            ((4, small), F32),
        ],
        "S" + "V" * 9,
        (meta, gain_a.reshape(2, part), embed.reshape(2, part), gq, up_sum, up_far, *gd),
        scratch=[pltpu.VMEM((24, part), F32)],
        moved=8 * dim * dim,
    )
    return (
        layer[None],
        input_grad[None],
        gq,
        go,
        gu,
        gbu[0],
        gd,
        rows[1],
        rows[3],
        rows[0],
        rows[2],
    )


def solution(mesh):
    plain = (mesh.shape["ctx"], mesh.shape["fsdp"]) != (8, 4)
    placed = (
        P("fsdp", None, "ctx", None),
        P("fsdp", "ctx"),
        P("fsdp", None),
        P("fsdp", None),
        P("fsdp", None),
        P("fsdp", None),
        P("fsdp"),
        P("fsdp", None),
        P("fsdp"),
        P("fsdp"),
        P("fsdp"),
        P("fsdp"),
        P("fsdp", None, "ctx", None),
    )
    return jax.shard_map(
        shards if plain else shards_by_heads,
        mesh=mesh,
        in_specs=placed,
        out_specs=(
            P("fsdp", None, "ctx", None),
            P("fsdp", None, "ctx", None),
            P(("ctx", "fsdp"), None),
            P(("ctx", "fsdp"), None),
            P(("ctx", "fsdp"), None),
            P(("ctx", "fsdp")),
            P(("ctx", "fsdp"), None),
            P(("ctx", "fsdp")),
            P(("ctx", "fsdp")),
            P(("ctx", "fsdp")),
            P(("ctx", "fsdp")),
        ),
        check_vma=False,
    )
```

```python
import functools
import math

import jax
import jax.numpy as jnp
from jax import lax
from jax.experimental import pallas as pl
from jax.experimental.pallas import tpu as pltpu
from jax.sharding import PartitionSpec as P

HEADS = 12
HEAD_DIM = 64
BLOCK = 16


LOWEST = -1e30
EPSILON = 1e-05


def layer_norm(inputs, gain):
    average = jnp.mean(inputs, axis=-1, keepdims=True)
    centered = inputs - average
    variance = jnp.mean(centered * centered, axis=-1, keepdims=True)
    return centered * lax.rsqrt(variance + EPSILON) * gain


def rotary_angles(positions):
    half_dim = HEAD_DIM // 2
    frequency = jnp.exp(
        jnp.arange(half_dim).astype(jnp.float32) * (-2.0 * math.log(10000.0) / HEAD_DIM)
    )
    return positions.astype(jnp.float32)[:, None] * frequency[None, :]


def rotate(heads_in, angles):
    half_dim = heads_in.shape[-1] // 2
    cosine = jnp.cos(angles)[:, None, :]
    sine_part = jnp.sin(angles)[:, None, :]
    first_half = heads_in[..., :half_dim]
    second_half = heads_in[..., half_dim:]
    return jnp.concatenate(
        [
            first_half * cosine - second_half * sine_part,
            second_half * cosine + first_half * sine_part,
        ],
        axis=-1,
    )


def segment_of(positions, doc_ends):
    return jnp.sum((positions[:, None] >= doc_ends[None, :]).astype(jnp.int32), axis=1)


def visible(query_stream, query_position, query_segment, key_stream, key_position, key_segment):
    query_block = query_position // BLOCK
    key_block = key_position // BLOCK
    same_doc = query_segment[:, None] == key_segment[None, :]
    clean_key = key_stream[None, :] == 0
    noisy_query = query_stream[:, None] == 1
    before = key_block[None, :] < query_block[:, None]
    same_block = key_block[None, :] == query_block[:, None]
    from_clean = clean_key & (before | same_block & jnp.logical_not(noisy_query))
    from_noisy = jnp.logical_not(clean_key) & noisy_query & same_block
    return same_doc & (from_clean | from_noisy)


def mix_tile(running, query_rows, key_tile, value_tile, allowed):
    run_max, run_sum, accum = running
    scores = (
        jnp.einsum("qhd,khd->hqk", query_rows, key_tile, preferred_element_type=jnp.float32) * 0.125
    )
    masked = jnp.where(allowed[None], scores, LOWEST)
    new_max = jnp.maximum(run_max, jnp.max(masked, axis=-1))
    exp_terms = jnp.where(allowed[None], jnp.exp(masked - new_max[..., None]), 0.0)
    factor = jnp.exp(run_max - new_max)
    new_sum = run_sum * factor + jnp.sum(exp_terms, axis=-1)
    accum = accum * factor[..., None] + jnp.einsum(
        "hqk,khd->hqd",
        exp_terms.astype(jnp.bfloat16),
        value_tile,
        preferred_element_type=jnp.float32,
    )
    return (new_max, new_sum, accum)


def tile_grads(query_rows, key_tile, value_tile, allowed, row_max, scaled_grad, correction):
    scores = (
        jnp.einsum("qhd,khd->hqk", query_rows, key_tile, preferred_element_type=jnp.float32) * 0.125
    )
    masked = jnp.where(allowed[None], scores, LOWEST)
    exp_terms = jnp.where(allowed[None], jnp.exp(masked - row_max[..., None]), 0.0)
    prob_grad = jnp.einsum(
        "hqd,khd->hqk", scaled_grad, value_tile, preferred_element_type=jnp.float32
    )
    score_grad = (exp_terms * (prob_grad - correction[..., None])).astype(jnp.bfloat16)
    query_part = jnp.einsum(
        "hqk,khd->qhd", score_grad, key_tile, preferred_element_type=jnp.float32
    )
    key_part = jnp.einsum(
        "hqk,qhd->khd", score_grad, query_rows, preferred_element_type=jnp.float32
    )
    value_part = jnp.einsum(
        "hqk,hqd->khd",
        exp_terms.astype(jnp.bfloat16),
        scaled_grad,
        preferred_element_type=jnp.float32,
    )
    return (query_part, key_part, value_part)


def build_inputs(hidden, noise_row, mask_row):
    clean_rows = hidden[0, 0].astype(jnp.float32)
    noisy_rows = jnp.where(
        noise_row[:, None] == 1,
        mask_row.astype(jnp.float32)[None, :],
        hidden[0, 1].astype(jnp.float32),
    )
    return jnp.concatenate([clean_rows, noisy_rows], axis=0)


def project(inputs, gathered, angles):
    row_count = inputs.shape[0]
    model_dim = inputs.shape[1]
    normed = layer_norm(inputs, gathered[6].astype(jnp.float32)).astype(jnp.bfloat16)
    projected = jnp.dot(normed, gathered[0], preferred_element_type=jnp.float32)
    query_rows = rotate(
        projected[:, :model_dim].reshape(row_count, HEADS, HEAD_DIM), angles
    ).astype(jnp.bfloat16)
    key_rows = rotate(
        projected[:, model_dim : 2 * model_dim].reshape(row_count, HEADS, HEAD_DIM), angles
    ).astype(jnp.bfloat16)
    value_rows = (
        projected[:, 2 * model_dim :].reshape(row_count, HEADS, HEAD_DIM).astype(jnp.bfloat16)
    )
    return (normed, query_rows, key_rows, value_rows)


def upper_half(inputs, attended_low, gathered):
    middle = inputs + jnp.dot(attended_low, gathered[1], preferred_element_type=jnp.float32)
    normed_two = layer_norm(middle, gathered[7].astype(jnp.float32)).astype(jnp.bfloat16)
    upper = jnp.dot(normed_two, gathered[2], preferred_element_type=jnp.float32) + gathered[
        3
    ].astype(jnp.float32)
    activated = jax.nn.gelu(upper, approximate=True).astype(jnp.bfloat16)
    return (middle, normed_two, upper, activated)


def shards(
    hidden,
    noise_mask,
    doc_lengths,
    w_qkv,
    w_out,
    w_up,
    b_up,
    w_down,
    b_down,
    gain_one,
    gain_two,
    mask_embed,
    out_grad,
):
    own_params = (w_qkv, w_out, w_up, b_up, w_down, b_down, gain_one, gain_two, mask_embed)
    local_count = hidden.shape[2]
    model_dim = hidden.shape[3]
    row_count = 2 * local_count
    ctx_index = lax.axis_index("ctx")
    offset = ctx_index * local_count
    local_place = offset + jnp.arange(local_count, dtype=jnp.int32)
    positions = jnp.concatenate([local_place, local_place])
    stream = jnp.concatenate(
        [jnp.zeros((local_count,), jnp.int32), jnp.ones((local_count,), jnp.int32)]
    )
    doc_ends = jnp.cumsum(doc_lengths[0])
    segments = segment_of(positions, doc_ends)
    angles = rotary_angles(positions)
    noise_row = noise_mask[0]
    noisy_stream = stream[local_count:]
    noisy_allowed = visible(
        stream, positions, segments, noisy_stream, positions[local_count:], segments[local_count:]
    )
    gathered = (
        lax.all_gather(own_params[0], "fsdp", axis=0, tiled=True),
        lax.all_gather(own_params[1], "fsdp", axis=0, tiled=True),
        lax.all_gather(own_params[2], "fsdp", axis=0, tiled=True),
        lax.all_gather(own_params[3], "fsdp", axis=0, tiled=True),
        lax.all_gather(own_params[4], "fsdp", axis=0, tiled=True),
        lax.all_gather(own_params[5], "fsdp", axis=0, tiled=True),
        lax.all_gather(own_params[6], "fsdp", axis=0, tiled=True),
        lax.all_gather(own_params[7], "fsdp", axis=0, tiled=True),
        lax.all_gather(own_params[8], "fsdp", axis=0, tiled=True),
    )
    inputs = build_inputs(hidden, noise_row, gathered[8])
    normed, query_rows, key_rows, value_rows = project(inputs, gathered, angles)
    clean_keys = key_rows[:local_count].reshape(local_count, model_dim)
    clean_values = value_rows[:local_count].reshape(local_count, model_dim)
    start_state = (
        jnp.full((HEADS, row_count), LOWEST, jnp.float32),
        jnp.zeros((HEADS, row_count), jnp.float32),
        jnp.zeros((HEADS, row_count, HEAD_DIM), jnp.float32),
    )
    running = start_state
    piece_keys = lax.all_gather(clean_keys, "ctx", axis=0, tiled=True)
    piece_values = lax.all_gather(clean_values, "ctx", axis=0, tiled=True)
    piece_rows = piece_keys.shape[0]
    fold_tile_size = math.gcd(piece_rows, 512)

    def step(carried, tile_index):
        tile_start = tile_index * fold_tile_size
        key_tile = lax.dynamic_slice_in_dim(piece_keys, tile_start, fold_tile_size, 0).reshape(
            fold_tile_size, HEADS, HEAD_DIM
        )
        value_tile = lax.dynamic_slice_in_dim(piece_values, tile_start, fold_tile_size, 0).reshape(
            fold_tile_size, HEADS, HEAD_DIM
        )
        key_position = tile_start + jnp.arange(fold_tile_size, dtype=jnp.int32)
        allowed = visible(
            stream,
            positions,
            segments,
            jnp.zeros((fold_tile_size,), jnp.int32),
            key_position,
            segment_of(key_position, doc_ends),
        )
        carried = lax.cond(
            jnp.any(allowed),
            lambda held: mix_tile(held, query_rows, key_tile, value_tile, allowed),
            lambda held: held,
            carried,
        )
        return (carried, None)

    running, _ = lax.scan(step, running, jnp.arange(piece_rows // fold_tile_size))
    run_max, run_sum, accum = mix_tile(
        running, query_rows, key_rows[local_count:], value_rows[local_count:], noisy_allowed
    )
    attended = accum / run_sum[..., None]
    attended_low = (
        jnp.transpose(attended, (1, 0, 2)).reshape(row_count, model_dim).astype(jnp.bfloat16)
    )
    middle, normed_two, upper, activated = upper_half(inputs, attended_low, gathered)
    result = (
        middle
        + jnp.dot(activated, gathered[4], preferred_element_type=jnp.float32)
        + gathered[5].astype(jnp.float32)
    )
    layer_out = result.astype(jnp.bfloat16).reshape(1, 2, local_count, model_dim)
    again = (
        lax.all_gather(own_params[0], "fsdp", axis=0, tiled=True),
        lax.all_gather(own_params[1], "fsdp", axis=0, tiled=True),
        lax.all_gather(own_params[2], "fsdp", axis=0, tiled=True),
        lax.all_gather(own_params[3], "fsdp", axis=0, tiled=True),
        lax.all_gather(own_params[4], "fsdp", axis=0, tiled=True),
        lax.all_gather(own_params[5], "fsdp", axis=0, tiled=True),
        lax.all_gather(own_params[6], "fsdp", axis=0, tiled=True),
        lax.all_gather(own_params[7], "fsdp", axis=0, tiled=True),
        lax.all_gather(own_params[8], "fsdp", axis=0, tiled=True),
    )
    normed, query_rows, key_rows, value_rows = project(inputs, again, angles)
    noisy_keys = key_rows[local_count:]
    noisy_values = value_rows[local_count:]
    middle, normed_two, upper, activated = upper_half(inputs, attended_low, again)
    grad_rows = out_grad[0].reshape(row_count, model_dim)
    grad_float = grad_rows.astype(jnp.float32)
    grad_down = jnp.einsum("qi,qj->ij", activated, grad_rows, preferred_element_type=jnp.float32)
    grad_down_bias = jnp.sum(grad_float, axis=0)
    activated_grad = jnp.einsum(
        "qj,ij->qi", grad_rows, again[4], preferred_element_type=jnp.float32
    )
    _, gelu_pull = jax.vjp(lambda upper_in: jax.nn.gelu(upper_in, approximate=True), upper)
    upper_grad = gelu_pull(activated_grad)[0].astype(jnp.bfloat16)
    grad_up = jnp.einsum("qi,qj->ij", normed_two, upper_grad, preferred_element_type=jnp.float32)
    grad_up_bias = jnp.sum(upper_grad.astype(jnp.float32), axis=0)
    normed_two_grad = jnp.einsum(
        "qj,ij->qi", upper_grad, again[2], preferred_element_type=jnp.float32
    )
    _, second_pull = jax.vjp(layer_norm, middle, again[7].astype(jnp.float32))
    middle_norm_grad, grad_gain_two = second_pull(normed_two_grad)
    middle_grad = (grad_float + middle_norm_grad).astype(jnp.bfloat16)
    grad_out_proj = jnp.einsum(
        "qi,qj->ij", attended_low, middle_grad, preferred_element_type=jnp.float32
    )
    attended_grad = jnp.einsum(
        "qj,ij->qi", middle_grad, again[1], preferred_element_type=jnp.float32
    )
    attended_grad = jnp.transpose(attended_grad.reshape(row_count, HEADS, HEAD_DIM), (1, 0, 2))
    scaled_grad = (attended_grad / run_sum[..., None]).astype(jnp.bfloat16)
    correction = jnp.sum(attended_grad * attended, axis=-1) / run_sum
    pair_rows = (
        lax.all_gather(
            key_rows[:local_count].reshape(local_count, model_dim), "ctx", axis=0, tiled=True
        ),
        lax.all_gather(
            value_rows[:local_count].reshape(local_count, model_dim), "ctx", axis=0, tiled=True
        ),
    )
    pair_keys, pair_values = pair_rows
    total_rows = pair_keys.shape[0]
    tile_size = math.gcd(total_rows, 512)
    zero_tile = jnp.zeros((tile_size, HEADS, HEAD_DIM), jnp.float32)

    def back_step(query_acc, tile_index):
        tile_start = tile_index * tile_size
        key_tile = lax.dynamic_slice_in_dim(pair_keys, tile_start, tile_size, 0).reshape(
            tile_size, HEADS, HEAD_DIM
        )
        value_tile = lax.dynamic_slice_in_dim(pair_values, tile_start, tile_size, 0).reshape(
            tile_size, HEADS, HEAD_DIM
        )
        key_position = tile_start + jnp.arange(tile_size, dtype=jnp.int32)
        allowed = visible(
            stream,
            positions,
            segments,
            jnp.zeros((tile_size,), jnp.int32),
            key_position,
            segment_of(key_position, doc_ends),
        )

        def live_tile(held):
            query_part, key_part, value_part = tile_grads(
                query_rows, key_tile, value_tile, allowed, run_max, scaled_grad, correction
            )
            return (held + query_part, key_part, value_part)

        query_acc, key_part, value_part = lax.cond(
            jnp.any(allowed), live_tile, lambda held: (held, zero_tile, zero_tile), query_acc
        )
        return (
            query_acc,
            (key_part.reshape(tile_size, model_dim), value_part.reshape(tile_size, model_dim)),
        )

    query_acc, (key_terms, value_terms) = lax.scan(
        back_step,
        jnp.zeros((row_count, HEADS, HEAD_DIM), jnp.float32),
        jnp.arange(total_rows // tile_size),
    )
    key_terms = key_terms.reshape(total_rows, model_dim)
    value_terms = value_terms.reshape(total_rows, model_dim)
    clean_key_grad, clean_value_grad = (
        lax.psum_scatter(
            key_terms.astype(jnp.bfloat16), "ctx", scatter_dimension=0, tiled=True
        ).astype(jnp.float32),
        lax.psum_scatter(
            value_terms.astype(jnp.bfloat16), "ctx", scatter_dimension=0, tiled=True
        ).astype(jnp.float32),
    )
    query_part, noisy_key_part, noisy_value_part = tile_grads(
        query_rows, noisy_keys, noisy_values, noisy_allowed, run_max, scaled_grad, correction
    )
    query_grad = (query_acc + query_part) * 0.125
    key_grad = (
        jnp.concatenate(
            [clean_key_grad.reshape(local_count, HEADS, HEAD_DIM), noisy_key_part], axis=0
        )
        * 0.125
    )
    value_grad = jnp.concatenate(
        [clean_value_grad.reshape(local_count, HEADS, HEAD_DIM), noisy_value_part], axis=0
    )
    _, rotate_pull = jax.vjp(lambda heads_in: rotate(heads_in, angles), query_grad)
    query_raw_grad = rotate_pull(query_grad)[0]
    key_raw_grad = rotate_pull(key_grad)[0]
    projected_grad = jnp.concatenate(
        [
            query_raw_grad.reshape(row_count, model_dim),
            key_raw_grad.reshape(row_count, model_dim),
            value_grad.reshape(row_count, model_dim),
        ],
        axis=1,
    ).astype(jnp.bfloat16)
    grad_qkv = jnp.einsum("qi,qj->ij", normed, projected_grad, preferred_element_type=jnp.float32)
    normed_grad = jnp.einsum(
        "qj,ij->qi", projected_grad, again[0], preferred_element_type=jnp.float32
    )
    _, first_pull = jax.vjp(layer_norm, inputs, again[6].astype(jnp.float32))
    inputs_norm_grad, grad_gain_one = first_pull(normed_grad)
    inputs_grad = middle_grad.astype(jnp.float32) + inputs_norm_grad
    noisy_flag = (noise_row == 1)[:, None]
    noisy_grad = inputs_grad[local_count:]
    grad_mask = jnp.sum(jnp.where(noisy_flag, noisy_grad, 0.0), axis=0)
    input_grad = jnp.concatenate(
        [inputs_grad[:local_count], jnp.where(noisy_flag, 0.0, noisy_grad)], axis=0
    )
    input_grad = input_grad.astype(jnp.bfloat16).reshape(1, 2, local_count, model_dim)
    shares = (
        lax.psum_scatter(grad_qkv, ("ctx", "fsdp"), scatter_dimension=0, tiled=True),
        lax.psum_scatter(grad_out_proj, ("ctx", "fsdp"), scatter_dimension=0, tiled=True),
        lax.psum_scatter(grad_up, ("ctx", "fsdp"), scatter_dimension=0, tiled=True),
        lax.psum_scatter(grad_up_bias, ("ctx", "fsdp"), scatter_dimension=0, tiled=True),
        lax.psum_scatter(grad_down, ("ctx", "fsdp"), scatter_dimension=0, tiled=True),
        lax.psum_scatter(grad_down_bias, ("ctx", "fsdp"), scatter_dimension=0, tiled=True),
        lax.psum_scatter(grad_gain_one, ("ctx", "fsdp"), scatter_dimension=0, tiled=True),
        lax.psum_scatter(grad_gain_two, ("ctx", "fsdp"), scatter_dimension=0, tiled=True),
        lax.psum_scatter(grad_mask, ("ctx", "fsdp"), scatter_dimension=0, tiled=True),
    )
    (
        qkv_share,
        out_share,
        up_share,
        up_bias_share,
        down_share,
        down_bias_share,
        gain_one_share,
        gain_two_share,
        mask_share,
    ) = shares
    return (
        layer_out,
        input_grad,
        qkv_share,
        out_share,
        up_share,
        up_bias_share,
        down_share,
        down_bias_share,
        gain_one_share,
        gain_two_share,
        mask_share,
    )


CHUNK = 256
COST = 10**9
GROUP = 3
WIDE = GROUP * HEAD_DIM
HALF = HEAD_DIM // 2
LANES = GROUP * CHUNK
BF = jnp.bfloat16
F32 = jnp.float32
HB = pl.BlockSpec(memory_space=pltpu.HBM)
SM = pl.BlockSpec(memory_space=pltpu.SMEM)
GELU_SCALE = math.sqrt(2.0 / math.pi)


def swap(v, bit):
    return lax.ppermute(v, "ctx", [(i, i ^ bit) for i in range(8)])


def turn(v, step):
    return lax.ppermute(v, "fsdp", [(i, (i + step) % 4) for i in range(4)])


def mm(a, b, ca=1, cb=0):
    return lax.dot_general(a, b, (((ca,), (cb,)), ((), ())), preferred_element_type=F32)


def flip(v):
    return jnp.transpose(v.astype(F32)).astype(v.dtype)


def call(body, outs, kinds, args, scratch=(), flops=0, moved=0, raw=()):
    staged = [i for i, kind in enumerate(kinds) if kind == "V"]
    space = {"S": SM, "V": HB, "A": HB}
    count = len(args)
    kept = [k for k in range(len(outs)) if k not in raw]
    made = len(kept)

    def run(*refs):
        ins, sinks, rest = list(refs[:count]), list(refs[count : count + len(outs)]), refs[count + len(outs) :]
        held, buffers = rest[: len(staged)], rest[len(staged) : len(staged) + made]
        results = list(sinks)
        for i, k in enumerate(kept):
            results[k] = buffers[i]
        sem_in, sem_out, sems = rest[len(staged) + made : len(staged) + made + 3]
        rest = rest[len(staged) + made + 3 :]
        first = [
            pltpu.make_async_copy(ins[i], held[k], sem_in.at[k]) for k, i in enumerate(staged)
        ]
        for copy in first:
            copy.start()
        for k, i in enumerate(staged):
            ins[i] = held[k]

        def load(pairs):
            more = [pltpu.make_async_copy(a, b, sems.at[i]) for i, (a, b) in enumerate(pairs)]
            for copy in more:
                copy.start()
            for copy in more + first:
                copy.wait()

        body(load, *ins, *results, *rest)
        last = [pltpu.make_async_copy(results[k], sinks[k], sem_out.at[i]) for i, k in enumerate(kept)]
        for copy in last:
            copy.start()
        for copy in last:
            copy.wait()

    return pl.pallas_call(
        run,
        out_shape=tuple(jax.ShapeDtypeStruct(s, d) for s, d in outs),
        in_specs=[space[kind] for kind in kinds],
        out_specs=tuple(HB for _ in outs),
        scratch_shapes=[pltpu.VMEM(args[i].shape, args[i].dtype) for i in staged]
        + [pltpu.VMEM(*outs[k]) for k in kept]
        + [
            pltpu.SemaphoreType.DMA((max(1, len(staged)),)),
            pltpu.SemaphoreType.DMA((made,)),
            pltpu.SemaphoreType.DMA((48,)),
        ]
        + list(scratch),
        compiler_params=pltpu.CompilerParams(vmem_limit_bytes=56 * 2**20),
        cost_estimate=pl.CostEstimate(flops=1 + flops // COST, bytes_accessed=1 + moved // COST, transcendentals=0),
    )(*args)


def at16(v):
    return pl.multiple_of(v, 16)


def shard_rows(meta, near, far, dst, unit):
    half = unit // 2
    pairs = []
    for zz in range(4):
        for core, part in ((meta[1], near), (1 - meta[1], far)):
            to = at16(zz * unit + core * half)
            pairs.append((part.at[zz, pl.ds(0, half)], dst.at[pl.ds(to, half)]))
    return pairs


def norm_parts(x):
    mean = jnp.mean(x, axis=-1, keepdims=True)
    centered = x - mean
    var = jnp.mean(centered * centered, axis=-1, keepdims=True)
    scale = lax.rsqrt(var + EPSILON)
    return centered * scale, scale


def unmark(x, embed):
    x = x.astype(F32)
    flag = x[:, :1] > 1e38
    return jnp.where(flag, embed, x), flag


def turn_heads(v, cos, sin):
    parts = []
    for g in range(GROUP):
        a = v[g * HEAD_DIM : g * HEAD_DIM + HALF]
        b = v[g * HEAD_DIM + HALF : (g + 1) * HEAD_DIM]
        parts += [a * cos - b * sin, b * cos + a * sin]
    return jnp.concatenate(parts, axis=0)


def project_body(load, meta, gain, embed, cos, sin, *refs):
    rows, refs = refs[:8], refs[8:]
    near, far, q_ref, kv_a, kv_b, n_out, mk_ref, w, xs, wp, n_ref, out_sems = refs
    load(shard_rows(meta, near, far, w, 192) + [(rows[i], xs.at[i]) for i in range(8)])
    for part in range(3):
        wp[part] = w[:, part * WIDE : (part + 1) * WIDE]

    @pl.loop(0, 8)
    def _(i):
        x, flag = unmark(xs[i], embed[...])
        hat, _ = norm_parts(x)
        n = (hat * gain[...]).astype(BF)
        n_ref[i] = n
        pltpu.make_async_copy(n_ref.at[i], n_out.at[i], out_sems.at[i]).start()
        mk_ref[i] = jnp.broadcast_to(jnp.where(flag, 1.0, 0.0), (CHUNK, 128)).astype(BF)
        q_ref[i] = turn_heads(jnp.transpose(mm(n, wp[0])), cos[i], sin[i]).astype(BF)
        keys = turn_heads(jnp.transpose(mm(n, wp[1])), cos[i], sin[i]).astype(BF)
        values = jnp.transpose(mm(n, wp[2])).astype(BF)
        for half, ref in enumerate((kv_a, kv_b)):

            @pl.when(i // 4 == half)
            def _():
                ref[i % 4, :WIDE] = keys
                ref[i % 4, WIDE:] = values

    for i in range(8):
        pltpu.make_async_copy(n_ref.at[i], n_out.at[i], out_sems.at[i]).wait()


def project_rows(meta, gain, embed, cos, sin, rows, weights):
    dim = rows[0].shape[1]
    wide = weights[0].shape[-1]
    return call(
        project_body,
        [
            ((8, WIDE, CHUNK), BF),
            ((4, 2 * WIDE, CHUNK), BF),
            ((4, 2 * WIDE, CHUNK), BF),
            ((8, CHUNK, dim), BF),
            ((8, CHUNK, 128), BF),
            ((dim, wide), BF),
        ],
        "SVVVV" + "A" * 10,
        (meta, gain, embed, cos, sin, *rows, *weights),
        scratch=[
            pltpu.VMEM((8, CHUNK, dim), BF),
            pltpu.VMEM((3, dim, WIDE), BF),
            pltpu.VMEM((8, CHUNK, dim), BF),
            pltpu.SemaphoreType.DMA((8,)),
        ],
        raw=(3,),
        flops=2 * 8 * CHUNK * dim * 3 * WIDE,
        moved=8 * CHUNK * dim * 6,
    )


def head_pairs(refs, qs, kv):
    pairs = [(refs[0], qs)]
    for i, ref in enumerate(refs[1:]):
        pairs.append((ref, kv.at[i // 2, pl.ds(i % 2 * 4, 4)]))
    return pairs


def thrice(v):
    return jnp.concatenate([v, v, v], axis=1)


def scores_of(keys, stacked, base, low, high, plain):
    s = mm(keys, stacked)
    if plain:
        return s
    place = base + lax.broadcasted_iota(jnp.int32, s.shape, 0)
    return jnp.where((place >= low) & (place < high), s, LOWEST)


def head_lanes(v, g):
    return None if v is None else v[:, g * CHUNK : (g + 1) * CHUNK]


def each_tile(meta, p, lims, tile, halves):
    r, c = meta[0], meta[1]

    @pl.loop(meta[4 + p], p + 1)
    def _(k):
        own = (k == p) & (c == 0)
        slot = jnp.where(own, p ^ r, k ^ r ^ c)
        whole = (k < p) & (meta[12 + p] <= k * CHUNK)

        @pl.when(whole)
        def _():
            tile(slot, own, k * CHUNK, None, None, True)

        @pl.when(jnp.logical_not(whole))
        def _():
            tile(slot, own, k * CHUNK, lims[0], lims[1], False)

    @pl.when(c != 0)
    def _():
        halves(p ^ r, p * CHUNK, lims[2], lims[3])


HALF_CHUNK = CHUNK // 2


def half_lanes(v, half):
    return jnp.concatenate([v[:, half_span(g, half)] for g in range(GROUP)], axis=1)


def half_span(g, half):
    first = g * CHUNK + half * HALF_CHUNK
    return slice(first, first + HALF_CHUNK)


def stack_heads(q, stacked):
    for g in range(GROUP):
        stacked[g * HEAD_DIM : (g + 1) * HEAD_DIM, g * CHUNK : (g + 1) * CHUNK] = q[
            g * HEAD_DIM : (g + 1) * HEAD_DIM
        ]


def attend_body(load, meta, bounds, *refs):
    heads = refs[:5]
    send, o_ref, ml_ref, qs, kv, kr, stacked, m_s, l_s, acc = refs[5:]
    load(head_pairs(heads, qs, kv))
    stacked[...] = jnp.zeros_like(stacked)

    @pl.loop(0, 8)
    def _(s):
        for own in range(2):
            kr[own, s] = flip(kv[own, s, :WIDE])

    r, c = meta[0], meta[1]

    @pl.loop(0, 8)
    def _(p):
        s = p ^ r
        stack_heads(qs[s] * 0.125, stacked)
        lims = [thrice(bounds[p, i : i + 1]) for i in range(4)]

        def tile(slot, own, base, lo, hi, plain):
            keys = kr[c, slot]
            scores = [
                scores_of(keys, head_lanes(stacked, g), base, head_lanes(lo, g), head_lanes(hi, g), plain)
                for g in range(GROUP)
            ]
            for g in range(GROUP):
                cut = slice(g * CHUNK, (g + 1) * CHUNK)
                first = WIDE + g * HEAD_DIM
                m_old = m_s[:, cut]
                m_new = jnp.maximum(m_old, jnp.max(scores[g], axis=0, keepdims=True))
                e = jnp.exp(scores[g] - m_new)
                f = jnp.exp(m_old - m_new)
                m_s[:, cut] = m_new
                l_s[:, cut] = l_s[:, cut] * f + jnp.sum(e, axis=0, keepdims=True)
                acc[g] = acc[g] * f + mm(kv[c, slot, first : first + HEAD_DIM], e.astype(BF))

        def halves(slot, base, lo, hi):
            for half in range(2):
                keys = slice(half * HALF_CHUNK, (half + 1) * HALF_CHUNK)
                masked = scores_of(
                    kr[0, slot, keys], half_lanes(stacked[...], half), base + half * HALF_CHUNK,
                    half_lanes(lo, half), half_lanes(hi, half), False,
                )
                m_old = half_lanes(m_s[...], half)
                m_new = jnp.maximum(m_old, jnp.max(masked, axis=0, keepdims=True))
                e = jnp.exp(masked - m_new)
                f = jnp.exp(m_old - m_new)
                total = half_lanes(l_s[...], half) * f + jnp.sum(e, axis=0, keepdims=True)
                e = e.astype(BF)
                for g in range(GROUP):
                    cut = slice(g * HALF_CHUNK, (g + 1) * HALF_CHUNK)
                    first = WIDE + g * HEAD_DIM
                    m_s[:, half_span(g, half)] = m_new[:, cut]
                    l_s[:, half_span(g, half)] = total[:, cut]
                    new = mm(kv[0, slot, first : first + HEAD_DIM, keys], e[:, cut])
                    acc[g, :, keys] = acc[g, :, keys] * f[:, cut] + new

        m_s[...] = jnp.full_like(m_s, LOWEST)
        l_s[...] = jnp.zeros_like(l_s)
        acc[...] = jnp.zeros_like(acc)
        each_tile(meta, p, lims, tile, halves)
        total = l_s[...]
        inv = 1.0 / total
        out = jnp.concatenate(
            [acc[g] * inv[:, g * CHUNK : (g + 1) * CHUNK] for g in range(GROUP)], axis=0
        )
        o_ref[s] = out
        ml_ref[s, 0:1] = m_s[...]
        ml_ref[s, 1:2] = total
        send[p] = out.astype(BF)


HEAD_SCRATCH = [pltpu.VMEM((8, WIDE, CHUNK), BF), pltpu.VMEM((2, 8, 2 * WIDE, CHUNK), BF)]


def attend_rows(meta, bounds, heads):
    return call(
        attend_body,
        [((8, WIDE, CHUNK), BF), ((8, WIDE, CHUNK), F32), ((8, 8, LANES), F32)],
        "SV" + "A" * 5,
        (meta, bounds, *heads),
        scratch=HEAD_SCRATCH
        + [
            pltpu.VMEM((2, 8, CHUNK, WIDE), BF),
            pltpu.VMEM((WIDE, LANES), BF),
            pltpu.VMEM((1, LANES), F32),
            pltpu.VMEM((1, LANES), F32),
            pltpu.VMEM((GROUP, HEAD_DIM, CHUNK), F32),
        ],
        flops=20 * 2 * 2 * CHUNK * LANES * 256,
        moved=8 * CHUNK * WIDE * 16,
    )


def rows_body(load, *refs):
    kv, (k_rows, v_rows) = refs[:4], refs[4:]
    load([])
    for i in range(4):

        @pl.loop(0, 4)
        def _(s):
            k_rows[i // 2, i % 2 * 4 + s] = flip(kv[i][s, :WIDE])
            v_rows[i // 2, i % 2 * 4 + s] = flip(kv[i][s, WIDE:])


def rows_of_heads(heads):
    return call(rows_body, [((2, 8, CHUNK, WIDE), BF)] * 2, "VVVV", heads[1:], flops=1)


def attend_back_body(load, meta, bounds, cos, sin, o_ref, ml_ref, *refs):
    heads, k_rows, v_rows, gs = refs[:5], refs[5], refs[6], refs[7]
    (
        pq_ref, own_ref, far_a, far_b,
        qs, kv, kr, vr, st_q, st_g, row_q, row_g, dk, dv, dq,
    ) = refs[8:]
    for ref in (st_q, st_g, dk, dv):
        ref[...] = jnp.zeros_like(ref)
    load(head_pairs(heads, qs, kv) + [(k_rows, kr), (v_rows, vr)])
    r, c = meta[0], meta[1]
    lane = lax.broadcasted_iota(jnp.int32, (CHUNK, WIDE), 1) // HEAD_DIM

    @pl.loop(0, 8)
    def _(p):
        s = p ^ r
        q = qs[s] * 0.125
        stack_heads(q, st_q)
        total = ml_ref[s, 1:2]
        top = ml_ref[s, 0:1]
        g_in = gs[p].astype(F32)
        attended = o_ref[s]
        scaled, fix = [], []
        for g in range(GROUP):
            part = slice(g * HEAD_DIM, (g + 1) * HEAD_DIM)
            inv = 1.0 / total[:, g * CHUNK : (g + 1) * CHUNK]
            scaled.append(g_in[part] * inv)
            fix.append(jnp.sum(g_in[part] * attended[part], axis=0, keepdims=True) * inv)
        scaled = jnp.concatenate(scaled, axis=0)
        fix = jnp.concatenate(fix, axis=1)
        stack_heads(scaled.astype(BF), st_g)
        q_rows = jnp.transpose(q.astype(F32))
        g_rows = jnp.transpose(scaled)
        for g in range(GROUP):
            row_q[g * CHUNK : (g + 1) * CHUNK] = jnp.where(lane == g, q_rows, 0.0).astype(BF)
            row_g[g * CHUNK : (g + 1) * CHUNK] = jnp.where(lane == g, g_rows, 0.0).astype(BF)
        lims = [thrice(bounds[p, i : i + 1]) for i in range(4)]
        dq[...] = jnp.zeros_like(dq)

        def tile(slot, own, base, lo, hi, plain):
            e = jnp.exp(scores_of(kr[c, slot], st_q[...], base, lo, hi, plain) - top)
            d = (e * (mm(vr[c, slot], st_g[...]) - fix)).astype(BF)
            e = e.astype(BF)
            kind = jnp.where(own, 0, 1)
            dv[kind, slot] += mm(e, row_g[...])
            dk[kind, slot] += mm(d, row_q[...])
            for g in range(GROUP):
                part = slice(g * HEAD_DIM, (g + 1) * HEAD_DIM)
                dq[part] += mm(kv[c, slot, part], d[:, g * CHUNK : (g + 1) * CHUNK])

        def halves(slot, base, lo, hi):
            for half in range(2):
                keys = slice(half * HALF_CHUNK, (half + 1) * HALF_CHUNK)
                s_half = scores_of(
                    kr[0, slot, keys], half_lanes(st_q[...], half), base + half * HALF_CHUNK,
                    half_lanes(lo, half), half_lanes(hi, half), False,
                )
                e = jnp.exp(s_half - half_lanes(top, half))
                d = e * (mm(vr[0, slot, keys], half_lanes(st_g[...], half)) - half_lanes(fix, half))
                e, d = e.astype(BF), d.astype(BF)
                rows_of = [jnp.concatenate([ref[half_span(g, half)] for g in range(GROUP)]) for ref in (row_g, row_q)]
                dv[0, slot, keys] += mm(e, rows_of[0])
                dk[0, slot, keys] += mm(d, rows_of[1])
                for g in range(GROUP):
                    part = slice(g * HEAD_DIM, (g + 1) * HEAD_DIM)
                    cut = slice(g * HALF_CHUNK, (g + 1) * HALF_CHUNK)
                    dq[part, keys] += mm(kv[0, slot, part, keys], d[:, cut])

        each_tile(meta, p, lims, tile, halves)
        pq_ref[s] = turn_heads(dq[...] * 0.125, cos[s], -sin[s]).astype(BF)

    both = 1.0 - c.astype(F32)

    @pl.loop(0, 8)
    def _(s):
        far_k, far_v = jnp.transpose(dk[1, s]), jnp.transpose(dv[1, s])
        for half, far_ref in enumerate((far_a, far_b)):

            @pl.when(s // 4 == half)
            def _():
                far_ref[s % 4, :WIDE] = far_k.astype(BF)
                far_ref[s % 4, WIDE:] = far_v.astype(BF)

        own_ref[s, :WIDE] = (jnp.transpose(dk[0, s]) + both * far_k).astype(BF)
        own_ref[s, WIDE:] = (jnp.transpose(dv[0, s]) + both * far_v).astype(BF)


def attend_back(meta, bounds, cos, sin, attended, stats, heads, rows_first, grads):
    rows = pltpu.VMEM((2, 8, CHUNK, WIDE), BF)
    sums = pltpu.VMEM((2, 8, CHUNK, WIDE), F32)
    return call(
        attend_back_body,
        [((8, WIDE, CHUNK), BF), ((8, 2 * WIDE, CHUNK), BF)] + [((4, 2 * WIDE, CHUNK), BF)] * 2,
        "SVVVVV" + "A" * 7 + "V",
        (meta, bounds, cos, sin, attended, stats, *heads, *rows_first, grads),
        scratch=HEAD_SCRATCH
        + [
            rows,
            rows,
            pltpu.VMEM((WIDE, LANES), BF),
            pltpu.VMEM((WIDE, LANES), BF),
            pltpu.VMEM((LANES, WIDE), BF),
            pltpu.VMEM((LANES, WIDE), BF),
        ]
        + [sums] * 2
        + [pltpu.VMEM((WIDE, CHUNK), F32)],
        flops=20 * 2 * 5 * CHUNK * LANES * 256,
        moved=8 * CHUNK * WIDE * 30,
    )


def share_pairs(meta, own, parts, dst, unit, skip):
    h, z = meta[2], meta[3]
    part = unit // 4
    pairs = [(own, dst.at[pl.ds(at16(z * unit), unit)])]
    for t in range(1, 4):
        zz = (z + 4 - t) & 3
        for k in range(4):
            to = at16(zz * unit + (h ^ k) * part)
            pairs.append((parts[k].at[t - 1, pl.ds(skip, part)], dst.at[pl.ds(to, part)]))
    return pairs


def middle_body(load, meta, gain, embed, x_ref, heads, own, *refs):
    mid_ref, n_ref, att_ref, w_ref = refs[4:]
    pairs = share_pairs(meta, own, refs[:4], w_ref, 192, 0)
    for d in range(8):
        pairs.append((heads.at[d], att_ref.at[d % 2, pl.ds(d // 2 * WIDE, WIDE)]))
    load(pairs)

    @pl.loop(0, 2)
    def _(stream):
        x, _ = unmark(x_ref[stream], embed[...])
        mid = x + mm(att_ref[stream], w_ref[...], 0, 0)
        hat, _ = norm_parts(mid)
        mid_ref[stream] = mid
        n_ref[pl.ds(pl.multiple_of(stream * CHUNK, CHUNK), CHUNK)] = (hat * gain[...]).astype(BF)


def middle_rows(meta, gain, embed, marked, heads, own, parts):
    dim = marked.shape[2]
    return call(
        middle_body,
        [((2, CHUNK, dim), F32), ((2 * CHUNK, dim), BF), ((2, dim, CHUNK), BF), ((dim, dim), BF)],
        "SVVV" + "A" * 6,
        (meta, gain, embed, marked, heads, own, *parts),
        flops=2 * 2 * CHUNK * dim * dim,
        moved=8 * CHUNK * dim * 2,
    )


def feed_body(load, meta, bias, n_own, n_far, g_own, g_far, up_own, down_own, *refs):
    shares, refs = refs[:4], refs[4:]
    (
        *sinks, gb_ref, d_out, u_ref,
        ns, gs, wu, wd, acts, slopes, out_ref, outf_ref, ngf_ref, ng_ref, d_ref, out_sems,
    ) = refs
    c, h, z = meta[1], meta[2], meta[3]
    rows = 2 * CHUNK
    part = bias.shape[1] // 4
    pairs = [
        (n_own, ns.at[pl.ds(0, rows)]),
        (n_far, ns.at[pl.ds(rows, rows)]),
        (g_own, gs.at[pl.ds(0, rows)]),
        (g_far, gs.at[pl.ds(rows, rows)]),
    ]
    pairs += share_pairs(meta, down_own.at[pl.ds(at16(c * part), part)], shares, wd, part, 48)
    for k in range(4):
        cols = pl.ds(pl.multiple_of(k * 2 * part + c * part, 128), part)
        pairs.append((up_own.at[:, cols], wu.at[pl.ds(at16(z * 192), 192), pl.ds(k * part, part)]))
    for t in range(1, 4):
        zz = (z + 4 - t) & 3
        for k in range(4):
            dst = pl.ds(at16(zz * 192 + (h ^ k) * 48), 48)
            for b in range(2):
                pairs.append(
                    (
                        shares[k].at[t - 1, pl.ds(144 + 48 * b, 48)],
                        wu.at[dst, pl.ds(2 * part * b, 2 * part)],
                    )
                )
    load(pairs)
    gb_ref[...] = jnp.zeros_like(gb_ref)

    @pl.loop(0, 4)
    def _(i):
        span = pl.ds(pl.multiple_of(i * CHUNK, CHUNK), CHUNK)
        v = mm(ns[span], wu[...]) + bias[...]
        square = v * v
        th = jnp.tanh(v * (GELU_SCALE + (GELU_SCALE * 0.044715) * square))
        half = 0.5 + 0.5 * th
        act = (v * half).astype(BF)
        slope = half + (v * half) * (1.0 - th) * (GELU_SCALE + (3.0 * 0.044715 * GELU_SCALE) * square)
        acts[span] = act
        ug = (slope * mm(gs[span], wd[...], 1, 1)).astype(BF)
        slopes[span] = ug
        gb_ref[...] += jnp.sum(ug.astype(F32), axis=0, keepdims=True)
        out = mm(act, wd[...]).astype(BF)
        ng = mm(ug, wu[...], 1, 1).astype(BF)
        to = pl.ds(pl.multiple_of((i & 1) * CHUNK, CHUNK), CHUNK)

        @pl.when(i < 2)
        def _():
            out_ref[to] = out
            ng_ref[to] = ng

        @pl.when(i >= 2)
        def _():
            outf_ref[to] = out
            ngf_ref[to] = ng

    early = [
        pltpu.make_async_copy(ref, sinks[k], out_sems.at[k])
        for k, ref in enumerate((out_ref, outf_ref, ngf_ref, ng_ref))
    ]
    for copy in early:
        copy.start()

    @pl.loop(0, 4)
    def _(j):
        cols = pl.ds(pl.multiple_of(j * part, 128), part)
        gd = mm(acts[:, cols], gs[...], 0, 0).astype(BF)
        for b in range(4):
            d_ref[b, j ^ h] = gd[96 * b : 96 * (b + 1)]
        pltpu.make_async_copy(d_ref.at[:, j ^ h], d_out.at[:, j ^ h], out_sems.at[4 + j]).start()
        gu = mm(ns[...], slopes[:, cols], 0, 0)
        side = pl.ds(pl.multiple_of((j & 1) * part, 128), part)
        line = pl.ds(at16((j >> 1) * 48), 48)
        for b in range(16):
            first = 192 * (b // 4) + 24 * (b % 4)
            block = jnp.concatenate([gu[first : first + 24], gu[first + 96 : first + 120]])
            u_ref[(b // 4) ^ h, b % 4, line, side] = block.astype(BF)

    for copy in early:
        copy.wait()
    for j in range(4):
        pltpu.make_async_copy(d_ref.at[:, j ^ h], d_out.at[:, j ^ h], out_sems.at[4 + j]).wait()


def feed_rows(meta, bias, args):
    rows = 2 * CHUNK
    dim = args[0].shape[1]
    hid = bias.shape[1]
    return call(
        feed_body,
        [((rows, dim), BF)] * 4
        + [((1, hid), F32)]
        + [((4, 4, hid // 16, dim), BF)] * 2,
        "SV" + "A" * 10,
        (meta, bias, *args),
        scratch=[
            pltpu.VMEM((2 * rows, dim), BF),
            pltpu.VMEM((2 * rows, dim), BF),
            pltpu.VMEM((dim, hid), BF),
            pltpu.VMEM((hid, dim), BF),
            pltpu.VMEM((2 * rows, hid), BF),
            pltpu.VMEM((2 * rows, hid), BF),
        ]
        + [pltpu.VMEM((rows, dim), BF)] * 4
        + [pltpu.VMEM((4, 4, hid // 16, dim), BF), pltpu.SemaphoreType.DMA((8,))],
        raw=(0, 1, 2, 3, 5),
        flops=6 * 2 * 2 * rows * dim * hid,
        moved=12 * dim * hid,
    )


def pack_body(load, meta, w_out, w_down, w_up, share):
    c, h = meta[1], meta[2]
    part = w_up.shape[1] // 8
    pairs = [
        (w_out.at[pl.ds(at16(48 * h), 48)], share.at[pl.ds(0, 48)]),
        (w_down.at[pl.ds(at16(part * c + 96 * h), 96)], share.at[pl.ds(48, 96)]),
    ]
    for k in range(4):
        cols = pl.ds(pl.multiple_of((2 * k + c) * part, 128), part)
        to = share.at[pl.ds(144 + 48 * (k // 2), 48), pl.ds(part * (k % 2), part)]
        pairs.append((w_up.at[pl.ds(at16(48 * h), 48), cols], to))
    load(pairs)


def pack_share(place, w_out, w_down, w_up):
    return call(pack_body, [((240, w_out.shape[1]), BF)], "SAAA", (place, w_out, w_down, w_up))[0]


def middle_back_body(
    load, meta, gain, b_down, mid_ref, ng_ref, out_ref, outf_ref, ngf_ref, g_ref, x_ref, w_ref,
    lay_ref, mg_ref, sum_ref, send,
):
    load([])
    sum_ref[...] = jnp.zeros_like(sum_ref)

    @pl.loop(0, 2)
    def _(stream):
        span = pl.ds(pl.multiple_of(stream * CHUNK, CHUNK), CHUNK)
        mid = mid_ref[stream]
        lay = mid + out_ref[span].astype(F32) + outf_ref[span].astype(F32) + b_down[...]
        lay_ref[stream] = lay.astype(BF)
        hat, scale = norm_parts(mid)
        ng = ng_ref[span].astype(F32) + ngf_ref[span].astype(F32)
        sum_ref[0:1] += jnp.sum(ng * hat, axis=0, keepdims=True)
        t = ng * gain[...]
        g = g_ref[stream].astype(F32)
        sum_ref[1:2] += jnp.sum(g, axis=0, keepdims=True)
        t_mean = jnp.mean(t, axis=-1, keepdims=True)
        t_hat = jnp.mean(t * hat, axis=-1, keepdims=True)
        mg = (g + scale * (t - t_mean - hat * t_hat)).astype(BF)
        mg_ref[stream] = mg
        flag = (x_ref[stream][:, :1].astype(F32) > 1e38) & (stream == 1)
        sum_ref[2:3] += jnp.sum(jnp.where(flag, mg.astype(F32), 0.0), axis=0, keepdims=True)
        for d in range(4):
            send[2 * d + stream] = mm(w_ref[d * WIDE : (d + 1) * WIDE], mg, 1, 1).astype(BF)


def middle_back(meta, gain, b_down, args):
    dim = gain.shape[1]
    return call(
        middle_back_body,
        [((2, CHUNK, dim), BF), ((2, CHUNK, dim), BF), ((8, dim), F32), ((8, WIDE, CHUNK), BF)],
        "S" + "V" * 10,
        (meta, gain, b_down, *args),
        flops=4 * CHUNK * dim * dim,
        moved=20 * CHUNK * dim,
    )


def by_z(grad, ref):
    for zz in range(4):
        for h in range(4):
            first = 192 * h + 24 * zz
            pair = jnp.concatenate([grad[first : first + 24], grad[first + 96 : first + 120]])
            ref[zz, 48 * h : 48 * (h + 1)] = pair.astype(BF)


def out_grad_body(load, meta, att_ref, mg_ref, up, *o_refs):
    load([(up.at[k], o_refs[k].at[:, pl.ds(0, 96)]) for k in range(4)])
    grad = mm(att_ref[0], mg_ref[0]) + mm(att_ref[1], mg_ref[1])
    for owner in range(4):
        blocks = []
        for b in range(4):
            first = 192 * owner + 24 * b
            blocks.append(jnp.concatenate([grad[first : first + 24], grad[first + 96 : first + 120]]).astype(BF))
        for k in range(4):

            @pl.when((owner ^ meta[2]) == k)
            def _():
                for b in range(4):
                    o_refs[k][b, 96:] = blocks[b]


def project_back_body(
    own, f0, f1, pq, n_ref, mk_ref, cos, sin, w_ref, flat,
    away_x, away_y, stay, gq_ref, wp, acc, gs_ref, sums,
):
    i = pl.program_id(0)

    @pl.when(i == 0)
    def _():
        for part in range(3):
            wp[part] = w_ref[:, part * WIDE : (part + 1) * WIDE]
        acc[...] = jnp.zeros_like(acc)
        gs_ref[...] = jnp.zeros_like(gs_ref)

    early = (i == 0) | (i == 4) | (i == 6) | (i == 7)
    far = jnp.where(early, f0[0], f1[0])
    kv = own[0].astype(F32) + far.astype(F32)
    parts = [
        pq[0],
        turn_heads(kv[:WIDE], cos[0], -sin[0]).astype(BF),
        kv[WIDE:].astype(BF),
    ]
    n, mk = n_ref[0], mk_ref[0]
    ng = jnp.zeros((CHUNK, n.shape[1]), F32)
    for k in range(3):
        ng += mm(flip(parts[k]), wp[k], 1, 1)
        acc[k * WIDE : (k + 1) * WIDE] += mm(parts[k], n)
    low = ng.astype(BF)

    @pl.when(i < 2)
    def _():
        away_x[0] = low

    @pl.when((i >= 2) & (i < 4))
    def _():
        away_y[0] = low

    @pl.when(i >= 4)
    def _():
        stay[0] = low

    gs_ref[0:1] += jnp.sum(ng * n.astype(F32), axis=0, keepdims=True)
    gs_ref[1:2] += jnp.sum(ng * mk[:, :1].astype(F32), axis=0, keepdims=True)

    @pl.when(i == 7)
    def _():
        by_z(jnp.transpose(acc[...]), gq_ref)
        part = sums.shape[1]
        sums[...] = flat[...]
        for k in range(2):
            for side in range(2):
                to = 14 + 2 * k + side
                sums[to : to + 1] = gs_ref[k : k + 1, side * part : (side + 1) * part]
        tail = sums[...].astype(BF)
        rows = gq_ref.shape[1] - 24
        for zz in range(4):
            gq_ref[zz, rows:] = jnp.zeros((24, gq_ref.shape[2]), BF)
            gq_ref[zz, rows:, :part] = tail


def pick(order):
    def slot_of(i):
        slot = jnp.int32(order[-1])
        for k in range(len(order) - 2, -1, -1):
            slot = jnp.where(i == k, order[k], slot)
        return slot

    return slot_of


def project_back(own, far, pq, n, mk, cos, sin, w, flat):
    dim = n.shape[2]
    wide = w.shape[1] + HEAD_DIM
    slot = pick((2, 6, 5, 7, 0, 4, 1, 3))

    def block(rows, cols, index):
        return pl.BlockSpec((1, rows, cols), lambda i: (index(i), 0, 0))

    def whole(*shape):
        return pl.BlockSpec(shape, lambda i: tuple(0 for _ in shape))

    return pl.pallas_call(
        project_back_body,
        grid=(8,),
        out_shape=(
            jax.ShapeDtypeStruct((2, CHUNK, dim), BF),
            jax.ShapeDtypeStruct((2, CHUNK, dim), BF),
            jax.ShapeDtypeStruct((4, CHUNK, dim), BF),
            jax.ShapeDtypeStruct((4, dim // 4 + 24, wide), BF),
        ),
        in_specs=[
            block(2 * WIDE, CHUNK, slot),
            *[block(2 * WIDE, CHUNK, lambda i: slot(i) % 4)] * 2,
            block(WIDE, CHUNK, slot),
            block(CHUNK, dim, slot), block(CHUNK, 128, slot),
            block(HALF, CHUNK, slot), block(HALF, CHUNK, slot), whole(*w.shape), whole(*flat.shape),
        ],
        out_specs=(
            block(CHUNK, dim, lambda i: jnp.minimum(i, 1)),
            block(CHUNK, dim, lambda i: jnp.clip(i - 2, 0, 1)),
            block(CHUNK, dim, lambda i: jnp.clip(i - 4, 0, 3)),
            whole(4, dim // 4 + 24, wide),
        ),
        scratch_shapes=[
            pltpu.VMEM((3, dim, WIDE), BF),
            pltpu.VMEM((wide, dim), F32),
            pltpu.VMEM((8, dim), F32),
            pltpu.VMEM(flat.shape, F32),
        ],
        compiler_params=pltpu.CompilerParams(vmem_limit_bytes=56 * 2**20),
        cost_estimate=pl.CostEstimate(
            flops=1 + 4 * 8 * CHUNK * dim * 3 * WIDE // COST, bytes_accessed=1, transcendentals=0
        ),
    )(own, *far, pq, n, mk, cos, sin, w, flat)


def last_body(load, meta, gain, embed, x_ref, mg_ref, keep_ref, far_ref, o_ref):
    load([])

    @pl.loop(0, 2)
    def _(stream):
        ng = jnp.where(stream == meta[1], keep_ref[...], far_ref[...].astype(F32))
        x, flag = unmark(x_ref[stream], embed[...])
        hat, scale = norm_parts(x)
        t = ng * gain[...]
        t_mean = jnp.mean(t, axis=-1, keepdims=True)
        t_hat = jnp.mean(t * hat, axis=-1, keepdims=True)
        grad = mg_ref[stream].astype(F32) + scale * (t - t_mean - hat * t_hat)
        o_ref[stream] = jnp.where(flag, 0.0, grad).astype(BF)


def finish_body(load, meta, gain, embed, x_ref, up_own, up_far, *refs):
    gd_refs, (gq_ref, go_ref, gu_ref, gd_ref, bu_ref, rows_ref, sums) = refs[:4], refs[4:]
    load([])
    r, c, z = meta[0], meta[1], meta[3]
    own = 4 * r + z
    small = gq_ref.shape[0]
    for h in range(4):
        part = x_ref[2 * h, :small].astype(F32) + x_ref[2 * h + 1, :small].astype(F32)
        for k in range(3):
            first = k * 4 * WIDE + h * WIDE
            gq_ref[:, first : first + WIDE] = part[:, k * WIDE : (k + 1) * WIDE]
    total = add(gd_refs[0][...], gd_refs[1][...])
    gd_ref[...] = total + add(gd_refs[2][...], gd_refs[3][...])

    rows = up_own[...].astype(F32)
    mine = [jnp.where(c == 0, rows[48 * q : 48 * q + 24], rows[48 * q + 24 : 48 * q + 48]) for q in range(3)]
    go_ref[...] = mine[2] + up_far[2].astype(F32)
    part = gu_ref.shape[1] // 8
    for q in range(2):
        for side in range(2):
            lanes = slice(side * part, (side + 1) * part)
            for core, block in ((c, mine[q]), (1 - c, up_far[q].astype(F32))):
                first = pl.multiple_of((2 * (2 * q + side) + core) * part, 128)
                gu_ref[:, pl.ds(first, part)] = block[:, lanes]

    total = x_ref[0, small:, :part].astype(F32)
    for d in range(1, 8):
        total += x_ref[d, small:, :part].astype(F32)
    sums[...] = total

    def pair(i):
        return total[8 + 2 * i : 10 + 2 * i]

    def over(v):
        return jnp.sum(v, keepdims=True) * (1.0 / (2 * part))

    centered = embed[...] - over(embed[...])
    scale = lax.rsqrt(over(centered * centered) + EPSILON)
    hat = centered * scale
    t = pair(4) * gain[...]
    sums[12:14] = pair(2) + scale * (t - over(t) - hat * over(t * hat))
    sums[14:16] = pair(3) / gain[...]
    row = sums[pl.ds(own // 4, 1)]
    bu_ref[...] = pltpu.roll(row, (4 * 96 - own % 4 * 96) % part, 1)[:, :96]
    shift = (16 * 24 - own % 16 * 24) % part
    for i in range(4):
        row = sums[pl.ds(8 + 2 * i + own // 16, 1)]
        rows_ref[i : i + 1] = pltpu.roll(row, shift, 1)[:, :24]


def cut(v, index, size, axis=0):
    return lax.dynamic_slice_in_dim(v, index * size, size, axis)


def at(v, index, axis=0):
    return lax.dynamic_index_in_dim(v, index, axis, keepdims=False)


def after(value, *needed):
    return lax.optimization_barrier((value, *needed))[0]


def add(a, b):
    return a.astype(F32) + b.astype(F32)


def exchange(v):
    return lax.all_to_all(v, "ctx", 0, 0, tiled=True)


def exchange_chips(v):
    groups = [[i + core for i in range(0, 8, 2)] for core in range(2)]
    return lax.all_to_all(v, "ctx", 0, 0, axis_index_groups=groups, tiled=True)


def exchange_z(v):
    return lax.all_to_all(v, "fsdp", 0, 0, tiled=True)


def shards_by_heads(
    hidden,
    noise_mask,
    doc_lengths,
    w_qkv,
    w_out,
    w_up,
    b_up,
    w_down,
    b_down,
    gain_one,
    gain_two,
    mask_embed,
    out_grad,
):
    r = lax.axis_index("ctx")
    z = lax.axis_index("fsdp")
    c, h = r & 1, r >> 1
    dim = hidden.shape[3]
    hid = w_up.shape[1]
    part = hid // 8
    total = CHUNK * 8
    clean = c == 0

    share = pack_share(jnp.stack([r, c, h, z]).astype(jnp.int32), w_out, w_down, w_up)
    ff_t = lax.all_gather(share, "fsdp")
    hidden = after(hidden, share)

    noisy = jnp.where(noise_mask[0][:, None] == 1, jnp.asarray(jnp.inf, BF), hidden[0, 1])
    mine = jnp.where(clean, hidden[0, 0], noisy)
    other = swap(jnp.where(clean, noisy, hidden[0, 0]), 1)
    mine_x, mine_y = swap(mine, 2), swap(mine, 4)
    other_x, other_y = swap(other, 2), swap(other, 4)
    marked = jnp.stack([hidden[0, 0], noisy])

    lengths = doc_lengths[0]
    index = jnp.arange(lengths.shape[0])
    ends = jnp.sum(jnp.where(index[None, :] <= index[:, None], lengths[None, :], 0), axis=1)
    place = jnp.arange(total, dtype=jnp.int32)
    later = ends[None, :] > place[:, None]
    start = jnp.max(jnp.where(later, 0, ends[None, :]), axis=1)
    stop = jnp.min(jnp.where(later, ends[None, :], total), axis=1)
    block = place // BLOCK * BLOCK
    limit = jnp.minimum(block + BLOCK, stop)
    bounds = jnp.stack(
        [start, jnp.where(clean, limit, block), jnp.where(clean, start, jnp.maximum(start, block)), limit]
    )
    bounds = jnp.pad(bounds.reshape(4, 8, CHUNK).transpose(1, 0, 2), ((0, 0), (0, 4), (0, 0)))
    meta = jnp.concatenate(
        [jnp.stack([r, c, h, z]), start[::CHUNK] // CHUNK, start[CHUNK - 1 :: CHUNK]]
    ).astype(jnp.int32)
    slots = (jnp.arange(8) ^ r)[:, None] * CHUNK + jnp.arange(CHUNK)[None, :]
    frequency = jnp.exp(jnp.arange(HALF).astype(F32) * (-2.0 * math.log(10000.0) / HEAD_DIM))
    angles = slots.astype(F32)[:, None, :] * frequency[None, :, None]
    cos, sin = jnp.cos(angles), jnp.sin(angles)
    size = hid // 4 + dim
    w_qkv = after(w_qkv, other)
    small = jnp.concatenate([b_up, b_down, gain_one, gain_two, mask_embed])
    small = jnp.pad(small, (0, 16 * 3 * WIDE - size)).reshape(16, 3 * WIDE)
    own_qkv = jnp.concatenate([cut(w_qkv[:, k * dim : (k + 1) * dim], h, WIDE, 1) for k in range(3)], 1)
    quarter = dim // 4
    half = jnp.concatenate([cut(own_qkv, c, quarter // 2), small])
    half = jnp.broadcast_to(half, (4, *half.shape))
    near = exchange_z(half)
    mine_x, mine_y, other_x, other_y, cos, sin, bounds, meta = lax.optimization_barrier(
        (mine_x, mine_y, other_x, other_y, cos, sin, bounds, meta)
    )
    mine_d, other_d = swap(mine_x, 4), swap(other_y, 2)
    mine_d, other_d, near = lax.optimization_barrier((mine_d, other_d, near))
    far = swap(near, 1)
    small = near[:, quarter // 2 :].reshape(4, -1)[:, :size].astype(F32)
    bias = at(small[:, : hid // 4].reshape(4, 2, part), c, 1).reshape(1, 4 * part)
    b_down_all, gain_a, gain_b, embed = [
        small[:, hid // 4 + k * quarter : hid // 4 + (k + 1) * quarter].reshape(1, dim)
        for k in range(4)
    ]

    grads = out_grad[0]
    grad_rows = grads.reshape(2 * CHUNK, dim)

    ff_r = jnp.take(ff_t, (z - jnp.arange(1, 4)) % 4, axis=0)
    far, ff_r = lax.optimization_barrier((far, ff_r))
    shares = (ff_r, swap(ff_r, 2), swap(ff_r, 4), swap(ff_r, 6))
    rows = (mine, other, mine_x, other_x, mine_y, other_y, mine_d, other_d)
    q, *kv, normed_one, marks, w_all = project_rows(meta, gain_a, embed, cos, sin, rows, (near, far))
    give = [(i, i + 1) for i in range(0, 8, 2)]
    heads = (q, *kv, *[lax.ppermute(v, "ctx", give) for v in kv])
    send, attended, stats = attend_rows(meta, bounds, heads)
    send, *shares = lax.optimization_barrier((send, *shares))
    grad_far = swap(after(grad_rows, kv[0]), 1)
    heads_late = lax.optimization_barrier((*heads, send))[:5]
    rows_first = rows_of_heads(heads_late)
    got, *rows_first = lax.optimization_barrier((exchange(send), *rows_first))
    middle, normed, att, w_out_all = middle_rows(meta, gain_b, embed, marked, got, w_out, shares)
    out_own, out_far, ng_far, ng_own, gbu, gd, gu = feed_rows(
        meta, bias, (normed, swap(normed, 1), grad_rows, grad_far, w_up, w_down, *shares)
    )
    ng_far, out_far = swap(ng_far, 1), swap(out_far, 1)
    gd = lax.psum_scatter(gd.reshape(-1, dim), "fsdp", scatter_dimension=0, tiled=True)

    layer, mid_grad, sums, send = middle_back(
        meta, gain_b, b_down_all, (middle, ng_own, out_own, out_far, ng_far, grads, marked, w_out_all)
    )
    got = exchange(send)
    up_out = call(
        out_grad_body,
        [((4, part // 4 + dim // 16, dim), BF)] * 4,
        "SVVA",
        (meta, att, mid_grad, gu),
        flops=4 * CHUNK * dim * dim,
    )
    gbu = gbu.reshape(4, 1, part)
    gbu = jnp.where(clean, jnp.concatenate([gbu, 0 * gbu], 1), jnp.concatenate([0 * gbu, gbu], 1))
    flat = jnp.concatenate([gbu.reshape(8, part), sums[:3].reshape(6, part), jnp.zeros((10, part), F32)])
    got, flat, *up_out = lax.optimization_barrier((got, flat, *up_out))
    up_out = [up_out[0]] + [swap(up_out[k], 2 * k) for k in range(1, 4)]
    pq, own_kv, *far_kv = attend_back(meta, bounds, cos, sin, attended, stats, heads, rows_first, got)
    far_kv = [lax.ppermute(v, "ctx", [(b, a) for a, b in give]) for v in far_kv]

    *up_out, _ = lax.optimization_barrier((*up_out, pq))
    up_out = (add(up_out[0], up_out[1]) + add(up_out[2], up_out[3])).astype(BF).reshape(-1, dim)
    gd = after(gd, pq).reshape(4, part // 4, dim)
    *far_kv, up_out, gd = lax.optimization_barrier((*far_kv, up_out, gd))
    up_out = lax.psum_scatter(up_out, "fsdp", scatter_dimension=0, tiled=True)

    away_x, away_y, stay, gq = project_back(
        own_kv, far_kv, pq, normed_one, marks, cos, sin, w_all, flat
    )
    in_x, in_y = swap(away_x, 2), swap(away_y, 4)
    wide = gq.shape[2]
    rows = dim // 4
    gq = gq.reshape(-1, wide)
    gq = lax.psum_scatter(gq, "fsdp", scatter_dimension=0, tiled=True)
    over_y, over_x = add(stay[1], in_x[1]).astype(BF), add(stay[3], in_y[1]).astype(BF)
    near_one, near_two = swap(over_y, 4), swap(over_x, 2)
    gd = after(gd, over_y, over_x)
    gd = [gd[0]] + [swap(gd[k], 2 * k) for k in range(1, 4)]
    gq = after(gq, over_y, over_x)
    flat = jnp.broadcast_to(gq[rows:], (8, 24, wide))
    gq = jnp.concatenate([gq[:rows].reshape(8, dim // 32, wide), flat], 1)
    near_one, near_two, gq = lax.optimization_barrier((near_one, near_two, gq))
    gq = exchange(gq)
    keep = add(stay[0], in_x[0]) + near_one.astype(F32)
    pair = (add(stay[2], in_y[0]) + near_two.astype(F32)).astype(BF)
    pair = swap(pair, 1)
    *gd, gq = lax.optimization_barrier((*gd, gq, keep, pair))[:5]
    (input_grad,) = call(
        last_body,
        [((2, CHUNK, dim), BF)],
        "S" + "V" * 6,
        (meta, gain_a, embed, marked, mid_grad, keep, pair),
        moved=10 * CHUNK * dim,
    )

    up_sum = after(up_out, input_grad)
    up_out = up_sum.reshape(3, 2, dim // 32, dim)
    up_far = swap(at(up_out, 1 - c, 1), 1)
    small = dim // 32
    gq, go, gu, gd, gbu, rows = call(
        finish_body,
        [
            ((small, 3 * dim), F32),
            ((small, dim), F32),
            ((small, hid), F32),
            ((part // 4, dim), F32),
            ((1, hid // 32), F32),
            ((4, small), F32),
        ],
        "S" + "V" * 9,
        (meta, gain_a.reshape(2, part), embed.reshape(2, part), gq, up_sum, up_far, *gd),
        scratch=[pltpu.VMEM((24, part), F32)],
        moved=8 * dim * dim,
    )
    return (
        layer[None],
        input_grad[None],
        gq,
        go,
        gu,
        gbu[0],
        gd,
        rows[1],
        rows[3],
        rows[0],
        rows[2],
    )


def solution(mesh):
    plain = (mesh.shape["ctx"], mesh.shape["fsdp"]) != (8, 4)
    placed = (
        P("fsdp", None, "ctx", None),
        P("fsdp", "ctx"),
        P("fsdp", None),
        P("fsdp", None),
        P("fsdp", None),
        P("fsdp", None),
        P("fsdp"),
        P("fsdp", None),
        P("fsdp"),
        P("fsdp"),
        P("fsdp"),
        P("fsdp"),
        P("fsdp", None, "ctx", None),
    )
    return jax.shard_map(
        shards if plain else shards_by_heads,
        mesh=mesh,
        in_specs=placed,
        out_specs=(
            P("fsdp", None, "ctx", None),
            P("fsdp", None, "ctx", None),
            P(("ctx", "fsdp"), None),
            P(("ctx", "fsdp"), None),
            P(("ctx", "fsdp"), None),
            P(("ctx", "fsdp")),
            P(("ctx", "fsdp"), None),
            P(("ctx", "fsdp")),
            P(("ctx", "fsdp")),
            P(("ctx", "fsdp")),
            P(("ctx", "fsdp")),
        ),
        check_vma=False,
    )
```
